32 devices in a mesh: ctx: 4 (over y, x), mp: 8 (over z, core).
Axes of the slice: x: 2, y: 2, z: 4, core: 2. Of those that a mesh axis runs over, the one named last changes fastest.
Arguments:
- tokens: bfloat16 [768, 8192], P('ctx'), may hold values from -120 to 120
- norm_gain: float32 [8192], replicated, may hold values from 0.1 to 1.9
- in_weight: bfloat16 [8192, 3, 8192], P(None, None, 'mp'), may hold values from -0.0625 to 0.0625
- short_filter: float32 [3, 3, 8192], P(None, None, 'mp'), may hold values from -3 to 3
- rates: float32 [16, 8192], P(None, 'mp'), may hold values from 0.00013020834 to 0.020833334
- residues: float32 [16, 8192], P(None, 'mp'), may hold values from -4 to 4
- skip: float32 [8192], P('mp'), may hold values from -4 to 4
- out_weight: bfloat16 [8192, 8192], P('mp'), may hold values from -0.09375 to 0.09375
- segment_ids: int32 [768], replicated, may hold values from 0 to 3, never falling along the last dimension, each value on 1 to 576 neighbouring positions
Outputs:
- mixed: bfloat16 [768, 8192], P('ctx', 'mp')
The draws below stay inside these ranges and needn't reach their ends.
Inputs may be any that keep to these rules, and one draw needn't show every extreme that they name: `segment_ids`: never falls along the sequence; each document spans 1 to 576 positions.
All inputs are finite; a program needn't handle non-finite values.
Results may differ from the reference program's by a relative error of at most 0.0085.
Values may be sent and summed in bfloat16 or wider, within the bound.
No kernel may reach another device: no remote copies, remote signals or barrier semaphores. Data moves between devices by JAX's collectives and lax.ppermute only.
A program may use at most 192 MiB of HBM per device.

```python
import math
import jax
import jax.numpy as jnp
import numpy as np
from jax import lax

D = 8192
ORDER = 16
KSHORT = 3
TOK_DEV = 192
SEQ = 768
N_CTX = 4


def draw_tokens(key, part):
    key_rows, key_columns, key_values = jax.random.split(jax.random.fold_in(key, 11), 3)
    row_scale = jnp.exp(jax.random.uniform(key_rows, (SEQ, 1), minval=0.0, maxval=jnp.log(10.0)))
    column_scale = jnp.exp(jax.random.uniform(key_columns, (1, D), minval=jnp.log(0.3), maxval=jnp.log(3.0)))
    base = jnp.clip(jax.random.normal(key_values, (SEQ, D)), -4.0, 4.0)
    return (base * row_scale * column_scale).astype(jnp.float32).astype(jnp.bfloat16)


def spiked(values, rng, source, target, parts, factor):
    owner, partner = [(jnp.arange(values.shape[axis_at]) // (values.shape[axis_at] // parts)).reshape([-1 if axis == axis_at else 1 for axis in range(values.ndim)]) for axis_at in (source, target)]
    chosen = jax.random.permutation(rng, parts)[partner]
    strong = (owner == chosen) | (owner == (partner + parts // 2) % parts)
    return jnp.where(strong, factor * values, values)


def levels(key, extent, shards, least, high):
    loudness, own = 1.0, jax.random.fold_in(key, 6)
    for position, shards_of in shards:
        steps = jnp.exp(jax.random.uniform(jax.random.fold_in(own, position), (shards_of,), jnp.float32, least / len(shards), high / len(shards)))
        loudness = loudness * jnp.repeat(steps, extent[position] // shards_of).reshape([-1 if axis == position else 1 for axis in range(len(extent))])
    return loudness


def profile(number_of, total, limit, lean):
    loads = [(1 << 20) // math.isqrt(rank ** lean) + 1 for rank in range(2, number_of + 1)]
    surplus, holding = total - limit - (number_of - 1), [1] * (number_of - 1)
    while surplus > 0:
        candidates = [i for i in range(number_of - 1) if holding[i] < limit]
        mass, left = sum([loads[i] for i in candidates]), surplus
        for i in candidates:
            addition = min(limit - holding[i], max(1, left * loads[i] // mass), surplus)
            holding[i] = holding[i] + addition
            surplus = surplus - addition
    return np.array([limit] + holding)


def ragged_sizes(stream_key, amount, total, reach, lean):
    if amount == 2:
        one = jax.random.randint(stream_key, (), max(1, total - reach), min(reach, total - 1) + 1)
        return jnp.stack([one, total - one])
    lengths = jnp.asarray(profile(amount, total, reach, lean), jnp.int32)
    twos = (amount - 1) // 2
    source_of, taker = lengths[1:1 + 2 * twos:2], lengths[2:2 + 2 * twos:2]
    room = jnp.minimum(source_of - 1, reach - taker)
    passed = jax.random.randint(jax.random.fold_in(stream_key, 1), (twos,), 0, 1 << 20) % (room + 1)
    lengths = lengths.at[1:1 + 2 * twos:2].set(source_of - passed).at[2:2 + 2 * twos:2].set(taker + passed)
    return lengths[jax.random.permutation(jax.random.fold_in(stream_key, 2), amount)]


def normal_values(rng, shape, spread, most, pieces=(), held_as=jnp.bfloat16):
    gain = levels(rng, shape, pieces, -0.22, 0.18) if pieces else 1.0
    values = jax.random.normal(rng, shape, jnp.float32) * spread * gain
    return jnp.minimum(jnp.maximum(values, -most), most).astype(held_as)


def heavy_noise(rng, dims, spread, bound, pieces, heavy, kind=jnp.bfloat16):
    result = spread * jax.random.normal(rng, dims, jnp.float32)
    if pieces:
        result = result * levels(rng, dims, pieces, -0.22, 0.18)
    return jnp.clip(spiked(result, jax.random.fold_in(rng, 3), *heavy), -bound, bound).astype(kind)


def setup_inputs(seed: int = 0) -> dict:
    key_of = jax.random.split(jax.random.key(seed), 10)
    tokens = draw_tokens(jax.random.fold_in(key_of[9], 71), 0)
    norm_gain = jnp.clip(1.0 + 0.18 * jax.random.normal(key_of[1], (D,), jnp.float32), 0.1, 1.9)
    in_weight = normal_values(key_of[2], (D, 3, D), D ** -0.5, 0.0625, ((2, 8),))
    short_filter = normal_values(key_of[3], (KSHORT, 3, D), 0.5, 3.0, ((2, 8),), jnp.float32)
    rates = jnp.clip(jnp.exp(math.log(0.020833334) - 5.075174 * jax.random.uniform(key_of[4], (ORDER, D), jnp.float32) ** levels(key_of[4], (ORDER, D), ((1, 8),), -0.2, 0.2)), 0.00013020834, 0.020833334)
    residues = normal_values(key_of[5], (ORDER, D), (ORDER ** -0.5), 4.0, ((1, 8),), jnp.float32)
    skip = normal_values(key_of[6], (D,), 1.0, 4.0, ((0, 8),), jnp.float32)
    out_weight = heavy_noise(key_of[7], (D, D), D ** -0.5, 0.09375, ((0, 8),), (0, 1, 8, 2.0))
    segment_ids = jnp.searchsorted(jnp.cumsum(ragged_sizes(key_of[8], N_CTX, SEQ, 3 * TOK_DEV, 1)), jnp.arange(SEQ), side="right").astype(jnp.int32)
    return dict(tokens=tokens, norm_gain=norm_gain, in_weight=in_weight, short_filter=short_filter, rates=rates, residues=residues, skip=skip, out_weight=out_weight, segment_ids=segment_ids)


epsilon = 1e-06

def reference(tokens, norm_gain, in_weight, short_filter, rates, residues, skip, out_weight, segment_ids):
    floats = tokens.astype(jnp.float32)
    mean_square = lax.optimization_barrier(jnp.mean(floats * floats, axis=-1, keepdims=True))
    normed = (floats * lax.rsqrt(mean_square + epsilon) * norm_gain[None, :]).astype(jnp.bfloat16)
    projected = jnp.dot(normed, in_weight.reshape(D, 3 * D), preferred_element_type=jnp.float32)
    projected = projected.astype(jnp.bfloat16).reshape(SEQ, 3, D)
    featured = jnp.zeros((SEQ, 3, D), jnp.float32)
    for lag_index in range(KSHORT):
        lagged = jnp.concatenate([jnp.zeros((lag_index, 3, D), jnp.bfloat16), projected[:SEQ - lag_index]], axis=0)
        lagged_ids = jnp.concatenate([jnp.full((lag_index,), -1, jnp.int32), segment_ids[:SEQ - lag_index]], axis=0)
        matches = segment_ids == lagged_ids
        term = short_filter[lag_index][None] * lagged.astype(jnp.float32)
        featured = featured + jnp.where(matches[:, None, None], term, jnp.zeros_like(term))
    query_part = featured[:, 0]
    key_part = featured[:, 1]
    value_part = featured[:, 2]
    product = key_part * value_part
    decay = jnp.exp(-rates)
    pole_weight = residues * jnp.sqrt(-jnp.expm1(-2.0 * rates))
    keeping = jnp.concatenate([jnp.zeros((1,), bool), segment_ids[1:] == segment_ids[:-1]], axis=0)

    def advance(state, inputs):
        product_row, keep_row = inputs
        state = jnp.where(keep_row, decay * state, jnp.zeros_like(state)) + product_row[None, :]
        return (state, lax.optimization_barrier(jnp.sum(pole_weight * state, axis=0)))
    _, longconv = lax.scan(advance, jnp.zeros((ORDER, D), jnp.float32), (product, keeping))
    gated = (query_part * (longconv + skip[None, :] * product)).astype(jnp.bfloat16)
    return jnp.dot(gated, out_weight, preferred_element_type=jnp.float32).astype(jnp.bfloat16)
```

```python
import functools
import jax
import jax.numpy as jnp
from jax import lax
from jax.experimental import pallas as pl
from jax.experimental.pallas import tpu as pltpu
from jax.sharding import PartitionSpec as P

epsilon = 1e-06
f32 = jnp.float32
bf16 = jnp.bfloat16

PARTS = 8
HEAD = 16


def vmem():
    return pl.BlockSpec(memory_space=pltpu.VMEM)


def smem():
    return pl.BlockSpec(memory_space=pltpu.SMEM)


def same_id(ids_ref, a, b):
    def get(t):
        return jnp.where(t < 0, -1, ids_ref[jnp.maximum(t, 0)])

    return (get(a) == get(b)).astype(f32)


def front_kernel(
    geometry, position, ids_ref, tokens_ref, gain_ref, weight_ref, taps_ref, rates_ref, pole_ref, skip_ref, ids2_ref,
    query_out, local_out, state_out, block_out, visible_out,
    tok, normed, ring, total, proj, prod, head, idcol, near, same, tok_sem, ring_sem,
):
    T, depth, channels, cb_size, kc_size, slots, poles = geometry
    run = T // PARTS
    kcs, cbs = depth // kc_size, channels // cb_size
    steps = kcs * cbs
    base = pl.multiple_of(position[0] * T, 8)

    def fetch(step):
        cb, kc, slot = step // kcs, step % kcs, step % slots
        return pltpu.make_async_copy(
            weight_ref.at[:, pl.ds(pl.multiple_of(kc * kc_size, kc_size), kc_size),
                          pl.ds(pl.multiple_of(cb * cb_size, cb_size), cb_size)],
            ring.at[slot], ring_sem.at[slot])

    tok_copy = pltpu.make_async_copy(tokens_ref, tok, tok_sem)
    tok_copy.start()
    for s in range(min(slots, steps)):
        fetch(s).start()

    idcol[0:8, :] = jnp.full((8, 128), -1.0, f32)
    for b in range(ids2_ref.shape[0]):
        row = ids2_ref[b : b + 1, :].astype(f32)
        idcol[8 + b * 128 : 8 + (b + 1) * 128, :] = jnp.broadcast_to(row, (128, 128)).T
    near[...] = idcol[pl.ds(base, T + 8), :]
    same[0] = (near[8 : 8 + T, :] == near[7 : 7 + T, :]).astype(f32)
    same[1] = (near[8 : 8 + T, :] == near[6 : 6 + T, :]).astype(f32)
    before = near[pl.ds(7, PARTS, stride=run), :]
    for i in range(run):
        visible_out[i * 8 : (i + 1) * 8, :] = (near[pl.ds(8 + i, PARTS, stride=run), :] == before).astype(f32)
    for i in range(3):
        proj[i, 0:8, :] = jnp.zeros((8, cb_size), f32)
    head[...] = jnp.zeros(head.shape, f32)
    tok_copy.wait()

    def norm_rows(g, _):
        rows = pl.ds(pl.multiple_of(g * 16, 16), 16)
        x = tok[rows, :].astype(f32)
        scale = lax.rsqrt(jnp.sum(x * x, axis=-1, keepdims=True) * (1.0 / depth) + epsilon)
        normed[rows, :] = (x * scale * gain_ref[...]).astype(bf16)
        return 0

    lax.fori_loop(0, T // 16, norm_rows, 0)

    def epilogue(cb):
        cols = pl.ds(pl.multiple_of(cb * cb_size, cb_size), cb_size)
        feats = []
        m1 = jnp.concatenate([same[0]] * (cb_size // 128), axis=1)
        m2 = jnp.concatenate([same[1]] * (cb_size // 128), axis=1)
        for i in range(3):
            p = total[i].astype(bf16).astype(f32)
            proj[i, 8 : 8 + T, :] = p
            tap = [taps_ref[j, i : i + 1, cols] for j in range(3)]
            feats.append(
                tap[0] * p + m1 * (tap[1] * proj[i, 7 : 7 + T, :]) + m2 * (tap[2] * proj[i, 6 : 6 + T, :]))
        query_out[:, cols] = feats[0]
        for i in range(1, 3):
            head[2 * (i - 1) : 2 * i, :] = proj[i, 8:10, :]
        for i in range(3):
            head[4 + 2 * i : 6 + 2 * i, :] = proj[i, 6 + T : 8 + T, :]
        block_out[poles : poles + HEAD, cols] = head[...].astype(bf16)
        for lane in range(cb_size // 128):
            prod[lane] = feats[1][:, lane * 128 : lane * 128 + 128] * feats[2][:, lane * 128 : lane * 128 + 128]
        for lane in range(cb_size // 128):
            tile = cb * (cb_size // 128) + lane
            lanes = pl.ds(pl.multiple_of(cb * cb_size + lane * 128, 128), 128)
            d16 = jnp.exp(-rates_ref[:, lanes])
            w16 = pole_ref[:, lanes]
            decay = [jnp.broadcast_to(d16[n : n + 1], (8, 128)) for n in range(poles)]
            weight = [jnp.broadcast_to(w16[n : n + 1], (8, 128)) for n in range(poles)]
            skip = skip_ref[0:1, lanes]

            def token(i, states):
                p = prod[lane, pl.ds(i, PARTS, stride=run), :]
                keep = same[0, pl.ds(i, PARTS, stride=run), :]
                acc = skip * p
                after = []
                for n in range(poles):
                    s = states[n] * decay[n] * keep + p
                    acc = acc + weight[n] * s
                    after.append(s)
                local_out[tile, pl.ds(i, PARTS, stride=run), :] = acc
                return tuple(after)

            states = lax.fori_loop(0, run, token, tuple(jnp.zeros((8, 128), f32) for _ in range(poles)))
            for n in range(poles):
                state_out[tile, pl.ds(n, PARTS, stride=poles), :] = states[n]
            jump = jnp.exp(-rates_ref[:, lanes] * float(run))
            end = state_out[tile, 0:poles, :]
            for s in range(1, PARTS):
                whole = same_id(ids_ref, base + s * run + run - 1, base + s * run - 1)
                end = end * (jump * whole) + state_out[tile, s * poles : (s + 1) * poles, :]
            block_out[0:poles, lanes] = end.astype(bf16)

    def step_body(step, _):
        cb, kc, slot = step // kcs, step % kcs, step % slots
        fetch(step).wait()
        lhs = normed[:, pl.ds(pl.multiple_of(kc * kc_size, kc_size), kc_size)]
        for i in range(3):
            part = jnp.dot(lhs, ring[slot, i], preferred_element_type=f32)
            total[i] = jnp.where(kc == 0, part, total[i] + part)

        @pl.when(step + slots < steps)
        def _():
            fetch(step + slots).start()

        @pl.when(kc == kcs - 1)
        def _():
            epilogue(cb)

        return 0

    total[...] = jnp.zeros(total.shape, f32)
    lax.fori_loop(0, steps, step_body, 0)


def front(position, ids, tokens, gain, weight3, taps, rates, pole_weight, skip):
    T, depth = tokens.shape
    channels, poles = weight3.shape[2], rates.shape[0]
    cb_size, kc_size, slots = 256, 2048, 5
    geometry = (T, depth, channels, cb_size, kc_size, slots, poles)
    return pl.pallas_call(
        functools.partial(front_kernel, geometry),
        out_shape=(
            jax.ShapeDtypeStruct((T, channels), f32),
            jax.ShapeDtypeStruct((channels // 128, T, 128), f32),
            jax.ShapeDtypeStruct((channels // 128, PARTS * poles, 128), f32),
            jax.ShapeDtypeStruct((poles + HEAD, channels), bf16),
            jax.ShapeDtypeStruct((T, 128), f32),
        ),
        in_specs=[smem(), smem(), pl.BlockSpec(memory_space=pl.ANY), vmem(),
                  pl.BlockSpec(memory_space=pl.ANY)] + [vmem()] * 5,
        out_specs=[vmem()] * 5,
        scratch_shapes=[
            pltpu.VMEM((T, depth), bf16),
            pltpu.VMEM((T, depth), bf16),
            pltpu.VMEM((slots, 3, kc_size, cb_size), bf16),
            pltpu.VMEM((3, T, cb_size), f32),
            pltpu.VMEM((3, T + 8, cb_size), f32),
            pltpu.VMEM((cb_size // 128, T, 128), f32),
            pltpu.VMEM((HEAD, cb_size), f32),
            pltpu.VMEM((ids.shape[0] + 8, 128), f32),
            pltpu.VMEM((T + 8, 128), f32),
            pltpu.VMEM((2, T, 128), f32),
            pltpu.SemaphoreType.DMA,
            pltpu.SemaphoreType.DMA((slots,)),
        ],
        compiler_params=pltpu.CompilerParams(vmem_limit_bytes=40 << 20),
        name="front",
    )(position, ids, tokens, gain, weight3, taps, rates, pole_weight, skip, ids.reshape(-1, 128))


def first_products(first, last, taps, ids_ref, base):
    s01, s0m1 = same_id(ids_ref, base + 1, base), same_id(ids_ref, base, base - 1)
    s0m2, s1m1 = same_id(ids_ref, base, base - 2), same_id(ids_ref, base + 1, base - 1)

    def shift(i):
        near, far = last[i][1:2], last[i][0:1]
        t1, t2 = taps[1][i : i + 1], taps[2][i : i + 1]
        return s0m1 * (t1 * near) + s0m2 * (t2 * far), s1m1 * (t2 * near)

    def plain(i):
        t0, t1 = taps[0][i : i + 1], taps[1][i : i + 1]
        return t0 * first[i][0:1], t0 * first[i][1:2] + s01 * (t1 * first[i][0:1])

    k, v, dk, dv = plain(1), plain(2), shift(1), shift(2)
    delta = [(k[j] + dk[j]) * (v[j] + dv[j]) - k[j] * v[j] for j in range(2)]
    return shift(0), delta


def unpack(block, poles):
    first = [None, block[poles : poles + 2], block[poles + 2 : poles + 4]]
    last = [block[poles + 4 + 2 * i : poles + 6 + 2 * i] for i in range(3)]
    return block[0:poles], first, last


def joined_state(low_state, low_last, up_state, up_first, taps, rates, ids_ref, base, length):
    _, delta = first_products(up_first, low_last, taps, ids_ref, base)
    grown = low_state + delta[0] * jnp.exp(rates) + delta[1] * jnp.exp(2.0 * rates)
    open_ = same_id(ids_ref, base + length - 1, base - 1)
    return up_state + grown * (jnp.exp(-rates * jnp.float32(length)) * open_)


def join_kernel(T, poles, span, position, ids_ref, mine_ref, other_ref, taps_ref, rates_ref, out):
    me = position[0]
    is_upper = (me // span) % 2 == 1
    base = (me // (2 * span)) * (2 * span * T) + span * T
    mine, other = mine_ref[...].astype(f32), other_ref[...].astype(f32)
    lower, upper = jnp.where(is_upper, other, mine), jnp.where(is_upper, mine, other)
    taps = [taps_ref[j] for j in range(3)]
    low_state, low_first, low_last = unpack(lower, poles)
    up_state, up_first, up_last = unpack(upper, poles)
    state = joined_state(low_state, low_last, up_state, up_first, taps, rates_ref[...], ids_ref, base, span * T)
    out[0:poles, :] = state.astype(bf16)
    row = lax.broadcasted_iota(jnp.int32, (HEAD, lower.shape[1]), 0)
    out[poles : poles + HEAD, :] = jnp.where(row < 4, lower[poles:], upper[poles:]).astype(bf16)


def join(span, T, position, ids, mine, other, taps, rates):
    poles = rates.shape[0]
    return pl.pallas_call(
        functools.partial(join_kernel, T, poles, span),
        out_shape=jax.ShapeDtypeStruct(mine.shape, bf16),
        in_specs=[smem(), smem()] + [vmem()] * 4,
        out_specs=vmem(),
        name="join",
    )(position, ids, mine, other, taps, rates)


def gate_kernel(
    T, poles, spans, position, ids_ref, query_ref, local_ref, state_ref, block_ref, visible_ref, taps_ref, rates_ref,
    pole_ref, skip_ref, *rest,
):
    arrived, (gated_out, carry, full) = rest[: len(spans)], rest[len(spans) :]
    run = T // PARTS
    tiles = query_ref.shape[1] // 128
    me = position[0]
    base = me * T
    taps = [taps_ref[j] for j in range(3)]
    rates, weight, skip = rates_ref[...], pole_ref[...], skip_ref[...]
    prior = jnp.zeros(block_ref.shape, f32)
    prior_state, prior_first, prior_last = unpack(prior, poles)
    for span, ref in zip(spans, arrived):
        state, first, last = unpack(ref[...].astype(f32), poles)
        upper, held = (me // span) % 2 == 1, me % span
        if span == 1:
            both = state
        else:
            both = joined_state(
                state, last, prior_state, prior_first, taps, rates, ids_ref, (me - held) * T, held * T)
        fresh = upper & (held == 0)
        prior_state = jnp.where(fresh, state, jnp.where(upper, both, prior_state))
        prior_first = [None] + [jnp.where(upper, first[i], prior_first[i]) for i in (1, 2)]
        prior_last = [jnp.where(fresh, last[i], prior_last[i]) for i in range(3)]
    _, first, _ = unpack(block_ref[...].astype(f32), poles)
    q_shift, delta = first_products(first, prior_last, taps, ids_ref, base)
    second = delta[1] * jnp.exp(rates)
    now = prior_state + (delta[0] + second) * jnp.exp(rates)
    fix0 = skip * delta[0] - jnp.sum(weight * second, axis=0, keepdims=True)
    fix1 = skip * delta[1]
    jump = jnp.exp(-rates * float(run))
    for s in range(PARTS):
        part = slice(s * poles, (s + 1) * poles)
        began = weight * now
        for tile in range(tiles):
            carry[tile, part, :] = began[:, tile * 128 : tile * 128 + 128]
        if s < PARTS - 1:
            whole = same_id(ids_ref, base + s * run + run - 1, base + s * run - 1)
            ends = jnp.concatenate([state_ref[tile, part, :] for tile in range(tiles)], axis=1)
            now = now * (jump * whole) + ends

    def lane_body(tile, _):
        lanes = pl.ds(pl.multiple_of(tile * 128, 128), 128)
        d16 = jnp.exp(-rates_ref[:, lanes])
        decay = [jnp.broadcast_to(d16[n : n + 1], (8, 128)) for n in range(poles)]
        start = tuple(carry[tile, pl.ds(n, PARTS, stride=poles), :] for n in range(poles))

        def token(i, states):
            after = [states[n] * decay[n] for n in range(poles)]
            terms = list(after)
            while len(terms) > 1:
                terms = [a + b for a, b in zip(terms[0::2], terms[1::2])] + terms[len(terms) // 2 * 2 :]
            see = visible_ref[pl.ds(pl.multiple_of(i * 8, 8), 8), :]
            at = pl.ds(i, PARTS, stride=run)
            full[tile, at, :] = local_ref[tile, at, :] + see * terms[0]
            return tuple(after)

        lax.fori_loop(0, run, token, start)
        return 0

    lax.fori_loop(0, tiles, lane_body, 0)
    row = lax.broadcasted_iota(jnp.int32, (16, 128), 0)
    for tile in range(tiles):
        lanes = slice(tile * 128, tile * 128 + 128)
        gated_out[:, lanes] = (query_ref[:, lanes] * full[tile]).astype(bf16)
        top_q, top = query_ref[0:16, lanes], full[tile, 0:16, :]
        top_q = top_q + jnp.where(row == 0, q_shift[0][:, lanes], 0.0) + jnp.where(row == 1, q_shift[1][:, lanes], 0.0)
        top = top + jnp.where(row == 0, fix0[:, lanes], 0.0) + jnp.where(row == 1, fix1[:, lanes], 0.0)
        gated_out[0:16, lanes] = (top_q * top).astype(bf16)


def gate(T, spans, arrived, position, ids, query, local_part, state, block, visible, taps, rates, pole_weight, skip):
    poles = rates.shape[0]
    return pl.pallas_call(
        functools.partial(gate_kernel, T, poles, tuple(spans)),
        out_shape=jax.ShapeDtypeStruct(query.shape, bf16),
        in_specs=[smem(), smem()] + [vmem()] * (9 + len(spans)),
        out_specs=vmem(),
        scratch_shapes=[pltpu.VMEM(state.shape, f32), pltpu.VMEM(local_part.shape, f32)],
        name="gate",
    )(position, ids, query, local_part, state, block, visible, taps, rates, pole_weight, skip, *arrived)


def spread_kernel(_, gated_ref, weight_ref, send_out, mine_out):
    step = pl.program_id(0)
    half = pl.num_programs(0) // 2
    part = jnp.dot(gated_ref[...], weight_ref[...], preferred_element_type=f32).astype(bf16)

    @pl.when(step < half)
    def _():
        send_out[...] = part

    @pl.when(step >= half)
    def _():
        mine_out[...] = part


def spread(place, gated, out_weight, width):
    T, channels = gated.shape
    tile = 512
    per = width // tile
    grid_spec = pltpu.PrefetchScalarGridSpec(
        num_scalar_prefetch=1,
        grid=(2 * per,),
        in_specs=[
            pl.BlockSpec((T, channels), lambda s, p: (0, 0)),
            pl.BlockSpec((channels, tile), lambda s, p: (0, p[s // per] * per + s % per)),
        ],
        out_specs=[
            pl.BlockSpec((T, tile), lambda s, p: (0, jnp.minimum(s, per - 1))),
            pl.BlockSpec((T, tile), lambda s, p: (0, jnp.maximum(s - per, 0))),
        ],
    )
    return pl.pallas_call(
        spread_kernel,
        out_shape=(jax.ShapeDtypeStruct((T, width), bf16),) * 2,
        grid_spec=grid_spec,
        cost_estimate=pl.CostEstimate(flops=4 * T * channels * width, bytes_accessed=4 * channels * width, transcendentals=0),
        name="spread",
    )(place, gated, out_weight)


def total(*terms):
    return functools.reduce(lambda a, b: a + b, [t.astype(f32) for t in terms]).astype(bf16)


def scatter_line(gated, out_weight, width):
    index = lax.axis_index("mp")
    chip, core = index // 2, index % 2
    order = jnp.array([[3, 2, 1, 0], [3, 2, 0, 1], [0, 1, 3, 2], [0, 1, 2, 3]], jnp.int32)[chip]
    pair = [(m, m ^ 1) for m in range(8)]

    def along(hops):
        return [(a * 2 + c, b * 2 + c) for a, b in hops for c in range(2)]

    ends = along([(0, 1), (3, 2)])
    middle = along([(1, 2), (2, 1)])
    near = along([(0, 1), (1, 0), (2, 3), (3, 2)])
    sums = []
    for k in range(4):
        place = jnp.stack([order[k] * 2 + 1 - core, order[k] * 2 + core]).astype(jnp.int32)
        send, mine = spread(place, gated, out_weight, width)
        sums.append(total(mine, lax.ppermute(send, "mp", pair)))
    first = lax.ppermute(sums[0], "mp", ends)
    second = lax.ppermute(sums[1], "mp", ends)
    across = lax.ppermute(total(sums[0], first), "mp", middle)
    across2 = lax.ppermute(total(sums[1], second), "mp", middle)
    last = lax.ppermute(total(sums[2], across), "mp", near)
    return total(sums[3], across2, last)


def shifted(value, axis, steps):
    count = lax.axis_size(axis)
    leading, last = (max(0, -steps), min(count, count - steps))
    return lax.ppermute(value, axis, [(source, source + steps) for source in range(leading, last)])


def project(block, norm_gain, weights):
    floats = block.astype(jnp.float32)
    mean_square = jnp.mean(floats * floats, axis=-1, keepdims=True)
    normed = (floats * lax.rsqrt(mean_square + epsilon) * norm_gain[None, :]).astype(jnp.bfloat16)
    return jnp.dot(normed, weights, preferred_element_type=jnp.float32).astype(jnp.bfloat16)


def general(
    tokens, norm_gain, in_weight, short_filter, rates, residues, skip, out_weight, segment_ids
):
    tok_rows = tokens.shape[0]
    model_width = tokens.shape[1]
    channels = in_weight.shape[2]
    filter_taps = short_filter.shape[0]
    pole_count = rates.shape[0]
    device_index = lax.axis_index("ctx")
    row_offset = device_index * tok_rows
    weights = in_weight.reshape(model_width, 3 * channels)
    projected = project(tokens, norm_gain, weights)
    previous = shifted(projected[tok_rows - (filter_taps - 1) :], "ctx", 1)
    extended = jnp.concatenate([previous, projected], axis=0)
    padded_ids = jnp.concatenate([jnp.full((filter_taps,), -1, jnp.int32), segment_ids], axis=0)
    window = lax.dynamic_slice_in_dim(padded_ids, row_offset, tok_rows + filter_taps, 0)
    local_ids = window[filter_taps:]
    taps_table = short_filter.reshape(filter_taps, 3 * channels)
    featured = jnp.zeros((tok_rows, 3 * channels), jnp.float32)
    for lag_index in range(filter_taps):
        begin = filter_taps - 1 - lag_index
        lagged = extended[begin : begin + tok_rows].astype(jnp.float32)
        matches = window[filter_taps - lag_index : filter_taps - lag_index + tok_rows] == local_ids
        term = taps_table[lag_index][None, :] * lagged
        featured = featured + jnp.where(matches[:, None], term, jnp.zeros_like(term))
    query_part = featured[:, :channels]
    key_part = featured[:, channels : 2 * channels]
    value_part = featured[:, 2 * channels :]
    product = key_part * value_part
    offsets = jnp.arange(tok_rows, dtype=jnp.float32)
    center = float(tok_rows // 2)
    growth = jnp.exp(-(offsets - center)[:, None, None] * rates[None])
    shrinkage = jnp.exp((offsets - center)[:, None, None] * rates[None])
    weighted = (shrinkage * product[:, None, :]).reshape(tok_rows, pole_count * channels)
    visible = (offsets[:, None] >= offsets[None, :]) & (local_ids[:, None] == local_ids[None, :])
    in_block = jnp.dot(visible.astype(jnp.float32), weighted, precision=lax.Precision.HIGHEST)
    in_block = in_block.reshape(tok_rows, pole_count, channels) * growth
    survives = local_ids == window[filter_taps - 1]
    block_factor = jnp.exp(-rates * tok_rows)
    block_end = in_block[tok_rows - 1]
    block_ends = lax.all_gather(block_end[None], "ctx", axis=0, tiled=True)
    shard_count = segment_ids.shape[0] // tok_rows
    last_ids = segment_ids.reshape(shard_count, tok_rows)[:, tok_rows - 1]
    prior_ids = jnp.concatenate([jnp.full((1,), -1, jnp.int32), last_ids[:-1]], axis=0)
    shard_decays = block_factor[None] * (last_ids == prior_ids).astype(jnp.float32)[:, None, None]

    def absorb(running, inputs):
        shard, factor, shard_end = inputs
        advanced = running * factor + shard_end
        return (jnp.where(shard < device_index, advanced, running), None)

    incoming, _ = lax.scan(
        absorb,
        jnp.zeros_like(block_end),
        (jnp.arange(shard_count, dtype=jnp.int32), shard_decays, block_ends),
    )
    carried = incoming[None] * jnp.exp(-(offsets + 1.0)[:, None, None] * rates[None])
    carried = carried * survives.astype(jnp.float32)[:, None, None]
    states = in_block + carried
    pole_weight = residues * jnp.sqrt(-jnp.expm1(-2.0 * rates))
    longconv = jnp.sum(pole_weight[None] * states, axis=1)
    gated = (query_part * (longconv + skip[None, :] * product)).astype(jnp.bfloat16)
    partial_terms = jnp.dot(gated, out_weight, preferred_element_type=jnp.float32)
    return lax.psum_scatter(partial_terms, "mp", scatter_dimension=1, tiled=True).astype(
        jnp.bfloat16
    )


def local(tokens, norm_gain, in_weight, short_filter, rates, residues, skip, out_weight, segment_ids):
    T = tokens.shape[0]
    shards = lax.axis_size("ctx")
    me = lax.axis_index("ctx")
    position = me.astype(jnp.int32)[None]
    weight3 = jnp.transpose(in_weight, (1, 0, 2))
    pole_weight = residues * jnp.sqrt(-jnp.expm1(-2.0 * rates))
    skip = skip[None]
    query, local_part, state, block, visible = front(
        position, segment_ids, tokens, norm_gain[None], weight3, short_filter, rates, pole_weight, skip)
    group, span, spans, arrived = block, 1, [], []
    while span < shards:
        final = 2 * span == shards
        hops = [(a, a ^ span) for a in range(shards) if not (final and a & span)]
        other = lax.ppermute(group, "ctx", hops)
        spans.append(span)
        arrived.append(other)
        if not final:
            group = join(span, T, position, segment_ids, group, other, short_filter, rates)
        span *= 2
    gated = gate(T, spans, arrived, position, segment_ids, query, local_part, state, block, visible, short_filter, rates,
                 pole_weight, skip)
    return scatter_line(gated, out_weight, out_weight.shape[1] // lax.axis_size("mp"))


def solution(mesh):
    placed = (
        P("ctx", None),
        P(),
        P(None, None, "mp"),
        P(None, None, "mp"),
        P(None, "mp"),
        P(None, "mp"),
        P("mp"),
        P("mp", None),
        P(),
    )
    shards, groups = mesh.shape["ctx"], mesh.shape["mp"]

    def body(tokens, norm_gain, in_weight, *rest):
        suits = groups == 8 and shards & (shards - 1) == 0 and shards > 1
        suits = suits and in_weight.shape[2] % 512 == 0 and in_weight.shape[0] % 2048 == 0
        suits = suits and tokens.shape[0] % 64 == 0 and rest[-1].shape[0] % 128 == 0 and rest[1].shape[0] % 8 == 0
        return (local if suits else general)(tokens, norm_gain, in_weight, *rest)

    return jax.shard_map(
        body, mesh=mesh, in_specs=placed, out_specs=P("ctx", "mp"), check_vma=False
    )
```

```python
import functools
import jax
import jax.numpy as jnp
from jax import lax
from jax.experimental import pallas as pl
from jax.experimental.pallas import tpu as pltpu
from jax.sharding import PartitionSpec as P

epsilon = 1e-06
f32 = jnp.float32
bf16 = jnp.bfloat16

PARTS = 8
HEAD = 16
MIB = 1 << 20


def vmem():
    return pl.BlockSpec(memory_space=pltpu.VMEM)


def smem():
    return pl.BlockSpec(memory_space=pltpu.SMEM)


def same_id(ids_ref, a, b):
    def get(t):
        return jnp.where(t < 0, -1, ids_ref[jnp.maximum(t, 0)])

    return (get(a) == get(b)).astype(f32)


def hbm():
    return pl.BlockSpec(memory_space=pltpu.HBM)


def front_kernel(
    geometry, position, ids_ref, tokens_ref, gain_ref, weight_ref, taps_ref, rates_ref, residues_ref, skip_ref,
    query_out, prod_out, block_out, keep_out, visible_out, taps, rates, residues, skip,
    ids, gain, tok, normed, ring, total, proj, head, idcol, near, twice, ending, sem, tok_sem, ring_sem,
):
    T, depth, channels, cb_size, kc_size, slots, poles = geometry
    run = T // PARTS
    kcs, cbs = depth // kc_size, channels // cb_size
    steps = kcs * cbs
    base = pl.multiple_of(position[0] * T, 8)

    def fetch(step):
        cb, kc, slot = step // kcs, step % kcs, step % slots
        return pltpu.make_async_copy(
            weight_ref.at[:, pl.ds(pl.multiple_of(kc * kc_size, kc_size), kc_size),
                          pl.ds(pl.multiple_of(cb * cb_size, cb_size), cb_size)],
            ring.at[slot], ring_sem.at[slot])

    small = [
        pltpu.make_async_copy(a, b, sem.at[i])
        for i, (a, b) in enumerate(
            ((ids_ref, ids), (gain_ref, gain), (taps_ref, taps), (rates_ref, rates), (residues_ref, residues),
             (skip_ref, skip)))
    ]
    small[0].start()
    small[1].start()
    tok_copy = pltpu.make_async_copy(tokens_ref, tok, tok_sem)
    tok_copy.start()
    for copy in small[2:]:
        copy.start()
    for s in range(min(slots, steps)):
        fetch(s).start()

    small[0].wait()
    idcol[0:8, :] = jnp.full((8, 128), -1.0, f32)
    for b in range(ids.shape[0]):
        row = ids[b : b + 1, :].astype(f32)
        idcol[8 + b * 128 : 8 + (b + 1) * 128, :] = jnp.broadcast_to(row, (128, 128)).T
    near[...] = idcol[pl.ds(base, T + 8), :]
    here = near[8 : 8 + T, :]
    keep_out[...] = (here == near[7 : 7 + T, :]).astype(f32)
    twice[...] = (here == near[6 : 6 + T, :]).astype(f32)
    ending[...] = (here == near[7 + T : 8 + T, :]).astype(f32)
    before = near[pl.ds(7, PARTS, stride=run), :]
    for i in range(run):
        visible_out[i * 8 : (i + 1) * 8, :] = (near[pl.ds(8 + i, PARTS, stride=run), :] == before).astype(f32)
    for i in range(3):
        proj[i, 0:8, :] = jnp.zeros((8, cb_size), f32)
    head[...] = jnp.zeros(head.shape, f32)
    small[1].wait()
    tok_copy.wait()

    def norm_rows(g, _):
        part = pl.ds(pl.multiple_of(g * 16, 16), 16)
        x = tok[part, :].astype(f32)
        scale = lax.rsqrt(jnp.sum(x * x, axis=-1, keepdims=True) * (1.0 / depth) + epsilon)
        normed[part, :] = (x * scale * gain[...]).astype(bf16)
        return 0

    lax.fori_loop(0, T // 16, norm_rows, 0)
    for copy in small[2:]:
        copy.wait()

    def epilogue(cb):
        cols = pl.ds(pl.multiple_of(cb * cb_size, cb_size), cb_size)
        feats = []
        m1 = jnp.concatenate([keep_out[...]] * (cb_size // 128), axis=1)
        m2 = jnp.concatenate([twice[...]] * (cb_size // 128), axis=1)
        for i in range(3):
            p = total[i].astype(bf16).astype(f32)
            proj[i, 8 : 8 + T, :] = p
            tap = [taps[j, i : i + 1, cols] for j in range(3)]
            feats.append(
                tap[0] * p + m1 * (tap[1] * proj[i, 7 : 7 + T, :]) + m2 * (tap[2] * proj[i, 6 : 6 + T, :]))
        query_out[:, cols] = feats[0]
        for i in range(1, 3):
            head[2 * (i - 1) : 2 * i, :] = proj[i, 8:10, :]
        for i in range(3):
            head[4 + 2 * i : 6 + 2 * i, :] = proj[i, 6 + T : 8 + T, :]
        block_out[poles : poles + HEAD, cols] = head[...].astype(bf16)
        product = feats[1] * feats[2]
        back = 7.0 - lax.broadcasted_iota(jnp.int32, (8, 128), 0).astype(f32)
        for lane in range(cb_size // 128):
            tile = cb * (cb_size // 128) + lane
            lanes = pl.ds(pl.multiple_of(tile * 128, 128), 128)
            prod_out[tile] = product[:, lane * 128 : lane * 128 + 128]
            r16 = rates[:, lanes]
            jump = jnp.exp(-8.0 * r16)
            leap = [jnp.broadcast_to(jump[n : n + 1], (8, 128)) for n in range(poles)]

            def eight(g, sums):
                part = pl.ds(pl.multiple_of(g * 8, 8), 8)
                p = prod_out[tile, part, :] * ending[part, :]
                return tuple(sums[n] * leap[n] + p for n in range(poles))

            sums = lax.fori_loop(
                0, T // 8, eight, tuple(jnp.zeros((8, 128), f32) for _ in range(poles)), unroll=4)
            ends = [
                jnp.sum(sums[n] * jnp.exp(-back * r16[n : n + 1]), axis=0, keepdims=True) for n in range(poles)
            ]
            block_out[0:poles, lanes] = jnp.concatenate(ends, axis=0).astype(bf16)

    def step_body(step, _):
        cb, kc, slot = step // kcs, step % kcs, step % slots
        fetch(step).wait()
        lhs = normed[:, pl.ds(pl.multiple_of(kc * kc_size, kc_size), kc_size)]
        for i in range(3):
            part = jnp.dot(lhs, ring[slot, i], preferred_element_type=f32)
            total[i] = jnp.where(kc == 0, part, total[i] + part)

        @pl.when(step + slots < steps)
        def _():
            fetch(step + slots).start()

        @pl.when(kc == kcs - 1)
        def _():
            epilogue(cb)

        return 0

    total[...] = jnp.zeros(total.shape, f32)
    lax.fori_loop(0, steps, step_body, 0)


def front(position, ids2, tokens, gain, weight3, taps, rates, residues, skip):
    T, depth = tokens.shape
    channels, poles = weight3.shape[2], rates.shape[0]
    cb_size, kc_size, slots = 256, 2048, 5
    geometry = (T, depth, channels, cb_size, kc_size, slots, poles)
    kept = [pltpu.VMEM(a.shape, a.dtype) for a in (taps, rates, residues, skip)]
    ids2, tokens, gain, weight3, taps, rates, residues, skip = [
        pltpu.with_memory_space_constraint(a, pltpu.HBM)
        for a in (ids2, tokens, gain, weight3, taps, rates, residues, skip)
    ]
    return pl.pallas_call(
        functools.partial(front_kernel, geometry),
        out_shape=[
            jax.ShapeDtypeStruct((T, channels), f32),
            jax.ShapeDtypeStruct((channels // 128, T, 128), f32),
            jax.ShapeDtypeStruct((poles + HEAD, channels), bf16),
            jax.ShapeDtypeStruct((T, 128), f32),
            jax.ShapeDtypeStruct((T, 128), f32),
        ] + kept,
        in_specs=[smem()] + [hbm()] * 8,
        out_specs=[vmem()] * 9,
        scratch_shapes=[
            pltpu.VMEM(ids2.shape, ids2.dtype),
            pltpu.VMEM(gain.shape, f32),
            pltpu.VMEM((T, depth), bf16),
            pltpu.VMEM((T, depth), bf16),
            pltpu.VMEM((slots, 3, kc_size, cb_size), bf16),
            pltpu.VMEM((3, T, cb_size), f32),
            pltpu.VMEM((3, T + 8, cb_size), f32),
            pltpu.VMEM((HEAD, cb_size), f32),
            pltpu.VMEM((ids2.shape[0] * 128 + 8, 128), f32),
            pltpu.VMEM((T + 8, 128), f32),
            pltpu.VMEM((T, 128), f32),
            pltpu.VMEM((T, 128), f32),
            pltpu.SemaphoreType.DMA((6,)),
            pltpu.SemaphoreType.DMA,
            pltpu.SemaphoreType.DMA((slots,)),
        ],
        compiler_params=pltpu.CompilerParams(vmem_limit_bytes=28 * MIB),
        name="front",
    )(position, ids2, tokens, gain, weight3, taps, rates, residues, skip)


def expm1(x):
    series = jnp.ones_like(x)
    for k in range(9, 1, -1):
        series = 1.0 + series * x * (1.0 / k)
    return jnp.where(jnp.abs(x) < 0.5, x * series, jnp.exp(x) - 1.0)


def local_kernel(poles, prod_ref, keep_ref, rates_ref, residues_ref, skip_ref, local_out, state_out, pole_out):
    tiles, T, _ = prod_ref.shape
    run = T // PARTS
    pole_out[...] = residues_ref[...] * jnp.sqrt(-expm1(-2.0 * rates_ref[...]))

    def tile_body(tile, _):
        lanes = pl.ds(pl.multiple_of(tile * 128, 128), 128)
        d16 = jnp.exp(-rates_ref[:, lanes])
        w16 = pole_out[:, lanes]
        decay = [jnp.broadcast_to(d16[n : n + 1], (8, 128)) for n in range(poles)]
        weight = [jnp.broadcast_to(w16[n : n + 1], (8, 128)) for n in range(poles)]
        skip = skip_ref[0:1, lanes]

        def token(i, states):
            at = pl.ds(i, PARTS, stride=run)
            p, keep = prod_ref[tile, at, :], keep_ref[at, :]
            after = [states[n] * decay[n] * keep + p for n in range(poles)]
            local_out[tile, at, :] = tree([skip * p] + [weight[n] * after[n] for n in range(poles)])
            return tuple(after)

        states = lax.fori_loop(0, run, token, tuple(jnp.zeros((8, 128), f32) for _ in range(poles)), unroll=2)
        for n in range(poles):
            state_out[tile, pl.ds(n, PARTS, stride=poles), :] = states[n]
        return 0

    lax.fori_loop(0, tiles, tile_body, 0)


def tree(terms):
    while len(terms) > 1:
        terms = [a + b for a, b in zip(terms[0::2], terms[1::2])] + terms[len(terms) // 2 * 2 :]
    return terms[0]


def local_pass(product, keep, rates, residues, skip):
    tiles, T, _ = product.shape
    poles = rates.shape[0]
    return pl.pallas_call(
        functools.partial(local_kernel, poles),
        out_shape=(
            jax.ShapeDtypeStruct(product.shape, f32),
            jax.ShapeDtypeStruct((tiles, PARTS * poles, 128), f32),
            jax.ShapeDtypeStruct(rates.shape, f32),
        ),
        in_specs=[vmem()] * 5,
        out_specs=[vmem()] * 3,
        compiler_params=pltpu.CompilerParams(vmem_limit_bytes=4 * MIB),
        cost_estimate=pl.CostEstimate(flops=6 * T * poles * tiles * 128, bytes_accessed=16 * MIB, transcendentals=0),
        name="local_pass",
    )(product, keep, rates, residues, skip)


def first_products(first, last, taps, ids_ref, base):
    s01, s0m1 = same_id(ids_ref, base + 1, base), same_id(ids_ref, base, base - 1)
    s0m2, s1m1 = same_id(ids_ref, base, base - 2), same_id(ids_ref, base + 1, base - 1)

    def shift(i):
        near, far = last[i][1:2], last[i][0:1]
        t1, t2 = taps[1][i : i + 1], taps[2][i : i + 1]
        return s0m1 * (t1 * near) + s0m2 * (t2 * far), s1m1 * (t2 * near)

    def plain(i):
        t0, t1 = taps[0][i : i + 1], taps[1][i : i + 1]
        return t0 * first[i][0:1], t0 * first[i][1:2] + s01 * (t1 * first[i][0:1])

    k, v, dk, dv = plain(1), plain(2), shift(1), shift(2)
    delta = [(k[j] + dk[j]) * (v[j] + dv[j]) - k[j] * v[j] for j in range(2)]
    return shift(0), delta


def unpack(block, poles):
    first = [None, block[poles : poles + 2], block[poles + 2 : poles + 4]]
    last = [block[poles + 4 + 2 * i : poles + 6 + 2 * i] for i in range(3)]
    return block[0:poles], first, last


def joined_state(low_state, low_last, up_state, up_first, taps, rates, ids_ref, base, length):
    _, delta = first_products(up_first, low_last, taps, ids_ref, base)
    grown = low_state + delta[0] * jnp.exp(rates) + delta[1] * jnp.exp(2.0 * rates)
    open_ = same_id(ids_ref, base + length - 1, base - 1)
    return up_state + grown * (jnp.exp(-rates * jnp.float32(length)) * open_)


def join_kernel(T, poles, span, position, ids_ref, mine_ref, other_ref, taps_ref, rates_ref, out):
    me = position[0]
    is_upper = (me // span) % 2 == 1
    base = (me // (2 * span)) * (2 * span * T) + span * T
    mine, other = mine_ref[...].astype(f32), other_ref[...].astype(f32)
    lower, upper = jnp.where(is_upper, other, mine), jnp.where(is_upper, mine, other)
    taps = [taps_ref[j] for j in range(3)]
    low_state, low_first, low_last = unpack(lower, poles)
    up_state, up_first, up_last = unpack(upper, poles)
    state = joined_state(low_state, low_last, up_state, up_first, taps, rates_ref[...], ids_ref, base, span * T)
    out[0:poles, :] = state.astype(bf16)
    row = lax.broadcasted_iota(jnp.int32, (HEAD, lower.shape[1]), 0)
    out[poles : poles + HEAD, :] = jnp.where(row < 4, lower[poles:], upper[poles:]).astype(bf16)


def join(span, T, position, ids, mine, other, taps, rates):
    poles = rates.shape[0]
    return pl.pallas_call(
        functools.partial(join_kernel, T, poles, span),
        out_shape=jax.ShapeDtypeStruct(mine.shape, bf16),
        in_specs=[smem(), smem()] + [vmem()] * 4,
        out_specs=vmem(),
        compiler_params=pltpu.CompilerParams(vmem_limit_bytes=4 * MIB),
        name="join",
    )(position, ids, mine, other, taps, rates)


def gate_kernel(
    T, poles, spans, position, lane_position, ids_ref, query_ref, local_ref, state_ref, block_ref, visible_ref, taps_ref, rates_ref,
    pole_ref, skip_ref, out_ref, *rest,
):
    arrived, (gated_out, send_out, mine_out, carry, full, window, sem) = rest[: len(spans)], rest[len(spans) :]
    run = T // PARTS
    tiles = query_ref.shape[1] // 128
    columns(lane_position[0], 0, out_ref, window, sem).start()
    me = position[0]
    base = me * T
    taps = [taps_ref[j] for j in range(3)]
    rates, weight, skip = rates_ref[...], pole_ref[...], skip_ref[...]
    prior = jnp.zeros(block_ref.shape, f32)
    prior_state, prior_first, prior_last = unpack(prior, poles)
    for span, ref in zip(spans, arrived):
        state, first, last = unpack(ref[...].astype(f32), poles)
        upper, held = (me // span) % 2 == 1, me % span
        if span == 1:
            both = state
        else:
            both = joined_state(
                state, last, prior_state, prior_first, taps, rates, ids_ref, (me - held) * T, held * T)
        fresh = upper & (held == 0)
        prior_state = jnp.where(fresh, state, jnp.where(upper, both, prior_state))
        prior_first = [None] + [jnp.where(upper, first[i], prior_first[i]) for i in (1, 2)]
        prior_last = [jnp.where(fresh, last[i], prior_last[i]) for i in range(3)]
    _, first, _ = unpack(block_ref[...].astype(f32), poles)
    q_shift, delta = first_products(first, prior_last, taps, ids_ref, base)
    second = delta[1] * jnp.exp(rates)
    now = prior_state + (delta[0] + second) * jnp.exp(rates)
    fix0 = skip * delta[0] - jnp.sum(weight * second, axis=0, keepdims=True)
    fix1 = skip * delta[1]
    jump = jnp.exp(-rates * float(run))
    for s in range(PARTS):
        part = slice(s * poles, (s + 1) * poles)
        began = weight * now
        for tile in range(tiles):
            carry[tile, part, :] = began[:, tile * 128 : tile * 128 + 128]
        if s < PARTS - 1:
            whole = same_id(ids_ref, base + s * run + run - 1, base + s * run - 1)
            ends = jnp.concatenate([state_ref[tile, part, :] for tile in range(tiles)], axis=1)
            now = now * (jump * whole) + ends

    def lane_body(tile, _):
        lanes = pl.ds(pl.multiple_of(tile * 128, 128), 128)
        d16 = jnp.exp(-rates_ref[:, lanes])
        decay = [jnp.broadcast_to(d16[n : n + 1], (8, 128)) for n in range(poles)]
        start = tuple(carry[tile, pl.ds(n, PARTS, stride=poles), :] for n in range(poles))

        def token(i, states):
            after = [states[n] * decay[n] for n in range(poles)]
            see = visible_ref[pl.ds(pl.multiple_of(i * 8, 8), 8), :]
            at = pl.ds(i, PARTS, stride=run)
            full[tile, at, :] = local_ref[tile, at, :] + see * tree(list(after))
            return tuple(after)

        lax.fori_loop(0, run, token, start, unroll=4)
        return 0

    lax.fori_loop(0, tiles, lane_body, 0)
    row = lax.broadcasted_iota(jnp.int32, (16, 128), 0)
    for tile in range(tiles):
        lanes = slice(tile * 128, tile * 128 + 128)
        gated_out[:, lanes] = (query_ref[:, lanes] * full[tile]).astype(bf16)
        top_q, top = query_ref[0:16, lanes], full[tile, 0:16, :]
        top_q = top_q + jnp.where(row == 0, q_shift[0][:, lanes], 0.0) + jnp.where(row == 1, q_shift[1][:, lanes], 0.0)
        top = top + jnp.where(row == 0, fix0[:, lanes], 0.0) + jnp.where(row == 1, fix1[:, lanes], 0.0)
        gated_out[0:16, lanes] = (top_q * top).astype(bf16)
    columns(lane_position[0], 0, out_ref, window, sem).wait()
    share(lane_position[0], gated_out, window, send_out, mine_out)


def target(index, slot):
    chip = index // 2
    low = chip < 2
    if slot < 2:
        return jnp.where(low, 3 - slot, slot)
    if slot == 2:
        return jnp.where(low, 1 - chip, 5 - chip)
    return chip


def columns(index, slot, out_ref, window, sem):
    both = window.shape[1]
    start = pl.multiple_of(target(index, slot) * both, both)
    return pltpu.make_async_copy(out_ref.at[:, pl.ds(start, both)], window, sem)


def share(index, gated_ref, window, send_out, mine_out):
    width = send_out.shape[1]
    tile = 256
    core = index % 2

    def tile_body(j, _):
        at = pl.ds(pl.multiple_of(j * tile, tile), tile)
        for out, half in ((send_out, 1 - core), (mine_out, core)):
            cols = pl.ds(pl.multiple_of(half * width + j * tile, tile), tile)
            out[:, at] = jnp.dot(gated_ref[...], window[:, cols], preferred_element_type=f32).astype(out.dtype)
        return 0

    lax.fori_loop(0, width // tile, tile_body, 0)


def share_kernel(slots, lane_position, gated_ref, out_ref, *rest):
    outs, (windows, sem) = rest[:-2], rest[-2:]
    copies = [columns(lane_position[0], slot, out_ref, windows.at[k], sem.at[k]) for k, slot in enumerate(slots)]
    for copy in copies:
        copy.start()
    for k, copy in enumerate(copies):
        copy.wait()
        share(lane_position[0], gated_ref, windows.at[k], outs[2 * k], outs[2 * k + 1])


def share_rest(slots, lane_position, gated, out_weight, width):
    T, channels = gated.shape
    return pl.pallas_call(
        functools.partial(share_kernel, slots),
        out_shape=[jax.ShapeDtypeStruct((T, width), d) for _ in slots for d in (bf16, f32)],
        in_specs=[smem(), vmem(), hbm()],
        out_specs=[vmem()] * (2 * len(slots)),
        scratch_shapes=[
            pltpu.VMEM((len(slots), channels, 2 * width), bf16),
            pltpu.SemaphoreType.DMA((len(slots),)),
        ],
        compiler_params=pltpu.CompilerParams(vmem_limit_bytes=20 * MIB),
        cost_estimate=pl.CostEstimate(
            flops=4 * T * channels * width * len(slots), bytes_accessed=4 * channels * width * len(slots), transcendentals=0),
        name="share_rest",
    )(lane_position, gated, out_weight)


def gate(T, spans, arrived, position, lane_position, ids, query, local_part, state, block, visible, taps, rates,
         pole_weight, skip, out_weight, width):
    poles = rates.shape[0]
    return pl.pallas_call(
        functools.partial(gate_kernel, T, poles, tuple(spans)),
        out_shape=[
            jax.ShapeDtypeStruct(query.shape, bf16),
            jax.ShapeDtypeStruct((T, width), bf16),
            jax.ShapeDtypeStruct((T, width), f32),
        ],
        in_specs=[smem()] * 3 + [vmem()] * 9 + [hbm()] + [vmem()] * len(spans),
        out_specs=[vmem()] * 3,
        scratch_shapes=[
            pltpu.VMEM(state.shape, f32),
            pltpu.VMEM(local_part.shape, f32),
            pltpu.VMEM((query.shape[1], 2 * width), bf16),
            pltpu.SemaphoreType.DMA,
        ],
        compiler_params=pltpu.CompilerParams(vmem_limit_bytes=10 * MIB),
        name="gate",
    )(position, lane_position, ids, query, local_part, state, block, visible, taps, rates, pole_weight, skip, out_weight,
      *arrived)


def total(*terms):
    return functools.reduce(lambda a, b: a + b, [t.astype(f32) for t in terms]).astype(bf16)


def scatter_line(shares):
    pair = [(m, m ^ 1) for m in range(8)]

    def along(hops):
        return [(a * 2 + c, b * 2 + c) for a, b in hops for c in range(2)]

    ends = along([(0, 1), (3, 2)])
    middle = along([(1, 2), (2, 1)])
    near = along([(0, 1), (1, 0), (2, 3), (3, 2)])
    sums = [total(mine, lax.ppermute(send, "mp", pair)) for send, mine in shares]
    first = lax.ppermute(sums[0], "mp", ends)
    second = lax.ppermute(sums[1], "mp", ends)
    across = lax.ppermute(total(sums[0], first), "mp", middle)
    across2 = lax.ppermute(total(sums[1], second), "mp", middle)
    last = lax.ppermute(total(sums[2], across), "mp", near)
    return total(sums[3], across2, last)


def shifted(value, axis, steps):
    count = lax.axis_size(axis)
    leading, last = (max(0, -steps), min(count, count - steps))
    return lax.ppermute(value, axis, [(source, source + steps) for source in range(leading, last)])


def project(block, norm_gain, weights):
    floats = block.astype(jnp.float32)
    mean_square = jnp.mean(floats * floats, axis=-1, keepdims=True)
    normed = (floats * lax.rsqrt(mean_square + epsilon) * norm_gain[None, :]).astype(jnp.bfloat16)
    return jnp.dot(normed, weights, preferred_element_type=jnp.float32).astype(jnp.bfloat16)


def general(
    tokens, norm_gain, in_weight, short_filter, rates, residues, skip, out_weight, segment_ids
):
    tok_rows = tokens.shape[0]
    model_width = tokens.shape[1]
    channels = in_weight.shape[2]
    filter_taps = short_filter.shape[0]
    pole_count = rates.shape[0]
    device_index = lax.axis_index("ctx")
    row_offset = device_index * tok_rows
    weights = in_weight.reshape(model_width, 3 * channels)
    projected = project(tokens, norm_gain, weights)
    previous = shifted(projected[tok_rows - (filter_taps - 1) :], "ctx", 1)
    extended = jnp.concatenate([previous, projected], axis=0)
    padded_ids = jnp.concatenate([jnp.full((filter_taps,), -1, jnp.int32), segment_ids], axis=0)
    window = lax.dynamic_slice_in_dim(padded_ids, row_offset, tok_rows + filter_taps, 0)
    local_ids = window[filter_taps:]
    taps_table = short_filter.reshape(filter_taps, 3 * channels)
    featured = jnp.zeros((tok_rows, 3 * channels), jnp.float32)
    for lag_index in range(filter_taps):
        begin = filter_taps - 1 - lag_index
        lagged = extended[begin : begin + tok_rows].astype(jnp.float32)
        matches = window[filter_taps - lag_index : filter_taps - lag_index + tok_rows] == local_ids
        term = taps_table[lag_index][None, :] * lagged
        featured = featured + jnp.where(matches[:, None], term, jnp.zeros_like(term))
    query_part = featured[:, :channels]
    key_part = featured[:, channels : 2 * channels]
    value_part = featured[:, 2 * channels :]
    product = key_part * value_part
    offsets = jnp.arange(tok_rows, dtype=jnp.float32)
    center = float(tok_rows // 2)
    growth = jnp.exp(-(offsets - center)[:, None, None] * rates[None])
    shrinkage = jnp.exp((offsets - center)[:, None, None] * rates[None])
    weighted = (shrinkage * product[:, None, :]).reshape(tok_rows, pole_count * channels)
    visible = (offsets[:, None] >= offsets[None, :]) & (local_ids[:, None] == local_ids[None, :])
    in_block = jnp.dot(visible.astype(jnp.float32), weighted, precision=lax.Precision.HIGHEST)
    in_block = in_block.reshape(tok_rows, pole_count, channels) * growth
    survives = local_ids == window[filter_taps - 1]
    block_factor = jnp.exp(-rates * tok_rows)
    block_end = in_block[tok_rows - 1]
    block_ends = lax.all_gather(block_end[None], "ctx", axis=0, tiled=True)
    shard_count = segment_ids.shape[0] // tok_rows
    last_ids = segment_ids.reshape(shard_count, tok_rows)[:, tok_rows - 1]
    prior_ids = jnp.concatenate([jnp.full((1,), -1, jnp.int32), last_ids[:-1]], axis=0)
    shard_decays = block_factor[None] * (last_ids == prior_ids).astype(jnp.float32)[:, None, None]

    def absorb(running, inputs):
        shard, factor, shard_end = inputs
        advanced = running * factor + shard_end
        return (jnp.where(shard < device_index, advanced, running), None)

    incoming, _ = lax.scan(
        absorb,
        jnp.zeros_like(block_end),
        (jnp.arange(shard_count, dtype=jnp.int32), shard_decays, block_ends),
    )
    carried = incoming[None] * jnp.exp(-(offsets + 1.0)[:, None, None] * rates[None])
    carried = carried * survives.astype(jnp.float32)[:, None, None]
    states = in_block + carried
    pole_weight = residues * jnp.sqrt(-jnp.expm1(-2.0 * rates))
    longconv = jnp.sum(pole_weight[None] * states, axis=1)
    gated = (query_part * (longconv + skip[None, :] * product)).astype(jnp.bfloat16)
    partial_terms = jnp.dot(gated, out_weight, preferred_element_type=jnp.float32)
    return lax.psum_scatter(partial_terms, "mp", scatter_dimension=1, tiled=True).astype(
        jnp.bfloat16
    )


def local(tokens, norm_gain, in_weight, short_filter, rates, residues, skip, out_weight, segment_ids):
    T = tokens.shape[0]
    shards = lax.axis_size("ctx")
    me = lax.axis_index("ctx")
    position = me.astype(jnp.int32)[None]
    lane_position = lax.axis_index("mp").astype(jnp.int32)[None]
    width = out_weight.shape[1] // lax.axis_size("mp")
    weight3 = jnp.transpose(in_weight, (1, 0, 2))
    out_weight = pltpu.with_memory_space_constraint(out_weight, pltpu.HBM)
    query, product, block, keep, visible, taps, rates, residues, skip = front(
        position, segment_ids.reshape(-1, 128), tokens, norm_gain[None], weight3, short_filter, rates, residues, skip[None])
    local_part, state, pole_weight = local_pass(product, keep, rates, residues, skip)
    group, span, spans, arrived = block, 1, [], []
    while span < shards:
        final = 2 * span == shards
        hops = [(a, a ^ span) for a in range(shards) if not (final and a & span)]
        other = lax.ppermute(group, "ctx", hops)
        spans.append(span)
        arrived.append(other)
        if not final:
            group = join(span, T, position, segment_ids, group, other, taps, rates)
        span *= 2
    gated, send, mine = gate(T, spans, arrived, position, lane_position, segment_ids, query, local_part, state, block, visible,
                             taps, rates, pole_weight, skip, out_weight, width)
    rest = share_rest((1, 2, 3), lane_position, gated, out_weight, width)
    return scatter_line([(send, mine)] + [(rest[2 * k], rest[2 * k + 1]) for k in range(3)])


def solution(mesh):
    placed = (
        P("ctx", None),
        P(),
        P(None, None, "mp"),
        P(None, None, "mp"),
        P(None, "mp"),
        P(None, "mp"),
        P("mp"),
        P("mp", None),
        P(),
    )
    shards, groups = mesh.shape["ctx"], mesh.shape["mp"]

    def body(tokens, norm_gain, in_weight, *rest):
        suits = groups == 8 and shards & (shards - 1) == 0 and shards > 1
        suits = suits and in_weight.shape[2] % 512 == 0 and in_weight.shape[0] % 2048 == 0
        suits = suits and tokens.shape[0] % 64 == 0 and rest[-1].shape[0] % 128 == 0 and rest[1].shape[0] % 8 == 0
        return (local if suits else general)(tokens, norm_gain, in_weight, *rest)

    return jax.shard_map(
        body, mesh=mesh, in_specs=placed, out_specs=P("ctx", "mp"), check_vma=False
    )
```

```python
import functools
import jax
import jax.numpy as jnp
from jax import lax
from jax.experimental import pallas as pl
from jax.experimental.pallas import tpu as pltpu
from jax.sharding import PartitionSpec as P

epsilon = 1e-06
f32 = jnp.float32
bf16 = jnp.bfloat16

PARTS = 8
HEAD = 16
MIB = 1 << 20


def vmem():
    return pl.BlockSpec(memory_space=pltpu.VMEM)


def smem():
    return pl.BlockSpec(memory_space=pltpu.SMEM)


def same_id(ids_ref, a, b):
    def get(t):
        return jnp.where(t < 0, -1, ids_ref[jnp.maximum(t, 0)])

    return (get(a) == get(b)).astype(f32)


def hbm():
    return pl.BlockSpec(memory_space=pltpu.HBM)


def front_kernel(
    geometry, position, ids_ref, tokens_ref, gain_ref, weight_ref, taps_ref, rates_ref, residues_ref, skip_ref,
    query_out, prod_out, block_out, keep_out, visible_out, taps, rates, residues, skip,
    ids, gain, tok, normed, ring, total, proj, head, idcol, near, twice, ending, sem, tok_sem, ring_sem,
):
    T, depth, channels, cb_size, kc_size, slots, poles = geometry
    run = T // PARTS
    kcs, cbs = depth // kc_size, channels // cb_size
    steps = kcs * cbs
    base = pl.multiple_of(position[0] * T, 8)

    def fetch(step):
        cb, kc, slot = step // kcs, step % kcs, step % slots
        return pltpu.make_async_copy(
            weight_ref.at[:, pl.ds(pl.multiple_of(kc * kc_size, kc_size), kc_size),
                          pl.ds(pl.multiple_of(cb * cb_size, cb_size), cb_size)],
            ring.at[slot], ring_sem.at[slot])

    small = [
        pltpu.make_async_copy(a, b, sem.at[i])
        for i, (a, b) in enumerate(
            ((ids_ref, ids), (gain_ref, gain), (taps_ref, taps), (rates_ref, rates), (residues_ref, residues),
             (skip_ref, skip)))
    ]
    small[0].start()
    small[1].start()
    chunk = T // 4
    tok_copies = [
        pltpu.make_async_copy(tokens_ref.at[pl.ds(c * chunk, chunk)], tok.at[pl.ds(c * chunk, chunk)], tok_sem.at[c])
        for c in range(4)
    ]
    for copy in tok_copies:
        copy.start()
    for copy in small[2:]:
        copy.start()
    for s in range(min(slots, steps)):
        fetch(s).start()

    small[0].wait()
    idcol[0:8, :] = jnp.full((8, 128), -1.0, f32)
    for b in range(ids.shape[0]):
        row = ids[b : b + 1, :].astype(f32)
        idcol[8 + b * 128 : 8 + (b + 1) * 128, :] = jnp.broadcast_to(row, (128, 128)).T
    near[...] = idcol[pl.ds(base, T + 8), :]
    here = near[8 : 8 + T, :]
    keep_out[...] = (here == near[7 : 7 + T, :]).astype(f32)
    twice[...] = (here == near[6 : 6 + T, :]).astype(f32)
    ending[...] = (here == near[7 + T : 8 + T, :]).astype(f32)
    before = near[pl.ds(7, PARTS, stride=run), :]
    for i in range(run):
        visible_out[i * 8 : (i + 1) * 8, :] = (near[pl.ds(8 + i, PARTS, stride=run), :] == before).astype(f32)
    for i in range(3):
        proj[i, 0:8, :] = jnp.zeros((8, cb_size), f32)
    head[...] = jnp.zeros(head.shape, f32)
    small[1].wait()

    def norm_rows(g, _):
        part = pl.ds(pl.multiple_of(g * 16, 16), 16)
        x = tok[part, :].astype(f32)
        scale = lax.rsqrt(jnp.sum(x * x, axis=-1, keepdims=True) * (1.0 / depth) + epsilon)
        normed[part, :] = (x * scale * gain[...]).astype(bf16)
        return 0

    for c, copy in enumerate(tok_copies):
        copy.wait()
        lax.fori_loop(c * chunk // 16, (c + 1) * chunk // 16, norm_rows, 0)
    for copy in small[2:]:
        copy.wait()

    def epilogue(cb):
        cols = pl.ds(pl.multiple_of(cb * cb_size, cb_size), cb_size)
        feats = []
        m1 = jnp.concatenate([keep_out[...]] * (cb_size // 128), axis=1)
        m2 = jnp.concatenate([twice[...]] * (cb_size // 128), axis=1)
        for i in range(3):
            p = total[i].astype(bf16).astype(f32)
            proj[i, 8 : 8 + T, :] = p
            tap = [taps[j, i : i + 1, cols] for j in range(3)]
            feats.append(
                tap[0] * p + m1 * (tap[1] * proj[i, 7 : 7 + T, :]) + m2 * (tap[2] * proj[i, 6 : 6 + T, :]))
        query_out[:, cols] = feats[0]
        for i in range(1, 3):
            head[2 * (i - 1) : 2 * i, :] = proj[i, 8:10, :]
        for i in range(3):
            head[4 + 2 * i : 6 + 2 * i, :] = proj[i, 6 + T : 8 + T, :]
        block_out[poles : poles + HEAD, cols] = head[...].astype(bf16)
        product = feats[1] * feats[2]
        back = 7.0 - lax.broadcasted_iota(jnp.int32, (8, 128), 0).astype(f32)
        for lane in range(cb_size // 128):
            tile = cb * (cb_size // 128) + lane
            lanes = pl.ds(pl.multiple_of(tile * 128, 128), 128)
            prod_out[tile] = product[:, lane * 128 : lane * 128 + 128]
            r16 = rates[:, lanes]
            jump = jnp.exp(-8.0 * r16)
            leap = [jnp.broadcast_to(jump[n : n + 1], (8, 128)) for n in range(poles)]

            def eight(g, sums):
                part = pl.ds(pl.multiple_of(g * 8, 8), 8)
                p = prod_out[tile, part, :] * ending[part, :]
                return tuple(sums[n] * leap[n] + p for n in range(poles))

            sums = lax.fori_loop(
                0, T // 8, eight, tuple(jnp.zeros((8, 128), f32) for _ in range(poles)), unroll=4)
            ends = [
                jnp.sum(sums[n] * jnp.exp(-back * r16[n : n + 1]), axis=0, keepdims=True) for n in range(poles)
            ]
            block_out[0:poles, lanes] = jnp.concatenate(ends, axis=0).astype(bf16)

    def step_body(step, _):
        cb, kc, slot = step // kcs, step % kcs, step % slots
        fetch(step).wait()
        lhs = normed[:, pl.ds(pl.multiple_of(kc * kc_size, kc_size), kc_size)]
        for i in range(3):
            part = jnp.dot(lhs, ring[slot, i], preferred_element_type=f32)
            total[i] = jnp.where(kc == 0, part, total[i] + part)

        @pl.when(step + slots < steps)
        def _():
            fetch(step + slots).start()

        @pl.when(kc == kcs - 1)
        def _():
            epilogue(cb)

        return 0

    total[...] = jnp.zeros(total.shape, f32)
    lax.fori_loop(0, steps, step_body, 0)


def front(position, ids2, tokens, gain, weight3, taps, rates, residues, skip):
    T, depth = tokens.shape
    channels, poles = weight3.shape[2], rates.shape[0]
    cb_size, kc_size, slots = 256, 2048, 5
    geometry = (T, depth, channels, cb_size, kc_size, slots, poles)
    kept = [pltpu.VMEM(a.shape, a.dtype) for a in (taps, rates, residues, skip)]
    ids2, tokens, gain, weight3, taps, rates, residues, skip = [
        pltpu.with_memory_space_constraint(a, pltpu.HBM)
        for a in (ids2, tokens, gain, weight3, taps, rates, residues, skip)
    ]
    return pl.pallas_call(
        functools.partial(front_kernel, geometry),
        out_shape=[
            jax.ShapeDtypeStruct((T, channels), f32),
            jax.ShapeDtypeStruct((channels // 128, T, 128), f32),
            jax.ShapeDtypeStruct((poles + HEAD, channels), bf16),
            jax.ShapeDtypeStruct((T, 128), f32),
            jax.ShapeDtypeStruct((T, 128), f32),
        ] + kept,
        in_specs=[smem()] + [hbm()] * 8,
        out_specs=[vmem()] * 9,
        scratch_shapes=[
            pltpu.VMEM(ids2.shape, ids2.dtype),
            pltpu.VMEM(gain.shape, f32),
            pltpu.VMEM((T, depth), bf16),
            pltpu.VMEM((T, depth), bf16),
            pltpu.VMEM((slots, 3, kc_size, cb_size), bf16),
            pltpu.VMEM((3, T, cb_size), f32),
            pltpu.VMEM((3, T + 8, cb_size), f32),
            pltpu.VMEM((HEAD, cb_size), f32),
            pltpu.VMEM((ids2.shape[0] * 128 + 8, 128), f32),
            pltpu.VMEM((T + 8, 128), f32),
            pltpu.VMEM((T, 128), f32),
            pltpu.VMEM((T, 128), f32),
            pltpu.SemaphoreType.DMA((6,)),
            pltpu.SemaphoreType.DMA((4,)),
            pltpu.SemaphoreType.DMA((slots,)),
        ],
        compiler_params=pltpu.CompilerParams(vmem_limit_bytes=28 * MIB),
        name="front",
    )(position, ids2, tokens, gain, weight3, taps, rates, residues, skip)


def expm1(x):
    series = jnp.ones_like(x)
    for k in range(9, 1, -1):
        series = 1.0 + series * x * (1.0 / k)
    return jnp.where(jnp.abs(x) < 0.5, x * series, jnp.exp(x) - 1.0)


def local_kernel(poles, first, prod_ref, keep_ref, rates_ref, residues_ref, skip_ref, _, local_out, state_out, pole_out):
    tiles, T, _ = local_out.shape
    run = T // PARTS
    mine = slice(first * 128, (first + tiles) * 128)
    pole_out[...] = residues_ref[:, mine] * jnp.sqrt(-expm1(-2.0 * rates_ref[:, mine]))

    def tile_body(tile, _):
        lanes = pl.ds(pl.multiple_of((first + tile) * 128, 128), 128)
        d16 = jnp.exp(-rates_ref[:, lanes])
        w16 = pole_out[:, pl.ds(pl.multiple_of(tile * 128, 128), 128)]
        decay = [jnp.broadcast_to(d16[n : n + 1], (8, 128)) for n in range(poles)]
        weight = [jnp.broadcast_to(w16[n : n + 1], (8, 128)) for n in range(poles)]
        skip = skip_ref[0:1, lanes]

        def token(i, states):
            at = pl.ds(i, PARTS, stride=run)
            p, keep = prod_ref[first + tile, at, :], keep_ref[at, :]
            after = [states[n] * decay[n] * keep + p for n in range(poles)]
            local_out[tile, at, :] = tree([skip * p] + [weight[n] * after[n] for n in range(poles)])
            return tuple(after)

        states = lax.fori_loop(0, run, token, tuple(jnp.zeros((8, 128), f32) for _ in range(poles)), unroll=2)
        for n in range(poles):
            state_out[tile, pl.ds(n, PARTS, stride=poles), :] = states[n]
        return 0

    lax.fori_loop(0, tiles, tile_body, 0)


def tree(terms):
    while len(terms) > 1:
        terms = [a + b for a, b in zip(terms[0::2], terms[1::2])] + terms[len(terms) // 2 * 2 :]
    return terms[0]


def local_pass(first, tiles, product, keep, rates, residues, skip, after):
    T, poles = product.shape[1], rates.shape[0]
    return pl.pallas_call(
        functools.partial(local_kernel, poles, first),
        out_shape=(
            jax.ShapeDtypeStruct((tiles, T, 128), f32),
            jax.ShapeDtypeStruct((tiles, PARTS * poles, 128), f32),
            jax.ShapeDtypeStruct((poles, tiles * 128), f32),
        ),
        in_specs=[vmem()] * 5 + [pl.BlockSpec(memory_space=pl.ANY)],
        out_specs=[vmem()] * 3,
        compiler_params=pltpu.CompilerParams(vmem_limit_bytes=4 * MIB),
        cost_estimate=pl.CostEstimate(flops=6 * T * poles * tiles * 128, bytes_accessed=8 * MIB, transcendentals=0),
        name="local_pass",
    )(product, keep, rates, residues, skip, after)


def first_products(first, last, taps, ids_ref, base):
    s01, s0m1 = same_id(ids_ref, base + 1, base), same_id(ids_ref, base, base - 1)
    s0m2, s1m1 = same_id(ids_ref, base, base - 2), same_id(ids_ref, base + 1, base - 1)

    def shift(i):
        near, far = last[i][1:2], last[i][0:1]
        t1, t2 = taps[1][i : i + 1], taps[2][i : i + 1]
        return s0m1 * (t1 * near) + s0m2 * (t2 * far), s1m1 * (t2 * near)

    def plain(i):
        t0, t1 = taps[0][i : i + 1], taps[1][i : i + 1]
        return t0 * first[i][0:1], t0 * first[i][1:2] + s01 * (t1 * first[i][0:1])

    k, v, dk, dv = plain(1), plain(2), shift(1), shift(2)
    delta = [(k[j] + dk[j]) * (v[j] + dv[j]) - k[j] * v[j] for j in range(2)]
    return shift(0), delta


def unpack(block, poles):
    first = [None, block[poles : poles + 2], block[poles + 2 : poles + 4]]
    last = [block[poles + 4 + 2 * i : poles + 6 + 2 * i] for i in range(3)]
    return block[0:poles], first, last


def joined_state(low_state, low_last, up_state, up_first, taps, rates, ids_ref, base, length):
    _, delta = first_products(up_first, low_last, taps, ids_ref, base)
    grown = low_state + delta[0] * jnp.exp(rates) + delta[1] * jnp.exp(2.0 * rates)
    open_ = same_id(ids_ref, base + length - 1, base - 1)
    return up_state + grown * (jnp.exp(-rates * jnp.float32(length)) * open_)


def join_kernel(T, poles, span, position, ids_ref, mine_ref, other_ref, taps_ref, rates_ref, _, out):
    me = position[0]
    is_upper = (me // span) % 2 == 1
    base = (me // (2 * span)) * (2 * span * T) + span * T
    mine, other = mine_ref[...].astype(f32), other_ref[...].astype(f32)
    lower, upper = jnp.where(is_upper, other, mine), jnp.where(is_upper, mine, other)
    taps = [taps_ref[j] for j in range(3)]
    low_state, _, low_last = unpack(lower, poles)
    up_state, up_first, _ = unpack(upper, poles)
    state = joined_state(low_state, low_last, up_state, up_first, taps, rates_ref[...], ids_ref, base, span * T)
    out[0:poles, :] = state.astype(bf16)
    row = lax.broadcasted_iota(jnp.int32, (HEAD, lower.shape[1]), 0)
    out[poles : poles + HEAD, :] = jnp.where(row < 4, lower[poles:], upper[poles:]).astype(bf16)


def join(span, T, position, ids, mine, other, taps, rates, after):
    poles = rates.shape[0]
    return pl.pallas_call(
        functools.partial(join_kernel, T, poles, span),
        out_shape=jax.ShapeDtypeStruct(mine.shape, bf16),
        in_specs=[smem(), smem()] + [vmem()] * 4 + [pl.BlockSpec(memory_space=pl.ANY)],
        out_specs=vmem(),
        compiler_params=pltpu.CompilerParams(vmem_limit_bytes=4 * MIB),
        name="join",
    )(position, ids, mine, other, taps, rates, after)


def gate_kernel(
    T, poles, spans, cuts, position, lane_position, ids_ref, query_ref, block_ref, visible_ref, taps_ref, rates_ref, skip_ref,
    out_ref, *rest,
):
    arrived, rest = rest[: len(spans)], rest[len(spans) :]
    parts, rest = [rest[3 * c : 3 * c + 3] for c in range(cuts)], rest[3 * cuts :]
    (gated_out, send_out, mine_out, carry, full, window, sem) = rest
    run = T // PARTS
    tiles = query_ref.shape[1] // 128
    columns(lane_position[0], 0, out_ref, window, sem).start()
    me = position[0]
    base = me * T
    taps = [taps_ref[j] for j in range(3)]
    rates, skip = rates_ref[...], skip_ref[...]
    weight = jnp.concatenate([pole_ref[...] for _, _, pole_ref in parts], axis=1)
    each = tiles // cuts
    prior = jnp.zeros(block_ref.shape, f32)
    prior_state, prior_first, prior_last = unpack(prior, poles)
    for span, ref in zip(spans, arrived):
        state, first, last = unpack(ref[...].astype(f32), poles)
        upper, held = (me // span) % 2 == 1, me % span
        if span == 1:
            both = state
        else:
            both = joined_state(
                state, last, prior_state, prior_first, taps, rates, ids_ref, (me - held) * T, held * T)
        fresh = upper & (held == 0)
        prior_state = jnp.where(fresh, state, jnp.where(upper, both, prior_state))
        prior_first = [None] + [jnp.where(upper, first[i], prior_first[i]) for i in (1, 2)]
        prior_last = [jnp.where(fresh, last[i], prior_last[i]) for i in range(3)]
    _, first, _ = unpack(block_ref[...].astype(f32), poles)
    q_shift, delta = first_products(first, prior_last, taps, ids_ref, base)
    second = delta[1] * jnp.exp(rates)
    now = prior_state + (delta[0] + second) * jnp.exp(rates)
    fix0 = skip * delta[0] - jnp.sum(weight * second, axis=0, keepdims=True)
    fix1 = skip * delta[1]
    jump = jnp.exp(-rates * float(run))
    for s in range(PARTS):
        part = slice(s * poles, (s + 1) * poles)
        began = weight * now
        for tile in range(tiles):
            carry[tile, part, :] = began[:, tile * 128 : tile * 128 + 128]
        if s < PARTS - 1:
            whole = same_id(ids_ref, base + s * run + run - 1, base + s * run - 1)
            ends = jnp.concatenate([parts[tile // each][1][tile % each, part, :] for tile in range(tiles)], axis=1)
            now = now * (jump * whole) + ends

    def lane_body(cut, inner, _):
        tile = cut * each + inner
        lanes = pl.ds(pl.multiple_of(tile * 128, 128), 128)
        d16 = jnp.exp(-rates_ref[:, lanes])
        decay = [jnp.broadcast_to(d16[n : n + 1], (8, 128)) for n in range(poles)]
        start = tuple(carry[tile, pl.ds(n, PARTS, stride=poles), :] for n in range(poles))

        def token(i, states):
            after = [states[n] * decay[n] for n in range(poles)]
            see = visible_ref[pl.ds(pl.multiple_of(i * 8, 8), 8), :]
            at = pl.ds(i, PARTS, stride=run)
            full[tile, at, :] = parts[cut][0][inner, at, :] + see * tree(list(after))
            return tuple(after)

        lax.fori_loop(0, run, token, start, unroll=4)
        return 0

    for cut in range(cuts):
        lax.fori_loop(0, each, functools.partial(lane_body, cut), 0)
    row = lax.broadcasted_iota(jnp.int32, (16, 128), 0)
    for tile in range(tiles):
        lanes = slice(tile * 128, tile * 128 + 128)
        gated_out[:, lanes] = (query_ref[:, lanes] * full[tile]).astype(bf16)
        top_q, top = query_ref[0:16, lanes], full[tile, 0:16, :]
        top_q = top_q + jnp.where(row == 0, q_shift[0][:, lanes], 0.0) + jnp.where(row == 1, q_shift[1][:, lanes], 0.0)
        top = top + jnp.where(row == 0, fix0[:, lanes], 0.0) + jnp.where(row == 1, fix1[:, lanes], 0.0)
        gated_out[0:16, lanes] = (top_q * top).astype(bf16)
    columns(lane_position[0], 0, out_ref, window, sem).wait()
    share(lane_position[0], gated_out, window, send_out, mine_out)


def target(index, slot):
    chip = index // 2
    low = chip < 2
    if slot < 2:
        return jnp.where(low, 3 - slot, slot)
    if slot == 2:
        return jnp.where(low, 1 - chip, 5 - chip)
    return chip


def columns(index, slot, out_ref, window, sem):
    both = window.shape[1]
    start = pl.multiple_of(target(index, slot) * both, both)
    return pltpu.make_async_copy(out_ref.at[:, pl.ds(start, both)], window, sem)


def share(index, gated_ref, window, send_out, mine_out):
    width = send_out.shape[1]
    tile = 256
    core = index % 2

    for j in range(width // tile):
        at = slice(j * tile, j * tile + tile)
        for out, half in ((send_out, 1 - core), (mine_out, core)):
            cols = pl.ds(pl.multiple_of(half * width + j * tile, tile), tile)
            out[:, at] = jnp.dot(gated_ref[...], window[:, cols], preferred_element_type=f32).astype(out.dtype)


def share_kernel(slots, lane_position, gated_ref, out_ref, *rest):
    outs, (windows, sem) = rest[:-2], rest[-2:]
    copies = [columns(lane_position[0], slot, out_ref, windows.at[k], sem.at[k]) for k, slot in enumerate(slots)]
    for copy in copies:
        copy.start()
    for k, copy in enumerate(copies):
        copy.wait()
        share(lane_position[0], gated_ref, windows.at[k], outs[2 * k], outs[2 * k + 1])


def share_rest(slots, lane_position, gated, out_weight, width):
    T, channels = gated.shape
    return pl.pallas_call(
        functools.partial(share_kernel, slots),
        out_shape=[jax.ShapeDtypeStruct((T, width), d) for _ in slots for d in (bf16, f32)],
        in_specs=[smem(), vmem(), hbm()],
        out_specs=[vmem()] * (2 * len(slots)),
        scratch_shapes=[
            pltpu.VMEM((len(slots), channels, 2 * width), bf16),
            pltpu.SemaphoreType.DMA((len(slots),)),
        ],
        compiler_params=pltpu.CompilerParams(vmem_limit_bytes=20 * MIB),
        cost_estimate=pl.CostEstimate(
            flops=4 * T * channels * width * len(slots), bytes_accessed=4 * channels * width * len(slots), transcendentals=0),
        name="share_rest",
    )(lane_position, gated, out_weight)


def gate(T, spans, arrived, position, lane_position, ids, query, parts, block, visible, taps, rates, skip, out_weight, width):
    poles, channels = rates.shape
    return pl.pallas_call(
        functools.partial(gate_kernel, T, poles, tuple(spans), len(parts)),
        out_shape=[
            jax.ShapeDtypeStruct(query.shape, bf16),
            jax.ShapeDtypeStruct((T, width), bf16),
            jax.ShapeDtypeStruct((T, width), f32),
        ],
        in_specs=[smem()] * 3 + [vmem()] * 6 + [hbm()] + [vmem()] * (len(spans) + 3 * len(parts)),
        out_specs=[vmem()] * 3,
        scratch_shapes=[
            pltpu.VMEM((channels // 128, PARTS * poles, 128), f32),
            pltpu.VMEM((channels // 128, T, 128), f32),
            pltpu.VMEM((channels, 2 * width), bf16),
            pltpu.SemaphoreType.DMA,
        ],
        compiler_params=pltpu.CompilerParams(vmem_limit_bytes=10 * MIB),
        name="gate",
    )(position, lane_position, ids, query, block, visible, taps, rates, skip, out_weight, *arrived,
      *[a for part in parts for a in part])


def total(*terms):
    return functools.reduce(lambda a, b: a + b, [t.astype(f32) for t in terms]).astype(bf16)


def scatter_line(lane_position, gated, send, mine, out_weight, width):
    pair = [(m, m ^ 1) for m in range(8)]

    def along(hops):
        return [(a * 2 + c, b * 2 + c) for a, b in hops for c in range(2)]

    ends = along([(0, 1), (3, 2)])
    middle = along([(1, 2), (2, 1)])
    near = along([(0, 1), (1, 0), (2, 3), (3, 2)])
    sums = [total(mine, lax.ppermute(send, "mp", pair))]
    first = lax.ppermute(sums[0], "mp", ends)
    rest = share_rest((1, 2, 3), lane_position, gated, out_weight, width)
    sums += [total(rest[2 * k + 1], lax.ppermute(rest[2 * k], "mp", pair)) for k in range(3)]
    second = lax.ppermute(sums[1], "mp", ends)
    across = lax.ppermute(total(sums[0], first), "mp", middle)
    across2 = lax.ppermute(total(sums[1], second), "mp", middle)
    last = lax.ppermute(total(sums[2], across), "mp", near)
    return total(sums[3], across2, last)


def shifted(value, axis, steps):
    count = lax.axis_size(axis)
    leading, last = (max(0, -steps), min(count, count - steps))
    return lax.ppermute(value, axis, [(source, source + steps) for source in range(leading, last)])


def project(block, norm_gain, weights):
    floats = block.astype(jnp.float32)
    mean_square = jnp.mean(floats * floats, axis=-1, keepdims=True)
    normed = (floats * lax.rsqrt(mean_square + epsilon) * norm_gain[None, :]).astype(jnp.bfloat16)
    return jnp.dot(normed, weights, preferred_element_type=jnp.float32).astype(jnp.bfloat16)


def general(
    tokens, norm_gain, in_weight, short_filter, rates, residues, skip, out_weight, segment_ids
):
    tok_rows = tokens.shape[0]
    model_width = tokens.shape[1]
    channels = in_weight.shape[2]
    filter_taps = short_filter.shape[0]
    pole_count = rates.shape[0]
    device_index = lax.axis_index("ctx")
    row_offset = device_index * tok_rows
    weights = in_weight.reshape(model_width, 3 * channels)
    projected = project(tokens, norm_gain, weights)
    previous = shifted(projected[tok_rows - (filter_taps - 1) :], "ctx", 1)
    extended = jnp.concatenate([previous, projected], axis=0)
    padded_ids = jnp.concatenate([jnp.full((filter_taps,), -1, jnp.int32), segment_ids], axis=0)
    window = lax.dynamic_slice_in_dim(padded_ids, row_offset, tok_rows + filter_taps, 0)
    local_ids = window[filter_taps:]
    taps_table = short_filter.reshape(filter_taps, 3 * channels)
    featured = jnp.zeros((tok_rows, 3 * channels), jnp.float32)
    for lag_index in range(filter_taps):
        begin = filter_taps - 1 - lag_index
        lagged = extended[begin : begin + tok_rows].astype(jnp.float32)
        matches = window[filter_taps - lag_index : filter_taps - lag_index + tok_rows] == local_ids
        term = taps_table[lag_index][None, :] * lagged
        featured = featured + jnp.where(matches[:, None], term, jnp.zeros_like(term))
    query_part = featured[:, :channels]
    key_part = featured[:, channels : 2 * channels]
    value_part = featured[:, 2 * channels :]
    product = key_part * value_part
    offsets = jnp.arange(tok_rows, dtype=jnp.float32)
    center = float(tok_rows // 2)
    growth = jnp.exp(-(offsets - center)[:, None, None] * rates[None])
    shrinkage = jnp.exp((offsets - center)[:, None, None] * rates[None])
    weighted = (shrinkage * product[:, None, :]).reshape(tok_rows, pole_count * channels)
    visible = (offsets[:, None] >= offsets[None, :]) & (local_ids[:, None] == local_ids[None, :])
    in_block = jnp.dot(visible.astype(jnp.float32), weighted, precision=lax.Precision.HIGHEST)
    in_block = in_block.reshape(tok_rows, pole_count, channels) * growth
    survives = local_ids == window[filter_taps - 1]
    block_factor = jnp.exp(-rates * tok_rows)
    block_end = in_block[tok_rows - 1]
    block_ends = lax.all_gather(block_end[None], "ctx", axis=0, tiled=True)
    shard_count = segment_ids.shape[0] // tok_rows
    last_ids = segment_ids.reshape(shard_count, tok_rows)[:, tok_rows - 1]
    prior_ids = jnp.concatenate([jnp.full((1,), -1, jnp.int32), last_ids[:-1]], axis=0)
    shard_decays = block_factor[None] * (last_ids == prior_ids).astype(jnp.float32)[:, None, None]

    def absorb(running, inputs):
        shard, factor, shard_end = inputs
        advanced = running * factor + shard_end
        return (jnp.where(shard < device_index, advanced, running), None)

    incoming, _ = lax.scan(
        absorb,
        jnp.zeros_like(block_end),
        (jnp.arange(shard_count, dtype=jnp.int32), shard_decays, block_ends),
    )
    carried = incoming[None] * jnp.exp(-(offsets + 1.0)[:, None, None] * rates[None])
    carried = carried * survives.astype(jnp.float32)[:, None, None]
    states = in_block + carried
    pole_weight = residues * jnp.sqrt(-jnp.expm1(-2.0 * rates))
    longconv = jnp.sum(pole_weight[None] * states, axis=1)
    gated = (query_part * (longconv + skip[None, :] * product)).astype(jnp.bfloat16)
    partial_terms = jnp.dot(gated, out_weight, preferred_element_type=jnp.float32)
    return lax.psum_scatter(partial_terms, "mp", scatter_dimension=1, tiled=True).astype(
        jnp.bfloat16
    )


def local(tokens, norm_gain, in_weight, short_filter, rates, residues, skip, out_weight, segment_ids):
    T = tokens.shape[0]
    shards = lax.axis_size("ctx")
    me = lax.axis_index("ctx")
    position = me.astype(jnp.int32)[None]
    lane_position = lax.axis_index("mp").astype(jnp.int32)[None]
    width = out_weight.shape[1] // lax.axis_size("mp")
    weight3 = jnp.transpose(in_weight, (1, 0, 2))
    out_weight = pltpu.with_memory_space_constraint(out_weight, pltpu.HBM)
    query, product, block, keep, visible, taps, rates, residues, skip = front(
        position, segment_ids.reshape(-1, 128), tokens, norm_gain[None], weight3, short_filter, rates, residues, skip[None])
    cuts = shards.bit_length() - 1
    each = product.shape[0] // cuts
    group, spans, arrived, parts = block, [], [], []
    for k in range(cuts):
        span = 1 << k
        other = lax.ppermute(group, "ctx", [(a, a ^ span) for a in range(shards)])
        spans.append(span)
        arrived.append(other)
        parts.append(local_pass(k * each, each, product, keep, rates, residues, skip, group))
        if k < cuts - 1:
            group = join(span, T, position, segment_ids, group, other, taps, rates, parts[k][0])
    gated, send, mine = gate(T, spans, arrived, position, lane_position, segment_ids, query, parts, block, visible, taps, rates,
                             skip, out_weight, width)
    return scatter_line(lane_position, gated, send, mine, out_weight, width)


def solution(mesh):
    placed = (
        P("ctx", None),
        P(),
        P(None, None, "mp"),
        P(None, None, "mp"),
        P(None, "mp"),
        P(None, "mp"),
        P("mp"),
        P("mp", None),
        P(),
    )
    shards, groups = mesh.shape["ctx"], mesh.shape["mp"]

    def body(tokens, norm_gain, in_weight, *rest):
        suits = groups == 8 and shards & (shards - 1) == 0 and shards > 1
        suits = suits and in_weight.shape[2] % 512 == 0 and in_weight.shape[0] % 2048 == 0
        suits = suits and tokens.shape[0] % 64 == 0 and rest[-1].shape[0] % 128 == 0 and rest[1].shape[0] % 8 == 0
        return (local if suits else general)(tokens, norm_gain, in_weight, *rest)

    return jax.shard_map(
        body, mesh=mesh, in_specs=placed, out_specs=P("ctx", "mp"), check_vma=False
    )
```

```python
import functools
import jax
import jax.numpy as jnp
from jax import lax
from jax.experimental import pallas as pl
from jax.experimental.pallas import tpu as pltpu
from jax.sharding import PartitionSpec as P

epsilon = 1e-06
f32 = jnp.float32
bf16 = jnp.bfloat16

PARTS = 8
HEAD = 16
MIB = 1 << 20


def vmem():
    return pl.BlockSpec(memory_space=pltpu.VMEM)


def smem():
    return pl.BlockSpec(memory_space=pltpu.SMEM)


def same_id(ids_ref, a, b):
    def get(t):
        return jnp.where(t < 0, -1, ids_ref[jnp.maximum(t, 0)])

    return (get(a) == get(b)).astype(f32)


def hbm():
    return pl.BlockSpec(memory_space=pltpu.HBM)


def front_kernel(
    geometry, position, ids_ref, tokens_ref, gain_ref, weight_ref, taps_ref, rates_ref, residues_ref, skip_ref,
    query_out, prod_out, block_out, keep_out, visible_out, taps, rates, residues, skip,
    ids, gain, tok, normed, ring, total, proj, head, idcol, near, twice, ending, sem, tok_sem, ring_sem,
):
    T, depth, channels, cb_size, kc_size, slots, poles = geometry
    run = T // PARTS
    kcs, cbs = depth // kc_size, channels // cb_size
    steps = kcs * cbs
    base = pl.multiple_of(position[0] * T, 8)

    def fetch(step):
        cb, kc, slot = step // kcs, step % kcs, step % slots
        return pltpu.make_async_copy(
            weight_ref.at[:, pl.ds(pl.multiple_of(kc * kc_size, kc_size), kc_size),
                          pl.ds(pl.multiple_of(cb * cb_size, cb_size), cb_size)],
            ring.at[slot], ring_sem.at[slot])

    small = [
        pltpu.make_async_copy(a, b, sem.at[i])
        for i, (a, b) in enumerate(
            ((ids_ref, ids), (gain_ref, gain), (taps_ref, taps), (rates_ref, rates), (residues_ref, residues),
             (skip_ref, skip)))
    ]
    small[0].start()
    small[1].start()
    chunk = T // 4
    tok_copies = [
        pltpu.make_async_copy(tokens_ref.at[pl.ds(c * chunk, chunk)], tok.at[pl.ds(c * chunk, chunk)], tok_sem.at[c])
        for c in range(4)
    ]
    for copy in tok_copies:
        copy.start()
    for copy in small[2:]:
        copy.start()
    for s in range(min(slots, steps)):
        fetch(s).start()

    small[0].wait()
    idcol[0:8, :] = jnp.full((8, 128), -1.0, f32)
    for b in range(ids.shape[0]):
        row = ids[b : b + 1, :].astype(f32)
        idcol[8 + b * 128 : 8 + (b + 1) * 128, :] = jnp.broadcast_to(row, (128, 128)).T
    near[...] = idcol[pl.ds(base, T + 8), :]
    here = near[8 : 8 + T, :]
    keep_out[...] = (here == near[7 : 7 + T, :]).astype(f32)
    twice[...] = (here == near[6 : 6 + T, :]).astype(f32)
    ending[...] = (here == near[7 + T : 8 + T, :]).astype(f32)
    before = near[pl.ds(7, PARTS, stride=run), :]
    for i in range(run):
        visible_out[i * 8 : (i + 1) * 8, :] = (near[pl.ds(8 + i, PARTS, stride=run), :] == before).astype(f32)
    for i in range(3):
        proj[i, 0:8, :] = jnp.zeros((8, cb_size), f32)
    head[...] = jnp.zeros(head.shape, f32)
    small[1].wait()

    def norm_rows(g, _):
        part = pl.ds(pl.multiple_of(g * 16, 16), 16)
        x = tok[part, :].astype(f32)
        scale = lax.rsqrt(jnp.sum(x * x, axis=-1, keepdims=True) * (1.0 / depth) + epsilon)
        normed[part, :] = (x * scale * gain[...]).astype(bf16)
        return 0

    for c, copy in enumerate(tok_copies):
        copy.wait()
        lax.fori_loop(c * chunk // 16, (c + 1) * chunk // 16, norm_rows, 0)
    for copy in small[2:]:
        copy.wait()

    def epilogue(cb):
        cols = pl.ds(pl.multiple_of(cb * cb_size, cb_size), cb_size)
        feats = []
        m1 = jnp.concatenate([keep_out[...]] * (cb_size // 128), axis=1)
        m2 = jnp.concatenate([twice[...]] * (cb_size // 128), axis=1)
        for i in range(3):
            p = total[i].astype(bf16).astype(f32)
            proj[i, 8 : 8 + T, :] = p
            tap = [taps[j, i : i + 1, cols] for j in range(3)]
            feats.append(
                tap[0] * p + m1 * (tap[1] * proj[i, 7 : 7 + T, :]) + m2 * (tap[2] * proj[i, 6 : 6 + T, :]))
        query_out[:, cols] = feats[0]
        for i in range(1, 3):
            head[2 * (i - 1) : 2 * i, :] = proj[i, 8:10, :]
        for i in range(3):
            head[4 + 2 * i : 6 + 2 * i, :] = proj[i, 6 + T : 8 + T, :]
        block_out[poles : poles + HEAD, cols] = head[...].astype(bf16)
        product = feats[1] * feats[2]
        back = 7.0 - lax.broadcasted_iota(jnp.int32, (8, 128), 0).astype(f32)
        for lane in range(cb_size // 128):
            tile = cb * (cb_size // 128) + lane
            lanes = pl.ds(pl.multiple_of(tile * 128, 128), 128)
            prod_out[tile] = product[:, lane * 128 : lane * 128 + 128]
            r16 = rates[:, lanes]
            jump = jnp.exp(-8.0 * r16)
            leap = [jnp.broadcast_to(jump[n : n + 1], (8, 128)) for n in range(poles)]

            def eight(g, sums):
                part = pl.ds(pl.multiple_of(g * 8, 8), 8)
                p = prod_out[tile, part, :] * ending[part, :]
                return tuple(sums[n] * leap[n] + p for n in range(poles))

            sums = lax.fori_loop(
                0, T // 8, eight, tuple(jnp.zeros((8, 128), f32) for _ in range(poles)), unroll=4)
            ends = [
                jnp.sum(sums[n] * jnp.exp(-back * r16[n : n + 1]), axis=0, keepdims=True) for n in range(poles)
            ]
            block_out[0:poles, lanes] = jnp.concatenate(ends, axis=0).astype(bf16)

    def step_body(step, _):
        cb, kc, slot = step // kcs, step % kcs, step % slots
        fetch(step).wait()
        lhs = normed[:, pl.ds(pl.multiple_of(kc * kc_size, kc_size), kc_size)]
        for i in range(3):
            part = jnp.dot(lhs, ring[slot, i], preferred_element_type=f32)
            total[i] = jnp.where(kc == 0, part, total[i] + part)

        @pl.when(step + slots < steps)
        def _():
            fetch(step + slots).start()

        @pl.when(kc == kcs - 1)
        def _():
            epilogue(cb)

        return 0

    total[...] = jnp.zeros(total.shape, f32)
    lax.fori_loop(0, steps, step_body, 0)


def front(position, ids2, tokens, gain, weight3, taps, rates, residues, skip):
    T, depth = tokens.shape
    channels, poles = weight3.shape[2], rates.shape[0]
    cb_size, kc_size, slots = 256, 2048, 5
    geometry = (T, depth, channels, cb_size, kc_size, slots, poles)
    kept = [pltpu.VMEM(a.shape, a.dtype) for a in (taps, rates, residues, skip)]
    ids2, tokens, gain, weight3, taps, rates, residues, skip = [
        pltpu.with_memory_space_constraint(a, pltpu.HBM)
        for a in (ids2, tokens, gain, weight3, taps, rates, residues, skip)
    ]
    return pl.pallas_call(
        functools.partial(front_kernel, geometry),
        out_shape=[
            jax.ShapeDtypeStruct((T, channels), f32),
            jax.ShapeDtypeStruct((channels // 128, T, 128), f32),
            jax.ShapeDtypeStruct((poles + HEAD, channels), bf16),
            jax.ShapeDtypeStruct((T, 128), f32),
            jax.ShapeDtypeStruct((T, 128), f32),
        ] + kept,
        in_specs=[smem()] + [hbm()] * 8,
        out_specs=[vmem()] * 9,
        scratch_shapes=[
            pltpu.VMEM(ids2.shape, ids2.dtype),
            pltpu.VMEM(gain.shape, f32),
            pltpu.VMEM((T, depth), bf16),
            pltpu.VMEM((T, depth), bf16),
            pltpu.VMEM((slots, 3, kc_size, cb_size), bf16),
            pltpu.VMEM((3, T, cb_size), f32),
            pltpu.VMEM((3, T + 8, cb_size), f32),
            pltpu.VMEM((HEAD, cb_size), f32),
            pltpu.VMEM((ids2.shape[0] * 128 + 8, 128), f32),
            pltpu.VMEM((T + 8, 128), f32),
            pltpu.VMEM((T, 128), f32),
            pltpu.VMEM((T, 128), f32),
            pltpu.SemaphoreType.DMA((6,)),
            pltpu.SemaphoreType.DMA((4,)),
            pltpu.SemaphoreType.DMA((slots,)),
        ],
        compiler_params=pltpu.CompilerParams(vmem_limit_bytes=28 * MIB),
        name="front",
    )(position, ids2, tokens, gain, weight3, taps, rates, residues, skip)


def expm1(x):
    series = jnp.ones_like(x)
    for k in range(9, 1, -1):
        series = 1.0 + series * x * (1.0 / k)
    return jnp.where(jnp.abs(x) < 0.5, x * series, jnp.exp(x) - 1.0)


def local_kernel(
    poles, first, slot, lane_position, prod_ref, keep_ref, rates_ref, residues_ref, skip_ref, out_ref, _,
    local_out, state_out, pole_out, window_out, sem,
):
    copy = columns(lane_position[0], slot, out_ref, window_out, sem)
    copy.start()
    tiles, T, _ = local_out.shape
    run = T // PARTS
    mine = slice(first * 128, (first + tiles) * 128)
    pole_out[...] = residues_ref[:, mine] * jnp.sqrt(-expm1(-2.0 * rates_ref[:, mine]))

    def tile_body(tile, _):
        lanes = pl.ds(pl.multiple_of((first + tile) * 128, 128), 128)
        d16 = jnp.exp(-rates_ref[:, lanes])
        w16 = pole_out[:, pl.ds(pl.multiple_of(tile * 128, 128), 128)]
        decay = [jnp.broadcast_to(d16[n : n + 1], (8, 128)) for n in range(poles)]
        weight = [jnp.broadcast_to(w16[n : n + 1], (8, 128)) for n in range(poles)]
        skip = skip_ref[0:1, lanes]

        def token(i, states):
            at = pl.ds(i, PARTS, stride=run)
            p, keep = prod_ref[first + tile, at, :], keep_ref[at, :]
            after = [states[n] * decay[n] * keep + p for n in range(poles)]
            local_out[tile, at, :] = tree([skip * p] + [weight[n] * after[n] for n in range(poles)])
            return tuple(after)

        states = lax.fori_loop(0, run, token, tuple(jnp.zeros((8, 128), f32) for _ in range(poles)), unroll=2)
        for n in range(poles):
            state_out[tile, pl.ds(n, PARTS, stride=poles), :] = states[n]
        return 0

    lax.fori_loop(0, tiles, tile_body, 0)
    copy.wait()


def tree(terms):
    while len(terms) > 1:
        terms = [a + b for a, b in zip(terms[0::2], terms[1::2])] + terms[len(terms) // 2 * 2 :]
    return terms[0]


def local_pass(first, tiles, slot, lane_position, product, keep, rates, residues, skip, out_weight, width, after):
    T, poles = product.shape[1], rates.shape[0]
    return pl.pallas_call(
        functools.partial(local_kernel, poles, first, slot),
        out_shape=(
            jax.ShapeDtypeStruct((tiles, T, 128), f32),
            jax.ShapeDtypeStruct((tiles, PARTS * poles, 128), f32),
            jax.ShapeDtypeStruct((poles, tiles * 128), f32),
            jax.ShapeDtypeStruct((out_weight.shape[0], 2 * width), bf16),
        ),
        in_specs=[smem()] + [vmem()] * 5 + [hbm(), pl.BlockSpec(memory_space=pl.ANY)],
        out_specs=[vmem()] * 4,
        scratch_shapes=[pltpu.SemaphoreType.DMA],
        compiler_params=pltpu.CompilerParams(vmem_limit_bytes=8 * MIB),
        cost_estimate=pl.CostEstimate(flops=6 * T * poles * tiles * 128, bytes_accessed=8 * MIB, transcendentals=0),
        name="local_pass",
    )(lane_position, product, keep, rates, residues, skip, out_weight, after)


def first_products(first, last, taps, ids_ref, base):
    s01, s0m1 = same_id(ids_ref, base + 1, base), same_id(ids_ref, base, base - 1)
    s0m2, s1m1 = same_id(ids_ref, base, base - 2), same_id(ids_ref, base + 1, base - 1)

    def shift(i):
        near, far = last[i][1:2], last[i][0:1]
        t1, t2 = taps[1][i : i + 1], taps[2][i : i + 1]
        return s0m1 * (t1 * near) + s0m2 * (t2 * far), s1m1 * (t2 * near)

    def plain(i):
        t0, t1 = taps[0][i : i + 1], taps[1][i : i + 1]
        return t0 * first[i][0:1], t0 * first[i][1:2] + s01 * (t1 * first[i][0:1])

    k, v, dk, dv = plain(1), plain(2), shift(1), shift(2)
    delta = [(k[j] + dk[j]) * (v[j] + dv[j]) - k[j] * v[j] for j in range(2)]
    return shift(0), delta


def unpack(block, poles):
    first = [None, block[poles : poles + 2], block[poles + 2 : poles + 4]]
    last = [block[poles + 4 + 2 * i : poles + 6 + 2 * i] for i in range(3)]
    return block[0:poles], first, last


def joined_state(low_state, low_last, up_state, up_first, taps, rates, ids_ref, base, length):
    _, delta = first_products(up_first, low_last, taps, ids_ref, base)
    grown = low_state + delta[0] * jnp.exp(rates) + delta[1] * jnp.exp(2.0 * rates)
    open_ = same_id(ids_ref, base + length - 1, base - 1)
    return up_state + grown * (jnp.exp(-rates * jnp.float32(length)) * open_)


def join_kernel(T, poles, span, position, ids_ref, mine_ref, other_ref, taps_ref, rates_ref, _, out):
    me = position[0]
    is_upper = (me // span) % 2 == 1
    base = (me // (2 * span)) * (2 * span * T) + span * T
    mine, other = mine_ref[...].astype(f32), other_ref[...].astype(f32)
    lower, upper = jnp.where(is_upper, other, mine), jnp.where(is_upper, mine, other)
    taps = [taps_ref[j] for j in range(3)]
    low_state, _, low_last = unpack(lower, poles)
    up_state, up_first, _ = unpack(upper, poles)
    state = joined_state(low_state, low_last, up_state, up_first, taps, rates_ref[...], ids_ref, base, span * T)
    out[0:poles, :] = state.astype(bf16)
    row = lax.broadcasted_iota(jnp.int32, (HEAD, lower.shape[1]), 0)
    out[poles : poles + HEAD, :] = jnp.where(row < 4, lower[poles:], upper[poles:]).astype(bf16)


def join(span, T, position, ids, mine, other, taps, rates, after):
    poles = rates.shape[0]
    return pl.pallas_call(
        functools.partial(join_kernel, T, poles, span),
        out_shape=jax.ShapeDtypeStruct(mine.shape, bf16),
        in_specs=[smem(), smem()] + [vmem()] * 4 + [pl.BlockSpec(memory_space=pl.ANY)],
        out_specs=vmem(),
        compiler_params=pltpu.CompilerParams(vmem_limit_bytes=4 * MIB),
        name="join",
    )(position, ids, mine, other, taps, rates, after)


def gate_kernel(
    T, poles, spans, cuts, position, lane_position, ids_ref, query_ref, block_ref, visible_ref, taps_ref, rates_ref, skip_ref,
    out_ref, window_ref, *rest,
):
    arrived, rest = rest[: len(spans)], rest[len(spans) :]
    parts, rest = [rest[3 * c : 3 * c + 3] for c in range(cuts)], rest[3 * cuts :]
    gated_out, send_out, mine_out, third_out, fourth_out, carry, full, sem = rest
    run = T // PARTS
    tiles = query_ref.shape[1] // 128
    copies = [
        columns(lane_position[0], slot, out_ref, out, sem.at[k])
        for k, (slot, out) in enumerate(((2, third_out), (3, fourth_out)))
    ]
    for copy in copies:
        copy.start()
    me = position[0]
    base = me * T
    taps = [taps_ref[j] for j in range(3)]
    rates, skip = rates_ref[...], skip_ref[...]
    weight = jnp.concatenate([pole_ref[...] for _, _, pole_ref in parts], axis=1)
    each = tiles // cuts
    prior = jnp.zeros(block_ref.shape, f32)
    prior_state, prior_first, prior_last = unpack(prior, poles)
    for span, ref in zip(spans, arrived):
        state, first, last = unpack(ref[...].astype(f32), poles)
        upper, held = (me // span) % 2 == 1, me % span
        if span == 1:
            both = state
        else:
            both = joined_state(
                state, last, prior_state, prior_first, taps, rates, ids_ref, (me - held) * T, held * T)
        fresh = upper & (held == 0)
        prior_state = jnp.where(fresh, state, jnp.where(upper, both, prior_state))
        prior_first = [None] + [jnp.where(upper, first[i], prior_first[i]) for i in (1, 2)]
        prior_last = [jnp.where(fresh, last[i], prior_last[i]) for i in range(3)]
    _, first, _ = unpack(block_ref[...].astype(f32), poles)
    q_shift, delta = first_products(first, prior_last, taps, ids_ref, base)
    second = delta[1] * jnp.exp(rates)
    now = prior_state + (delta[0] + second) * jnp.exp(rates)
    fix0 = skip * delta[0] - jnp.sum(weight * second, axis=0, keepdims=True)
    fix1 = skip * delta[1]
    jump = jnp.exp(-rates * float(run))
    for s in range(PARTS):
        part = slice(s * poles, (s + 1) * poles)
        began = weight * now
        for tile in range(tiles):
            carry[tile, part, :] = began[:, tile * 128 : tile * 128 + 128]
        if s < PARTS - 1:
            whole = same_id(ids_ref, base + s * run + run - 1, base + s * run - 1)
            ends = jnp.concatenate([parts[tile // each][1][tile % each, part, :] for tile in range(tiles)], axis=1)
            now = now * (jump * whole) + ends

    def lane_body(cut, inner, _):
        tile = cut * each + inner
        lanes = pl.ds(pl.multiple_of(tile * 128, 128), 128)
        d16 = jnp.exp(-rates_ref[:, lanes])
        decay = [jnp.broadcast_to(d16[n : n + 1], (8, 128)) for n in range(poles)]
        start = tuple(carry[tile, pl.ds(n, PARTS, stride=poles), :] for n in range(poles))

        def token(i, states):
            after = [states[n] * decay[n] for n in range(poles)]
            see = visible_ref[pl.ds(pl.multiple_of(i * 8, 8), 8), :]
            at = pl.ds(i, PARTS, stride=run)
            full[tile, at, :] = parts[cut][0][inner, at, :] + see * tree(list(after))
            return tuple(after)

        lax.fori_loop(0, run, token, start, unroll=4)
        return 0

    for cut in range(cuts):
        lax.fori_loop(0, each, functools.partial(lane_body, cut), 0)
    row = lax.broadcasted_iota(jnp.int32, (16, 128), 0)
    for tile in range(tiles):
        lanes = slice(tile * 128, tile * 128 + 128)
        gated_out[:, lanes] = (query_ref[:, lanes] * full[tile]).astype(bf16)
        top_q, top = query_ref[0:16, lanes], full[tile, 0:16, :]
        top_q = top_q + jnp.where(row == 0, q_shift[0][:, lanes], 0.0) + jnp.where(row == 1, q_shift[1][:, lanes], 0.0)
        top = top + jnp.where(row == 0, fix0[:, lanes], 0.0) + jnp.where(row == 1, fix1[:, lanes], 0.0)
        gated_out[0:16, lanes] = (top_q * top).astype(bf16)
    share(lane_position[0], gated_out, window_ref, send_out, mine_out)
    for copy in copies:
        copy.wait()


def target(index, slot):
    chip = index // 2
    odd = chip % 2
    if slot == 0:
        return 3 - 3 * odd
    if slot == 1:
        return 1 + odd
    if slot == 2:
        return (chip + 2) % 4
    return chip


def columns(index, slot, out_ref, window, sem):
    both = window.shape[1]
    start = pl.multiple_of(target(index, slot) * both, both)
    return pltpu.make_async_copy(out_ref.at[:, pl.ds(start, both)], window, sem)


def share(index, gated_ref, window, send_out, mine_out):
    width = send_out.shape[1]
    tile = 256
    core = index % 2

    for j in range(width // tile):
        at = slice(j * tile, j * tile + tile)
        for out, half in ((send_out, 1 - core), (mine_out, core)):
            cols = pl.ds(pl.multiple_of(half * width + j * tile, tile), tile)
            out[:, at] = jnp.dot(gated_ref[...], window[:, cols], preferred_element_type=f32).astype(out.dtype)


def share_kernel(count, lane_position, gated_ref, *rest):
    windows, outs = rest[:count], rest[count:]
    for k, window in enumerate(windows):
        share(lane_position[0], gated_ref, window, outs[2 * k], outs[2 * k + 1])


def shares(lane_position, gated, windows, width):
    T, channels = gated.shape
    count = len(windows)
    return pl.pallas_call(
        functools.partial(share_kernel, count),
        out_shape=[jax.ShapeDtypeStruct((T, width), d) for _ in windows for d in (bf16, f32)],
        in_specs=[smem(), vmem()] + [vmem()] * count,
        out_specs=[vmem()] * (2 * count),
        compiler_params=pltpu.CompilerParams(vmem_limit_bytes=4 * MIB),
        cost_estimate=pl.CostEstimate(
            flops=4 * T * channels * width * count, bytes_accessed=4 * channels * width * count, transcendentals=0),
        name="shares",
    )(lane_position, gated, *windows)


def gate(T, spans, arrived, position, lane_position, ids, query, parts, block, visible, taps, rates, skip, out_weight, window, width):
    poles, channels = rates.shape
    return pl.pallas_call(
        functools.partial(gate_kernel, T, poles, tuple(spans), len(parts)),
        out_shape=[
            jax.ShapeDtypeStruct(query.shape, bf16),
            jax.ShapeDtypeStruct((T, width), bf16),
            jax.ShapeDtypeStruct((T, width), f32),
            jax.ShapeDtypeStruct(window.shape, bf16),
            jax.ShapeDtypeStruct(window.shape, bf16),
        ],
        in_specs=[smem()] * 3 + [vmem()] * 6 + [hbm()] + [vmem()] * (1 + len(spans) + 3 * len(parts)),
        out_specs=[vmem()] * 5,
        scratch_shapes=[
            pltpu.VMEM((channels // 128, PARTS * poles, 128), f32),
            pltpu.VMEM((channels // 128, T, 128), f32),
            pltpu.SemaphoreType.DMA((2,)),
        ],
        compiler_params=pltpu.CompilerParams(vmem_limit_bytes=12 * MIB),
        name="gate",
    )(position, lane_position, ids, query, block, visible, taps, rates, skip, out_weight, window, *arrived,
      *[a for part in parts for a in part])


def total(*terms):
    return functools.reduce(lambda a, b: a + b, [t.astype(f32) for t in terms]).astype(bf16)


def scatter_line(lane_position, gated, send, mine, windows, width):
    chip = lax.axis_index("mp") // 2
    inner = (chip == 1) | (chip == 2)
    pair = [(m, m ^ 1) for m in range(8)]

    def along(hops):
        return [(a * 2 + c, b * 2 + c) for a, b in hops for c in range(2)]

    def where(mask, x):
        return jnp.where(mask, x.astype(f32), 0.0)

    far = total(mine, lax.ppermute(send, "mp", pair))
    from_near = lax.ppermute(far, "mp", along([(0, 1), (1, 0), (2, 3), (3, 2)]))
    send, mine = shares(lane_position, gated, windows[:1], width)
    second = total(mine, lax.ppermute(send, "mp", pair))
    from_middle = lax.ppermute(second, "mp", along([(1, 2), (2, 1)]))
    from_end = lax.ppermute(second, "mp", along([(0, 1), (3, 2)]))
    send2, mine2, send3, mine3 = shares(lane_position, gated, windows[1:], width)
    across = total(mine2, lax.ppermute(send2, "mp", pair), where(inner, from_near))
    own = total(mine3, lax.ppermute(send3, "mp", pair))
    from_across = lax.ppermute(across, "mp", along([(0, 2), (1, 3), (2, 0), (3, 1)]))
    return total(own, where(~inner, from_near), from_middle, from_end, from_across)


def shifted(value, axis, steps):
    count = lax.axis_size(axis)
    leading, last = (max(0, -steps), min(count, count - steps))
    return lax.ppermute(value, axis, [(source, source + steps) for source in range(leading, last)])


def project(block, norm_gain, weights):
    floats = block.astype(jnp.float32)
    mean_square = jnp.mean(floats * floats, axis=-1, keepdims=True)
    normed = (floats * lax.rsqrt(mean_square + epsilon) * norm_gain[None, :]).astype(jnp.bfloat16)
    return jnp.dot(normed, weights, preferred_element_type=jnp.float32).astype(jnp.bfloat16)


def general(
    tokens, norm_gain, in_weight, short_filter, rates, residues, skip, out_weight, segment_ids
):
    tok_rows = tokens.shape[0]
    model_width = tokens.shape[1]
    channels = in_weight.shape[2]
    filter_taps = short_filter.shape[0]
    pole_count = rates.shape[0]
    device_index = lax.axis_index("ctx")
    row_offset = device_index * tok_rows
    weights = in_weight.reshape(model_width, 3 * channels)
    projected = project(tokens, norm_gain, weights)
    previous = shifted(projected[tok_rows - (filter_taps - 1) :], "ctx", 1)
    extended = jnp.concatenate([previous, projected], axis=0)
    padded_ids = jnp.concatenate([jnp.full((filter_taps,), -1, jnp.int32), segment_ids], axis=0)
    window = lax.dynamic_slice_in_dim(padded_ids, row_offset, tok_rows + filter_taps, 0)
    local_ids = window[filter_taps:]
    taps_table = short_filter.reshape(filter_taps, 3 * channels)
    featured = jnp.zeros((tok_rows, 3 * channels), jnp.float32)
    for lag_index in range(filter_taps):
        begin = filter_taps - 1 - lag_index
        lagged = extended[begin : begin + tok_rows].astype(jnp.float32)
        matches = window[filter_taps - lag_index : filter_taps - lag_index + tok_rows] == local_ids
        term = taps_table[lag_index][None, :] * lagged
        featured = featured + jnp.where(matches[:, None], term, jnp.zeros_like(term))
    query_part = featured[:, :channels]
    key_part = featured[:, channels : 2 * channels]
    value_part = featured[:, 2 * channels :]
    product = key_part * value_part
    offsets = jnp.arange(tok_rows, dtype=jnp.float32)
    center = float(tok_rows // 2)
    growth = jnp.exp(-(offsets - center)[:, None, None] * rates[None])
    shrinkage = jnp.exp((offsets - center)[:, None, None] * rates[None])
    weighted = (shrinkage * product[:, None, :]).reshape(tok_rows, pole_count * channels)
    visible = (offsets[:, None] >= offsets[None, :]) & (local_ids[:, None] == local_ids[None, :])
    in_block = jnp.dot(visible.astype(jnp.float32), weighted, precision=lax.Precision.HIGHEST)
    in_block = in_block.reshape(tok_rows, pole_count, channels) * growth
    survives = local_ids == window[filter_taps - 1]
    block_factor = jnp.exp(-rates * tok_rows)
    block_end = in_block[tok_rows - 1]
    block_ends = lax.all_gather(block_end[None], "ctx", axis=0, tiled=True)
    shard_count = segment_ids.shape[0] // tok_rows
    last_ids = segment_ids.reshape(shard_count, tok_rows)[:, tok_rows - 1]
    prior_ids = jnp.concatenate([jnp.full((1,), -1, jnp.int32), last_ids[:-1]], axis=0)
    shard_decays = block_factor[None] * (last_ids == prior_ids).astype(jnp.float32)[:, None, None]

    def absorb(running, inputs):
        shard, factor, shard_end = inputs
        advanced = running * factor + shard_end
        return (jnp.where(shard < device_index, advanced, running), None)

    incoming, _ = lax.scan(
        absorb,
        jnp.zeros_like(block_end),
        (jnp.arange(shard_count, dtype=jnp.int32), shard_decays, block_ends),
    )
    carried = incoming[None] * jnp.exp(-(offsets + 1.0)[:, None, None] * rates[None])
    carried = carried * survives.astype(jnp.float32)[:, None, None]
    states = in_block + carried
    pole_weight = residues * jnp.sqrt(-jnp.expm1(-2.0 * rates))
    longconv = jnp.sum(pole_weight[None] * states, axis=1)
    gated = (query_part * (longconv + skip[None, :] * product)).astype(jnp.bfloat16)
    partial_terms = jnp.dot(gated, out_weight, preferred_element_type=jnp.float32)
    return lax.psum_scatter(partial_terms, "mp", scatter_dimension=1, tiled=True).astype(
        jnp.bfloat16
    )


def local(tokens, norm_gain, in_weight, short_filter, rates, residues, skip, out_weight, segment_ids):
    T = tokens.shape[0]
    shards = lax.axis_size("ctx")
    me = lax.axis_index("ctx")
    position = me.astype(jnp.int32)[None]
    lane_position = lax.axis_index("mp").astype(jnp.int32)[None]
    width = out_weight.shape[1] // lax.axis_size("mp")
    weight3 = jnp.transpose(in_weight, (1, 0, 2))
    out_weight = pltpu.with_memory_space_constraint(out_weight, pltpu.HBM)
    query, product, block, keep, visible, taps, rates, residues, skip = front(
        position, segment_ids.reshape(-1, 128), tokens, norm_gain[None], weight3, short_filter, rates, residues, skip[None])
    cuts = shards.bit_length() - 1
    each = product.shape[0] // cuts
    group, spans, arrived, parts, windows = block, [], [], [], []
    for k in range(cuts):
        span = 1 << k
        other = lax.ppermute(group, "ctx", [(a, a ^ span) for a in range(shards)])
        spans.append(span)
        arrived.append(other)
        *part, window = local_pass(
            k * each, each, min(k, 1), lane_position, product, keep, rates, residues, skip, out_weight, width, group)
        parts.append(part)
        windows.append(window)
        if k < cuts - 1:
            group = join(span, T, position, segment_ids, group, other, taps, rates, part[0])
    gated, send, mine, third, fourth = gate(T, spans, arrived, position, lane_position, segment_ids, query, parts, block,
                                            visible, taps, rates, skip, out_weight, windows[0], width)
    return scatter_line(lane_position, gated, send, mine, [windows[1], third, fourth], width)


def solution(mesh):
    placed = (
        P("ctx", None),
        P(),
        P(None, None, "mp"),
        P(None, None, "mp"),
        P(None, "mp"),
        P(None, "mp"),
        P("mp"),
        P("mp", None),
        P(),
    )
    shards, groups = mesh.shape["ctx"], mesh.shape["mp"]

    def body(tokens, norm_gain, in_weight, *rest):
        suits = groups == 8 and shards & (shards - 1) == 0 and shards > 2
        suits = suits and in_weight.shape[2] % 512 == 0 and in_weight.shape[0] % 2048 == 0
        suits = suits and tokens.shape[0] % 64 == 0 and rest[-1].shape[0] % 128 == 0 and rest[1].shape[0] % 8 == 0
        return (local if suits else general)(tokens, norm_gain, in_weight, *rest)

    return jax.shard_map(
        body, mesh=mesh, in_specs=placed, out_specs=P("ctx", "mp"), check_vma=False
    )
```

```python
import functools
import jax
import jax.numpy as jnp
from jax import lax
from jax.experimental import pallas as pl
from jax.experimental.pallas import tpu as pltpu
from jax.sharding import PartitionSpec as P

epsilon = 1e-06
f32 = jnp.float32
bf16 = jnp.bfloat16

PARTS = 8
HEAD = 16
MIB = 1 << 20


def vmem():
    return pl.BlockSpec(memory_space=pltpu.VMEM)


def smem():
    return pl.BlockSpec(memory_space=pltpu.SMEM)


def same_id(ids_ref, a, b):
    def get(t):
        return jnp.where(t < 0, -1, ids_ref[jnp.maximum(t, 0)])

    return (get(a) == get(b)).astype(f32)


def hbm():
    return pl.BlockSpec(memory_space=pltpu.HBM)


def front_kernel(
    geometry, position, ids_ref, tokens_ref, gain_ref, weight_ref, taps_ref, rates_ref, residues_ref, skip_ref,
    query_out, prod_out, block_out, keep_out, visible_out, taps, rates, residues, skip,
    ids, gain, tok, normed, ring, total, proj, head, idcol, near, twice, ending, sem, tok_sem, ring_sem,
):
    T, depth, channels, cb_size, kc_size, slots, poles = geometry
    run = T // PARTS
    kcs, cbs = depth // kc_size, channels // cb_size
    steps = kcs * cbs
    base = pl.multiple_of(position[0] * T, 8)

    def fetch(step):
        cb, kc, slot = step // kcs, step % kcs, step % slots
        return pltpu.make_async_copy(
            weight_ref.at[:, pl.ds(pl.multiple_of(kc * kc_size, kc_size), kc_size),
                          pl.ds(pl.multiple_of(cb * cb_size, cb_size), cb_size)],
            ring.at[slot], ring_sem.at[slot])

    small = [
        pltpu.make_async_copy(a, b, sem.at[i])
        for i, (a, b) in enumerate(
            ((ids_ref, ids), (gain_ref, gain), (taps_ref, taps), (rates_ref, rates), (residues_ref, residues),
             (skip_ref, skip)))
    ]
    small[0].start()
    small[1].start()
    chunk = T // 4
    tok_copies = [
        pltpu.make_async_copy(tokens_ref.at[pl.ds(c * chunk, chunk)], tok.at[pl.ds(c * chunk, chunk)], tok_sem.at[c])
        for c in range(4)
    ]
    for copy in tok_copies:
        copy.start()
    for copy in small[2:]:
        copy.start()
    for s in range(min(slots, steps)):
        fetch(s).start()

    small[0].wait()
    idcol[0:8, :] = jnp.full((8, 128), -1.0, f32)
    for b in range(ids.shape[0]):
        row = ids[b : b + 1, :].astype(f32)
        idcol[8 + b * 128 : 8 + (b + 1) * 128, :] = jnp.broadcast_to(row, (128, 128)).T
    near[...] = idcol[pl.ds(base, T + 8), :]
    here = near[8 : 8 + T, :]
    keep_out[...] = (here == near[7 : 7 + T, :]).astype(f32)
    twice[...] = (here == near[6 : 6 + T, :]).astype(f32)
    ending[...] = (here == near[7 + T : 8 + T, :]).astype(f32)
    before = near[pl.ds(7, PARTS, stride=run), :]
    for i in range(run):
        visible_out[i * 8 : (i + 1) * 8, :] = (near[pl.ds(8 + i, PARTS, stride=run), :] == before).astype(f32)
    for i in range(3):
        proj[i, 0:8, :] = jnp.zeros((8, cb_size), f32)
    head[...] = jnp.zeros(head.shape, f32)
    small[1].wait()

    def norm_rows(g, _):
        part = pl.ds(pl.multiple_of(g * 16, 16), 16)
        x = tok[part, :].astype(f32)
        scale = lax.rsqrt(jnp.sum(x * x, axis=-1, keepdims=True) * (1.0 / depth) + epsilon)
        normed[part, :] = (x * scale * gain[...]).astype(bf16)
        return 0

    for c, copy in enumerate(tok_copies):
        copy.wait()
        lax.fori_loop(c * chunk // 16, (c + 1) * chunk // 16, norm_rows, 0)
    for copy in small[2:]:
        copy.wait()

    def epilogue(cb):
        cols = pl.ds(pl.multiple_of(cb * cb_size, cb_size), cb_size)
        feats = []
        m1 = jnp.concatenate([keep_out[...]] * (cb_size // 128), axis=1)
        m2 = jnp.concatenate([twice[...]] * (cb_size // 128), axis=1)
        for i in range(3):
            p = total[i].astype(bf16).astype(f32)
            proj[i, 8 : 8 + T, :] = p
            tap = [taps[j, i : i + 1, cols] for j in range(3)]
            feats.append(
                tap[0] * p + m1 * (tap[1] * proj[i, 7 : 7 + T, :]) + m2 * (tap[2] * proj[i, 6 : 6 + T, :]))
        query_out[:, cols] = feats[0]
        for i in range(1, 3):
            head[2 * (i - 1) : 2 * i, :] = proj[i, 8:10, :]
        for i in range(3):
            head[4 + 2 * i : 6 + 2 * i, :] = proj[i, 6 + T : 8 + T, :]
        block_out[poles : poles + HEAD, cols] = head[...].astype(bf16)
        product = feats[1] * feats[2]
        back = 7.0 - lax.broadcasted_iota(jnp.int32, (8, 128), 0).astype(f32)
        for lane in range(cb_size // 128):
            tile = cb * (cb_size // 128) + lane
            lanes = pl.ds(pl.multiple_of(tile * 128, 128), 128)
            prod_out[tile] = product[:, lane * 128 : lane * 128 + 128]
            r16 = rates[:, lanes]
            jump = jnp.exp(-8.0 * r16)
            leap = [jnp.broadcast_to(jump[n : n + 1], (8, 128)) for n in range(poles)]

            def eight(g, sums):
                part = pl.ds(pl.multiple_of(g * 8, 8), 8)
                p = prod_out[tile, part, :] * ending[part, :]
                return tuple(sums[n] * leap[n] + p for n in range(poles))

            sums = lax.fori_loop(
                0, T // 8, eight, tuple(jnp.zeros((8, 128), f32) for _ in range(poles)), unroll=4)
            ends = [
                jnp.sum(sums[n] * jnp.exp(-back * r16[n : n + 1]), axis=0, keepdims=True) for n in range(poles)
            ]
            block_out[0:poles, lanes] = jnp.concatenate(ends, axis=0).astype(bf16)

    def step_body(step, _):
        cb, kc, slot = step // kcs, step % kcs, step % slots
        fetch(step).wait()
        lhs = normed[:, pl.ds(pl.multiple_of(kc * kc_size, kc_size), kc_size)]
        for i in range(3):
            part = jnp.dot(lhs, ring[slot, i], preferred_element_type=f32)
            total[i] = jnp.where(kc == 0, part, total[i] + part)

        @pl.when(step + slots < steps)
        def _():
            fetch(step + slots).start()

        @pl.when(kc == kcs - 1)
        def _():
            epilogue(cb)

        return 0

    total[...] = jnp.zeros(total.shape, f32)
    lax.fori_loop(0, steps, step_body, 0)


def front(position, ids2, tokens, gain, weight3, taps, rates, residues, skip):
    T, depth = tokens.shape
    channels, poles = weight3.shape[2], rates.shape[0]
    cb_size, kc_size, slots = 256, 2048, 5
    geometry = (T, depth, channels, cb_size, kc_size, slots, poles)
    kept = [pltpu.VMEM(a.shape, a.dtype) for a in (taps, rates, residues, skip)]
    ids2, tokens, gain, weight3, taps, rates, residues, skip = [
        pltpu.with_memory_space_constraint(a, pltpu.HBM)
        for a in (ids2, tokens, gain, weight3, taps, rates, residues, skip)
    ]
    return pl.pallas_call(
        functools.partial(front_kernel, geometry),
        out_shape=[
            jax.ShapeDtypeStruct((T, channels), f32),
            jax.ShapeDtypeStruct((channels // 128, T, 128), f32),
            jax.ShapeDtypeStruct((poles + HEAD, channels), bf16),
            jax.ShapeDtypeStruct((T, 128), f32),
            jax.ShapeDtypeStruct((T, 128), f32),
        ] + kept,
        in_specs=[smem()] + [hbm()] * 8,
        out_specs=[vmem()] * 9,
        scratch_shapes=[
            pltpu.VMEM(ids2.shape, ids2.dtype),
            pltpu.VMEM(gain.shape, f32),
            pltpu.VMEM((T, depth), bf16),
            pltpu.VMEM((T, depth), bf16),
            pltpu.VMEM((slots, 3, kc_size, cb_size), bf16),
            pltpu.VMEM((3, T, cb_size), f32),
            pltpu.VMEM((3, T + 8, cb_size), f32),
            pltpu.VMEM((HEAD, cb_size), f32),
            pltpu.VMEM((ids2.shape[0] * 128 + 8, 128), f32),
            pltpu.VMEM((T + 8, 128), f32),
            pltpu.VMEM((T, 128), f32),
            pltpu.VMEM((T, 128), f32),
            pltpu.SemaphoreType.DMA((6,)),
            pltpu.SemaphoreType.DMA((4,)),
            pltpu.SemaphoreType.DMA((slots,)),
        ],
        compiler_params=pltpu.CompilerParams(vmem_limit_bytes=28 * MIB),
        name="front",
    )(position, ids2, tokens, gain, weight3, taps, rates, residues, skip)


def expm1(x):
    series = jnp.ones_like(x)
    for k in range(9, 1, -1):
        series = 1.0 + series * x * (1.0 / k)
    return jnp.where(jnp.abs(x) < 0.5, x * series, jnp.exp(x) - 1.0)


def local_kernel(
    poles, first, slot, lane_position, prod_ref, keep_ref, rates_ref, residues_ref, skip_ref, out_ref, _,
    local_out, state_out, pole_out, window_out, sem,
):
    copy = columns(lane_position[0], slot, out_ref, window_out, sem)
    copy.start()
    tiles, T, _ = local_out.shape
    run = T // PARTS
    mine = slice(first * 128, (first + tiles) * 128)
    pole_out[...] = residues_ref[:, mine] * jnp.sqrt(-expm1(-2.0 * rates_ref[:, mine]))

    def tile_body(tile, _):
        lanes = pl.ds(pl.multiple_of((first + tile) * 128, 128), 128)
        d16 = jnp.exp(-rates_ref[:, lanes])
        w16 = pole_out[:, pl.ds(pl.multiple_of(tile * 128, 128), 128)]
        decay = [jnp.broadcast_to(d16[n : n + 1], (8, 128)) for n in range(poles)]
        weight = [jnp.broadcast_to(w16[n : n + 1], (8, 128)) for n in range(poles)]
        skip = skip_ref[0:1, lanes]

        def token(i, states):
            at = pl.ds(i, PARTS, stride=run)
            p, keep = prod_ref[first + tile, at, :], keep_ref[at, :]
            after = [states[n] * decay[n] * keep + p for n in range(poles)]
            local_out[tile, at, :] = tree([skip * p] + [weight[n] * after[n] for n in range(poles)])
            return tuple(after)

        states = lax.fori_loop(0, run, token, tuple(jnp.zeros((8, 128), f32) for _ in range(poles)), unroll=2)
        for n in range(poles):
            state_out[tile, pl.ds(n, PARTS, stride=poles), :] = states[n]
        return 0

    lax.fori_loop(0, tiles, tile_body, 0)
    copy.wait()


def tree(terms):
    while len(terms) > 1:
        terms = [a + b for a, b in zip(terms[0::2], terms[1::2])] + terms[len(terms) // 2 * 2 :]
    return terms[0]


def local_pass(first, tiles, slot, lane_position, product, keep, rates, residues, skip, out_weight, width, after):
    T, poles = product.shape[1], rates.shape[0]
    return pl.pallas_call(
        functools.partial(local_kernel, poles, first, slot),
        out_shape=(
            jax.ShapeDtypeStruct((tiles, T, 128), f32),
            jax.ShapeDtypeStruct((tiles, PARTS * poles, 128), f32),
            jax.ShapeDtypeStruct((poles, tiles * 128), f32),
            jax.ShapeDtypeStruct((out_weight.shape[0], 2 * width), bf16),
        ),
        in_specs=[smem()] + [vmem()] * 5 + [hbm(), pl.BlockSpec(memory_space=pl.ANY)],
        out_specs=[vmem()] * 4,
        scratch_shapes=[pltpu.SemaphoreType.DMA],
        compiler_params=pltpu.CompilerParams(vmem_limit_bytes=8 * MIB),
        cost_estimate=pl.CostEstimate(flops=6 * T * poles * tiles * 128, bytes_accessed=8 * MIB, transcendentals=0),
        name="local_pass",
    )(lane_position, product, keep, rates, residues, skip, out_weight, after)


def first_products(first, last, taps, ids_ref, base):
    s01, s0m1 = same_id(ids_ref, base + 1, base), same_id(ids_ref, base, base - 1)
    s0m2, s1m1 = same_id(ids_ref, base, base - 2), same_id(ids_ref, base + 1, base - 1)

    def shift(i):
        near, far = last[i][1:2], last[i][0:1]
        t1, t2 = taps[1][i : i + 1], taps[2][i : i + 1]
        return s0m1 * (t1 * near) + s0m2 * (t2 * far), s1m1 * (t2 * near)

    def plain(i):
        t0, t1 = taps[0][i : i + 1], taps[1][i : i + 1]
        return t0 * first[i][0:1], t0 * first[i][1:2] + s01 * (t1 * first[i][0:1])

    k, v, dk, dv = plain(1), plain(2), shift(1), shift(2)
    delta = [(k[j] + dk[j]) * (v[j] + dv[j]) - k[j] * v[j] for j in range(2)]
    return shift(0), delta


def unpack(block, poles):
    first = [None, block[poles : poles + 2], block[poles + 2 : poles + 4]]
    last = [block[poles + 4 + 2 * i : poles + 6 + 2 * i] for i in range(3)]
    return block[0:poles], first, last


def joined_state(low_state, low_last, up_state, up_first, taps, rates, ids_ref, base, length):
    _, delta = first_products(up_first, low_last, taps, ids_ref, base)
    grown = low_state + delta[0] * jnp.exp(rates) + delta[1] * jnp.exp(2.0 * rates)
    open_ = same_id(ids_ref, base + length - 1, base - 1)
    return up_state + grown * (jnp.exp(-rates * jnp.float32(length)) * open_)


def join_kernel(T, poles, span, position, ids_ref, mine_ref, other_ref, taps_ref, rates_ref, _, out):
    me = position[0]
    is_upper = (me // span) % 2 == 1
    base = (me // (2 * span)) * (2 * span * T) + span * T
    mine, other = mine_ref[...].astype(f32), other_ref[...].astype(f32)
    lower, upper = jnp.where(is_upper, other, mine), jnp.where(is_upper, mine, other)
    taps = [taps_ref[j] for j in range(3)]
    low_state, _, low_last = unpack(lower, poles)
    up_state, up_first, _ = unpack(upper, poles)
    state = joined_state(low_state, low_last, up_state, up_first, taps, rates_ref[...], ids_ref, base, span * T)
    out[0:poles, :] = state.astype(bf16)
    row = lax.broadcasted_iota(jnp.int32, (HEAD, lower.shape[1]), 0)
    out[poles : poles + HEAD, :] = jnp.where(row < 4, lower[poles:], upper[poles:]).astype(bf16)


def join(span, T, position, ids, mine, other, taps, rates, after):
    poles = rates.shape[0]
    return pl.pallas_call(
        functools.partial(join_kernel, T, poles, span),
        out_shape=jax.ShapeDtypeStruct(mine.shape, bf16),
        in_specs=[smem(), smem()] + [vmem()] * 4 + [pl.BlockSpec(memory_space=pl.ANY)],
        out_specs=vmem(),
        compiler_params=pltpu.CompilerParams(vmem_limit_bytes=4 * MIB),
        name="join",
    )(position, ids, mine, other, taps, rates, after)


def gate_kernel(
    T, poles, spans, cuts, position, lane_position, ids_ref, query_ref, block_ref, visible_ref, taps_ref, rates_ref, skip_ref,
    window_ref, *rest,
):
    arrived, rest = rest[: len(spans)], rest[len(spans) :]
    parts, rest = [rest[3 * c : 3 * c + 3] for c in range(cuts)], rest[3 * cuts :]
    gated_out, send_out, mine_out, carry, full = rest
    run = T // PARTS
    tiles = query_ref.shape[1] // 128
    me = position[0]
    base = me * T
    taps = [taps_ref[j] for j in range(3)]
    rates, skip = rates_ref[...], skip_ref[...]
    weight = jnp.concatenate([pole_ref[...] for _, _, pole_ref in parts], axis=1)
    each = tiles // cuts
    prior = jnp.zeros(block_ref.shape, f32)
    prior_state, prior_first, prior_last = unpack(prior, poles)
    for span, ref in zip(spans, arrived):
        state, first, last = unpack(ref[...].astype(f32), poles)
        upper, held = (me // span) % 2 == 1, me % span
        if span == 1:
            both = state
        else:
            both = joined_state(
                state, last, prior_state, prior_first, taps, rates, ids_ref, (me - held) * T, held * T)
        fresh = upper & (held == 0)
        prior_state = jnp.where(fresh, state, jnp.where(upper, both, prior_state))
        prior_first = [None] + [jnp.where(upper, first[i], prior_first[i]) for i in (1, 2)]
        prior_last = [jnp.where(fresh, last[i], prior_last[i]) for i in range(3)]
    _, first, _ = unpack(block_ref[...].astype(f32), poles)
    q_shift, delta = first_products(first, prior_last, taps, ids_ref, base)
    second = delta[1] * jnp.exp(rates)
    now = prior_state + (delta[0] + second) * jnp.exp(rates)
    fix0 = skip * delta[0] - jnp.sum(weight * second, axis=0, keepdims=True)
    fix1 = skip * delta[1]
    jump = jnp.exp(-rates * float(run))
    for s in range(PARTS):
        part = slice(s * poles, (s + 1) * poles)
        began = weight * now
        for tile in range(tiles):
            carry[tile, part, :] = began[:, tile * 128 : tile * 128 + 128]
        if s < PARTS - 1:
            whole = same_id(ids_ref, base + s * run + run - 1, base + s * run - 1)
            ends = jnp.concatenate([parts[tile // each][1][tile % each, part, :] for tile in range(tiles)], axis=1)
            now = now * (jump * whole) + ends

    def lane_body(cut, inner, _):
        tile = cut * each + inner
        lanes = pl.ds(pl.multiple_of(tile * 128, 128), 128)
        d16 = jnp.exp(-rates_ref[:, lanes])
        decay = [jnp.broadcast_to(d16[n : n + 1], (8, 128)) for n in range(poles)]
        start = tuple(carry[tile, pl.ds(n, PARTS, stride=poles), :] for n in range(poles))

        def token(i, states):
            after = [states[n] * decay[n] for n in range(poles)]
            see = visible_ref[pl.ds(pl.multiple_of(i * 8, 8), 8), :]
            at = pl.ds(i, PARTS, stride=run)
            full[tile, at, :] = parts[cut][0][inner, at, :] + see * tree(list(after))
            return tuple(after)

        lax.fori_loop(0, run, token, start, unroll=4)
        return 0

    for cut in range(cuts):
        lax.fori_loop(0, each, functools.partial(lane_body, cut), 0)
    row = lax.broadcasted_iota(jnp.int32, (16, 128), 0)
    for tile in range(tiles):
        lanes = slice(tile * 128, tile * 128 + 128)
        gated_out[:, lanes] = (query_ref[:, lanes] * full[tile]).astype(bf16)
        top_q, top = query_ref[0:16, lanes], full[tile, 0:16, :]
        top_q = top_q + jnp.where(row == 0, q_shift[0][:, lanes], 0.0) + jnp.where(row == 1, q_shift[1][:, lanes], 0.0)
        top = top + jnp.where(row == 0, fix0[:, lanes], 0.0) + jnp.where(row == 1, fix1[:, lanes], 0.0)
        gated_out[0:16, lanes] = (top_q * top).astype(bf16)
    share(lane_position[0], gated_out, window_ref, send_out, mine_out)


def target(index, slot):
    chip = index // 2
    odd = chip % 2
    if slot == 0:
        return 3 - 3 * odd
    if slot == 1:
        return 1 + odd
    if slot == 2:
        return (chip + 2) % 4
    return chip


def columns(index, slot, out_ref, window, sem):
    both = window.shape[1]
    start = pl.multiple_of(target(index, slot) * both, both)
    return pltpu.make_async_copy(out_ref.at[:, pl.ds(start, both)], window, sem)


def share(index, gated_ref, window, send_out, mine_out):
    width = send_out.shape[1]
    tile = 256
    core = index % 2

    for j in range(width // tile):
        at = slice(j * tile, j * tile + tile)
        for out, half in ((send_out, 1 - core), (mine_out, core)):
            cols = pl.ds(pl.multiple_of(half * width + j * tile, tile), tile)
            out[:, at] = jnp.dot(gated_ref[...], window[:, cols], preferred_element_type=f32).astype(out.dtype)


def share_kernel(count, lane_position, gated_ref, *rest):
    windows, outs = rest[:count], rest[count:]
    for k, window in enumerate(windows):
        share(lane_position[0], gated_ref, window, outs[2 * k], outs[2 * k + 1])


def shares(lane_position, gated, windows, width):
    T, channels = gated.shape
    count = len(windows)
    return pl.pallas_call(
        functools.partial(share_kernel, count),
        out_shape=[jax.ShapeDtypeStruct((T, width), d) for _ in windows for d in (bf16, f32)],
        in_specs=[smem(), vmem()] + [vmem()] * count,
        out_specs=[vmem()] * (2 * count),
        compiler_params=pltpu.CompilerParams(vmem_limit_bytes=4 * MIB),
        cost_estimate=pl.CostEstimate(
            flops=4 * T * channels * width * count, bytes_accessed=4 * channels * width * count, transcendentals=0),
        name="shares",
    )(lane_position, gated, *windows)


def late_share_kernel(slots, lane_position, gated_ref, out_ref, *rest):
    outs, (windows, sem) = rest[:-2], rest[-2:]
    copies = [columns(lane_position[0], slot, out_ref, windows.at[k], sem.at[k]) for k, slot in enumerate(slots)]
    for copy in copies:
        copy.start()
    for k, copy in enumerate(copies):
        copy.wait()
        share(lane_position[0], gated_ref, windows.at[k], outs[2 * k], outs[2 * k + 1])


def late_shares(slots, lane_position, gated, out_weight, width):
    T, channels = gated.shape
    count = len(slots)
    return pl.pallas_call(
        functools.partial(late_share_kernel, slots),
        out_shape=[jax.ShapeDtypeStruct((T, width), d) for _ in slots for d in (bf16, f32)],
        in_specs=[smem(), vmem(), hbm()],
        out_specs=[vmem()] * (2 * count),
        scratch_shapes=[pltpu.VMEM((count, channels, 2 * width), bf16), pltpu.SemaphoreType.DMA((count,))],
        compiler_params=pltpu.CompilerParams(vmem_limit_bytes=10 * MIB),
        cost_estimate=pl.CostEstimate(
            flops=4 * T * channels * width * count, bytes_accessed=4 * channels * width * count, transcendentals=0),
        name="late_shares",
    )(lane_position, gated, out_weight)


def gate(T, spans, arrived, position, lane_position, ids, query, parts, block, visible, taps, rates, skip, window, width):
    poles, channels = rates.shape
    return pl.pallas_call(
        functools.partial(gate_kernel, T, poles, tuple(spans), len(parts)),
        out_shape=[
            jax.ShapeDtypeStruct(query.shape, bf16),
            jax.ShapeDtypeStruct((T, width), bf16),
            jax.ShapeDtypeStruct((T, width), f32),
        ],
        in_specs=[smem()] * 3 + [vmem()] * (7 + len(spans) + 3 * len(parts)),
        out_specs=[vmem()] * 3,
        scratch_shapes=[
            pltpu.VMEM((channels // 128, PARTS * poles, 128), f32),
            pltpu.VMEM((channels // 128, T, 128), f32),
        ],
        compiler_params=pltpu.CompilerParams(vmem_limit_bytes=6 * MIB),
        name="gate",
    )(position, lane_position, ids, query, block, visible, taps, rates, skip, window, *arrived,
      *[a for part in parts for a in part])


def total(*terms):
    return functools.reduce(lambda a, b: a + b, [t.astype(f32) for t in terms]).astype(bf16)


def scatter_line(lane_position, gated, send, mine, window, out_weight, width):
    chip = lax.axis_index("mp") // 2
    inner = (chip == 1) | (chip == 2)
    pair = [(m, m ^ 1) for m in range(8)]

    def along(hops):
        return [(a * 2 + c, b * 2 + c) for a, b in hops for c in range(2)]

    def where(mask, x):
        return jnp.where(mask, x.astype(f32), 0.0)

    def hop(x, hops):
        return lax.ppermute(x, "mp", hops)

    near = along([(0, 1), (1, 0), (2, 3), (3, 2)])
    traded = hop(send, pair)
    far = total(mine, traded)
    from_near = hop(far, near)
    send, mine = shares(lane_position, gated, [window], width)
    second = total(mine, hop(send, pair))
    from_end = hop(second, near)
    from_middle = hop(second, along([(1, 2), (2, 1)]))
    send2, mine2, send3, mine3 = late_shares((2, 3), lane_position, gated, out_weight, width)
    across = total(mine2, hop(send2, pair), where(inner, from_near))
    own = total(mine3, hop(send3, pair))
    from_across = lax.ppermute(across, "mp", along([(0, 2), (1, 3), (2, 0), (3, 1)]))
    return total(own, jnp.where(inner, from_end.astype(f32), from_near.astype(f32)), from_middle, from_across)


def shifted(value, axis, steps):
    count = lax.axis_size(axis)
    leading, last = (max(0, -steps), min(count, count - steps))
    return lax.ppermute(value, axis, [(source, source + steps) for source in range(leading, last)])


def project(block, norm_gain, weights):
    floats = block.astype(jnp.float32)
    mean_square = jnp.mean(floats * floats, axis=-1, keepdims=True)
    normed = (floats * lax.rsqrt(mean_square + epsilon) * norm_gain[None, :]).astype(jnp.bfloat16)
    return jnp.dot(normed, weights, preferred_element_type=jnp.float32).astype(jnp.bfloat16)


def general(
    tokens, norm_gain, in_weight, short_filter, rates, residues, skip, out_weight, segment_ids
):
    tok_rows = tokens.shape[0]
    model_width = tokens.shape[1]
    channels = in_weight.shape[2]
    filter_taps = short_filter.shape[0]
    pole_count = rates.shape[0]
    device_index = lax.axis_index("ctx")
    row_offset = device_index * tok_rows
    weights = in_weight.reshape(model_width, 3 * channels)
    projected = project(tokens, norm_gain, weights)
    previous = shifted(projected[tok_rows - (filter_taps - 1) :], "ctx", 1)
    extended = jnp.concatenate([previous, projected], axis=0)
    padded_ids = jnp.concatenate([jnp.full((filter_taps,), -1, jnp.int32), segment_ids], axis=0)
    window = lax.dynamic_slice_in_dim(padded_ids, row_offset, tok_rows + filter_taps, 0)
    local_ids = window[filter_taps:]
    taps_table = short_filter.reshape(filter_taps, 3 * channels)
    featured = jnp.zeros((tok_rows, 3 * channels), jnp.float32)
    for lag_index in range(filter_taps):
        begin = filter_taps - 1 - lag_index
        lagged = extended[begin : begin + tok_rows].astype(jnp.float32)
        matches = window[filter_taps - lag_index : filter_taps - lag_index + tok_rows] == local_ids
        term = taps_table[lag_index][None, :] * lagged
        featured = featured + jnp.where(matches[:, None], term, jnp.zeros_like(term))
    query_part = featured[:, :channels]
    key_part = featured[:, channels : 2 * channels]
    value_part = featured[:, 2 * channels :]
    product = key_part * value_part
    offsets = jnp.arange(tok_rows, dtype=jnp.float32)
    center = float(tok_rows // 2)
    growth = jnp.exp(-(offsets - center)[:, None, None] * rates[None])
    shrinkage = jnp.exp((offsets - center)[:, None, None] * rates[None])
    weighted = (shrinkage * product[:, None, :]).reshape(tok_rows, pole_count * channels)
    visible = (offsets[:, None] >= offsets[None, :]) & (local_ids[:, None] == local_ids[None, :])
    in_block = jnp.dot(visible.astype(jnp.float32), weighted, precision=lax.Precision.HIGHEST)
    in_block = in_block.reshape(tok_rows, pole_count, channels) * growth
    survives = local_ids == window[filter_taps - 1]
    block_factor = jnp.exp(-rates * tok_rows)
    block_end = in_block[tok_rows - 1]
    block_ends = lax.all_gather(block_end[None], "ctx", axis=0, tiled=True)
    shard_count = segment_ids.shape[0] // tok_rows
    last_ids = segment_ids.reshape(shard_count, tok_rows)[:, tok_rows - 1]
    prior_ids = jnp.concatenate([jnp.full((1,), -1, jnp.int32), last_ids[:-1]], axis=0)
    shard_decays = block_factor[None] * (last_ids == prior_ids).astype(jnp.float32)[:, None, None]

    def absorb(running, inputs):
        shard, factor, shard_end = inputs
        advanced = running * factor + shard_end
        return (jnp.where(shard < device_index, advanced, running), None)

    incoming, _ = lax.scan(
        absorb,
        jnp.zeros_like(block_end),
        (jnp.arange(shard_count, dtype=jnp.int32), shard_decays, block_ends),
    )
    carried = incoming[None] * jnp.exp(-(offsets + 1.0)[:, None, None] * rates[None])
    carried = carried * survives.astype(jnp.float32)[:, None, None]
    states = in_block + carried
    pole_weight = residues * jnp.sqrt(-jnp.expm1(-2.0 * rates))
    longconv = jnp.sum(pole_weight[None] * states, axis=1)
    gated = (query_part * (longconv + skip[None, :] * product)).astype(jnp.bfloat16)
    partial_terms = jnp.dot(gated, out_weight, preferred_element_type=jnp.float32)
    return lax.psum_scatter(partial_terms, "mp", scatter_dimension=1, tiled=True).astype(
        jnp.bfloat16
    )


def local(tokens, norm_gain, in_weight, short_filter, rates, residues, skip, out_weight, segment_ids):
    T = tokens.shape[0]
    shards = lax.axis_size("ctx")
    me = lax.axis_index("ctx")
    position = me.astype(jnp.int32)[None]
    lane_position = lax.axis_index("mp").astype(jnp.int32)[None]
    width = out_weight.shape[1] // lax.axis_size("mp")
    weight3 = jnp.transpose(in_weight, (1, 0, 2))
    out_weight = pltpu.with_memory_space_constraint(out_weight, pltpu.HBM)
    query, product, block, keep, visible, taps, rates, residues, skip = front(
        position, segment_ids.reshape(-1, 128), tokens, norm_gain[None], weight3, short_filter, rates, residues, skip[None])
    cuts = shards.bit_length() - 1
    each = product.shape[0] // cuts
    group, spans, arrived, parts, windows = block, [], [], [], []
    for k in range(cuts):
        span = 1 << k
        other = lax.ppermute(group, "ctx", [(a, a ^ span) for a in range(shards)])
        spans.append(span)
        arrived.append(other)
        *part, window = local_pass(
            k * each, each, min(k, 1), lane_position, product, keep, rates, residues, skip, out_weight, width, group)
        parts.append(part)
        windows.append(window)
        if k < cuts - 1:
            group = join(span, T, position, segment_ids, group, other, taps, rates, part[0])
    gated, send, mine = gate(T, spans, arrived, position, lane_position, segment_ids, query, parts, block, visible, taps, rates,
                             skip, windows[0], width)
    return scatter_line(lane_position, gated, send, mine, windows[1], out_weight, width)


def solution(mesh):
    placed = (
        P("ctx", None),
        P(),
        P(None, None, "mp"),
        P(None, None, "mp"),
        P(None, "mp"),
        P(None, "mp"),
        P("mp"),
        P("mp", None),
        P(),
    )
    shards, groups = mesh.shape["ctx"], mesh.shape["mp"]

    def body(tokens, norm_gain, in_weight, *rest):
        suits = groups == 8 and shards & (shards - 1) == 0 and shards > 2
        suits = suits and in_weight.shape[2] % 512 == 0 and in_weight.shape[0] % 2048 == 0
        suits = suits and tokens.shape[0] % 64 == 0 and rest[-1].shape[0] % 128 == 0 and rest[1].shape[0] % 8 == 0
        return (local if suits else general)(tokens, norm_gain, in_weight, *rest)

    return jax.shard_map(
        body, mesh=mesh, in_specs=placed, out_specs=P("ctx", "mp"), check_vma=False
    )
```

```python
import functools
import jax
import jax.numpy as jnp
from jax import lax
from jax.experimental import pallas as pl
from jax.experimental.pallas import tpu as pltpu
from jax.sharding import PartitionSpec as P

epsilon = 1e-06
f32 = jnp.float32
bf16 = jnp.bfloat16

PARTS = 8
HEAD = 16
MIB = 1 << 20


def vmem():
    return pl.BlockSpec(memory_space=pltpu.VMEM)


def smem():
    return pl.BlockSpec(memory_space=pltpu.SMEM)


def same_id(ids_ref, a, b):
    def get(t):
        return jnp.where(t < 0, -1, ids_ref[jnp.maximum(t, 0)])

    return (get(a) == get(b)).astype(f32)


def hbm():
    return pl.BlockSpec(memory_space=pltpu.HBM)


def front_kernel(
    geometry, position, ids_ref, tokens_ref, gain_ref, weight_ref, taps_ref, rates_ref, residues_ref, skip_ref,
    query_out, prod_out, block_out, keep_out, visible_out, taps, rates, residues, skip,
    ids, gain, tok, normed, ring, total, proj, head, idcol, near, twice, ending, sem, tok_sem, ring_sem,
):
    T, depth, channels, cb_size, kc_size, slots, poles = geometry
    run = T // PARTS
    kcs, cbs = depth // kc_size, channels // cb_size
    steps = kcs * cbs
    base = pl.multiple_of(position[0] * T, 8)

    def fetch(step):
        cb, kc, slot = step // kcs, step % kcs, step % slots
        return pltpu.make_async_copy(
            weight_ref.at[:, pl.ds(pl.multiple_of(kc * kc_size, kc_size), kc_size),
                          pl.ds(pl.multiple_of(cb * cb_size, cb_size), cb_size)],
            ring.at[slot], ring_sem.at[slot])

    small = [
        pltpu.make_async_copy(a, b, sem.at[i])
        for i, (a, b) in enumerate(
            ((ids_ref, ids), (gain_ref, gain), (taps_ref, taps), (rates_ref, rates), (residues_ref, residues),
             (skip_ref, skip)))
    ]
    small[0].start()
    small[1].start()
    chunk = T // 4
    tok_copies = [
        pltpu.make_async_copy(tokens_ref.at[pl.ds(c * chunk, chunk)], tok.at[pl.ds(c * chunk, chunk)], tok_sem.at[c])
        for c in range(4)
    ]
    for copy in tok_copies:
        copy.start()
    for copy in small[2:]:
        copy.start()
    for s in range(min(slots, steps)):
        fetch(s).start()

    small[0].wait()
    idcol[0:8, :] = jnp.full((8, 128), -1.0, f32)
    for b in range(ids.shape[0]):
        row = ids[b : b + 1, :].astype(f32)
        idcol[8 + b * 128 : 8 + (b + 1) * 128, :] = jnp.broadcast_to(row, (128, 128)).T
    near[...] = idcol[pl.ds(base, T + 8), :]
    here = near[8 : 8 + T, :]
    keep_out[...] = (here == near[7 : 7 + T, :]).astype(f32)
    twice[...] = (here == near[6 : 6 + T, :]).astype(f32)
    ending[...] = (here == near[7 + T : 8 + T, :]).astype(f32)
    before = near[pl.ds(7, PARTS, stride=run), :]
    for i in range(run):
        visible_out[i * 8 : (i + 1) * 8, :] = (near[pl.ds(8 + i, PARTS, stride=run), :] == before).astype(f32)
    for i in range(3):
        proj[i, 0:8, :] = jnp.zeros((8, cb_size), f32)
    head[...] = jnp.zeros(head.shape, f32)
    small[1].wait()

    def norm_rows(g, _):
        part = pl.ds(pl.multiple_of(g * 16, 16), 16)
        x = tok[part, :].astype(f32)
        scale = lax.rsqrt(jnp.sum(x * x, axis=-1, keepdims=True) * (1.0 / depth) + epsilon)
        normed[part, :] = (x * scale * gain[...]).astype(bf16)
        return 0

    for c, copy in enumerate(tok_copies):
        copy.wait()
        lax.fori_loop(c * chunk // 16, (c + 1) * chunk // 16, norm_rows, 0)
    for copy in small[2:]:
        copy.wait()

    def epilogue(cb):
        cols = pl.ds(pl.multiple_of(cb * cb_size, cb_size), cb_size)
        feats = []
        m1 = jnp.concatenate([keep_out[...]] * (cb_size // 128), axis=1)
        m2 = jnp.concatenate([twice[...]] * (cb_size // 128), axis=1)
        for i in range(3):
            p = total[i].astype(bf16).astype(f32)
            proj[i, 8 : 8 + T, :] = p
            tap = [taps[j, i : i + 1, cols] for j in range(3)]
            feats.append(
                tap[0] * p + m1 * (tap[1] * proj[i, 7 : 7 + T, :]) + m2 * (tap[2] * proj[i, 6 : 6 + T, :]))
        query_out[:, cols] = feats[0]
        for i in range(1, 3):
            head[2 * (i - 1) : 2 * i, :] = proj[i, 8:10, :]
        for i in range(3):
            head[4 + 2 * i : 6 + 2 * i, :] = proj[i, 6 + T : 8 + T, :]
        block_out[poles : poles + HEAD, cols] = head[...].astype(bf16)
        product = feats[1] * feats[2]
        back = 7.0 - lax.broadcasted_iota(jnp.int32, (8, 128), 0).astype(f32)
        for lane in range(cb_size // 128):
            tile = cb * (cb_size // 128) + lane
            lanes = pl.ds(pl.multiple_of(tile * 128, 128), 128)
            prod_out[tile] = product[:, lane * 128 : lane * 128 + 128]
            r16 = rates[:, lanes]
            jump = jnp.exp(-8.0 * r16)
            leap = [jnp.broadcast_to(jump[n : n + 1], (8, 128)) for n in range(poles)]

            def eight(g, sums):
                part = pl.ds(pl.multiple_of(g * 8, 8), 8)
                p = prod_out[tile, part, :] * ending[part, :]
                return tuple(sums[n] * leap[n] + p for n in range(poles))

            sums = lax.fori_loop(
                0, T // 8, eight, tuple(jnp.zeros((8, 128), f32) for _ in range(poles)), unroll=4)
            ends = [
                jnp.sum(sums[n] * jnp.exp(-back * r16[n : n + 1]), axis=0, keepdims=True) for n in range(poles)
            ]
            block_out[0:poles, lanes] = jnp.concatenate(ends, axis=0).astype(bf16)

    def step_body(step, _):
        cb, kc, slot = step // kcs, step % kcs, step % slots
        fetch(step).wait()
        lhs = normed[:, pl.ds(pl.multiple_of(kc * kc_size, kc_size), kc_size)]
        for i in range(3):
            part = jnp.dot(lhs, ring[slot, i], preferred_element_type=f32)
            total[i] = jnp.where(kc == 0, part, total[i] + part)

        @pl.when(step + slots < steps)
        def _():
            fetch(step + slots).start()

        @pl.when(kc == kcs - 1)
        def _():
            epilogue(cb)

        return 0

    total[...] = jnp.zeros(total.shape, f32)
    lax.fori_loop(0, steps, step_body, 0)


def front(position, ids2, tokens, gain, weight3, taps, rates, residues, skip):
    T, depth = tokens.shape
    channels, poles = weight3.shape[2], rates.shape[0]
    cb_size, kc_size, slots = 256, 2048, 5
    geometry = (T, depth, channels, cb_size, kc_size, slots, poles)
    kept = [pltpu.VMEM(a.shape, a.dtype) for a in (taps, rates, residues, skip)]
    ids2, tokens, gain, weight3, taps, rates, residues, skip = [
        pltpu.with_memory_space_constraint(a, pltpu.HBM)
        for a in (ids2, tokens, gain, weight3, taps, rates, residues, skip)
    ]
    return pl.pallas_call(
        functools.partial(front_kernel, geometry),
        out_shape=[
            jax.ShapeDtypeStruct((T, channels), f32),
            jax.ShapeDtypeStruct((channels // 128, T, 128), f32),
            jax.ShapeDtypeStruct((poles + HEAD, channels), bf16),
            jax.ShapeDtypeStruct((T, 128), f32),
            jax.ShapeDtypeStruct((T, 128), f32),
        ] + kept,
        in_specs=[smem()] + [hbm()] * 8,
        out_specs=[vmem()] * 9,
        scratch_shapes=[
            pltpu.VMEM(ids2.shape, ids2.dtype),
            pltpu.VMEM(gain.shape, f32),
            pltpu.VMEM((T, depth), bf16),
            pltpu.VMEM((T, depth), bf16),
            pltpu.VMEM((slots, 3, kc_size, cb_size), bf16),
            pltpu.VMEM((3, T, cb_size), f32),
            pltpu.VMEM((3, T + 8, cb_size), f32),
            pltpu.VMEM((HEAD, cb_size), f32),
            pltpu.VMEM((ids2.shape[0] * 128 + 8, 128), f32),
            pltpu.VMEM((T + 8, 128), f32),
            pltpu.VMEM((T, 128), f32),
            pltpu.VMEM((T, 128), f32),
            pltpu.SemaphoreType.DMA((6,)),
            pltpu.SemaphoreType.DMA((4,)),
            pltpu.SemaphoreType.DMA((slots,)),
        ],
        compiler_params=pltpu.CompilerParams(vmem_limit_bytes=28 * MIB),
        name="front",
    )(position, ids2, tokens, gain, weight3, taps, rates, residues, skip)


def expm1(x):
    series = jnp.ones_like(x)
    for k in range(9, 1, -1):
        series = 1.0 + series * x * (1.0 / k)
    return jnp.where(jnp.abs(x) < 0.5, x * series, jnp.exp(x) - 1.0)


def local_kernel(
    poles, first, slot, lane_position, prod_ref, keep_ref, rates_ref, residues_ref, skip_ref, out_ref, _,
    local_out, state_out, pole_out, window_out, sem,
):
    copy = columns(lane_position[0], slot, out_ref, window_out, sem)
    copy.start()
    tiles, T, _ = local_out.shape
    run = T // PARTS
    mine = slice(first * 128, (first + tiles) * 128)
    pole_out[...] = residues_ref[:, mine] * jnp.sqrt(-expm1(-2.0 * rates_ref[:, mine]))

    def tile_body(tile, _):
        lanes = pl.ds(pl.multiple_of((first + tile) * 128, 128), 128)
        d16 = jnp.exp(-rates_ref[:, lanes])
        w16 = pole_out[:, pl.ds(pl.multiple_of(tile * 128, 128), 128)]
        decay = [jnp.broadcast_to(d16[n : n + 1], (8, 128)) for n in range(poles)]
        weight = [jnp.broadcast_to(w16[n : n + 1], (8, 128)) for n in range(poles)]
        skip = skip_ref[0:1, lanes]

        def token(i, states):
            at = pl.ds(i, PARTS, stride=run)
            p, keep = prod_ref[first + tile, at, :], keep_ref[at, :]
            after = [states[n] * decay[n] * keep + p for n in range(poles)]
            local_out[tile, at, :] = tree([skip * p] + [weight[n] * after[n] for n in range(poles)])
            return tuple(after)

        states = lax.fori_loop(0, run, token, tuple(jnp.zeros((8, 128), f32) for _ in range(poles)), unroll=2)
        for n in range(poles):
            state_out[tile, pl.ds(n, PARTS, stride=poles), :] = states[n]
        return 0

    lax.fori_loop(0, tiles, tile_body, 0)
    copy.wait()


def tree(terms):
    while len(terms) > 1:
        terms = [a + b for a, b in zip(terms[0::2], terms[1::2])] + terms[len(terms) // 2 * 2 :]
    return terms[0]


def local_pass(first, tiles, slot, lane_position, product, keep, rates, residues, skip, out_weight, width, after):
    T, poles = product.shape[1], rates.shape[0]
    return pl.pallas_call(
        functools.partial(local_kernel, poles, first, slot),
        out_shape=(
            jax.ShapeDtypeStruct((tiles, T, 128), f32),
            jax.ShapeDtypeStruct((tiles, PARTS * poles, 128), f32),
            jax.ShapeDtypeStruct((poles, tiles * 128), f32),
            jax.ShapeDtypeStruct((out_weight.shape[0], 2 * width), bf16),
        ),
        in_specs=[smem()] + [vmem()] * 5 + [hbm(), pl.BlockSpec(memory_space=pl.ANY)],
        out_specs=[vmem()] * 4,
        scratch_shapes=[pltpu.SemaphoreType.DMA],
        compiler_params=pltpu.CompilerParams(vmem_limit_bytes=8 * MIB),
        cost_estimate=pl.CostEstimate(flops=6 * T * poles * tiles * 128, bytes_accessed=8 * MIB, transcendentals=0),
        name="local_pass",
    )(lane_position, product, keep, rates, residues, skip, out_weight, after)


def first_products(first, last, taps, ids_ref, base):
    s01, s0m1 = same_id(ids_ref, base + 1, base), same_id(ids_ref, base, base - 1)
    s0m2, s1m1 = same_id(ids_ref, base, base - 2), same_id(ids_ref, base + 1, base - 1)

    def shift(i):
        near, far = last[i][1:2], last[i][0:1]
        t1, t2 = taps[1][i : i + 1], taps[2][i : i + 1]
        return s0m1 * (t1 * near) + s0m2 * (t2 * far), s1m1 * (t2 * near)

    def plain(i):
        t0, t1 = taps[0][i : i + 1], taps[1][i : i + 1]
        return t0 * first[i][0:1], t0 * first[i][1:2] + s01 * (t1 * first[i][0:1])

    k, v, dk, dv = plain(1), plain(2), shift(1), shift(2)
    delta = [(k[j] + dk[j]) * (v[j] + dv[j]) - k[j] * v[j] for j in range(2)]
    return shift(0), delta


def unpack(block, poles):
    first = [None, block[poles : poles + 2], block[poles + 2 : poles + 4]]
    last = [block[poles + 4 + 2 * i : poles + 6 + 2 * i] for i in range(3)]
    return block[0:poles], first, last


def joined_state(low_state, low_last, up_state, up_first, taps, rates, ids_ref, base, length):
    _, delta = first_products(up_first, low_last, taps, ids_ref, base)
    grown = low_state + delta[0] * jnp.exp(rates) + delta[1] * jnp.exp(2.0 * rates)
    open_ = same_id(ids_ref, base + length - 1, base - 1)
    return up_state + grown * (jnp.exp(-rates * jnp.float32(length)) * open_)


def join_kernel(T, poles, span, position, ids_ref, mine_ref, other_ref, taps_ref, rates_ref, _, out):
    me = position[0]
    is_upper = (me // span) % 2 == 1
    base = (me // (2 * span)) * (2 * span * T) + span * T
    mine, other = mine_ref[...].astype(f32), other_ref[...].astype(f32)
    lower, upper = jnp.where(is_upper, other, mine), jnp.where(is_upper, mine, other)
    taps = [taps_ref[j] for j in range(3)]
    low_state, _, low_last = unpack(lower, poles)
    up_state, up_first, _ = unpack(upper, poles)
    state = joined_state(low_state, low_last, up_state, up_first, taps, rates_ref[...], ids_ref, base, span * T)
    out[0:poles, :] = state.astype(bf16)
    row = lax.broadcasted_iota(jnp.int32, (HEAD, lower.shape[1]), 0)
    out[poles : poles + HEAD, :] = jnp.where(row < 4, lower[poles:], upper[poles:]).astype(bf16)


def join(span, T, position, ids, mine, other, taps, rates, after):
    poles = rates.shape[0]
    return pl.pallas_call(
        functools.partial(join_kernel, T, poles, span),
        out_shape=jax.ShapeDtypeStruct(mine.shape, bf16),
        in_specs=[smem(), smem()] + [vmem()] * 4 + [pl.BlockSpec(memory_space=pl.ANY)],
        out_specs=vmem(),
        compiler_params=pltpu.CompilerParams(vmem_limit_bytes=4 * MIB),
        name="join",
    )(position, ids, mine, other, taps, rates, after)


def gate_kernel(
    T, poles, spans, cuts, position, lane_position, ids_ref, query_ref, block_ref, visible_ref, taps_ref, rates_ref, skip_ref,
    window_ref, *rest,
):
    arrived, rest = rest[: len(spans)], rest[len(spans) :]
    parts, rest = [rest[3 * c : 3 * c + 3] for c in range(cuts)], rest[3 * cuts :]
    gated_out, send_out, mine_out, carry, full = rest
    run = T // PARTS
    tiles = query_ref.shape[1] // 128
    me = position[0]
    base = me * T
    taps = [taps_ref[j] for j in range(3)]
    rates, skip = rates_ref[...], skip_ref[...]
    weight = jnp.concatenate([pole_ref[...] for _, _, pole_ref in parts], axis=1)
    each = tiles // cuts
    prior = jnp.zeros(block_ref.shape, f32)
    prior_state, prior_first, prior_last = unpack(prior, poles)
    for span, ref in zip(spans, arrived):
        state, first, last = unpack(ref[...].astype(f32), poles)
        upper, held = (me // span) % 2 == 1, me % span
        if span == 1:
            both = state
        else:
            both = joined_state(
                state, last, prior_state, prior_first, taps, rates, ids_ref, (me - held) * T, held * T)
        fresh = upper & (held == 0)
        prior_state = jnp.where(fresh, state, jnp.where(upper, both, prior_state))
        prior_first = [None] + [jnp.where(upper, first[i], prior_first[i]) for i in (1, 2)]
        prior_last = [jnp.where(fresh, last[i], prior_last[i]) for i in range(3)]
    _, first, _ = unpack(block_ref[...].astype(f32), poles)
    q_shift, delta = first_products(first, prior_last, taps, ids_ref, base)
    second = delta[1] * jnp.exp(rates)
    now = prior_state + (delta[0] + second) * jnp.exp(rates)
    fix0 = skip * delta[0] - jnp.sum(weight * second, axis=0, keepdims=True)
    fix1 = skip * delta[1]
    jump = jnp.exp(-rates * float(run))
    for s in range(PARTS):
        part = slice(s * poles, (s + 1) * poles)
        began = weight * now
        for tile in range(tiles):
            carry[tile, part, :] = began[:, tile * 128 : tile * 128 + 128]
        if s < PARTS - 1:
            whole = same_id(ids_ref, base + s * run + run - 1, base + s * run - 1)
            ends = jnp.concatenate([parts[tile // each][1][tile % each, part, :] for tile in range(tiles)], axis=1)
            now = now * (jump * whole) + ends

    def lane_body(cut, inner, _):
        tile = cut * each + inner
        lanes = pl.ds(pl.multiple_of(tile * 128, 128), 128)
        d16 = jnp.exp(-rates_ref[:, lanes])
        decay = [jnp.broadcast_to(d16[n : n + 1], (8, 128)) for n in range(poles)]
        start = tuple(carry[tile, pl.ds(n, PARTS, stride=poles), :] for n in range(poles))

        def token(i, states):
            after = [states[n] * decay[n] for n in range(poles)]
            see = visible_ref[pl.ds(pl.multiple_of(i * 8, 8), 8), :]
            at = pl.ds(i, PARTS, stride=run)
            full[tile, at, :] = parts[cut][0][inner, at, :] + see * tree(list(after))
            return tuple(after)

        lax.fori_loop(0, run, token, start, unroll=4)
        return 0

    for cut in range(cuts):
        lax.fori_loop(0, each, functools.partial(lane_body, cut), 0)
    row = lax.broadcasted_iota(jnp.int32, (16, 128), 0)
    for tile in range(tiles):
        lanes = slice(tile * 128, tile * 128 + 128)
        gated_out[:, lanes] = (query_ref[:, lanes] * full[tile]).astype(bf16)
        top_q, top = query_ref[0:16, lanes], full[tile, 0:16, :]
        top_q = top_q + jnp.where(row == 0, q_shift[0][:, lanes], 0.0) + jnp.where(row == 1, q_shift[1][:, lanes], 0.0)
        top = top + jnp.where(row == 0, fix0[:, lanes], 0.0) + jnp.where(row == 1, fix1[:, lanes], 0.0)
        gated_out[0:16, lanes] = (top_q * top).astype(bf16)
    share(lane_position[0], gated_out, window_ref, send_out, mine_out)


def target(index, slot):
    chip = index // 2
    odd = chip % 2
    if slot == 0:
        return 3 - 3 * odd
    if slot == 1:
        return 1 + odd
    if slot == 2:
        return (chip + 2) % 4
    return chip


def columns(index, slot, out_ref, window, sem):
    both = window.shape[1]
    start = pl.multiple_of(target(index, slot) * both, both)
    return pltpu.make_async_copy(out_ref.at[:, pl.ds(start, both)], window, sem)


def share(index, gated_ref, window, send_out, mine_out):
    width = send_out.shape[1]
    tile = 256
    core = index % 2

    for j in range(width // tile):
        at = slice(j * tile, j * tile + tile)
        for out, half in ((send_out, 1 - core), (mine_out, core)):
            cols = pl.ds(pl.multiple_of(half * width + j * tile, tile), tile)
            out[:, at] = jnp.dot(gated_ref[...], window[:, cols], preferred_element_type=f32).astype(out.dtype)


def share_kernel(count, lane_position, gated_ref, *rest):
    windows, outs = rest[:count], rest[count:]
    for k, window in enumerate(windows):
        share(lane_position[0], gated_ref, window, outs[2 * k], outs[2 * k + 1])


def shares(lane_position, gated, windows, width):
    T, channels = gated.shape
    count = len(windows)
    return pl.pallas_call(
        functools.partial(share_kernel, count),
        out_shape=[jax.ShapeDtypeStruct((T, width), d) for _ in windows for d in (bf16, f32)],
        in_specs=[smem(), vmem()] + [vmem()] * count,
        out_specs=[vmem()] * (2 * count),
        compiler_params=pltpu.CompilerParams(vmem_limit_bytes=4 * MIB),
        cost_estimate=pl.CostEstimate(
            flops=4 * T * channels * width * count, bytes_accessed=4 * channels * width * count, transcendentals=0),
        name="shares",
    )(lane_position, gated, *windows)


def late_share_kernel(slots, lane_position, gated_ref, out_ref, *rest):
    outs, (windows, sem) = rest[:-2], rest[-2:]
    copies = [columns(lane_position[0], slot, out_ref, windows.at[k], sem.at[k]) for k, slot in enumerate(slots)]
    for copy in copies:
        copy.start()
    for k, copy in enumerate(copies):
        copy.wait()
        share(lane_position[0], gated_ref, windows.at[k], outs[2 * k], outs[2 * k + 1])


def late_shares(slots, lane_position, gated, out_weight, width):
    T, channels = gated.shape
    count = len(slots)
    return pl.pallas_call(
        functools.partial(late_share_kernel, slots),
        out_shape=[jax.ShapeDtypeStruct((T, width), d) for _ in slots for d in (bf16, f32)],
        in_specs=[smem(), vmem(), hbm()],
        out_specs=[vmem()] * (2 * count),
        scratch_shapes=[pltpu.VMEM((count, channels, 2 * width), bf16), pltpu.SemaphoreType.DMA((count,))],
        compiler_params=pltpu.CompilerParams(vmem_limit_bytes=10 * MIB),
        cost_estimate=pl.CostEstimate(
            flops=4 * T * channels * width * count, bytes_accessed=4 * channels * width * count, transcendentals=0),
        name="late_shares",
    )(lane_position, gated, out_weight)


def gate(T, spans, arrived, position, lane_position, ids, query, parts, block, visible, taps, rates, skip, window, width):
    poles, channels = rates.shape
    return pl.pallas_call(
        functools.partial(gate_kernel, T, poles, tuple(spans), len(parts)),
        out_shape=[
            jax.ShapeDtypeStruct(query.shape, bf16),
            jax.ShapeDtypeStruct((T, width), bf16),
            jax.ShapeDtypeStruct((T, width), f32),
        ],
        in_specs=[smem()] * 3 + [vmem()] * (7 + len(spans) + 3 * len(parts)),
        out_specs=[vmem()] * 3,
        scratch_shapes=[
            pltpu.VMEM((channels // 128, PARTS * poles, 128), f32),
            pltpu.VMEM((channels // 128, T, 128), f32),
        ],
        compiler_params=pltpu.CompilerParams(vmem_limit_bytes=6 * MIB),
        name="gate",
    )(position, lane_position, ids, query, block, visible, taps, rates, skip, window, *arrived,
      *[a for part in parts for a in part])


def total(*terms):
    return functools.reduce(lambda a, b: a + b, [t.astype(f32) for t in terms]).astype(bf16)


def merge_kernel(count, has_inner, lane_position, *rest):
    terms, picks, out = rest[:count], rest[count:-1], rest[-1]
    value = terms[0][...].astype(f32)
    for term in terms[1:]:
        value = value + term[...].astype(f32)
    chip = lane_position[0] // 2
    inner = (chip == 1) | (chip == 2)
    for pick, wanted in zip(picks, (inner, jnp.logical_not(inner)) if has_inner else (jnp.logical_not(inner),)):
        value = value + jnp.where(wanted, pick[...].astype(f32), 0.0)
    out[...] = value.astype(out.dtype)


def merge(lane_position, dtype, terms, inner=None, outer=None):
    picks = [a for a in (inner, outer) if a is not None]
    terms = [pltpu.with_memory_space_constraint(a, pltpu.VMEM) for a in (*terms, *picks)]
    return pl.pallas_call(
        functools.partial(merge_kernel, len(terms) - len(picks), inner is not None),
        out_shape=jax.ShapeDtypeStruct(terms[0].shape, dtype),
        in_specs=[smem()] + [vmem()] * len(terms),
        out_specs=vmem(),
        compiler_params=pltpu.CompilerParams(vmem_limit_bytes=3 * MIB),
        name="merge",
    )(lane_position, *terms)


def scatter_line(lane_position, gated, send, mine, window, out_weight, width):
    pair = [(m, m ^ 1) for m in range(8)]

    def along(hops):
        return [(a * 2 + c, b * 2 + c) for a, b in hops for c in range(2)]

    near = along([(0, 1), (1, 0), (2, 3), (3, 2)])
    traded = lax.ppermute(send, "mp", pair)
    far = merge(lane_position, bf16, (mine, traded))
    from_near = lax.ppermute(far, "mp", near)
    send, mine = shares(lane_position, gated, [window], width)
    second = merge(lane_position, bf16, (mine, lax.ppermute(send, "mp", pair)))
    from_middle = lax.ppermute(second, "mp", along([(1, 2), (2, 1)]))
    from_end = lax.ppermute(second, "mp", near)
    send2, mine2, send3, mine3 = late_shares((2, 3), lane_position, gated, out_weight, width)
    mine2 = merge(lane_position, f32, (mine2, lax.ppermute(send2, "mp", pair)))
    across = merge(lane_position, bf16, (mine2,), inner=from_near)
    from_across = lax.ppermute(across, "mp", along([(0, 2), (1, 3), (2, 0), (3, 1)]))
    own = merge(lane_position, f32, (mine3, lax.ppermute(send3, "mp", pair), from_middle), inner=from_end, outer=from_near)
    return total(own, from_across)


def shifted(value, axis, steps):
    count = lax.axis_size(axis)
    leading, last = (max(0, -steps), min(count, count - steps))
    return lax.ppermute(value, axis, [(source, source + steps) for source in range(leading, last)])


def project(block, norm_gain, weights):
    floats = block.astype(jnp.float32)
    mean_square = jnp.mean(floats * floats, axis=-1, keepdims=True)
    normed = (floats * lax.rsqrt(mean_square + epsilon) * norm_gain[None, :]).astype(jnp.bfloat16)
    return jnp.dot(normed, weights, preferred_element_type=jnp.float32).astype(jnp.bfloat16)


def general(
    tokens, norm_gain, in_weight, short_filter, rates, residues, skip, out_weight, segment_ids
):
    tok_rows = tokens.shape[0]
    model_width = tokens.shape[1]
    channels = in_weight.shape[2]
    filter_taps = short_filter.shape[0]
    pole_count = rates.shape[0]
    device_index = lax.axis_index("ctx")
    row_offset = device_index * tok_rows
    weights = in_weight.reshape(model_width, 3 * channels)
    projected = project(tokens, norm_gain, weights)
    previous = shifted(projected[tok_rows - (filter_taps - 1) :], "ctx", 1)
    extended = jnp.concatenate([previous, projected], axis=0)
    padded_ids = jnp.concatenate([jnp.full((filter_taps,), -1, jnp.int32), segment_ids], axis=0)
    window = lax.dynamic_slice_in_dim(padded_ids, row_offset, tok_rows + filter_taps, 0)
    local_ids = window[filter_taps:]
    taps_table = short_filter.reshape(filter_taps, 3 * channels)
    featured = jnp.zeros((tok_rows, 3 * channels), jnp.float32)
    for lag_index in range(filter_taps):
        begin = filter_taps - 1 - lag_index
        lagged = extended[begin : begin + tok_rows].astype(jnp.float32)
        matches = window[filter_taps - lag_index : filter_taps - lag_index + tok_rows] == local_ids
        term = taps_table[lag_index][None, :] * lagged
        featured = featured + jnp.where(matches[:, None], term, jnp.zeros_like(term))
    query_part = featured[:, :channels]
    key_part = featured[:, channels : 2 * channels]
    value_part = featured[:, 2 * channels :]
    product = key_part * value_part
    offsets = jnp.arange(tok_rows, dtype=jnp.float32)
    center = float(tok_rows // 2)
    growth = jnp.exp(-(offsets - center)[:, None, None] * rates[None])
    shrinkage = jnp.exp((offsets - center)[:, None, None] * rates[None])
    weighted = (shrinkage * product[:, None, :]).reshape(tok_rows, pole_count * channels)
    visible = (offsets[:, None] >= offsets[None, :]) & (local_ids[:, None] == local_ids[None, :])
    in_block = jnp.dot(visible.astype(jnp.float32), weighted, precision=lax.Precision.HIGHEST)
    in_block = in_block.reshape(tok_rows, pole_count, channels) * growth
    survives = local_ids == window[filter_taps - 1]
    block_factor = jnp.exp(-rates * tok_rows)
    block_end = in_block[tok_rows - 1]
    block_ends = lax.all_gather(block_end[None], "ctx", axis=0, tiled=True)
    shard_count = segment_ids.shape[0] // tok_rows
    last_ids = segment_ids.reshape(shard_count, tok_rows)[:, tok_rows - 1]
    prior_ids = jnp.concatenate([jnp.full((1,), -1, jnp.int32), last_ids[:-1]], axis=0)
    shard_decays = block_factor[None] * (last_ids == prior_ids).astype(jnp.float32)[:, None, None]

    def absorb(running, inputs):
        shard, factor, shard_end = inputs
        advanced = running * factor + shard_end
        return (jnp.where(shard < device_index, advanced, running), None)

    incoming, _ = lax.scan(
        absorb,
        jnp.zeros_like(block_end),
        (jnp.arange(shard_count, dtype=jnp.int32), shard_decays, block_ends),
    )
    carried = incoming[None] * jnp.exp(-(offsets + 1.0)[:, None, None] * rates[None])
    carried = carried * survives.astype(jnp.float32)[:, None, None]
    states = in_block + carried
    pole_weight = residues * jnp.sqrt(-jnp.expm1(-2.0 * rates))
    longconv = jnp.sum(pole_weight[None] * states, axis=1)
    gated = (query_part * (longconv + skip[None, :] * product)).astype(jnp.bfloat16)
    partial_terms = jnp.dot(gated, out_weight, preferred_element_type=jnp.float32)
    return lax.psum_scatter(partial_terms, "mp", scatter_dimension=1, tiled=True).astype(
        jnp.bfloat16
    )


def local(tokens, norm_gain, in_weight, short_filter, rates, residues, skip, out_weight, segment_ids):
    T = tokens.shape[0]
    shards = lax.axis_size("ctx")
    me = lax.axis_index("ctx")
    position = me.astype(jnp.int32)[None]
    lane_position = lax.axis_index("mp").astype(jnp.int32)[None]
    width = out_weight.shape[1] // lax.axis_size("mp")
    weight3 = jnp.transpose(in_weight, (1, 0, 2))
    out_weight = pltpu.with_memory_space_constraint(out_weight, pltpu.HBM)
    query, product, block, keep, visible, taps, rates, residues, skip = front(
        position, segment_ids.reshape(-1, 128), tokens, norm_gain[None], weight3, short_filter, rates, residues, skip[None])
    cuts = shards.bit_length() - 1
    each = product.shape[0] // cuts
    group, spans, arrived, parts, windows = block, [], [], [], []
    for k in range(cuts):
        span = 1 << k
        other = lax.ppermute(group, "ctx", [(a, a ^ span) for a in range(shards)])
        spans.append(span)
        arrived.append(other)
        *part, window = local_pass(
            k * each, each, min(k, 1), lane_position, product, keep, rates, residues, skip, out_weight, width, group)
        parts.append(part)
        windows.append(window)
        if k < cuts - 1:
            group = join(span, T, position, segment_ids, group, other, taps, rates, part[0])
    gated, send, mine = gate(T, spans, arrived, position, lane_position, segment_ids, query, parts, block, visible, taps, rates,
                             skip, windows[0], width)
    return scatter_line(lane_position, gated, send, mine, windows[1], out_weight, width)


def solution(mesh):
    placed = (
        P("ctx", None),
        P(),
        P(None, None, "mp"),
        P(None, None, "mp"),
        P(None, "mp"),
        P(None, "mp"),
        P("mp"),
        P("mp", None),
        P(),
    )
    shards, groups = mesh.shape["ctx"], mesh.shape["mp"]

    def body(tokens, norm_gain, in_weight, *rest):
        suits = groups == 8 and shards & (shards - 1) == 0 and shards > 2
        suits = suits and in_weight.shape[2] % 512 == 0 and in_weight.shape[0] % 2048 == 0
        suits = suits and tokens.shape[0] % 64 == 0 and rest[-1].shape[0] % 128 == 0 and rest[1].shape[0] % 8 == 0
        return (local if suits else general)(tokens, norm_gain, in_weight, *rest)

    return jax.shard_map(
        body, mesh=mesh, in_specs=placed, out_specs=P("ctx", "mp"), check_vma=False
    )
```

```python
import functools
import jax
import jax.numpy as jnp
from jax import lax
from jax.experimental import pallas as pl
from jax.experimental.pallas import tpu as pltpu
from jax.sharding import PartitionSpec as P

epsilon = 1e-06
f32 = jnp.float32
bf16 = jnp.bfloat16

PARTS = 8
HEAD = 16
MIB = 1 << 20


def vmem():
    return pl.BlockSpec(memory_space=pltpu.VMEM)


def smem():
    return pl.BlockSpec(memory_space=pltpu.SMEM)


def same_id(ids_ref, a, b):
    def get(t):
        return jnp.where(t < 0, -1, ids_ref[jnp.maximum(t, 0)])

    return (get(a) == get(b)).astype(f32)


def hbm():
    return pl.BlockSpec(memory_space=pltpu.HBM)


def front_kernel(
    geometry, position, ids_ref, tokens_ref, gain_ref, weight_ref, taps_ref, rates_ref, residues_ref, skip_ref,
    query_out, prod_out, block_out, keep_out, visible_out, taps, rates, residues, skip,
    ids, gain, tok, normed, ring, total, proj, head, idcol, near, twice, ending, sem, tok_sem, ring_sem,
):
    T, depth, channels, cb_size, kc_size, slots, poles = geometry
    run = T // PARTS
    kcs, cbs = depth // kc_size, channels // cb_size
    steps = kcs * cbs
    base = pl.multiple_of(position[0] * T, 8)

    def fetch(step):
        cb, kc, slot = step // kcs, step % kcs, step % slots
        return pltpu.make_async_copy(
            weight_ref.at[:, pl.ds(pl.multiple_of(kc * kc_size, kc_size), kc_size),
                          pl.ds(pl.multiple_of(cb * cb_size, cb_size), cb_size)],
            ring.at[slot], ring_sem.at[slot])

    small = [
        pltpu.make_async_copy(a, b, sem.at[i])
        for i, (a, b) in enumerate(
            ((ids_ref, ids), (gain_ref, gain), (taps_ref, taps), (rates_ref, rates), (residues_ref, residues),
             (skip_ref, skip)))
    ]
    small[0].start()
    small[1].start()
    chunk = T // 4
    tok_copies = [
        pltpu.make_async_copy(tokens_ref.at[pl.ds(c * chunk, chunk)], tok.at[pl.ds(c * chunk, chunk)], tok_sem.at[c])
        for c in range(4)
    ]
    for copy in tok_copies:
        copy.start()
    for copy in small[2:]:
        copy.start()
    for s in range(min(slots, steps)):
        fetch(s).start()

    small[0].wait()
    idcol[0:8, :] = jnp.full((8, 128), -1.0, f32)
    for b in range(ids.shape[0]):
        row = ids[b : b + 1, :].astype(f32)
        idcol[8 + b * 128 : 8 + (b + 1) * 128, :] = jnp.broadcast_to(row, (128, 128)).T
    near[...] = idcol[pl.ds(base, T + 8), :]
    here = near[8 : 8 + T, :]
    keep_out[...] = (here == near[7 : 7 + T, :]).astype(f32)
    twice[...] = (here == near[6 : 6 + T, :]).astype(f32)
    ending[...] = (here == near[7 + T : 8 + T, :]).astype(f32)
    before = near[pl.ds(7, PARTS, stride=run), :]
    for i in range(run):
        visible_out[i * 8 : (i + 1) * 8, :] = (near[pl.ds(8 + i, PARTS, stride=run), :] == before).astype(f32)
    for i in range(3):
        proj[i, 0:8, :] = jnp.zeros((8, cb_size), f32)
    head[...] = jnp.zeros(head.shape, f32)
    small[1].wait()

    def norm_rows(g, _):
        part = pl.ds(pl.multiple_of(g * 16, 16), 16)
        x = tok[part, :].astype(f32)
        scale = lax.rsqrt(jnp.sum(x * x, axis=-1, keepdims=True) * (1.0 / depth) + epsilon)
        normed[part, :] = (x * scale * gain[...]).astype(bf16)
        return 0

    for c, copy in enumerate(tok_copies):
        copy.wait()
        lax.fori_loop(c * chunk // 16, (c + 1) * chunk // 16, norm_rows, 0)
    for copy in small[2:]:
        copy.wait()

    def epilogue(cb):
        cols = pl.ds(pl.multiple_of(cb * cb_size, cb_size), cb_size)
        feats = []
        m1 = jnp.concatenate([keep_out[...]] * (cb_size // 128), axis=1)
        m2 = jnp.concatenate([twice[...]] * (cb_size // 128), axis=1)
        for i in range(3):
            p = total[i].astype(bf16).astype(f32)
            proj[i, 8 : 8 + T, :] = p
            tap = [taps[j, i : i + 1, cols] for j in range(3)]
            feats.append(
                tap[0] * p + m1 * (tap[1] * proj[i, 7 : 7 + T, :]) + m2 * (tap[2] * proj[i, 6 : 6 + T, :]))
        query_out[:, cols] = feats[0]
        for i in range(1, 3):
            head[2 * (i - 1) : 2 * i, :] = proj[i, 8:10, :]
        for i in range(3):
            head[4 + 2 * i : 6 + 2 * i, :] = proj[i, 6 + T : 8 + T, :]
        block_out[poles : poles + HEAD, cols] = head[...].astype(bf16)
        product = feats[1] * feats[2]
        back = 7.0 - lax.broadcasted_iota(jnp.int32, (8, 128), 0).astype(f32)
        for lane in range(cb_size // 128):
            tile = cb * (cb_size // 128) + lane
            lanes = pl.ds(pl.multiple_of(tile * 128, 128), 128)
            prod_out[tile] = product[:, lane * 128 : lane * 128 + 128]
            r16 = rates[:, lanes]
            jump = jnp.exp(-8.0 * r16)
            leap = [jnp.broadcast_to(jump[n : n + 1], (8, 128)) for n in range(poles)]

            def eight(g, sums):
                part = pl.ds(pl.multiple_of(g * 8, 8), 8)
                p = prod_out[tile, part, :] * ending[part, :]
                return tuple(sums[n] * leap[n] + p for n in range(poles))

            sums = lax.fori_loop(
                0, T // 8, eight, tuple(jnp.zeros((8, 128), f32) for _ in range(poles)), unroll=4)
            ends = [
                jnp.sum(sums[n] * jnp.exp(-back * r16[n : n + 1]), axis=0, keepdims=True) for n in range(poles)
            ]
            block_out[0:poles, lanes] = jnp.concatenate(ends, axis=0).astype(bf16)

    def step_body(step, _):
        cb, kc, slot = step // kcs, step % kcs, step % slots
        fetch(step).wait()
        lhs = normed[:, pl.ds(pl.multiple_of(kc * kc_size, kc_size), kc_size)]
        for i in range(3):
            part = jnp.dot(lhs, ring[slot, i], preferred_element_type=f32)
            total[i] = jnp.where(kc == 0, part, total[i] + part)

        @pl.when(step + slots < steps)
        def _():
            fetch(step + slots).start()

        @pl.when(kc == kcs - 1)
        def _():
            epilogue(cb)

        return 0

    total[...] = jnp.zeros(total.shape, f32)
    lax.fori_loop(0, steps, step_body, 0)


def front(position, ids2, tokens, gain, weight3, taps, rates, residues, skip):
    T, depth = tokens.shape
    channels, poles = weight3.shape[2], rates.shape[0]
    cb_size, kc_size, slots = 256, 2048, 5
    geometry = (T, depth, channels, cb_size, kc_size, slots, poles)
    kept = [pltpu.VMEM(a.shape, a.dtype) for a in (taps, rates, residues, skip)]
    ids2, tokens, gain, weight3, taps, rates, residues, skip = [
        pltpu.with_memory_space_constraint(a, pltpu.HBM)
        for a in (ids2, tokens, gain, weight3, taps, rates, residues, skip)
    ]
    return pl.pallas_call(
        functools.partial(front_kernel, geometry),
        out_shape=[
            jax.ShapeDtypeStruct((T, channels), f32),
            jax.ShapeDtypeStruct((channels // 128, T, 128), f32),
            jax.ShapeDtypeStruct((poles + HEAD, channels), bf16),
            jax.ShapeDtypeStruct((T, 128), f32),
            jax.ShapeDtypeStruct((T, 128), f32),
        ] + kept,
        in_specs=[smem()] + [hbm()] * 8,
        out_specs=[vmem()] * 9,
        scratch_shapes=[
            pltpu.VMEM(ids2.shape, ids2.dtype),
            pltpu.VMEM(gain.shape, f32),
            pltpu.VMEM((T, depth), bf16),
            pltpu.VMEM((T, depth), bf16),
            pltpu.VMEM((slots, 3, kc_size, cb_size), bf16),
            pltpu.VMEM((3, T, cb_size), f32),
            pltpu.VMEM((3, T + 8, cb_size), f32),
            pltpu.VMEM((HEAD, cb_size), f32),
            pltpu.VMEM((ids2.shape[0] * 128 + 8, 128), f32),
            pltpu.VMEM((T + 8, 128), f32),
            pltpu.VMEM((T, 128), f32),
            pltpu.VMEM((T, 128), f32),
            pltpu.SemaphoreType.DMA((6,)),
            pltpu.SemaphoreType.DMA((4,)),
            pltpu.SemaphoreType.DMA((slots,)),
        ],
        compiler_params=pltpu.CompilerParams(vmem_limit_bytes=28 * MIB),
        name="front",
    )(position, ids2, tokens, gain, weight3, taps, rates, residues, skip)


def expm1(x):
    series = jnp.ones_like(x)
    for k in range(9, 1, -1):
        series = 1.0 + series * x * (1.0 / k)
    return jnp.where(jnp.abs(x) < 0.5, x * series, jnp.exp(x) - 1.0)


def local_kernel(
    poles, first, slot, lane_position, prod_ref, keep_ref, rates_ref, residues_ref, skip_ref, out_ref, _,
    local_out, state_out, pole_out, window_out, sem,
):
    copy = columns(lane_position[0], slot, out_ref, window_out, sem)
    copy.start()
    tiles, T, _ = local_out.shape
    run = T // PARTS
    mine = slice(first * 128, (first + tiles) * 128)
    pole_out[...] = residues_ref[:, mine] * jnp.sqrt(-expm1(-2.0 * rates_ref[:, mine]))

    def tile_body(tile, _):
        lanes = pl.ds(pl.multiple_of((first + tile) * 128, 128), 128)
        d16 = jnp.exp(-rates_ref[:, lanes])
        w16 = pole_out[:, pl.ds(pl.multiple_of(tile * 128, 128), 128)]
        decay = [jnp.broadcast_to(d16[n : n + 1], (8, 128)) for n in range(poles)]
        weight = [jnp.broadcast_to(w16[n : n + 1], (8, 128)) for n in range(poles)]
        skip = skip_ref[0:1, lanes]

        def token(i, states):
            at = pl.ds(i, PARTS, stride=run)
            p, keep = prod_ref[first + tile, at, :], keep_ref[at, :]
            after = [states[n] * decay[n] * keep + p for n in range(poles)]
            local_out[tile, at, :] = tree([skip * p] + [weight[n] * after[n] for n in range(poles)])
            return tuple(after)

        states = lax.fori_loop(0, run, token, tuple(jnp.zeros((8, 128), f32) for _ in range(poles)), unroll=2)
        for n in range(poles):
            state_out[tile, pl.ds(n, PARTS, stride=poles), :] = states[n]
        return 0

    lax.fori_loop(0, tiles, tile_body, 0)
    copy.wait()


def tree(terms):
    while len(terms) > 1:
        terms = [a + b for a, b in zip(terms[0::2], terms[1::2])] + terms[len(terms) // 2 * 2 :]
    return terms[0]


def local_pass(first, tiles, slot, lane_position, product, keep, rates, residues, skip, out_weight, width, after):
    T, poles = product.shape[1], rates.shape[0]
    return pl.pallas_call(
        functools.partial(local_kernel, poles, first, slot),
        out_shape=(
            jax.ShapeDtypeStruct((tiles, T, 128), f32),
            jax.ShapeDtypeStruct((tiles, PARTS * poles, 128), f32),
            jax.ShapeDtypeStruct((poles, tiles * 128), f32),
            jax.ShapeDtypeStruct((out_weight.shape[0], 2 * width), bf16),
        ),
        in_specs=[smem()] + [vmem()] * 5 + [hbm(), pl.BlockSpec(memory_space=pl.ANY)],
        out_specs=[vmem()] * 4,
        scratch_shapes=[pltpu.SemaphoreType.DMA],
        compiler_params=pltpu.CompilerParams(vmem_limit_bytes=8 * MIB),
        cost_estimate=pl.CostEstimate(flops=6 * T * poles * tiles * 128, bytes_accessed=8 * MIB, transcendentals=0),
        name="local_pass",
    )(lane_position, product, keep, rates, residues, skip, out_weight, after)


def first_products(first, last, taps, ids_ref, base):
    s01, s0m1 = same_id(ids_ref, base + 1, base), same_id(ids_ref, base, base - 1)
    s0m2, s1m1 = same_id(ids_ref, base, base - 2), same_id(ids_ref, base + 1, base - 1)

    def shift(i):
        near, far = last[i][1:2], last[i][0:1]
        t1, t2 = taps[1][i : i + 1], taps[2][i : i + 1]
        return s0m1 * (t1 * near) + s0m2 * (t2 * far), s1m1 * (t2 * near)

    def plain(i):
        t0, t1 = taps[0][i : i + 1], taps[1][i : i + 1]
        return t0 * first[i][0:1], t0 * first[i][1:2] + s01 * (t1 * first[i][0:1])

    k, v, dk, dv = plain(1), plain(2), shift(1), shift(2)
    delta = [(k[j] + dk[j]) * (v[j] + dv[j]) - k[j] * v[j] for j in range(2)]
    return shift(0), delta


def unpack(block, poles):
    first = [None, block[poles : poles + 2], block[poles + 2 : poles + 4]]
    last = [block[poles + 4 + 2 * i : poles + 6 + 2 * i] for i in range(3)]
    return block[0:poles], first, last


def joined_state(low_state, low_last, up_state, up_first, taps, rates, ids_ref, base, length):
    _, delta = first_products(up_first, low_last, taps, ids_ref, base)
    grown = low_state + delta[0] * jnp.exp(rates) + delta[1] * jnp.exp(2.0 * rates)
    open_ = same_id(ids_ref, base + length - 1, base - 1)
    return up_state + grown * (jnp.exp(-rates * jnp.float32(length)) * open_)


def join_kernel(T, poles, span, position, ids_ref, mine_ref, other_ref, taps_ref, rates_ref, _, out):
    me = position[0]
    is_upper = (me // span) % 2 == 1
    base = (me // (2 * span)) * (2 * span * T) + span * T
    mine, other = mine_ref[...].astype(f32), other_ref[...].astype(f32)
    lower, upper = jnp.where(is_upper, other, mine), jnp.where(is_upper, mine, other)
    taps = [taps_ref[j] for j in range(3)]
    low_state, _, low_last = unpack(lower, poles)
    up_state, up_first, _ = unpack(upper, poles)
    state = joined_state(low_state, low_last, up_state, up_first, taps, rates_ref[...], ids_ref, base, span * T)
    out[0:poles, :] = state.astype(bf16)
    row = lax.broadcasted_iota(jnp.int32, (HEAD, lower.shape[1]), 0)
    out[poles : poles + HEAD, :] = jnp.where(row < 4, lower[poles:], upper[poles:]).astype(bf16)


def join(span, T, position, ids, mine, other, taps, rates, after):
    poles = rates.shape[0]
    return pl.pallas_call(
        functools.partial(join_kernel, T, poles, span),
        out_shape=jax.ShapeDtypeStruct(mine.shape, bf16),
        in_specs=[smem(), smem()] + [vmem()] * 4 + [pl.BlockSpec(memory_space=pl.ANY)],
        out_specs=vmem(),
        compiler_params=pltpu.CompilerParams(vmem_limit_bytes=4 * MIB),
        name="join",
    )(position, ids, mine, other, taps, rates, after)


def gate_kernel(
    T, poles, spans, cuts, position, lane_position, ids_ref, query_ref, block_ref, visible_ref, taps_ref, rates_ref, skip_ref,
    window_ref, out_ref, *rest,
):
    arrived, rest = rest[: len(spans)], rest[len(spans) :]
    parts, rest = [rest[3 * c : 3 * c + 3] for c in range(cuts)], rest[3 * cuts :]
    gated_out, send_out, mine_out, third_out, carry, full, sem = rest
    run = T // PARTS
    tiles = query_ref.shape[1] // 128
    copy = columns(lane_position[0], 2, out_ref, third_out, sem)
    copy.start()
    me = position[0]
    base = me * T
    taps = [taps_ref[j] for j in range(3)]
    rates, skip = rates_ref[...], skip_ref[...]
    weight = jnp.concatenate([pole_ref[...] for _, _, pole_ref in parts], axis=1)
    each = tiles // cuts
    prior = jnp.zeros(block_ref.shape, f32)
    prior_state, prior_first, prior_last = unpack(prior, poles)
    for span, ref in zip(spans, arrived):
        state, first, last = unpack(ref[...].astype(f32), poles)
        upper, held = (me // span) % 2 == 1, me % span
        if span == 1:
            both = state
        else:
            both = joined_state(
                state, last, prior_state, prior_first, taps, rates, ids_ref, (me - held) * T, held * T)
        fresh = upper & (held == 0)
        prior_state = jnp.where(fresh, state, jnp.where(upper, both, prior_state))
        prior_first = [None] + [jnp.where(upper, first[i], prior_first[i]) for i in (1, 2)]
        prior_last = [jnp.where(fresh, last[i], prior_last[i]) for i in range(3)]
    _, first, _ = unpack(block_ref[...].astype(f32), poles)
    q_shift, delta = first_products(first, prior_last, taps, ids_ref, base)
    second = delta[1] * jnp.exp(rates)
    now = prior_state + (delta[0] + second) * jnp.exp(rates)
    fix0 = skip * delta[0] - jnp.sum(weight * second, axis=0, keepdims=True)
    fix1 = skip * delta[1]
    jump = jnp.exp(-rates * float(run))
    for s in range(PARTS):
        part = slice(s * poles, (s + 1) * poles)
        began = weight * now
        for tile in range(tiles):
            carry[tile, part, :] = began[:, tile * 128 : tile * 128 + 128]
        if s < PARTS - 1:
            whole = same_id(ids_ref, base + s * run + run - 1, base + s * run - 1)
            ends = jnp.concatenate([parts[tile // each][1][tile % each, part, :] for tile in range(tiles)], axis=1)
            now = now * (jump * whole) + ends

    def lane_body(cut, inner, _):
        tile = cut * each + inner
        lanes = pl.ds(pl.multiple_of(tile * 128, 128), 128)
        d16 = jnp.exp(-rates_ref[:, lanes])
        decay = [jnp.broadcast_to(d16[n : n + 1], (8, 128)) for n in range(poles)]
        start = tuple(carry[tile, pl.ds(n, PARTS, stride=poles), :] for n in range(poles))

        def token(i, states):
            after = [states[n] * decay[n] for n in range(poles)]
            see = visible_ref[pl.ds(pl.multiple_of(i * 8, 8), 8), :]
            at = pl.ds(i, PARTS, stride=run)
            full[tile, at, :] = parts[cut][0][inner, at, :] + see * tree(list(after))
            return tuple(after)

        lax.fori_loop(0, run, token, start, unroll=4)
        return 0

    for cut in range(cuts):
        lax.fori_loop(0, each, functools.partial(lane_body, cut), 0)
    row = lax.broadcasted_iota(jnp.int32, (16, 128), 0)
    for tile in range(tiles):
        lanes = slice(tile * 128, tile * 128 + 128)
        gated_out[:, lanes] = (query_ref[:, lanes] * full[tile]).astype(bf16)
        top_q, top = query_ref[0:16, lanes], full[tile, 0:16, :]
        top_q = top_q + jnp.where(row == 0, q_shift[0][:, lanes], 0.0) + jnp.where(row == 1, q_shift[1][:, lanes], 0.0)
        top = top + jnp.where(row == 0, fix0[:, lanes], 0.0) + jnp.where(row == 1, fix1[:, lanes], 0.0)
        gated_out[0:16, lanes] = (top_q * top).astype(bf16)
    share(lane_position[0], gated_out, window_ref, send_out, mine_out)
    copy.wait()


def target(index, slot):
    chip = index // 2
    odd = chip % 2
    if slot == 0:
        return 3 - 3 * odd
    if slot == 1:
        return 1 + odd
    if slot == 2:
        return (chip + 2) % 4
    return chip


def columns(index, slot, out_ref, window, sem):
    both = window.shape[1]
    start = pl.multiple_of(target(index, slot) * both, both)
    return pltpu.make_async_copy(out_ref.at[:, pl.ds(start, both)], window, sem)


def share(index, gated_ref, window, send_out, mine_out):
    width = send_out.shape[1]
    tile = 256
    core = index % 2

    for j in range(width // tile):
        at = slice(j * tile, j * tile + tile)
        for out, half in ((send_out, 1 - core), (mine_out, core)):
            cols = pl.ds(pl.multiple_of(half * width + j * tile, tile), tile)
            out[:, at] = jnp.dot(gated_ref[...], window[:, cols], preferred_element_type=f32).astype(out.dtype)


def share_kernel(count, lane_position, gated_ref, *rest):
    windows, outs = rest[:count], rest[count:]
    for k, window in enumerate(windows):
        share(lane_position[0], gated_ref, window, outs[2 * k], outs[2 * k + 1])


def shares(lane_position, gated, windows, width):
    T, channels = gated.shape
    count = len(windows)
    return pl.pallas_call(
        functools.partial(share_kernel, count),
        out_shape=[jax.ShapeDtypeStruct((T, width), d) for _ in windows for d in (bf16, f32)],
        in_specs=[smem(), vmem()] + [vmem()] * count,
        out_specs=[vmem()] * (2 * count),
        compiler_params=pltpu.CompilerParams(vmem_limit_bytes=4 * MIB),
        cost_estimate=pl.CostEstimate(
            flops=4 * T * channels * width * count, bytes_accessed=4 * channels * width * count, transcendentals=0),
        name="shares",
    )(lane_position, gated, *windows)


def late_share_kernel(slot, lane_position, gated_ref, window_ref, out_ref, *rest):
    outs, (window, sem) = rest[:-2], rest[-2:]
    copy = columns(lane_position[0], slot, out_ref, window, sem)
    copy.start()
    share(lane_position[0], gated_ref, window_ref, outs[0], outs[1])
    copy.wait()
    share(lane_position[0], gated_ref, window, outs[2], outs[3])


def late_shares(slot, lane_position, gated, window, out_weight, width):
    T, channels = gated.shape
    return pl.pallas_call(
        functools.partial(late_share_kernel, slot),
        out_shape=[jax.ShapeDtypeStruct((T, width), d) for d in (bf16, f32, bf16, f32)],
        in_specs=[smem(), vmem(), vmem(), hbm()],
        out_specs=[vmem()] * 4,
        scratch_shapes=[pltpu.VMEM((channels, 2 * width), bf16), pltpu.SemaphoreType.DMA],
        compiler_params=pltpu.CompilerParams(vmem_limit_bytes=6 * MIB),
        cost_estimate=pl.CostEstimate(
            flops=8 * T * channels * width, bytes_accessed=8 * channels * width, transcendentals=0),
        name="late_shares",
    )(lane_position, gated, window, out_weight)


def gate(T, spans, arrived, position, lane_position, ids, query, parts, block, visible, taps, rates, skip, window, out_weight, width):
    poles, channels = rates.shape
    return pl.pallas_call(
        functools.partial(gate_kernel, T, poles, tuple(spans), len(parts)),
        out_shape=[
            jax.ShapeDtypeStruct(query.shape, bf16),
            jax.ShapeDtypeStruct((T, width), bf16),
            jax.ShapeDtypeStruct((T, width), f32),
            pltpu.VMEM(window.shape, bf16),
        ],
        in_specs=[smem()] * 3 + [vmem()] * 7 + [hbm()] + [vmem()] * (len(spans) + 3 * len(parts)),
        out_specs=[vmem()] * 4,
        scratch_shapes=[
            pltpu.VMEM((channels // 128, PARTS * poles, 128), f32),
            pltpu.VMEM((channels // 128, T, 128), f32),
            pltpu.SemaphoreType.DMA,
        ],
        compiler_params=pltpu.CompilerParams(vmem_limit_bytes=8 * MIB),
        name="gate",
    )(position, lane_position, ids, query, block, visible, taps, rates, skip, window, out_weight, *arrived,
      *[a for part in parts for a in part])


def total(*terms):
    return functools.reduce(lambda a, b: a + b, [t.astype(f32) for t in terms]).astype(bf16)


def merge_kernel(count, has_inner, lane_position, *rest):
    terms, picks, out = rest[:count], rest[count:-1], rest[-1]
    value = terms[0][...].astype(f32)
    for term in terms[1:]:
        value = value + term[...].astype(f32)
    chip = lane_position[0] // 2
    inner = (chip == 1) | (chip == 2)
    for pick, wanted in zip(picks, (inner, jnp.logical_not(inner)) if has_inner else (jnp.logical_not(inner),)):
        value = value + jnp.where(wanted, pick[...].astype(f32), 0.0)
    out[...] = value.astype(out.dtype)


def merge(lane_position, dtype, terms, inner=None, outer=None):
    picks = [a for a in (inner, outer) if a is not None]
    terms = [pltpu.with_memory_space_constraint(a, pltpu.VMEM) for a in (*terms, *picks)]
    return pl.pallas_call(
        functools.partial(merge_kernel, len(terms) - len(picks), inner is not None),
        out_shape=jax.ShapeDtypeStruct(terms[0].shape, dtype),
        in_specs=[smem()] + [vmem()] * len(terms),
        out_specs=vmem(),
        compiler_params=pltpu.CompilerParams(vmem_limit_bytes=3 * MIB),
        name="merge",
    )(lane_position, *terms)


def scatter_line(lane_position, gated, send, mine, window, third, out_weight, width):
    pair = [(m, m ^ 1) for m in range(8)]

    def along(hops):
        return [(a * 2 + c, b * 2 + c) for a, b in hops for c in range(2)]

    near = along([(0, 1), (1, 0), (2, 3), (3, 2)])
    traded = lax.ppermute(send, "mp", pair)
    far = merge(lane_position, bf16, (mine, traded))
    from_near = lax.ppermute(far, "mp", near)
    send, mine = shares(lane_position, gated, [window], width)
    second = merge(lane_position, bf16, (mine, lax.ppermute(send, "mp", pair)))
    from_middle = lax.ppermute(second, "mp", along([(1, 2), (2, 1)]))
    from_end = lax.ppermute(second, "mp", along([(0, 1), (3, 2)]))
    send2, mine2, send3, mine3 = late_shares(3, lane_position, gated, third, out_weight, width)
    mine2 = merge(lane_position, f32, (mine2, lax.ppermute(send2, "mp", pair)))
    across = merge(lane_position, bf16, (mine2,), inner=from_near)
    from_across = lax.ppermute(across, "mp", along([(0, 2), (1, 3), (2, 0), (3, 1)]))
    own = merge(lane_position, f32, (mine3, lax.ppermute(send3, "mp", pair), from_middle), inner=from_end, outer=from_near)
    return total(own, from_across)


def shifted(value, axis, steps):
    count = lax.axis_size(axis)
    leading, last = (max(0, -steps), min(count, count - steps))
    return lax.ppermute(value, axis, [(source, source + steps) for source in range(leading, last)])


def project(block, norm_gain, weights):
    floats = block.astype(jnp.float32)
    mean_square = jnp.mean(floats * floats, axis=-1, keepdims=True)
    normed = (floats * lax.rsqrt(mean_square + epsilon) * norm_gain[None, :]).astype(jnp.bfloat16)
    return jnp.dot(normed, weights, preferred_element_type=jnp.float32).astype(jnp.bfloat16)


def general(
    tokens, norm_gain, in_weight, short_filter, rates, residues, skip, out_weight, segment_ids
):
    tok_rows = tokens.shape[0]
    model_width = tokens.shape[1]
    channels = in_weight.shape[2]
    filter_taps = short_filter.shape[0]
    pole_count = rates.shape[0]
    device_index = lax.axis_index("ctx")
    row_offset = device_index * tok_rows
    weights = in_weight.reshape(model_width, 3 * channels)
    projected = project(tokens, norm_gain, weights)
    previous = shifted(projected[tok_rows - (filter_taps - 1) :], "ctx", 1)
    extended = jnp.concatenate([previous, projected], axis=0)
    padded_ids = jnp.concatenate([jnp.full((filter_taps,), -1, jnp.int32), segment_ids], axis=0)
    window = lax.dynamic_slice_in_dim(padded_ids, row_offset, tok_rows + filter_taps, 0)
    local_ids = window[filter_taps:]
    taps_table = short_filter.reshape(filter_taps, 3 * channels)
    featured = jnp.zeros((tok_rows, 3 * channels), jnp.float32)
    for lag_index in range(filter_taps):
        begin = filter_taps - 1 - lag_index
        lagged = extended[begin : begin + tok_rows].astype(jnp.float32)
        matches = window[filter_taps - lag_index : filter_taps - lag_index + tok_rows] == local_ids
        term = taps_table[lag_index][None, :] * lagged
        featured = featured + jnp.where(matches[:, None], term, jnp.zeros_like(term))
    query_part = featured[:, :channels]
    key_part = featured[:, channels : 2 * channels]
    value_part = featured[:, 2 * channels :]
    product = key_part * value_part
    offsets = jnp.arange(tok_rows, dtype=jnp.float32)
    center = float(tok_rows // 2)
    growth = jnp.exp(-(offsets - center)[:, None, None] * rates[None])
    shrinkage = jnp.exp((offsets - center)[:, None, None] * rates[None])
    weighted = (shrinkage * product[:, None, :]).reshape(tok_rows, pole_count * channels)
    visible = (offsets[:, None] >= offsets[None, :]) & (local_ids[:, None] == local_ids[None, :])
    in_block = jnp.dot(visible.astype(jnp.float32), weighted, precision=lax.Precision.HIGHEST)
    in_block = in_block.reshape(tok_rows, pole_count, channels) * growth
    survives = local_ids == window[filter_taps - 1]
    block_factor = jnp.exp(-rates * tok_rows)
    block_end = in_block[tok_rows - 1]
    block_ends = lax.all_gather(block_end[None], "ctx", axis=0, tiled=True)
    shard_count = segment_ids.shape[0] // tok_rows
    last_ids = segment_ids.reshape(shard_count, tok_rows)[:, tok_rows - 1]
    prior_ids = jnp.concatenate([jnp.full((1,), -1, jnp.int32), last_ids[:-1]], axis=0)
    shard_decays = block_factor[None] * (last_ids == prior_ids).astype(jnp.float32)[:, None, None]

    def absorb(running, inputs):
        shard, factor, shard_end = inputs
        advanced = running * factor + shard_end
        return (jnp.where(shard < device_index, advanced, running), None)

    incoming, _ = lax.scan(
        absorb,
        jnp.zeros_like(block_end),
        (jnp.arange(shard_count, dtype=jnp.int32), shard_decays, block_ends),
    )
    carried = incoming[None] * jnp.exp(-(offsets + 1.0)[:, None, None] * rates[None])
    carried = carried * survives.astype(jnp.float32)[:, None, None]
    states = in_block + carried
    pole_weight = residues * jnp.sqrt(-jnp.expm1(-2.0 * rates))
    longconv = jnp.sum(pole_weight[None] * states, axis=1)
    gated = (query_part * (longconv + skip[None, :] * product)).astype(jnp.bfloat16)
    partial_terms = jnp.dot(gated, out_weight, preferred_element_type=jnp.float32)
    return lax.psum_scatter(partial_terms, "mp", scatter_dimension=1, tiled=True).astype(
        jnp.bfloat16
    )


def local(tokens, norm_gain, in_weight, short_filter, rates, residues, skip, out_weight, segment_ids):
    T = tokens.shape[0]
    shards = lax.axis_size("ctx")
    me = lax.axis_index("ctx")
    position = me.astype(jnp.int32)[None]
    lane_position = lax.axis_index("mp").astype(jnp.int32)[None]
    width = out_weight.shape[1] // lax.axis_size("mp")
    weight3 = jnp.transpose(in_weight, (1, 0, 2))
    out_weight = pltpu.with_memory_space_constraint(out_weight, pltpu.HBM)
    query, product, block, keep, visible, taps, rates, residues, skip = front(
        position, segment_ids.reshape(-1, 128), tokens, norm_gain[None], weight3, short_filter, rates, residues, skip[None])
    cuts = shards.bit_length() - 1
    each = product.shape[0] // cuts
    group, spans, arrived, parts, windows = block, [], [], [], []
    for k in range(cuts):
        span = 1 << k
        other = lax.ppermute(group, "ctx", [(a, a ^ span) for a in range(shards)])
        spans.append(span)
        arrived.append(other)
        *part, window = local_pass(
            k * each, each, min(k, 1), lane_position, product, keep, rates, residues, skip, out_weight, width, group)
        parts.append(part)
        windows.append(window)
        if k < cuts - 1:
            group = join(span, T, position, segment_ids, group, other, taps, rates, part[0])
    gated, send, mine, third = gate(T, spans, arrived, position, lane_position, segment_ids, query, parts, block, visible, taps, rates,
                             skip, windows[0], out_weight, width)
    return scatter_line(lane_position, gated, send, mine, windows[1], third, out_weight, width)


def solution(mesh):
    placed = (
        P("ctx", None),
        P(),
        P(None, None, "mp"),
        P(None, None, "mp"),
        P(None, "mp"),
        P(None, "mp"),
        P("mp"),
        P("mp", None),
        P(),
    )
    shards, groups = mesh.shape["ctx"], mesh.shape["mp"]

    def body(tokens, norm_gain, in_weight, *rest):
        suits = groups == 8 and shards & (shards - 1) == 0 and shards > 2
        suits = suits and in_weight.shape[2] % 512 == 0 and in_weight.shape[0] % 2048 == 0
        suits = suits and tokens.shape[0] % 64 == 0 and rest[-1].shape[0] % 128 == 0 and rest[1].shape[0] % 8 == 0
        return (local if suits else general)(tokens, norm_gain, in_weight, *rest)

    return jax.shard_map(
        body, mesh=mesh, in_specs=placed, out_specs=P("ctx", "mp"), check_vma=False
    )
```

```python
import functools
import jax
import jax.numpy as jnp
from jax import lax
from jax.experimental import pallas as pl
from jax.experimental.pallas import tpu as pltpu
from jax.sharding import PartitionSpec as P

epsilon = 1e-06
f32 = jnp.float32
bf16 = jnp.bfloat16

PARTS = 8
HEAD = 16
MIB = 1 << 20


def vmem():
    return pl.BlockSpec(memory_space=pltpu.VMEM)


def smem():
    return pl.BlockSpec(memory_space=pltpu.SMEM)


def same_id(ids_ref, a, b):
    def get(t):
        return jnp.where(t < 0, -1, ids_ref[jnp.maximum(t, 0)])

    return (get(a) == get(b)).astype(f32)


def hbm():
    return pl.BlockSpec(memory_space=pltpu.HBM)


def front_kernel(
    geometry, position, ids_ref, tokens_ref, gain_ref, weight_ref, taps_ref, rates_ref, residues_ref, skip_ref,
    query_out, prod_out, block_out, keep_out, visible_out, taps, rates, residues, skip,
    ids, gain, tok, normed, ring, total, proj, head, idcol, near, twice, ending, sem, tok_sem, ring_sem,
):
    T, depth, channels, cb_size, kc_size, slots, poles = geometry
    run = T // PARTS
    kcs, cbs = depth // kc_size, channels // cb_size
    steps = kcs * cbs
    base = pl.multiple_of(position[0] * T, 8)

    def fetch(step):
        cb, kc, slot = step // kcs, step % kcs, step % slots
        return pltpu.make_async_copy(
            weight_ref.at[:, pl.ds(pl.multiple_of(kc * kc_size, kc_size), kc_size),
                          pl.ds(pl.multiple_of(cb * cb_size, cb_size), cb_size)],
            ring.at[slot], ring_sem.at[slot])

    small = [
        pltpu.make_async_copy(a, b, sem.at[i])
        for i, (a, b) in enumerate(
            ((ids_ref, ids), (gain_ref, gain), (taps_ref, taps), (rates_ref, rates), (residues_ref, residues),
             (skip_ref, skip)))
    ]
    small[0].start()
    small[1].start()
    chunk = T // 4
    tok_copies = [
        pltpu.make_async_copy(tokens_ref.at[pl.ds(c * chunk, chunk)], tok.at[pl.ds(c * chunk, chunk)], tok_sem.at[c])
        for c in range(4)
    ]
    for copy in tok_copies:
        copy.start()
    for copy in small[2:]:
        copy.start()
    for s in range(min(slots, steps)):
        fetch(s).start()

    small[0].wait()
    idcol[0:8, :] = jnp.full((8, 128), -1.0, f32)
    for b in range(ids.shape[0]):
        row = ids[b : b + 1, :].astype(f32)
        idcol[8 + b * 128 : 8 + (b + 1) * 128, :] = jnp.broadcast_to(row, (128, 128)).T
    near[...] = idcol[pl.ds(base, T + 8), :]
    here = near[8 : 8 + T, :]
    keep_out[...] = (here == near[7 : 7 + T, :]).astype(f32)
    twice[...] = (here == near[6 : 6 + T, :]).astype(f32)
    ending[...] = (here == near[7 + T : 8 + T, :]).astype(f32)
    before = near[pl.ds(7, PARTS, stride=run), :]
    for i in range(run):
        visible_out[i * 8 : (i + 1) * 8, :] = (near[pl.ds(8 + i, PARTS, stride=run), :] == before).astype(f32)
    for i in range(3):
        proj[i, 0:8, :] = jnp.zeros((8, cb_size), f32)
    head[...] = jnp.zeros(head.shape, f32)
    small[1].wait()

    def norm_rows(g, _):
        part = pl.ds(pl.multiple_of(g * 16, 16), 16)
        x = tok[part, :].astype(f32)
        scale = lax.rsqrt(jnp.sum(x * x, axis=-1, keepdims=True) * (1.0 / depth) + epsilon)
        normed[part, :] = (x * scale * gain[...]).astype(bf16)
        return 0

    for c, copy in enumerate(tok_copies):
        copy.wait()
        lax.fori_loop(c * chunk // 16, (c + 1) * chunk // 16, norm_rows, 0)
    for copy in small[2:]:
        copy.wait()

    def epilogue(cb):
        cols = pl.ds(pl.multiple_of(cb * cb_size, cb_size), cb_size)
        feats = []
        m1 = jnp.concatenate([keep_out[...]] * (cb_size // 128), axis=1)
        m2 = jnp.concatenate([twice[...]] * (cb_size // 128), axis=1)
        for i in range(3):
            p = total[i].astype(bf16).astype(f32)
            proj[i, 8 : 8 + T, :] = p
            tap = [taps[j, i : i + 1, cols] for j in range(3)]
            feats.append(
                tap[0] * p + m1 * (tap[1] * proj[i, 7 : 7 + T, :]) + m2 * (tap[2] * proj[i, 6 : 6 + T, :]))
        query_out[:, cols] = feats[0]
        for i in range(1, 3):
            head[2 * (i - 1) : 2 * i, :] = proj[i, 8:10, :]
        for i in range(3):
            head[4 + 2 * i : 6 + 2 * i, :] = proj[i, 6 + T : 8 + T, :]
        block_out[poles : poles + HEAD, cols] = head[...].astype(bf16)
        product = feats[1] * feats[2]
        back = 7.0 - lax.broadcasted_iota(jnp.int32, (8, 128), 0).astype(f32)
        for lane in range(cb_size // 128):
            tile = cb * (cb_size // 128) + lane
            lanes = pl.ds(pl.multiple_of(tile * 128, 128), 128)
            prod_out[tile] = product[:, lane * 128 : lane * 128 + 128]
            r16 = rates[:, lanes]
            jump = jnp.exp(-8.0 * r16)
            leap = [jnp.broadcast_to(jump[n : n + 1], (8, 128)) for n in range(poles)]

            def eight(g, sums):
                part = pl.ds(pl.multiple_of(g * 8, 8), 8)
                p = prod_out[tile, part, :] * ending[part, :]
                return tuple(sums[n] * leap[n] + p for n in range(poles))

            sums = lax.fori_loop(
                0, T // 8, eight, tuple(jnp.zeros((8, 128), f32) for _ in range(poles)), unroll=4)
            ends = [
                jnp.sum(sums[n] * jnp.exp(-back * r16[n : n + 1]), axis=0, keepdims=True) for n in range(poles)
            ]
            block_out[0:poles, lanes] = jnp.concatenate(ends, axis=0).astype(bf16)

    def step_body(step, _):
        cb, kc, slot = step // kcs, step % kcs, step % slots
        fetch(step).wait()
        lhs = normed[:, pl.ds(pl.multiple_of(kc * kc_size, kc_size), kc_size)]
        for i in range(3):
            part = jnp.dot(lhs, ring[slot, i], preferred_element_type=f32)
            total[i] = jnp.where(kc == 0, part, total[i] + part)

        @pl.when(step + slots < steps)
        def _():
            fetch(step + slots).start()

        @pl.when(kc == kcs - 1)
        def _():
            epilogue(cb)

        return 0

    total[...] = jnp.zeros(total.shape, f32)
    lax.fori_loop(0, steps, step_body, 0)


def front(position, ids2, tokens, gain, weight3, taps, rates, residues, skip):
    T, depth = tokens.shape
    channels, poles = weight3.shape[2], rates.shape[0]
    cb_size, kc_size, slots = 256, 2048, 5
    geometry = (T, depth, channels, cb_size, kc_size, slots, poles)
    kept = [pltpu.VMEM(a.shape, a.dtype) for a in (taps, rates, residues, skip)]
    ids2, tokens, gain, weight3, taps, rates, residues, skip = [
        pltpu.with_memory_space_constraint(a, pltpu.HBM)
        for a in (ids2, tokens, gain, weight3, taps, rates, residues, skip)
    ]
    return pl.pallas_call(
        functools.partial(front_kernel, geometry),
        out_shape=[
            jax.ShapeDtypeStruct((T, channels), f32),
            jax.ShapeDtypeStruct((channels // 128, T, 128), f32),
            jax.ShapeDtypeStruct((poles + HEAD, channels), bf16),
            jax.ShapeDtypeStruct((T, 128), f32),
            jax.ShapeDtypeStruct((T, 128), f32),
        ] + kept,
        in_specs=[smem()] + [hbm()] * 8,
        out_specs=[vmem()] * 9,
        scratch_shapes=[
            pltpu.VMEM(ids2.shape, ids2.dtype),
            pltpu.VMEM(gain.shape, f32),
            pltpu.VMEM((T, depth), bf16),
            pltpu.VMEM((T, depth), bf16),
            pltpu.VMEM((slots, 3, kc_size, cb_size), bf16),
            pltpu.VMEM((3, T, cb_size), f32),
            pltpu.VMEM((3, T + 8, cb_size), f32),
            pltpu.VMEM((HEAD, cb_size), f32),
            pltpu.VMEM((ids2.shape[0] * 128 + 8, 128), f32),
            pltpu.VMEM((T + 8, 128), f32),
            pltpu.VMEM((T, 128), f32),
            pltpu.VMEM((T, 128), f32),
            pltpu.SemaphoreType.DMA((6,)),
            pltpu.SemaphoreType.DMA((4,)),
            pltpu.SemaphoreType.DMA((slots,)),
        ],
        compiler_params=pltpu.CompilerParams(vmem_limit_bytes=28 * MIB),
        name="front",
    )(position, ids2, tokens, gain, weight3, taps, rates, residues, skip)


def expm1(x):
    series = jnp.ones_like(x)
    for k in range(9, 1, -1):
        series = 1.0 + series * x * (1.0 / k)
    return jnp.where(jnp.abs(x) < 0.5, x * series, jnp.exp(x) - 1.0)


def local_kernel(
    poles, first, slot, lane_position, prod_ref, keep_ref, rates_ref, residues_ref, skip_ref, out_ref, _,
    local_out, state_out, pole_out, window_out, sem,
):
    copy = columns(lane_position[0], slot, out_ref, window_out, sem)
    copy.start()
    tiles, T, _ = local_out.shape
    run = T // PARTS
    mine = slice(first * 128, (first + tiles) * 128)
    pole_out[...] = residues_ref[:, mine] * jnp.sqrt(-expm1(-2.0 * rates_ref[:, mine]))

    def tile_body(tile, _):
        lanes = pl.ds(pl.multiple_of((first + tile) * 128, 128), 128)
        d16 = jnp.exp(-rates_ref[:, lanes])
        w16 = pole_out[:, pl.ds(pl.multiple_of(tile * 128, 128), 128)]
        decay = [jnp.broadcast_to(d16[n : n + 1], (8, 128)) for n in range(poles)]
        weight = [jnp.broadcast_to(w16[n : n + 1], (8, 128)) for n in range(poles)]
        skip = skip_ref[0:1, lanes]

        def token(i, states):
            at = pl.ds(i, PARTS, stride=run)
            p, keep = prod_ref[first + tile, at, :], keep_ref[at, :]
            after = [states[n] * decay[n] * keep + p for n in range(poles)]
            local_out[tile, at, :] = tree([skip * p] + [weight[n] * after[n] for n in range(poles)])
            return tuple(after)

        states = lax.fori_loop(0, run, token, tuple(jnp.zeros((8, 128), f32) for _ in range(poles)), unroll=2)
        for n in range(poles):
            state_out[tile, pl.ds(n, PARTS, stride=poles), :] = states[n]
        return 0

    lax.fori_loop(0, tiles, tile_body, 0)
    copy.wait()


def tree(terms):
    while len(terms) > 1:
        terms = [a + b for a, b in zip(terms[0::2], terms[1::2])] + terms[len(terms) // 2 * 2 :]
    return terms[0]


def local_pass(first, tiles, slot, lane_position, product, keep, rates, residues, skip, out_weight, width, after):
    T, poles = product.shape[1], rates.shape[0]
    return pl.pallas_call(
        functools.partial(local_kernel, poles, first, slot),
        out_shape=(
            jax.ShapeDtypeStruct((tiles, T, 128), f32),
            jax.ShapeDtypeStruct((tiles, PARTS * poles, 128), f32),
            jax.ShapeDtypeStruct((poles, tiles * 128), f32),
            jax.ShapeDtypeStruct((out_weight.shape[0], 2 * width), bf16),
        ),
        in_specs=[smem()] + [vmem()] * 5 + [hbm(), pl.BlockSpec(memory_space=pl.ANY)],
        out_specs=[vmem()] * 4,
        scratch_shapes=[pltpu.SemaphoreType.DMA((STREAMS,))],
        compiler_params=pltpu.CompilerParams(vmem_limit_bytes=8 * MIB),
        cost_estimate=pl.CostEstimate(flops=6 * T * poles * tiles * 128, bytes_accessed=8 * MIB, transcendentals=0),
        name="local_pass",
    )(lane_position, product, keep, rates, residues, skip, out_weight, after)


def first_products(first, last, taps, ids_ref, base):
    s01, s0m1 = same_id(ids_ref, base + 1, base), same_id(ids_ref, base, base - 1)
    s0m2, s1m1 = same_id(ids_ref, base, base - 2), same_id(ids_ref, base + 1, base - 1)

    def shift(i):
        near, far = last[i][1:2], last[i][0:1]
        t1, t2 = taps[1][i : i + 1], taps[2][i : i + 1]
        return s0m1 * (t1 * near) + s0m2 * (t2 * far), s1m1 * (t2 * near)

    def plain(i):
        t0, t1 = taps[0][i : i + 1], taps[1][i : i + 1]
        return t0 * first[i][0:1], t0 * first[i][1:2] + s01 * (t1 * first[i][0:1])

    k, v, dk, dv = plain(1), plain(2), shift(1), shift(2)
    delta = [(k[j] + dk[j]) * (v[j] + dv[j]) - k[j] * v[j] for j in range(2)]
    return shift(0), delta


def unpack(block, poles):
    first = [None, block[poles : poles + 2], block[poles + 2 : poles + 4]]
    last = [block[poles + 4 + 2 * i : poles + 6 + 2 * i] for i in range(3)]
    return block[0:poles], first, last


def joined_state(low_state, low_last, up_state, up_first, taps, rates, ids_ref, base, length):
    _, delta = first_products(up_first, low_last, taps, ids_ref, base)
    grown = low_state + delta[0] * jnp.exp(rates) + delta[1] * jnp.exp(2.0 * rates)
    open_ = same_id(ids_ref, base + length - 1, base - 1)
    return up_state + grown * (jnp.exp(-rates * jnp.float32(length)) * open_)


def join_kernel(T, poles, span, position, ids_ref, mine_ref, other_ref, taps_ref, rates_ref, _, out):
    me = position[0]
    is_upper = (me // span) % 2 == 1
    base = (me // (2 * span)) * (2 * span * T) + span * T
    mine, other = mine_ref[...].astype(f32), other_ref[...].astype(f32)
    lower, upper = jnp.where(is_upper, other, mine), jnp.where(is_upper, mine, other)
    taps = [taps_ref[j] for j in range(3)]
    low_state, _, low_last = unpack(lower, poles)
    up_state, up_first, _ = unpack(upper, poles)
    state = joined_state(low_state, low_last, up_state, up_first, taps, rates_ref[...], ids_ref, base, span * T)
    out[0:poles, :] = state.astype(bf16)
    row = lax.broadcasted_iota(jnp.int32, (HEAD, lower.shape[1]), 0)
    out[poles : poles + HEAD, :] = jnp.where(row < 4, lower[poles:], upper[poles:]).astype(bf16)


def join(span, T, position, ids, mine, other, taps, rates, after):
    poles = rates.shape[0]
    return pl.pallas_call(
        functools.partial(join_kernel, T, poles, span),
        out_shape=jax.ShapeDtypeStruct(mine.shape, bf16),
        in_specs=[smem(), smem()] + [vmem()] * 4 + [pl.BlockSpec(memory_space=pl.ANY)],
        out_specs=vmem(),
        compiler_params=pltpu.CompilerParams(vmem_limit_bytes=4 * MIB),
        name="join",
    )(position, ids, mine, other, taps, rates, after)


def gate_kernel(
    T, poles, spans, cuts, position, lane_position, ids_ref, query_ref, block_ref, visible_ref, taps_ref, rates_ref, skip_ref,
    window_ref, out_ref, *rest,
):
    arrived, rest = rest[: len(spans)], rest[len(spans) :]
    parts, rest = [rest[3 * c : 3 * c + 3] for c in range(cuts)], rest[3 * cuts :]
    gated_out, send_out, mine_out, third_out, carry, full, sem = rest
    run = T // PARTS
    tiles = query_ref.shape[1] // 128
    copy = columns(lane_position[0], 2, out_ref, third_out, sem)
    copy.start()
    me = position[0]
    base = me * T
    taps = [taps_ref[j] for j in range(3)]
    rates, skip = rates_ref[...], skip_ref[...]
    weight = jnp.concatenate([pole_ref[...] for _, _, pole_ref in parts], axis=1)
    each = tiles // cuts
    prior = jnp.zeros(block_ref.shape, f32)
    prior_state, prior_first, prior_last = unpack(prior, poles)
    for span, ref in zip(spans, arrived):
        state, first, last = unpack(ref[...].astype(f32), poles)
        upper, held = (me // span) % 2 == 1, me % span
        if span == 1:
            both = state
        else:
            both = joined_state(
                state, last, prior_state, prior_first, taps, rates, ids_ref, (me - held) * T, held * T)
        fresh = upper & (held == 0)
        prior_state = jnp.where(fresh, state, jnp.where(upper, both, prior_state))
        prior_first = [None] + [jnp.where(upper, first[i], prior_first[i]) for i in (1, 2)]
        prior_last = [jnp.where(fresh, last[i], prior_last[i]) for i in range(3)]
    _, first, _ = unpack(block_ref[...].astype(f32), poles)
    q_shift, delta = first_products(first, prior_last, taps, ids_ref, base)
    second = delta[1] * jnp.exp(rates)
    now = prior_state + (delta[0] + second) * jnp.exp(rates)
    fix0 = skip * delta[0] - jnp.sum(weight * second, axis=0, keepdims=True)
    fix1 = skip * delta[1]
    jump = jnp.exp(-rates * float(run))
    for s in range(PARTS):
        part = slice(s * poles, (s + 1) * poles)
        began = weight * now
        for tile in range(tiles):
            carry[tile, part, :] = began[:, tile * 128 : tile * 128 + 128]
        if s < PARTS - 1:
            whole = same_id(ids_ref, base + s * run + run - 1, base + s * run - 1)
            ends = jnp.concatenate([parts[tile // each][1][tile % each, part, :] for tile in range(tiles)], axis=1)
            now = now * (jump * whole) + ends

    def lane_body(cut, inner, _):
        tile = cut * each + inner
        lanes = pl.ds(pl.multiple_of(tile * 128, 128), 128)
        d16 = jnp.exp(-rates_ref[:, lanes])
        decay = [jnp.broadcast_to(d16[n : n + 1], (8, 128)) for n in range(poles)]
        start = tuple(carry[tile, pl.ds(n, PARTS, stride=poles), :] for n in range(poles))

        def token(i, states):
            after = [states[n] * decay[n] for n in range(poles)]
            see = visible_ref[pl.ds(pl.multiple_of(i * 8, 8), 8), :]
            at = pl.ds(i, PARTS, stride=run)
            full[tile, at, :] = parts[cut][0][inner, at, :] + see * tree(list(after))
            return tuple(after)

        lax.fori_loop(0, run, token, start, unroll=4)
        return 0

    for cut in range(cuts):
        lax.fori_loop(0, each, functools.partial(lane_body, cut), 0)
    row = lax.broadcasted_iota(jnp.int32, (16, 128), 0)
    for tile in range(tiles):
        lanes = slice(tile * 128, tile * 128 + 128)
        gated_out[:, lanes] = (query_ref[:, lanes] * full[tile]).astype(bf16)
        top_q, top = query_ref[0:16, lanes], full[tile, 0:16, :]
        top_q = top_q + jnp.where(row == 0, q_shift[0][:, lanes], 0.0) + jnp.where(row == 1, q_shift[1][:, lanes], 0.0)
        top = top + jnp.where(row == 0, fix0[:, lanes], 0.0) + jnp.where(row == 1, fix1[:, lanes], 0.0)
        gated_out[0:16, lanes] = (top_q * top).astype(bf16)
    share(lane_position[0], gated_out, window_ref, send_out, mine_out)
    copy.wait()


def target(index, slot):
    chip = index // 2
    if slot == 0:
        return 3 - 3 * (chip % 2)
    if slot == 1:
        return jnp.where(chip < 2, 2, 1)
    if slot == 2:
        return jnp.where(chip < 2, 1 + 2 * chip, 2 * (chip - 2))
    return chip


class Copies:
    def __init__(self, copies):
        self.copies = copies

    def start(self):
        for copy in self.copies:
            copy.start()

    def wait(self):
        for copy in self.copies:
            copy.wait()


STREAMS = 4


def columns(index, slot, out_ref, window, sem):
    channels, both = window.shape
    start = pl.multiple_of(target(index, slot) * both, both)
    each = channels // STREAMS
    return Copies([
        pltpu.make_async_copy(
            out_ref.at[pl.ds(k * each, each), pl.ds(start, both)], window.at[pl.ds(k * each, each)], sem.at[k])
        for k in range(STREAMS)
    ])


def share(index, gated_ref, window, send_out, mine_out):
    width = send_out.shape[1]
    tile = 256
    core = index % 2

    for j in range(width // tile):
        at = slice(j * tile, j * tile + tile)
        for out, half in ((send_out, 1 - core), (mine_out, core)):
            cols = pl.ds(pl.multiple_of(half * width + j * tile, tile), tile)
            out[:, at] = jnp.dot(gated_ref[...], window[:, cols], preferred_element_type=f32).astype(out.dtype)


def share_kernel(count, lane_position, gated_ref, *rest):
    windows, outs = rest[:count], rest[count:]
    for k, window in enumerate(windows):
        share(lane_position[0], gated_ref, window, outs[2 * k], outs[2 * k + 1])


def shares(lane_position, gated, windows, width):
    T, channels = gated.shape
    count = len(windows)
    return pl.pallas_call(
        functools.partial(share_kernel, count),
        out_shape=[jax.ShapeDtypeStruct((T, width), d) for _ in windows for d in (bf16, f32)],
        in_specs=[smem(), vmem()] + [vmem()] * count,
        out_specs=[vmem()] * (2 * count),
        compiler_params=pltpu.CompilerParams(vmem_limit_bytes=4 * MIB),
        cost_estimate=pl.CostEstimate(
            flops=4 * T * channels * width * count, bytes_accessed=4 * channels * width * count, transcendentals=0),
        name="shares",
    )(lane_position, gated, *windows)


def late_share_kernel(slot, lane_position, gated_ref, window_ref, out_ref, *rest):
    outs, (window, sem) = rest[:-2], rest[-2:]
    copy = columns(lane_position[0], slot, out_ref, window, sem)
    copy.start()
    share(lane_position[0], gated_ref, window_ref, outs[0], outs[1])
    copy.wait()
    share(lane_position[0], gated_ref, window, outs[2], outs[3])


def late_shares(slot, lane_position, gated, window, out_weight, width):
    T, channels = gated.shape
    return pl.pallas_call(
        functools.partial(late_share_kernel, slot),
        out_shape=[jax.ShapeDtypeStruct((T, width), d) for d in (bf16, f32, bf16, f32)],
        in_specs=[smem(), vmem(), vmem(), hbm()],
        out_specs=[vmem()] * 4,
        scratch_shapes=[pltpu.VMEM((channels, 2 * width), bf16), pltpu.SemaphoreType.DMA((STREAMS,))],
        compiler_params=pltpu.CompilerParams(vmem_limit_bytes=6 * MIB),
        cost_estimate=pl.CostEstimate(
            flops=8 * T * channels * width, bytes_accessed=8 * channels * width, transcendentals=0),
        name="late_shares",
    )(lane_position, gated, window, out_weight)


def gate(T, spans, arrived, position, lane_position, ids, query, parts, block, visible, taps, rates, skip, window, out_weight, width):
    poles, channels = rates.shape
    return pl.pallas_call(
        functools.partial(gate_kernel, T, poles, tuple(spans), len(parts)),
        out_shape=[
            jax.ShapeDtypeStruct(query.shape, bf16),
            jax.ShapeDtypeStruct((T, width), bf16),
            jax.ShapeDtypeStruct((T, width), f32),
            pltpu.VMEM(window.shape, bf16),
        ],
        in_specs=[smem()] * 3 + [vmem()] * 7 + [hbm()] + [vmem()] * (len(spans) + 3 * len(parts)),
        out_specs=[vmem()] * 4,
        scratch_shapes=[
            pltpu.VMEM((channels // 128, PARTS * poles, 128), f32),
            pltpu.VMEM((channels // 128, T, 128), f32),
            pltpu.SemaphoreType.DMA((STREAMS,)),
        ],
        compiler_params=pltpu.CompilerParams(vmem_limit_bytes=8 * MIB),
        name="gate",
    )(position, lane_position, ids, query, block, visible, taps, rates, skip, window, out_weight, *arrived,
      *[a for part in parts for a in part])


def total(*terms):
    return functools.reduce(lambda a, b: a + b, [t.astype(f32) for t in terms]).astype(bf16)


def merge_kernel(count, has_inner, lane_position, *rest):
    terms, picks, out = rest[:count], rest[count:-1], rest[-1]
    value = terms[0][...].astype(f32)
    for term in terms[1:]:
        value = value + term[...].astype(f32)
    chip = lane_position[0] // 2
    inner = (chip == 1) | (chip == 2)
    for pick, wanted in zip(picks, (inner, jnp.logical_not(inner)) if has_inner else (jnp.logical_not(inner),)):
        value = value + jnp.where(wanted, pick[...].astype(f32), 0.0)
    out[...] = value.astype(out.dtype)


def merge(lane_position, dtype, terms, inner=None, outer=None):
    picks = [a for a in (inner, outer) if a is not None]
    terms = [pltpu.with_memory_space_constraint(a, pltpu.VMEM) for a in (*terms, *picks)]
    return pl.pallas_call(
        functools.partial(merge_kernel, len(terms) - len(picks), inner is not None),
        out_shape=jax.ShapeDtypeStruct(terms[0].shape, dtype),
        in_specs=[smem()] + [vmem()] * len(terms),
        out_specs=vmem(),
        compiler_params=pltpu.CompilerParams(vmem_limit_bytes=3 * MIB),
        name="merge",
    )(lane_position, *terms)


def scatter_line(lane_position, gated, send, mine, window, third, out_weight, width):
    pair = [(m, m ^ 1) for m in range(8)]

    def along(hops):
        return [(a * 2 + c, b * 2 + c) for a, b in hops for c in range(2)]

    near = along([(0, 1), (1, 0), (2, 3), (3, 2)])
    traded = lax.ppermute(send, "mp", pair)
    far = merge(lane_position, bf16, (mine, traded))
    from_near = lax.ppermute(far, "mp", near)
    send, mine = shares(lane_position, gated, [window], width)
    second = merge(lane_position, bf16, (mine, lax.ppermute(send, "mp", pair)))
    from_middle = lax.ppermute(second, "mp", along([(1, 2), (2, 1)]))
    from_end = lax.ppermute(second, "mp", along([(0, 2), (3, 1)]))
    send2, mine2, send3, mine3 = late_shares(3, lane_position, gated, third, out_weight, width)
    mine2 = merge(lane_position, f32, (mine2, lax.ppermute(send2, "mp", pair)))
    onward = merge(lane_position, bf16, (mine2,), inner=from_near)
    from_round = lax.ppermute(onward, "mp", along([(0, 1), (1, 3), (3, 2), (2, 0)]))
    own = merge(lane_position, f32, (mine3, lax.ppermute(send3, "mp", pair), from_middle, from_end), outer=from_near)
    return total(own, from_round)


def shifted(value, axis, steps):
    count = lax.axis_size(axis)
    leading, last = (max(0, -steps), min(count, count - steps))
    return lax.ppermute(value, axis, [(source, source + steps) for source in range(leading, last)])


def project(block, norm_gain, weights):
    floats = block.astype(jnp.float32)
    mean_square = jnp.mean(floats * floats, axis=-1, keepdims=True)
    normed = (floats * lax.rsqrt(mean_square + epsilon) * norm_gain[None, :]).astype(jnp.bfloat16)
    return jnp.dot(normed, weights, preferred_element_type=jnp.float32).astype(jnp.bfloat16)


def general(
    tokens, norm_gain, in_weight, short_filter, rates, residues, skip, out_weight, segment_ids
):
    tok_rows = tokens.shape[0]
    model_width = tokens.shape[1]
    channels = in_weight.shape[2]
    filter_taps = short_filter.shape[0]
    pole_count = rates.shape[0]
    device_index = lax.axis_index("ctx")
    row_offset = device_index * tok_rows
    weights = in_weight.reshape(model_width, 3 * channels)
    projected = project(tokens, norm_gain, weights)
    previous = shifted(projected[tok_rows - (filter_taps - 1) :], "ctx", 1)
    extended = jnp.concatenate([previous, projected], axis=0)
    padded_ids = jnp.concatenate([jnp.full((filter_taps,), -1, jnp.int32), segment_ids], axis=0)
    window = lax.dynamic_slice_in_dim(padded_ids, row_offset, tok_rows + filter_taps, 0)
    local_ids = window[filter_taps:]
    taps_table = short_filter.reshape(filter_taps, 3 * channels)
    featured = jnp.zeros((tok_rows, 3 * channels), jnp.float32)
    for lag_index in range(filter_taps):
        begin = filter_taps - 1 - lag_index
        lagged = extended[begin : begin + tok_rows].astype(jnp.float32)
        matches = window[filter_taps - lag_index : filter_taps - lag_index + tok_rows] == local_ids
        term = taps_table[lag_index][None, :] * lagged
        featured = featured + jnp.where(matches[:, None], term, jnp.zeros_like(term))
    query_part = featured[:, :channels]
    key_part = featured[:, channels : 2 * channels]
    value_part = featured[:, 2 * channels :]
    product = key_part * value_part
    offsets = jnp.arange(tok_rows, dtype=jnp.float32)
    center = float(tok_rows // 2)
    growth = jnp.exp(-(offsets - center)[:, None, None] * rates[None])
    shrinkage = jnp.exp((offsets - center)[:, None, None] * rates[None])
    weighted = (shrinkage * product[:, None, :]).reshape(tok_rows, pole_count * channels)
    visible = (offsets[:, None] >= offsets[None, :]) & (local_ids[:, None] == local_ids[None, :])
    in_block = jnp.dot(visible.astype(jnp.float32), weighted, precision=lax.Precision.HIGHEST)
    in_block = in_block.reshape(tok_rows, pole_count, channels) * growth
    survives = local_ids == window[filter_taps - 1]
    block_factor = jnp.exp(-rates * tok_rows)
    block_end = in_block[tok_rows - 1]
    block_ends = lax.all_gather(block_end[None], "ctx", axis=0, tiled=True)
    shard_count = segment_ids.shape[0] // tok_rows
    last_ids = segment_ids.reshape(shard_count, tok_rows)[:, tok_rows - 1]
    prior_ids = jnp.concatenate([jnp.full((1,), -1, jnp.int32), last_ids[:-1]], axis=0)
    shard_decays = block_factor[None] * (last_ids == prior_ids).astype(jnp.float32)[:, None, None]

    def absorb(running, inputs):
        shard, factor, shard_end = inputs
        advanced = running * factor + shard_end
        return (jnp.where(shard < device_index, advanced, running), None)

    incoming, _ = lax.scan(
        absorb,
        jnp.zeros_like(block_end),
        (jnp.arange(shard_count, dtype=jnp.int32), shard_decays, block_ends),
    )
    carried = incoming[None] * jnp.exp(-(offsets + 1.0)[:, None, None] * rates[None])
    carried = carried * survives.astype(jnp.float32)[:, None, None]
    states = in_block + carried
    pole_weight = residues * jnp.sqrt(-jnp.expm1(-2.0 * rates))
    longconv = jnp.sum(pole_weight[None] * states, axis=1)
    gated = (query_part * (longconv + skip[None, :] * product)).astype(jnp.bfloat16)
    partial_terms = jnp.dot(gated, out_weight, preferred_element_type=jnp.float32)
    return lax.psum_scatter(partial_terms, "mp", scatter_dimension=1, tiled=True).astype(
        jnp.bfloat16
    )


def local(tokens, norm_gain, in_weight, short_filter, rates, residues, skip, out_weight, segment_ids):
    T = tokens.shape[0]
    shards = lax.axis_size("ctx")
    me = lax.axis_index("ctx")
    position = me.astype(jnp.int32)[None]
    lane_position = lax.axis_index("mp").astype(jnp.int32)[None]
    width = out_weight.shape[1] // lax.axis_size("mp")
    weight3 = jnp.transpose(in_weight, (1, 0, 2))
    out_weight = pltpu.with_memory_space_constraint(out_weight, pltpu.HBM)
    query, product, block, keep, visible, taps, rates, residues, skip = front(
        position, segment_ids.reshape(-1, 128), tokens, norm_gain[None], weight3, short_filter, rates, residues, skip[None])
    cuts = shards.bit_length() - 1
    each = product.shape[0] // cuts
    group, spans, arrived, parts, windows = block, [], [], [], []
    for k in range(cuts):
        span = 1 << k
        other = lax.ppermute(group, "ctx", [(a, a ^ span) for a in range(shards)])
        spans.append(span)
        arrived.append(other)
        *part, window = local_pass(
            k * each, each, min(k, 1), lane_position, product, keep, rates, residues, skip, out_weight, width, group)
        parts.append(part)
        windows.append(window)
        if k < cuts - 1:
            group = join(span, T, position, segment_ids, group, other, taps, rates, part[0])
    gated, send, mine, third = gate(T, spans, arrived, position, lane_position, segment_ids, query, parts, block, visible, taps, rates,
                             skip, windows[0], out_weight, width)
    return scatter_line(lane_position, gated, send, mine, windows[1], third, out_weight, width)


def solution(mesh):
    placed = (
        P("ctx", None),
        P(),
        P(None, None, "mp"),
        P(None, None, "mp"),
        P(None, "mp"),
        P(None, "mp"),
        P("mp"),
        P("mp", None),
        P(),
    )
    shards, groups = mesh.shape["ctx"], mesh.shape["mp"]

    def body(tokens, norm_gain, in_weight, *rest):
        suits = groups == 8 and shards & (shards - 1) == 0 and shards > 2
        suits = suits and in_weight.shape[2] % 512 == 0 and in_weight.shape[0] % 2048 == 0
        suits = suits and tokens.shape[0] % 64 == 0 and rest[-1].shape[0] % 128 == 0 and rest[1].shape[0] % 8 == 0
        return (local if suits else general)(tokens, norm_gain, in_weight, *rest)

    return jax.shard_map(
        body, mesh=mesh, in_specs=placed, out_specs=P("ctx", "mp"), check_vma=False
    )
```

```python
import functools
import jax
import jax.numpy as jnp
from jax import lax
from jax.experimental import pallas as pl
from jax.experimental.pallas import tpu as pltpu
from jax.sharding import PartitionSpec as P

epsilon = 1e-06
f32 = jnp.float32
bf16 = jnp.bfloat16

PARTS = 8
HEAD = 16
MIB = 1 << 20


def vmem():
    return pl.BlockSpec(memory_space=pltpu.VMEM)


def smem():
    return pl.BlockSpec(memory_space=pltpu.SMEM)


def same_id(ids_ref, a, b):
    def get(t):
        return jnp.where(t < 0, -1, ids_ref[jnp.maximum(t, 0)])

    return (get(a) == get(b)).astype(f32)


def hbm():
    return pl.BlockSpec(memory_space=pltpu.HBM)


def front_kernel(
    geometry, position, ids_ref, tokens_ref, gain_ref, weight_ref, taps_ref, rates_ref, residues_ref, skip_ref,
    query_out, prod_out, block_out, keep_out, visible_out, taps, rates, residues, skip,
    ids, gain, tok, normed, ring, total, proj, head, idcol, near, twice, ending, sem, tok_sem, ring_sem,
):
    T, depth, channels, cb_size, kc_size, slots, poles = geometry
    run = T // PARTS
    kcs, cbs = depth // kc_size, channels // cb_size
    steps = kcs * cbs
    base = pl.multiple_of(position[0] * T, 8)

    def fetch(step):
        cb, kc, slot = step // kcs, step % kcs, step % slots
        return pltpu.make_async_copy(
            weight_ref.at[:, pl.ds(pl.multiple_of(kc * kc_size, kc_size), kc_size),
                          pl.ds(pl.multiple_of(cb * cb_size, cb_size), cb_size)],
            ring.at[slot], ring_sem.at[slot])

    small = [
        pltpu.make_async_copy(a, b, sem.at[i])
        for i, (a, b) in enumerate(
            ((ids_ref, ids), (gain_ref, gain), (taps_ref, taps), (rates_ref, rates), (residues_ref, residues),
             (skip_ref, skip)))
    ]
    small[0].start()
    small[1].start()
    chunk = T // 4
    tok_copies = [
        pltpu.make_async_copy(tokens_ref.at[pl.ds(c * chunk, chunk)], tok.at[pl.ds(c * chunk, chunk)], tok_sem.at[c])
        for c in range(4)
    ]
    for copy in tok_copies:
        copy.start()
    for copy in small[2:]:
        copy.start()
    for s in range(min(slots, steps)):
        fetch(s).start()

    small[0].wait()
    idcol[0:8, :] = jnp.full((8, 128), -1.0, f32)
    for b in range(ids.shape[0]):
        row = ids[b : b + 1, :].astype(f32)
        idcol[8 + b * 128 : 8 + (b + 1) * 128, :] = jnp.broadcast_to(row, (128, 128)).T
    near[...] = idcol[pl.ds(base, T + 8), :]
    here = near[8 : 8 + T, :]
    keep_out[...] = (here == near[7 : 7 + T, :]).astype(f32)
    twice[...] = (here == near[6 : 6 + T, :]).astype(f32)
    ending[...] = (here == near[7 + T : 8 + T, :]).astype(f32)
    before = near[pl.ds(7, PARTS, stride=run), :]
    for i in range(run):
        visible_out[i * 8 : (i + 1) * 8, :] = (near[pl.ds(8 + i, PARTS, stride=run), :] == before).astype(f32)
    for i in range(3):
        proj[i, 0:8, :] = jnp.zeros((8, cb_size), f32)
    head[...] = jnp.zeros(head.shape, f32)
    small[1].wait()

    def norm_rows(g, _):
        part = pl.ds(pl.multiple_of(g * 16, 16), 16)
        x = tok[part, :].astype(f32)
        scale = lax.rsqrt(jnp.sum(x * x, axis=-1, keepdims=True) * (1.0 / depth) + epsilon)
        normed[part, :] = (x * scale * gain[...]).astype(bf16)
        return 0

    for c, copy in enumerate(tok_copies):
        copy.wait()
        lax.fori_loop(c * chunk // 16, (c + 1) * chunk // 16, norm_rows, 0)
    for copy in small[2:]:
        copy.wait()

    def epilogue(cb):
        cols = pl.ds(pl.multiple_of(cb * cb_size, cb_size), cb_size)
        feats = []
        m1 = jnp.concatenate([keep_out[...]] * (cb_size // 128), axis=1)
        m2 = jnp.concatenate([twice[...]] * (cb_size // 128), axis=1)
        for i in range(3):
            p = total[i].astype(bf16).astype(f32)
            proj[i, 8 : 8 + T, :] = p
            tap = [taps[j, i : i + 1, cols] for j in range(3)]
            feats.append(
                tap[0] * p + m1 * (tap[1] * proj[i, 7 : 7 + T, :]) + m2 * (tap[2] * proj[i, 6 : 6 + T, :]))
        query_out[:, cols] = feats[0]
        for i in range(1, 3):
            head[2 * (i - 1) : 2 * i, :] = proj[i, 8:10, :]
        for i in range(3):
            head[4 + 2 * i : 6 + 2 * i, :] = proj[i, 6 + T : 8 + T, :]
        block_out[poles : poles + HEAD, cols] = head[...].astype(bf16)
        product = feats[1] * feats[2]
        back = 7.0 - lax.broadcasted_iota(jnp.int32, (8, 128), 0).astype(f32)
        for lane in range(cb_size // 128):
            tile = cb * (cb_size // 128) + lane
            lanes = pl.ds(pl.multiple_of(tile * 128, 128), 128)
            prod_out[tile] = product[:, lane * 128 : lane * 128 + 128]
            r16 = rates[:, lanes]
            jump = jnp.exp(-8.0 * r16)
            leap = [jnp.broadcast_to(jump[n : n + 1], (8, 128)) for n in range(poles)]

            def eight(g, sums):
                part = pl.ds(pl.multiple_of(g * 8, 8), 8)
                p = prod_out[tile, part, :] * ending[part, :]
                return tuple(sums[n] * leap[n] + p for n in range(poles))

            sums = lax.fori_loop(
                0, T // 8, eight, tuple(jnp.zeros((8, 128), f32) for _ in range(poles)), unroll=4)
            ends = [
                jnp.sum(sums[n] * jnp.exp(-back * r16[n : n + 1]), axis=0, keepdims=True) for n in range(poles)
            ]
            block_out[0:poles, lanes] = jnp.concatenate(ends, axis=0).astype(bf16)

    def step_body(step, _):
        cb, kc, slot = step // kcs, step % kcs, step % slots
        fetch(step).wait()
        lhs = normed[:, pl.ds(pl.multiple_of(kc * kc_size, kc_size), kc_size)]
        for i in range(3):
            part = jnp.dot(lhs, ring[slot, i], preferred_element_type=f32)
            total[i] = jnp.where(kc == 0, part, total[i] + part)

        @pl.when(step + slots < steps)
        def _():
            fetch(step + slots).start()

        @pl.when(kc == kcs - 1)
        def _():
            epilogue(cb)

        return 0

    total[...] = jnp.zeros(total.shape, f32)
    lax.fori_loop(0, steps, step_body, 0)


def front(position, ids2, tokens, gain, weight3, taps, rates, residues, skip):
    T, depth = tokens.shape
    channels, poles = weight3.shape[2], rates.shape[0]
    cb_size, kc_size, slots = 256, 2048, 5
    geometry = (T, depth, channels, cb_size, kc_size, slots, poles)
    kept = [pltpu.VMEM(a.shape, a.dtype) for a in (taps, rates, residues, skip)]
    ids2, tokens, gain, weight3, taps, rates, residues, skip = [
        pltpu.with_memory_space_constraint(a, pltpu.HBM)
        for a in (ids2, tokens, gain, weight3, taps, rates, residues, skip)
    ]
    return pl.pallas_call(
        functools.partial(front_kernel, geometry),
        out_shape=[
            jax.ShapeDtypeStruct((T, channels), f32),
            jax.ShapeDtypeStruct((channels // 128, T, 128), f32),
            jax.ShapeDtypeStruct((poles + HEAD, channels), bf16),
            jax.ShapeDtypeStruct((T, 128), f32),
            jax.ShapeDtypeStruct((T, 128), f32),
        ] + kept,
        in_specs=[smem()] + [hbm()] * 8,
        out_specs=[vmem()] * 9,
        scratch_shapes=[
            pltpu.VMEM(ids2.shape, ids2.dtype),
            pltpu.VMEM(gain.shape, f32),
            pltpu.VMEM((T, depth), bf16),
            pltpu.VMEM((T, depth), bf16),
            pltpu.VMEM((slots, 3, kc_size, cb_size), bf16),
            pltpu.VMEM((3, T, cb_size), f32),
            pltpu.VMEM((3, T + 8, cb_size), f32),
            pltpu.VMEM((HEAD, cb_size), f32),
            pltpu.VMEM((ids2.shape[0] * 128 + 8, 128), f32),
            pltpu.VMEM((T + 8, 128), f32),
            pltpu.VMEM((T, 128), f32),
            pltpu.VMEM((T, 128), f32),
            pltpu.SemaphoreType.DMA((6,)),
            pltpu.SemaphoreType.DMA((4,)),
            pltpu.SemaphoreType.DMA((slots,)),
        ],
        compiler_params=pltpu.CompilerParams(vmem_limit_bytes=28 * MIB),
        name="front",
    )(position, ids2, tokens, gain, weight3, taps, rates, residues, skip)


def expm1(x):
    series = jnp.ones_like(x)
    for k in range(9, 1, -1):
        series = 1.0 + series * x * (1.0 / k)
    return jnp.where(jnp.abs(x) < 0.5, x * series, jnp.exp(x) - 1.0)


def local_kernel(
    poles, first, slot, lane_position, prod_ref, keep_ref, rates_ref, residues_ref, skip_ref, out_ref, _,
    local_out, state_out, pole_out, window_out, sem,
):
    copy = columns(lane_position[0], slot, out_ref, window_out, sem)
    copy.start()
    tiles, T, _ = local_out.shape
    run = T // PARTS
    mine = slice(first * 128, (first + tiles) * 128)
    pole_out[...] = residues_ref[:, mine] * jnp.sqrt(-expm1(-2.0 * rates_ref[:, mine]))

    def tile_body(tile, _):
        lanes = pl.ds(pl.multiple_of((first + tile) * 128, 128), 128)
        d16 = jnp.exp(-rates_ref[:, lanes])
        w16 = pole_out[:, pl.ds(pl.multiple_of(tile * 128, 128), 128)]
        decay = [jnp.broadcast_to(d16[n : n + 1], (8, 128)) for n in range(poles)]
        weight = [jnp.broadcast_to(w16[n : n + 1], (8, 128)) for n in range(poles)]
        skip = skip_ref[0:1, lanes]

        def token(i, states):
            at = pl.ds(i, PARTS, stride=run)
            p, keep = prod_ref[first + tile, at, :], keep_ref[at, :]
            after = [states[n] * decay[n] * keep + p for n in range(poles)]
            local_out[tile, at, :] = tree([skip * p] + [weight[n] * after[n] for n in range(poles)])
            return tuple(after)

        states = lax.fori_loop(0, run, token, tuple(jnp.zeros((8, 128), f32) for _ in range(poles)), unroll=2)
        for n in range(poles):
            state_out[tile, pl.ds(n, PARTS, stride=poles), :] = states[n]
        return 0

    lax.fori_loop(0, tiles, tile_body, 0)
    copy.wait()


def tree(terms):
    while len(terms) > 1:
        terms = [a + b for a, b in zip(terms[0::2], terms[1::2])] + terms[len(terms) // 2 * 2 :]
    return terms[0]


def local_pass(first, tiles, slot, lane_position, product, keep, rates, residues, skip, out_weight, width, after):
    T, poles = product.shape[1], rates.shape[0]
    return pl.pallas_call(
        functools.partial(local_kernel, poles, first, slot),
        out_shape=(
            jax.ShapeDtypeStruct((tiles, T, 128), f32),
            jax.ShapeDtypeStruct((tiles, PARTS * poles, 128), f32),
            jax.ShapeDtypeStruct((poles, tiles * 128), f32),
            jax.ShapeDtypeStruct((out_weight.shape[0], 2 * width), bf16),
        ),
        in_specs=[smem()] + [vmem()] * 5 + [hbm(), pl.BlockSpec(memory_space=pl.ANY)],
        out_specs=[vmem()] * 4,
        scratch_shapes=[pltpu.SemaphoreType.DMA((STREAMS,))],
        compiler_params=pltpu.CompilerParams(vmem_limit_bytes=8 * MIB),
        cost_estimate=pl.CostEstimate(flops=6 * T * poles * tiles * 128, bytes_accessed=8 * MIB, transcendentals=0),
        name="local_pass",
    )(lane_position, product, keep, rates, residues, skip, out_weight, after)


def first_products(first, last, taps, ids_ref, base):
    s01, s0m1 = same_id(ids_ref, base + 1, base), same_id(ids_ref, base, base - 1)
    s0m2, s1m1 = same_id(ids_ref, base, base - 2), same_id(ids_ref, base + 1, base - 1)

    def shift(i):
        near, far = last[i][1:2], last[i][0:1]
        t1, t2 = taps[1][i : i + 1], taps[2][i : i + 1]
        return s0m1 * (t1 * near) + s0m2 * (t2 * far), s1m1 * (t2 * near)

    def plain(i):
        t0, t1 = taps[0][i : i + 1], taps[1][i : i + 1]
        return t0 * first[i][0:1], t0 * first[i][1:2] + s01 * (t1 * first[i][0:1])

    k, v, dk, dv = plain(1), plain(2), shift(1), shift(2)
    delta = [(k[j] + dk[j]) * (v[j] + dv[j]) - k[j] * v[j] for j in range(2)]
    return shift(0), delta


def unpack(block, poles):
    first = [None, block[poles : poles + 2], block[poles + 2 : poles + 4]]
    last = [block[poles + 4 + 2 * i : poles + 6 + 2 * i] for i in range(3)]
    return block[0:poles], first, last


def joined_state(low_state, low_last, up_state, up_first, taps, rates, ids_ref, base, length):
    _, delta = first_products(up_first, low_last, taps, ids_ref, base)
    grown = low_state + delta[0] * jnp.exp(rates) + delta[1] * jnp.exp(2.0 * rates)
    open_ = same_id(ids_ref, base + length - 1, base - 1)
    return up_state + grown * (jnp.exp(-rates * jnp.float32(length)) * open_)


def join_kernel(T, poles, span, position, ids_ref, mine_ref, other_ref, taps_ref, rates_ref, _, out):
    me = position[0]
    is_upper = (me // span) % 2 == 1
    base = (me // (2 * span)) * (2 * span * T) + span * T
    mine, other = mine_ref[...].astype(f32), other_ref[...].astype(f32)
    lower, upper = jnp.where(is_upper, other, mine), jnp.where(is_upper, mine, other)
    taps = [taps_ref[j] for j in range(3)]
    low_state, _, low_last = unpack(lower, poles)
    up_state, up_first, _ = unpack(upper, poles)
    state = joined_state(low_state, low_last, up_state, up_first, taps, rates_ref[...], ids_ref, base, span * T)
    out[0:poles, :] = state.astype(bf16)
    row = lax.broadcasted_iota(jnp.int32, (HEAD, lower.shape[1]), 0)
    out[poles : poles + HEAD, :] = jnp.where(row < 4, lower[poles:], upper[poles:]).astype(bf16)


def join(span, T, position, ids, mine, other, taps, rates, after):
    poles = rates.shape[0]
    return pl.pallas_call(
        functools.partial(join_kernel, T, poles, span),
        out_shape=jax.ShapeDtypeStruct(mine.shape, bf16),
        in_specs=[smem(), smem()] + [vmem()] * 4 + [pl.BlockSpec(memory_space=pl.ANY)],
        out_specs=vmem(),
        compiler_params=pltpu.CompilerParams(vmem_limit_bytes=4 * MIB),
        name="join",
    )(position, ids, mine, other, taps, rates, after)


def gate_kernel(
    T, poles, spans, cuts, position, lane_position, ids_ref, query_ref, block_ref, visible_ref, taps_ref, rates_ref, skip_ref,
    window_ref, out_ref, *rest,
):
    arrived, rest = rest[: len(spans)], rest[len(spans) :]
    parts, rest = [rest[3 * c : 3 * c + 3] for c in range(cuts)], rest[3 * cuts :]
    gated_out, send_out, mine_out, third_out, carry, full, sem = rest
    run = T // PARTS
    tiles = query_ref.shape[1] // 128
    copy = columns(lane_position[0], 2, out_ref, third_out, sem)
    copy.start()
    me = position[0]
    base = me * T
    taps = [taps_ref[j] for j in range(3)]
    rates, skip = rates_ref[...], skip_ref[...]
    weight = jnp.concatenate([pole_ref[...] for _, _, pole_ref in parts], axis=1)
    each = tiles // cuts
    prior = jnp.zeros(block_ref.shape, f32)
    prior_state, prior_first, prior_last = unpack(prior, poles)
    for span, ref in zip(spans, arrived):
        state, first, last = unpack(ref[...].astype(f32), poles)
        upper, held = (me // span) % 2 == 1, me % span
        if span == 1:
            both = state
        else:
            both = joined_state(
                state, last, prior_state, prior_first, taps, rates, ids_ref, (me - held) * T, held * T)
        fresh = upper & (held == 0)
        prior_state = jnp.where(fresh, state, jnp.where(upper, both, prior_state))
        prior_first = [None] + [jnp.where(upper, first[i], prior_first[i]) for i in (1, 2)]
        prior_last = [jnp.where(fresh, last[i], prior_last[i]) for i in range(3)]
    _, first, _ = unpack(block_ref[...].astype(f32), poles)
    q_shift, delta = first_products(first, prior_last, taps, ids_ref, base)
    second = delta[1] * jnp.exp(rates)
    now = prior_state + (delta[0] + second) * jnp.exp(rates)
    fix0 = skip * delta[0] - jnp.sum(weight * second, axis=0, keepdims=True)
    fix1 = skip * delta[1]
    jump = jnp.exp(-rates * float(run))
    for s in range(PARTS):
        part = slice(s * poles, (s + 1) * poles)
        began = weight * now
        for tile in range(tiles):
            carry[tile, part, :] = began[:, tile * 128 : tile * 128 + 128]
        if s < PARTS - 1:
            whole = same_id(ids_ref, base + s * run + run - 1, base + s * run - 1)
            ends = jnp.concatenate([parts[tile // each][1][tile % each, part, :] for tile in range(tiles)], axis=1)
            now = now * (jump * whole) + ends

    def lane_body(cut, inner, _):
        tile = cut * each + inner
        lanes = pl.ds(pl.multiple_of(tile * 128, 128), 128)
        d16 = jnp.exp(-rates_ref[:, lanes])
        decay = [jnp.broadcast_to(d16[n : n + 1], (8, 128)) for n in range(poles)]
        start = tuple(carry[tile, pl.ds(n, PARTS, stride=poles), :] for n in range(poles))

        def token(i, states):
            after = [states[n] * decay[n] for n in range(poles)]
            see = visible_ref[pl.ds(pl.multiple_of(i * 8, 8), 8), :]
            at = pl.ds(i, PARTS, stride=run)
            full[tile, at, :] = parts[cut][0][inner, at, :] + see * tree(list(after))
            return tuple(after)

        lax.fori_loop(0, run, token, start, unroll=4)
        return 0

    for cut in range(cuts):
        lax.fori_loop(0, each, functools.partial(lane_body, cut), 0)
    row = lax.broadcasted_iota(jnp.int32, (16, 128), 0)
    for tile in range(tiles):
        lanes = slice(tile * 128, tile * 128 + 128)
        gated_out[:, lanes] = (query_ref[:, lanes] * full[tile]).astype(bf16)
        top_q, top = query_ref[0:16, lanes], full[tile, 0:16, :]
        top_q = top_q + jnp.where(row == 0, q_shift[0][:, lanes], 0.0) + jnp.where(row == 1, q_shift[1][:, lanes], 0.0)
        top = top + jnp.where(row == 0, fix0[:, lanes], 0.0) + jnp.where(row == 1, fix1[:, lanes], 0.0)
        gated_out[0:16, lanes] = (top_q * top).astype(bf16)
    share(lane_position[0], gated_out, window_ref, send_out, mine_out)
    copy.wait()


def target(index, slot):
    chip = index // 2
    if slot == 0:
        return 3 - 3 * (chip % 2)
    if slot == 1:
        return jnp.where(chip < 2, 2, 1)
    if slot == 2:
        return jnp.where(chip < 2, 1 + 2 * chip, 2 * (chip - 2))
    return chip


class Copies:
    def __init__(self, copies):
        self.copies = copies

    def start(self):
        for copy in self.copies:
            copy.start()

    def wait(self):
        for copy in self.copies:
            copy.wait()


STREAMS = 4


def columns(index, slot, out_ref, window, sem):
    channels, both = window.shape
    start = pl.multiple_of(target(index, slot) * both, both)
    each = channels // STREAMS
    return Copies([
        pltpu.make_async_copy(
            out_ref.at[pl.ds(k * each, each), pl.ds(start, both)], window.at[pl.ds(k * each, each)], sem.at[k])
        for k in range(STREAMS)
    ])


def share(index, gated_ref, window, send_out, mine_out):
    width = send_out.shape[1]
    tile = 256
    core = index % 2

    for j in range(width // tile):
        at = slice(j * tile, j * tile + tile)
        for out, half in ((send_out, 1 - core), (mine_out, core)):
            cols = pl.ds(pl.multiple_of(half * width + j * tile, tile), tile)
            out[:, at] = jnp.dot(gated_ref[...], window[:, cols], preferred_element_type=f32).astype(out.dtype)


def share_kernel(count, lane_position, gated_ref, *rest):
    windows, outs = rest[:count], rest[count:]
    for k, window in enumerate(windows):
        share(lane_position[0], gated_ref, window, outs[2 * k], outs[2 * k + 1])


def shares(lane_position, gated, windows, width):
    T, channels = gated.shape
    count = len(windows)
    return pl.pallas_call(
        functools.partial(share_kernel, count),
        out_shape=[jax.ShapeDtypeStruct((T, width), d) for _ in windows for d in (bf16, f32)],
        in_specs=[smem(), vmem()] + [vmem()] * count,
        out_specs=[vmem()] * (2 * count),
        compiler_params=pltpu.CompilerParams(vmem_limit_bytes=4 * MIB),
        cost_estimate=pl.CostEstimate(
            flops=4 * T * channels * width * count, bytes_accessed=4 * channels * width * count, transcendentals=0),
        name="shares",
    )(lane_position, gated, *windows)


def late_share_kernel(slot, lane_position, gated_ref, out_ref, send_out, mine_out, window, sem):
    copy = columns(lane_position[0], slot, out_ref, window, sem)
    copy.start()
    copy.wait()
    share(lane_position[0], gated_ref, window, send_out, mine_out)


def late_share(slot, lane_position, gated, out_weight, width):
    T, channels = gated.shape
    return pl.pallas_call(
        functools.partial(late_share_kernel, slot),
        out_shape=[jax.ShapeDtypeStruct((T, width), d) for d in (bf16, f32)],
        in_specs=[smem(), vmem(), hbm()],
        out_specs=[vmem()] * 2,
        scratch_shapes=[pltpu.VMEM((channels, 2 * width), bf16), pltpu.SemaphoreType.DMA((STREAMS,))],
        compiler_params=pltpu.CompilerParams(vmem_limit_bytes=6 * MIB),
        cost_estimate=pl.CostEstimate(
            flops=4 * T * channels * width, bytes_accessed=4 * channels * width, transcendentals=0),
        name="late_share",
    )(lane_position, gated, out_weight)


def gate(T, spans, arrived, position, lane_position, ids, query, parts, block, visible, taps, rates, skip, window, out_weight, width):
    poles, channels = rates.shape
    return pl.pallas_call(
        functools.partial(gate_kernel, T, poles, tuple(spans), len(parts)),
        out_shape=[
            jax.ShapeDtypeStruct(query.shape, bf16),
            jax.ShapeDtypeStruct((T, width), bf16),
            jax.ShapeDtypeStruct((T, width), f32),
            pltpu.VMEM(window.shape, bf16),
        ],
        in_specs=[smem()] * 3 + [vmem()] * 7 + [hbm()] + [vmem()] * (len(spans) + 3 * len(parts)),
        out_specs=[vmem()] * 4,
        scratch_shapes=[
            pltpu.VMEM((channels // 128, PARTS * poles, 128), f32),
            pltpu.VMEM((channels // 128, T, 128), f32),
            pltpu.SemaphoreType.DMA((STREAMS,)),
        ],
        compiler_params=pltpu.CompilerParams(vmem_limit_bytes=8 * MIB),
        name="gate",
    )(position, lane_position, ids, query, block, visible, taps, rates, skip, window, out_weight, *arrived,
      *[a for part in parts for a in part])


def total(*terms):
    return functools.reduce(lambda a, b: a + b, [t.astype(f32) for t in terms]).astype(bf16)


def merge_kernel(count, has_inner, lane_position, *rest):
    terms, picks, out = rest[:count], rest[count:-1], rest[-1]
    value = terms[0][...].astype(f32)
    for term in terms[1:]:
        value = value + term[...].astype(f32)
    chip = lane_position[0] // 2
    inner = (chip == 1) | (chip == 2)
    for pick, wanted in zip(picks, (inner, jnp.logical_not(inner)) if has_inner else (jnp.logical_not(inner),)):
        value = value + jnp.where(wanted, pick[...].astype(f32), 0.0)
    out[...] = value.astype(out.dtype)


def merge(lane_position, dtype, terms, inner=None, outer=None):
    picks = [a for a in (inner, outer) if a is not None]
    terms = [pltpu.with_memory_space_constraint(a, pltpu.VMEM) for a in (*terms, *picks)]
    return pl.pallas_call(
        functools.partial(merge_kernel, len(terms) - len(picks), inner is not None),
        out_shape=jax.ShapeDtypeStruct(terms[0].shape, dtype),
        in_specs=[smem()] + [vmem()] * len(terms),
        out_specs=vmem(),
        compiler_params=pltpu.CompilerParams(vmem_limit_bytes=3 * MIB),
        name="merge",
    )(lane_position, *terms)


def scatter_line(lane_position, gated, send, mine, window, third, out_weight, width):
    pair = [(m, m ^ 1) for m in range(8)]

    def along(hops):
        return [(a * 2 + c, b * 2 + c) for a, b in hops for c in range(2)]

    near = along([(0, 1), (1, 0), (2, 3), (3, 2)])
    traded = lax.ppermute(send, "mp", pair)
    far = merge(lane_position, bf16, (mine, traded))
    from_near = lax.ppermute(far, "mp", near)
    send, mine = shares(lane_position, gated, [window], width)
    second = merge(lane_position, bf16, (mine, lax.ppermute(send, "mp", pair)))
    from_middle = lax.ppermute(second, "mp", along([(1, 2), (2, 1)]))
    from_end = lax.ppermute(second, "mp", along([(0, 2), (3, 1)]))
    send2, mine2 = shares(lane_position, gated, [third], width)
    mine2 = merge(lane_position, f32, (mine2, lax.ppermute(send2, "mp", pair)))
    onward = merge(lane_position, bf16, (mine2,), inner=from_near)
    from_round = lax.ppermute(onward, "mp", along([(0, 1), (1, 3), (3, 2), (2, 0)]))
    send3, mine3 = late_share(3, lane_position, gated, out_weight, width)
    own = merge(lane_position, f32, (mine3, lax.ppermute(send3, "mp", pair), from_middle, from_end), outer=from_near)
    return total(own, from_round)


def shifted(value, axis, steps):
    count = lax.axis_size(axis)
    leading, last = (max(0, -steps), min(count, count - steps))
    return lax.ppermute(value, axis, [(source, source + steps) for source in range(leading, last)])


def project(block, norm_gain, weights):
    floats = block.astype(jnp.float32)
    mean_square = jnp.mean(floats * floats, axis=-1, keepdims=True)
    normed = (floats * lax.rsqrt(mean_square + epsilon) * norm_gain[None, :]).astype(jnp.bfloat16)
    return jnp.dot(normed, weights, preferred_element_type=jnp.float32).astype(jnp.bfloat16)


def general(
    tokens, norm_gain, in_weight, short_filter, rates, residues, skip, out_weight, segment_ids
):
    tok_rows = tokens.shape[0]
    model_width = tokens.shape[1]
    channels = in_weight.shape[2]
    filter_taps = short_filter.shape[0]
    pole_count = rates.shape[0]
    device_index = lax.axis_index("ctx")
    row_offset = device_index * tok_rows
    weights = in_weight.reshape(model_width, 3 * channels)
    projected = project(tokens, norm_gain, weights)
    previous = shifted(projected[tok_rows - (filter_taps - 1) :], "ctx", 1)
    extended = jnp.concatenate([previous, projected], axis=0)
    padded_ids = jnp.concatenate([jnp.full((filter_taps,), -1, jnp.int32), segment_ids], axis=0)
    window = lax.dynamic_slice_in_dim(padded_ids, row_offset, tok_rows + filter_taps, 0)
    local_ids = window[filter_taps:]
    taps_table = short_filter.reshape(filter_taps, 3 * channels)
    featured = jnp.zeros((tok_rows, 3 * channels), jnp.float32)
    for lag_index in range(filter_taps):
        begin = filter_taps - 1 - lag_index
        lagged = extended[begin : begin + tok_rows].astype(jnp.float32)
        matches = window[filter_taps - lag_index : filter_taps - lag_index + tok_rows] == local_ids
        term = taps_table[lag_index][None, :] * lagged
        featured = featured + jnp.where(matches[:, None], term, jnp.zeros_like(term))
    query_part = featured[:, :channels]
    key_part = featured[:, channels : 2 * channels]
    value_part = featured[:, 2 * channels :]
    product = key_part * value_part
    offsets = jnp.arange(tok_rows, dtype=jnp.float32)
    center = float(tok_rows // 2)
    growth = jnp.exp(-(offsets - center)[:, None, None] * rates[None])
    shrinkage = jnp.exp((offsets - center)[:, None, None] * rates[None])
    weighted = (shrinkage * product[:, None, :]).reshape(tok_rows, pole_count * channels)
    visible = (offsets[:, None] >= offsets[None, :]) & (local_ids[:, None] == local_ids[None, :])
    in_block = jnp.dot(visible.astype(jnp.float32), weighted, precision=lax.Precision.HIGHEST)
    in_block = in_block.reshape(tok_rows, pole_count, channels) * growth
    survives = local_ids == window[filter_taps - 1]
    block_factor = jnp.exp(-rates * tok_rows)
    block_end = in_block[tok_rows - 1]
    block_ends = lax.all_gather(block_end[None], "ctx", axis=0, tiled=True)
    shard_count = segment_ids.shape[0] // tok_rows
    last_ids = segment_ids.reshape(shard_count, tok_rows)[:, tok_rows - 1]
    prior_ids = jnp.concatenate([jnp.full((1,), -1, jnp.int32), last_ids[:-1]], axis=0)
    shard_decays = block_factor[None] * (last_ids == prior_ids).astype(jnp.float32)[:, None, None]

    def absorb(running, inputs):
        shard, factor, shard_end = inputs
        advanced = running * factor + shard_end
        return (jnp.where(shard < device_index, advanced, running), None)

    incoming, _ = lax.scan(
        absorb,
        jnp.zeros_like(block_end),
        (jnp.arange(shard_count, dtype=jnp.int32), shard_decays, block_ends),
    )
    carried = incoming[None] * jnp.exp(-(offsets + 1.0)[:, None, None] * rates[None])
    carried = carried * survives.astype(jnp.float32)[:, None, None]
    states = in_block + carried
    pole_weight = residues * jnp.sqrt(-jnp.expm1(-2.0 * rates))
    longconv = jnp.sum(pole_weight[None] * states, axis=1)
    gated = (query_part * (longconv + skip[None, :] * product)).astype(jnp.bfloat16)
    partial_terms = jnp.dot(gated, out_weight, preferred_element_type=jnp.float32)
    return lax.psum_scatter(partial_terms, "mp", scatter_dimension=1, tiled=True).astype(
        jnp.bfloat16
    )


def local(tokens, norm_gain, in_weight, short_filter, rates, residues, skip, out_weight, segment_ids):
    T = tokens.shape[0]
    shards = lax.axis_size("ctx")
    me = lax.axis_index("ctx")
    position = me.astype(jnp.int32)[None]
    lane_position = lax.axis_index("mp").astype(jnp.int32)[None]
    width = out_weight.shape[1] // lax.axis_size("mp")
    weight3 = jnp.transpose(in_weight, (1, 0, 2))
    out_weight = pltpu.with_memory_space_constraint(out_weight, pltpu.HBM)
    query, product, block, keep, visible, taps, rates, residues, skip = front(
        position, segment_ids.reshape(-1, 128), tokens, norm_gain[None], weight3, short_filter, rates, residues, skip[None])
    cuts = shards.bit_length() - 1
    each = product.shape[0] // cuts
    group, spans, arrived, parts, windows = block, [], [], [], []
    for k in range(cuts):
        span = 1 << k
        other = lax.ppermute(group, "ctx", [(a, a ^ span) for a in range(shards)])
        spans.append(span)
        arrived.append(other)
        *part, window = local_pass(
            k * each, each, min(k, 1), lane_position, product, keep, rates, residues, skip, out_weight, width, group)
        parts.append(part)
        windows.append(window)
        if k < cuts - 1:
            group = join(span, T, position, segment_ids, group, other, taps, rates, part[0])
    gated, send, mine, third = gate(T, spans, arrived, position, lane_position, segment_ids, query, parts, block, visible, taps, rates,
                             skip, windows[0], out_weight, width)
    return scatter_line(lane_position, gated, send, mine, windows[1], third, out_weight, width)


def solution(mesh):
    placed = (
        P("ctx", None),
        P(),
        P(None, None, "mp"),
        P(None, None, "mp"),
        P(None, "mp"),
        P(None, "mp"),
        P("mp"),
        P("mp", None),
        P(),
    )
    shards, groups = mesh.shape["ctx"], mesh.shape["mp"]

    def body(tokens, norm_gain, in_weight, *rest):
        suits = groups == 8 and shards & (shards - 1) == 0 and shards > 2
        suits = suits and in_weight.shape[2] % 512 == 0 and in_weight.shape[0] % 2048 == 0
        suits = suits and tokens.shape[0] % 64 == 0 and rest[-1].shape[0] % 128 == 0 and rest[1].shape[0] % 8 == 0
        return (local if suits else general)(tokens, norm_gain, in_weight, *rest)

    return jax.shard_map(
        body, mesh=mesh, in_specs=placed, out_specs=P("ctx", "mp"), check_vma=False
    )
```

```python
import functools
import jax
import jax.numpy as jnp
from jax import lax
from jax.experimental import pallas as pl
from jax.experimental.pallas import tpu as pltpu
from jax.sharding import PartitionSpec as P

epsilon = 1e-06
f32 = jnp.float32
bf16 = jnp.bfloat16

PARTS = 8
HEAD = 16
MIB = 1 << 20


def vmem():
    return pl.BlockSpec(memory_space=pltpu.VMEM)


def smem():
    return pl.BlockSpec(memory_space=pltpu.SMEM)


def same_id(ids_ref, a, b):
    def get(t):
        return jnp.where(t < 0, -1, ids_ref[jnp.maximum(t, 0)])

    return (get(a) == get(b)).astype(f32)


def hbm():
    return pl.BlockSpec(memory_space=pltpu.HBM)


def front_kernel(
    geometry, position, ids_ref, tokens_ref, gain_ref, weight_ref, taps_ref, rates_ref, residues_ref, skip_ref,
    raw_out, prod_out, block_out, keep_out, twice, visible_out, taps, rates, residues, skip,
    ids, gain, tok, normed, ring, total, proj, head, idcol, near, ending, sem, tok_sem, ring_sem,
):
    T, depth, channels, cb_size, kc_size, slots, poles = geometry
    run = T // PARTS
    kcs, cbs = depth // kc_size, channels // cb_size
    steps = kcs * cbs
    base = pl.multiple_of(position[0] * T, 8)

    def fetch(step):
        cb, kc, slot = step // kcs, step % kcs, step % slots
        return pltpu.make_async_copy(
            weight_ref.at[:, pl.ds(pl.multiple_of(kc * kc_size, kc_size), kc_size),
                          pl.ds(pl.multiple_of(cb * cb_size, cb_size), cb_size)],
            ring.at[slot], ring_sem.at[slot])

    small = [
        pltpu.make_async_copy(a, b, sem.at[i])
        for i, (a, b) in enumerate(
            ((ids_ref, ids), (gain_ref, gain), (taps_ref, taps), (rates_ref, rates), (residues_ref, residues),
             (skip_ref, skip)))
    ]
    small[0].start()
    small[1].start()
    chunk = T // 4
    tok_copies = [
        pltpu.make_async_copy(tokens_ref.at[pl.ds(c * chunk, chunk)], tok.at[pl.ds(c * chunk, chunk)], tok_sem.at[c])
        for c in range(4)
    ]
    for copy in tok_copies:
        copy.start()
    for copy in small[2:]:
        copy.start()
    for s in range(min(slots, steps)):
        fetch(s).start()

    small[0].wait()
    idcol[0:8, :] = jnp.full((8, 128), -1.0, f32)
    for b in range(ids.shape[0]):
        row = ids[b : b + 1, :].astype(f32)
        idcol[8 + b * 128 : 8 + (b + 1) * 128, :] = jnp.broadcast_to(row, (128, 128)).T
    near[...] = idcol[pl.ds(base, T + 8), :]
    here = near[8 : 8 + T, :]
    keep_out[...] = (here == near[7 : 7 + T, :]).astype(f32)
    twice[...] = (here == near[6 : 6 + T, :]).astype(f32)
    ending[...] = (here == near[7 + T : 8 + T, :]).astype(f32)
    before = near[pl.ds(7, PARTS, stride=run), :]
    for i in range(run):
        visible_out[i * 8 : (i + 1) * 8, :] = (near[pl.ds(8 + i, PARTS, stride=run), :] == before).astype(f32)
    for i in range(2):
        proj[i, 0:8, :] = jnp.zeros((8, cb_size), f32)
    raw_out[0:8, :] = jnp.zeros((8, channels), f32)
    head[...] = jnp.zeros(head.shape, f32)
    small[1].wait()

    def norm_rows(g, _):
        part = pl.ds(pl.multiple_of(g * 16, 16), 16)
        x = tok[part, :].astype(f32)
        scale = lax.rsqrt(jnp.sum(x * x, axis=-1, keepdims=True) * (1.0 / depth) + epsilon)
        normed[part, :] = (x * scale * gain[...]).astype(bf16)
        return 0

    for c, copy in enumerate(tok_copies):
        copy.wait()
        lax.fori_loop(c * chunk // 16, (c + 1) * chunk // 16, norm_rows, 0)
    for copy in small[2:]:
        copy.wait()

    def epilogue(cb):
        cols = pl.ds(pl.multiple_of(cb * cb_size, cb_size), cb_size)
        feats = []
        m1 = jnp.concatenate([keep_out[...]] * (cb_size // 128), axis=1)
        m2 = jnp.concatenate([twice[...]] * (cb_size // 128), axis=1)
        query = total[0].astype(bf16).astype(f32)
        raw_out[8 : 8 + T, cols] = query
        head[4:6, :] = query[T - 2 : T]
        for i in range(2):
            p = total[i + 1].astype(bf16).astype(f32)
            proj[i, 8 : 8 + T, :] = p
            tap = [taps[j, i + 1 : i + 2, cols] for j in range(3)]
            feats.append(
                tap[0] * p + m1 * (tap[1] * proj[i, 7 : 7 + T, :]) + m2 * (tap[2] * proj[i, 6 : 6 + T, :]))
            head[2 * i : 2 * i + 2, :] = proj[i, 8:10, :]
            head[6 + 2 * i : 8 + 2 * i, :] = proj[i, 6 + T : 8 + T, :]
        block_out[poles : poles + HEAD, cols] = head[...].astype(bf16)
        product = feats[0] * feats[1]
        back = 7.0 - lax.broadcasted_iota(jnp.int32, (8, 128), 0).astype(f32)
        for lane in range(cb_size // 128):
            tile = cb * (cb_size // 128) + lane
            lanes = pl.ds(pl.multiple_of(tile * 128, 128), 128)
            prod_out[tile] = product[:, lane * 128 : lane * 128 + 128]
            r16 = rates[:, lanes]
            jump = jnp.exp(-8.0 * r16)
            leap = [jnp.broadcast_to(jump[n : n + 1], (8, 128)) for n in range(poles)]

            def eight(g, sums):
                part = pl.ds(pl.multiple_of(g * 8, 8), 8)
                p = prod_out[tile, part, :] * ending[part, :]
                return tuple(sums[n] * leap[n] + p for n in range(poles))

            sums = lax.fori_loop(
                0, T // 8, eight, tuple(jnp.zeros((8, 128), f32) for _ in range(poles)), unroll=4)
            ends = [
                jnp.sum(sums[n] * jnp.exp(-back * r16[n : n + 1]), axis=0, keepdims=True) for n in range(poles)
            ]
            block_out[0:poles, lanes] = jnp.concatenate(ends, axis=0).astype(bf16)

    def step_body(step, _):
        cb, kc, slot = step // kcs, step % kcs, step % slots
        fetch(step).wait()
        lhs = normed[:, pl.ds(pl.multiple_of(kc * kc_size, kc_size), kc_size)]
        for i in range(3):
            part = jnp.dot(lhs, ring[slot, i], preferred_element_type=f32)
            total[i] = jnp.where(kc == 0, part, total[i] + part)

        @pl.when(step + slots < steps)
        def _():
            fetch(step + slots).start()

        @pl.when(kc == kcs - 1)
        def _():
            epilogue(cb)

        return 0

    total[...] = jnp.zeros(total.shape, f32)
    lax.fori_loop(0, steps, step_body, 0)


def front(position, ids2, tokens, gain, weight3, taps, rates, residues, skip):
    T, depth = tokens.shape
    channels, poles = weight3.shape[2], rates.shape[0]
    cb_size, kc_size, slots = 256, 2048, 5
    geometry = (T, depth, channels, cb_size, kc_size, slots, poles)
    kept = [pltpu.VMEM(a.shape, a.dtype) for a in (taps, rates, residues, skip)]
    ids2, tokens, gain, weight3, taps, rates, residues, skip = [
        pltpu.with_memory_space_constraint(a, pltpu.HBM)
        for a in (ids2, tokens, gain, weight3, taps, rates, residues, skip)
    ]
    return pl.pallas_call(
        functools.partial(front_kernel, geometry),
        out_shape=[
            jax.ShapeDtypeStruct((T + 8, channels), f32),
            jax.ShapeDtypeStruct((channels // 128, T, 128), f32),
            jax.ShapeDtypeStruct((poles + HEAD, channels), bf16),
            jax.ShapeDtypeStruct((T, 128), f32),
            jax.ShapeDtypeStruct((T, 128), f32),
            jax.ShapeDtypeStruct((T, 128), f32),
        ] + kept,
        in_specs=[smem()] + [hbm()] * 8,
        out_specs=[vmem()] * 10,
        scratch_shapes=[
            pltpu.VMEM(ids2.shape, ids2.dtype),
            pltpu.VMEM(gain.shape, f32),
            pltpu.VMEM((T, depth), bf16),
            pltpu.VMEM((T, depth), bf16),
            pltpu.VMEM((slots, 3, kc_size, cb_size), bf16),
            pltpu.VMEM((3, T, cb_size), f32),
            pltpu.VMEM((2, T + 8, cb_size), f32),
            pltpu.VMEM((HEAD, cb_size), f32),
            pltpu.VMEM((ids2.shape[0] * 128 + 8, 128), f32),
            pltpu.VMEM((T + 8, 128), f32),
            pltpu.VMEM((T, 128), f32),
            pltpu.SemaphoreType.DMA((6,)),
            pltpu.SemaphoreType.DMA((4,)),
            pltpu.SemaphoreType.DMA((slots,)),
        ],
        compiler_params=pltpu.CompilerParams(vmem_limit_bytes=28 * MIB),
        name="front",
    )(position, ids2, tokens, gain, weight3, taps, rates, residues, skip)


def expm1(x):
    series = jnp.ones_like(x)
    for k in range(9, 1, -1):
        series = 1.0 + series * x * (1.0 / k)
    return jnp.where(jnp.abs(x) < 0.5, x * series, jnp.exp(x) - 1.0)


def local_kernel(
    poles, first, slot, lane_position, prod_ref, keep_ref, twice_ref, raw_ref, taps_ref, rates_ref, residues_ref, skip_ref,
    out_ref, _, local_out, state_out, pole_out, query_out, window_out, sem,
):
    copy = columns(lane_position[0], slot, out_ref, window_out, sem)
    copy.start()
    tiles, T, _ = local_out.shape
    run = T // PARTS
    mine = slice(first * 128, (first + tiles) * 128)
    pole_out[...] = residues_ref[:, mine] * jnp.sqrt(-expm1(-2.0 * rates_ref[:, mine]))

    def tile_body(tile, _):
        lanes = pl.ds(pl.multiple_of((first + tile) * 128, 128), 128)
        d16 = jnp.exp(-rates_ref[:, lanes])
        w16 = pole_out[:, pl.ds(pl.multiple_of(tile * 128, 128), 128)]
        decay = [jnp.broadcast_to(d16[n : n + 1], (8, 128)) for n in range(poles)]
        weight = [jnp.broadcast_to(w16[n : n + 1], (8, 128)) for n in range(poles)]
        skip = skip_ref[0:1, lanes]

        def token(i, states):
            at = pl.ds(i, PARTS, stride=run)
            p, keep = prod_ref[first + tile, at, :], keep_ref[at, :]
            after = [states[n] * decay[n] * keep + p for n in range(poles)]
            local_out[tile, at, :] = tree([skip * p] + [weight[n] * after[n] for n in range(poles)])
            return tuple(after)

        states = lax.fori_loop(0, run, token, tuple(jnp.zeros((8, 128), f32) for _ in range(poles)), unroll=2)
        for n in range(poles):
            state_out[tile, pl.ds(n, PARTS, stride=poles), :] = states[n]
        tap = [taps_ref[j, 0:1, lanes] for j in range(3)]
        query_out[tile] = (
            tap[0] * raw_ref[8 : 8 + T, lanes]
            + keep_ref[...] * (tap[1] * raw_ref[7 : 7 + T, lanes])
            + twice_ref[...] * (tap[2] * raw_ref[6 : 6 + T, lanes]))
        return 0

    lax.fori_loop(0, tiles, tile_body, 0)
    copy.wait()


def tree(terms):
    while len(terms) > 1:
        terms = [a + b for a, b in zip(terms[0::2], terms[1::2])] + terms[len(terms) // 2 * 2 :]
    return terms[0]


def local_pass(
    first, tiles, slot, lane_position, product, keep, twice, raw, taps, rates, residues, skip, out_weight, width, after,
):
    T, poles = product.shape[1], rates.shape[0]
    return pl.pallas_call(
        functools.partial(local_kernel, poles, first, slot),
        out_shape=(
            jax.ShapeDtypeStruct((tiles, T, 128), f32),
            jax.ShapeDtypeStruct((tiles, PARTS * poles, 128), f32),
            jax.ShapeDtypeStruct((poles, tiles * 128), f32),
            jax.ShapeDtypeStruct((tiles, T, 128), f32),
            jax.ShapeDtypeStruct((out_weight.shape[0], 2 * width), bf16),
        ),
        in_specs=[smem()] + [vmem()] * 8 + [hbm(), pl.BlockSpec(memory_space=pl.ANY)],
        out_specs=[vmem()] * 5,
        scratch_shapes=[pltpu.SemaphoreType.DMA((STREAMS,))],
        compiler_params=pltpu.CompilerParams(vmem_limit_bytes=8 * MIB),
        cost_estimate=pl.CostEstimate(flops=6 * T * poles * tiles * 128, bytes_accessed=8 * MIB, transcendentals=0),
        name="local_pass",
    )(lane_position, product, keep, twice, raw, taps, rates, residues, skip, out_weight, after)


def first_products(first, last, taps, ids_ref, base):
    s01, s0m1 = same_id(ids_ref, base + 1, base), same_id(ids_ref, base, base - 1)
    s0m2, s1m1 = same_id(ids_ref, base, base - 2), same_id(ids_ref, base + 1, base - 1)

    def shift(i):
        near, far = last[i][1:2], last[i][0:1]
        t1, t2 = taps[1][i : i + 1], taps[2][i : i + 1]
        return s0m1 * (t1 * near) + s0m2 * (t2 * far), s1m1 * (t2 * near)

    def plain(i):
        t0, t1 = taps[0][i : i + 1], taps[1][i : i + 1]
        return t0 * first[i][0:1], t0 * first[i][1:2] + s01 * (t1 * first[i][0:1])

    k, v, dk, dv = plain(1), plain(2), shift(1), shift(2)
    delta = [(k[j] + dk[j]) * (v[j] + dv[j]) - k[j] * v[j] for j in range(2)]
    return shift(0), delta


def unpack(block, poles):
    first = [None, block[poles : poles + 2], block[poles + 2 : poles + 4]]
    last = [block[poles + 4 + 2 * i : poles + 6 + 2 * i] for i in range(3)]
    return block[0:poles], first, last


def joined_state(low_state, low_last, up_state, up_first, taps, rates, ids_ref, base, length):
    _, delta = first_products(up_first, low_last, taps, ids_ref, base)
    grown = low_state + delta[0] * jnp.exp(rates) + delta[1] * jnp.exp(2.0 * rates)
    open_ = same_id(ids_ref, base + length - 1, base - 1)
    return up_state + grown * (jnp.exp(-rates * jnp.float32(length)) * open_)


def join_kernel(T, poles, span, position, ids_ref, mine_ref, other_ref, taps_ref, rates_ref, _, out):
    me = position[0]
    is_upper = (me // span) % 2 == 1
    base = (me // (2 * span)) * (2 * span * T) + span * T
    mine, other = mine_ref[...].astype(f32), other_ref[...].astype(f32)
    lower, upper = jnp.where(is_upper, other, mine), jnp.where(is_upper, mine, other)
    taps = [taps_ref[j] for j in range(3)]
    low_state, _, low_last = unpack(lower, poles)
    up_state, up_first, _ = unpack(upper, poles)
    state = joined_state(low_state, low_last, up_state, up_first, taps, rates_ref[...], ids_ref, base, span * T)
    out[0:poles, :] = state.astype(bf16)
    row = lax.broadcasted_iota(jnp.int32, (HEAD, lower.shape[1]), 0)
    out[poles : poles + HEAD, :] = jnp.where(row < 4, lower[poles:], upper[poles:]).astype(bf16)


def join(span, T, position, ids, mine, other, taps, rates, after):
    poles = rates.shape[0]
    return pl.pallas_call(
        functools.partial(join_kernel, T, poles, span),
        out_shape=jax.ShapeDtypeStruct(mine.shape, bf16),
        in_specs=[smem(), smem()] + [vmem()] * 4 + [pl.BlockSpec(memory_space=pl.ANY)],
        out_specs=vmem(),
        compiler_params=pltpu.CompilerParams(vmem_limit_bytes=4 * MIB),
        name="join",
    )(position, ids, mine, other, taps, rates, after)


def gate_kernel(
    T, poles, spans, cuts, position, lane_position, ids_ref, block_ref, visible_ref, taps_ref, rates_ref, skip_ref,
    window_ref, out_ref, *rest,
):
    arrived, rest = rest[: len(spans)], rest[len(spans) :]
    parts, rest = [rest[4 * c : 4 * c + 4] for c in range(cuts)], rest[4 * cuts :]
    gated_out, send_out, mine_out, third_out, carry, full, sem = rest
    run = T // PARTS
    tiles = block_ref.shape[1] // 128
    copy = columns(lane_position[0], 2, out_ref, third_out, sem)
    copy.start()
    me = position[0]
    base = me * T
    taps = [taps_ref[j] for j in range(3)]
    rates, skip = rates_ref[...], skip_ref[...]
    weight = jnp.concatenate([pole_ref[...] for _, _, pole_ref, _ in parts], axis=1)
    each = tiles // cuts
    prior = jnp.zeros(block_ref.shape, f32)
    prior_state, prior_first, prior_last = unpack(prior, poles)
    for span, ref in zip(spans, arrived):
        state, first, last = unpack(ref[...].astype(f32), poles)
        upper, held = (me // span) % 2 == 1, me % span
        if span == 1:
            both = state
        else:
            both = joined_state(
                state, last, prior_state, prior_first, taps, rates, ids_ref, (me - held) * T, held * T)
        fresh = upper & (held == 0)
        prior_state = jnp.where(fresh, state, jnp.where(upper, both, prior_state))
        prior_first = [None] + [jnp.where(upper, first[i], prior_first[i]) for i in (1, 2)]
        prior_last = [jnp.where(fresh, last[i], prior_last[i]) for i in range(3)]
    _, first, _ = unpack(block_ref[...].astype(f32), poles)
    q_shift, delta = first_products(first, prior_last, taps, ids_ref, base)
    second = delta[1] * jnp.exp(rates)
    now = prior_state + (delta[0] + second) * jnp.exp(rates)
    fix0 = skip * delta[0] - jnp.sum(weight * second, axis=0, keepdims=True)
    fix1 = skip * delta[1]
    jump = jnp.exp(-rates * float(run))
    for s in range(PARTS):
        part = slice(s * poles, (s + 1) * poles)
        began = weight * now
        for tile in range(tiles):
            carry[tile, part, :] = began[:, tile * 128 : tile * 128 + 128]
        if s < PARTS - 1:
            whole = same_id(ids_ref, base + s * run + run - 1, base + s * run - 1)
            ends = jnp.concatenate([parts[tile // each][1][tile % each, part, :] for tile in range(tiles)], axis=1)
            now = now * (jump * whole) + ends

    def lane_body(cut, inner, _):
        tile = cut * each + inner
        lanes = pl.ds(pl.multiple_of(tile * 128, 128), 128)
        d16 = jnp.exp(-rates_ref[:, lanes])
        decay = [jnp.broadcast_to(d16[n : n + 1], (8, 128)) for n in range(poles)]
        start = tuple(carry[tile, pl.ds(n, PARTS, stride=poles), :] for n in range(poles))

        def token(i, states):
            after = [states[n] * decay[n] for n in range(poles)]
            see = visible_ref[pl.ds(pl.multiple_of(i * 8, 8), 8), :]
            at = pl.ds(i, PARTS, stride=run)
            full[tile, at, :] = parts[cut][0][inner, at, :] + see * tree(list(after))
            return tuple(after)

        lax.fori_loop(0, run, token, start, unroll=4)
        return 0

    for cut in range(cuts):
        lax.fori_loop(0, each, functools.partial(lane_body, cut), 0)
    row = lax.broadcasted_iota(jnp.int32, (16, 128), 0)
    for tile in range(tiles):
        lanes = slice(tile * 128, tile * 128 + 128)
        query_ref = parts[tile // each][3].at[tile % each]
        gated_out[:, lanes] = (query_ref[...] * full[tile]).astype(bf16)
        top_q, top = query_ref[0:16, :], full[tile, 0:16, :]
        top_q = top_q + jnp.where(row == 0, q_shift[0][:, lanes], 0.0) + jnp.where(row == 1, q_shift[1][:, lanes], 0.0)
        top = top + jnp.where(row == 0, fix0[:, lanes], 0.0) + jnp.where(row == 1, fix1[:, lanes], 0.0)
        gated_out[0:16, lanes] = (top_q * top).astype(bf16)
    share(lane_position[0], gated_out, window_ref, send_out, mine_out)
    copy.wait()


def target(index, slot):
    chip = index // 2
    if slot == 0:
        return 3 - 3 * (chip % 2)
    if slot == 1:
        return jnp.where(chip < 2, 2, 1)
    if slot == 2:
        return jnp.where(chip < 2, 1 + 2 * chip, 2 * (chip - 2))
    return chip


class Copies:
    def __init__(self, copies):
        self.copies = copies

    def start(self):
        for copy in self.copies:
            copy.start()

    def wait(self):
        for copy in self.copies:
            copy.wait()


STREAMS = 4


def columns(index, slot, out_ref, window, sem):
    channels, both = window.shape
    start = pl.multiple_of(target(index, slot) * both, both)
    each = channels // STREAMS
    return Copies([
        pltpu.make_async_copy(
            out_ref.at[pl.ds(k * each, each), pl.ds(start, both)], window.at[pl.ds(k * each, each)], sem.at[k])
        for k in range(STREAMS)
    ])


def share(index, gated_ref, window, send_out, mine_out):
    width = send_out.shape[1]
    tile = 256
    core = index % 2

    for j in range(width // tile):
        at = slice(j * tile, j * tile + tile)
        for out, half in ((send_out, 1 - core), (mine_out, core)):
            cols = pl.ds(pl.multiple_of(half * width + j * tile, tile), tile)
            out[:, at] = jnp.dot(gated_ref[...], window[:, cols], preferred_element_type=f32).astype(out.dtype)


def share_kernel(count, lane_position, gated_ref, *rest):
    windows, outs = rest[:count], rest[count:]
    for k, window in enumerate(windows):
        share(lane_position[0], gated_ref, window, outs[2 * k], outs[2 * k + 1])


def shares(lane_position, gated, windows, width):
    T, channels = gated.shape
    count = len(windows)
    return pl.pallas_call(
        functools.partial(share_kernel, count),
        out_shape=[jax.ShapeDtypeStruct((T, width), d) for _ in windows for d in (bf16, f32)],
        in_specs=[smem(), vmem()] + [vmem()] * count,
        out_specs=[vmem()] * (2 * count),
        compiler_params=pltpu.CompilerParams(vmem_limit_bytes=4 * MIB),
        cost_estimate=pl.CostEstimate(
            flops=4 * T * channels * width * count, bytes_accessed=4 * channels * width * count, transcendentals=0),
        name="shares",
    )(lane_position, gated, *windows)


def late_share_kernel(slot, lane_position, gated_ref, out_ref, send_out, mine_out, window, sem):
    copy = columns(lane_position[0], slot, out_ref, window, sem)
    copy.start()
    copy.wait()
    share(lane_position[0], gated_ref, window, send_out, mine_out)


def late_share(slot, lane_position, gated, out_weight, width):
    T, channels = gated.shape
    return pl.pallas_call(
        functools.partial(late_share_kernel, slot),
        out_shape=[jax.ShapeDtypeStruct((T, width), d) for d in (bf16, f32)],
        in_specs=[smem(), vmem(), hbm()],
        out_specs=[vmem()] * 2,
        scratch_shapes=[pltpu.VMEM((channels, 2 * width), bf16), pltpu.SemaphoreType.DMA((STREAMS,))],
        compiler_params=pltpu.CompilerParams(vmem_limit_bytes=6 * MIB),
        cost_estimate=pl.CostEstimate(
            flops=4 * T * channels * width, bytes_accessed=4 * channels * width, transcendentals=0),
        name="late_share",
    )(lane_position, gated, out_weight)


def gate(T, spans, arrived, position, lane_position, ids, parts, block, visible, taps, rates, skip, window, out_weight, width):
    poles, channels = rates.shape
    return pl.pallas_call(
        functools.partial(gate_kernel, T, poles, tuple(spans), len(parts)),
        out_shape=[
            jax.ShapeDtypeStruct((T, channels), bf16),
            jax.ShapeDtypeStruct((T, width), bf16),
            jax.ShapeDtypeStruct((T, width), f32),
            pltpu.VMEM(window.shape, bf16),
        ],
        in_specs=[smem()] * 3 + [vmem()] * 6 + [hbm()] + [vmem()] * (len(spans) + 4 * len(parts)),
        out_specs=[vmem()] * 4,
        scratch_shapes=[
            pltpu.VMEM((channels // 128, PARTS * poles, 128), f32),
            pltpu.VMEM((channels // 128, T, 128), f32),
            pltpu.SemaphoreType.DMA((STREAMS,)),
        ],
        compiler_params=pltpu.CompilerParams(vmem_limit_bytes=8 * MIB),
        name="gate",
    )(position, lane_position, ids, block, visible, taps, rates, skip, window, out_weight, *arrived,
      *[a for part in parts for a in part])


def total(*terms):
    return functools.reduce(lambda a, b: a + b, [t.astype(f32) for t in terms]).astype(bf16)


def merge_kernel(count, has_inner, lane_position, *rest):
    terms, picks, out = rest[:count], rest[count:-1], rest[-1]
    value = terms[0][...].astype(f32)
    for term in terms[1:]:
        value = value + term[...].astype(f32)
    chip = lane_position[0] // 2
    inner = (chip == 1) | (chip == 2)
    for pick, wanted in zip(picks, (inner, jnp.logical_not(inner)) if has_inner else (jnp.logical_not(inner),)):
        value = value + jnp.where(wanted, pick[...].astype(f32), 0.0)
    out[...] = value.astype(out.dtype)


def merge(lane_position, dtype, terms, inner=None, outer=None):
    picks = [a for a in (inner, outer) if a is not None]
    terms = [pltpu.with_memory_space_constraint(a, pltpu.VMEM) for a in (*terms, *picks)]
    return pl.pallas_call(
        functools.partial(merge_kernel, len(terms) - len(picks), inner is not None),
        out_shape=jax.ShapeDtypeStruct(terms[0].shape, dtype),
        in_specs=[smem()] + [vmem()] * len(terms),
        out_specs=vmem(),
        compiler_params=pltpu.CompilerParams(vmem_limit_bytes=3 * MIB),
        name="merge",
    )(lane_position, *terms)


def scatter_line(lane_position, gated, send, mine, window, third, out_weight, width):
    pair = [(m, m ^ 1) for m in range(8)]

    def along(hops):
        return [(a * 2 + c, b * 2 + c) for a, b in hops for c in range(2)]

    near = along([(0, 1), (1, 0), (2, 3), (3, 2)])
    traded = lax.ppermute(send, "mp", pair)
    far = merge(lane_position, bf16, (mine, traded))
    from_near = lax.ppermute(far, "mp", near)
    send, mine = shares(lane_position, gated, [window], width)
    second = merge(lane_position, bf16, (mine, lax.ppermute(send, "mp", pair)))
    from_middle = lax.ppermute(second, "mp", along([(1, 2), (2, 1)]))
    from_end = lax.ppermute(second, "mp", along([(0, 2), (3, 1)]))
    send2, mine2 = shares(lane_position, gated, [third], width)
    mine2 = merge(lane_position, f32, (mine2, lax.ppermute(send2, "mp", pair)))
    onward = merge(lane_position, bf16, (mine2,), inner=from_near)
    from_round = lax.ppermute(onward, "mp", along([(0, 1), (1, 3), (3, 2), (2, 0)]))
    send3, mine3 = late_share(3, lane_position, gated, out_weight, width)
    own = merge(lane_position, f32, (mine3, lax.ppermute(send3, "mp", pair), from_middle, from_end), outer=from_near)
    return total(own, from_round)


def shifted(value, axis, steps):
    count = lax.axis_size(axis)
    leading, last = (max(0, -steps), min(count, count - steps))
    return lax.ppermute(value, axis, [(source, source + steps) for source in range(leading, last)])


def project(block, norm_gain, weights):
    floats = block.astype(jnp.float32)
    mean_square = jnp.mean(floats * floats, axis=-1, keepdims=True)
    normed = (floats * lax.rsqrt(mean_square + epsilon) * norm_gain[None, :]).astype(jnp.bfloat16)
    return jnp.dot(normed, weights, preferred_element_type=jnp.float32).astype(jnp.bfloat16)


def general(
    tokens, norm_gain, in_weight, short_filter, rates, residues, skip, out_weight, segment_ids
):
    tok_rows = tokens.shape[0]
    model_width = tokens.shape[1]
    channels = in_weight.shape[2]
    filter_taps = short_filter.shape[0]
    pole_count = rates.shape[0]
    device_index = lax.axis_index("ctx")
    row_offset = device_index * tok_rows
    weights = in_weight.reshape(model_width, 3 * channels)
    projected = project(tokens, norm_gain, weights)
    previous = shifted(projected[tok_rows - (filter_taps - 1) :], "ctx", 1)
    extended = jnp.concatenate([previous, projected], axis=0)
    padded_ids = jnp.concatenate([jnp.full((filter_taps,), -1, jnp.int32), segment_ids], axis=0)
    window = lax.dynamic_slice_in_dim(padded_ids, row_offset, tok_rows + filter_taps, 0)
    local_ids = window[filter_taps:]
    taps_table = short_filter.reshape(filter_taps, 3 * channels)
    featured = jnp.zeros((tok_rows, 3 * channels), jnp.float32)
    for lag_index in range(filter_taps):
        begin = filter_taps - 1 - lag_index
        lagged = extended[begin : begin + tok_rows].astype(jnp.float32)
        matches = window[filter_taps - lag_index : filter_taps - lag_index + tok_rows] == local_ids
        term = taps_table[lag_index][None, :] * lagged
        featured = featured + jnp.where(matches[:, None], term, jnp.zeros_like(term))
    query_part = featured[:, :channels]
    key_part = featured[:, channels : 2 * channels]
    value_part = featured[:, 2 * channels :]
    product = key_part * value_part
    offsets = jnp.arange(tok_rows, dtype=jnp.float32)
    center = float(tok_rows // 2)
    growth = jnp.exp(-(offsets - center)[:, None, None] * rates[None])
    shrinkage = jnp.exp((offsets - center)[:, None, None] * rates[None])
    weighted = (shrinkage * product[:, None, :]).reshape(tok_rows, pole_count * channels)
    visible = (offsets[:, None] >= offsets[None, :]) & (local_ids[:, None] == local_ids[None, :])
    in_block = jnp.dot(visible.astype(jnp.float32), weighted, precision=lax.Precision.HIGHEST)
    in_block = in_block.reshape(tok_rows, pole_count, channels) * growth
    survives = local_ids == window[filter_taps - 1]
    block_factor = jnp.exp(-rates * tok_rows)
    block_end = in_block[tok_rows - 1]
    block_ends = lax.all_gather(block_end[None], "ctx", axis=0, tiled=True)
    shard_count = segment_ids.shape[0] // tok_rows
    last_ids = segment_ids.reshape(shard_count, tok_rows)[:, tok_rows - 1]
    prior_ids = jnp.concatenate([jnp.full((1,), -1, jnp.int32), last_ids[:-1]], axis=0)
    shard_decays = block_factor[None] * (last_ids == prior_ids).astype(jnp.float32)[:, None, None]

    def absorb(running, inputs):
        shard, factor, shard_end = inputs
        advanced = running * factor + shard_end
        return (jnp.where(shard < device_index, advanced, running), None)

    incoming, _ = lax.scan(
        absorb,
        jnp.zeros_like(block_end),
        (jnp.arange(shard_count, dtype=jnp.int32), shard_decays, block_ends),
    )
    carried = incoming[None] * jnp.exp(-(offsets + 1.0)[:, None, None] * rates[None])
    carried = carried * survives.astype(jnp.float32)[:, None, None]
    states = in_block + carried
    pole_weight = residues * jnp.sqrt(-jnp.expm1(-2.0 * rates))
    longconv = jnp.sum(pole_weight[None] * states, axis=1)
    gated = (query_part * (longconv + skip[None, :] * product)).astype(jnp.bfloat16)
    partial_terms = jnp.dot(gated, out_weight, preferred_element_type=jnp.float32)
    return lax.psum_scatter(partial_terms, "mp", scatter_dimension=1, tiled=True).astype(
        jnp.bfloat16
    )


def local(tokens, norm_gain, in_weight, short_filter, rates, residues, skip, out_weight, segment_ids):
    T = tokens.shape[0]
    shards = lax.axis_size("ctx")
    me = lax.axis_index("ctx")
    position = me.astype(jnp.int32)[None]
    lane_position = lax.axis_index("mp").astype(jnp.int32)[None]
    width = out_weight.shape[1] // lax.axis_size("mp")
    weight3 = jnp.transpose(in_weight, (1, 0, 2))
    out_weight = pltpu.with_memory_space_constraint(out_weight, pltpu.HBM)
    raw, product, block, keep, twice, visible, taps, rates, residues, skip = front(
        position, segment_ids.reshape(-1, 128), tokens, norm_gain[None], weight3, short_filter, rates, residues, skip[None])
    cuts = shards.bit_length() - 1
    each = product.shape[0] // cuts
    group, spans, arrived, parts, windows = block, [], [], [], []
    for k in range(cuts):
        span = 1 << k
        other = lax.ppermute(group, "ctx", [(a, a ^ span) for a in range(shards)])
        spans.append(span)
        arrived.append(other)
        *part, window = local_pass(
            k * each, each, min(k, 1), lane_position, product, keep, twice, raw, taps, rates, residues, skip,
            out_weight, width, group)
        parts.append(part)
        windows.append(window)
        if k < cuts - 1:
            group = join(span, T, position, segment_ids, group, other, taps, rates, part[0])
    gated, send, mine, third = gate(T, spans, arrived, position, lane_position, segment_ids, parts, block, visible, taps, rates,
                             skip, windows[0], out_weight, width)
    return scatter_line(lane_position, gated, send, mine, windows[1], third, out_weight, width)


def solution(mesh):
    placed = (
        P("ctx", None),
        P(),
        P(None, None, "mp"),
        P(None, None, "mp"),
        P(None, "mp"),
        P(None, "mp"),
        P("mp"),
        P("mp", None),
        P(),
    )
    shards, groups = mesh.shape["ctx"], mesh.shape["mp"]

    def body(tokens, norm_gain, in_weight, *rest):
        suits = groups == 8 and shards & (shards - 1) == 0 and shards > 2
        suits = suits and in_weight.shape[2] % 512 == 0 and in_weight.shape[0] % 2048 == 0
        suits = suits and tokens.shape[0] % 64 == 0 and rest[-1].shape[0] % 128 == 0 and rest[1].shape[0] % 8 == 0
        return (local if suits else general)(tokens, norm_gain, in_weight, *rest)

    return jax.shard_map(
        body, mesh=mesh, in_specs=placed, out_specs=P("ctx", "mp"), check_vma=False
    )
```

```python
import functools
import jax
import jax.numpy as jnp
from jax import lax
from jax.experimental import pallas as pl
from jax.experimental.pallas import tpu as pltpu
from jax.sharding import PartitionSpec as P

epsilon = 1e-06
f32 = jnp.float32
bf16 = jnp.bfloat16

PARTS = 8
HEAD = 16
MIB = 1 << 20


def vmem():
    return pl.BlockSpec(memory_space=pltpu.VMEM)


def smem():
    return pl.BlockSpec(memory_space=pltpu.SMEM)


def same_id(ids_ref, a, b):
    def get(t):
        return jnp.where(t < 0, -1, ids_ref[jnp.maximum(t, 0)])

    return (get(a) == get(b)).astype(f32)


def hbm():
    return pl.BlockSpec(memory_space=pltpu.HBM)


def front_kernel(
    geometry, position, ids_ref, tokens_ref, gain_ref, weight_ref, taps_ref, rates_ref, residues_ref, skip_ref,
    raw_out, prod_out, block_out, keep_out, twice, visible_out, taps, rates, residues, skip,
    ids, gain, tok, normed, ring, total, proj, head, idcol, near, ending, sem, tok_sem, ring_sem,
):
    T, depth, channels, cb_size, kc_size, slots, poles = geometry
    run = T // PARTS
    kcs, cbs = depth // kc_size, channels // cb_size
    steps = kcs * cbs
    base = pl.multiple_of(position[0] * T, 8)

    def fetch(step):
        cb, kc, slot = step // kcs, step % kcs, step % slots
        return pltpu.make_async_copy(
            weight_ref.at[:, pl.ds(pl.multiple_of(kc * kc_size, kc_size), kc_size),
                          pl.ds(pl.multiple_of(cb * cb_size, cb_size), cb_size)],
            ring.at[slot], ring_sem.at[slot])

    small = [
        pltpu.make_async_copy(a, b, sem.at[i])
        for i, (a, b) in enumerate(
            ((ids_ref, ids), (gain_ref, gain), (taps_ref, taps), (rates_ref, rates), (residues_ref, residues),
             (skip_ref, skip)))
    ]
    small[0].start()
    small[1].start()
    chunk = T // 4
    tok_copies = [
        pltpu.make_async_copy(tokens_ref.at[pl.ds(c * chunk, chunk)], tok.at[pl.ds(c * chunk, chunk)], tok_sem.at[c])
        for c in range(4)
    ]
    for copy in tok_copies:
        copy.start()
    for copy in small[2:]:
        copy.start()
    for s in range(min(slots, steps)):
        fetch(s).start()

    small[0].wait()
    idcol[0:8, :] = jnp.full((8, 128), -1.0, f32)
    for b in range(ids.shape[0]):
        row = ids[b : b + 1, :].astype(f32)
        idcol[8 + b * 128 : 8 + (b + 1) * 128, :] = jnp.broadcast_to(row, (128, 128)).T
    near[...] = idcol[pl.ds(base, T + 8), :]
    here = near[8 : 8 + T, :]
    keep_out[...] = (here == near[7 : 7 + T, :]).astype(f32)
    twice[...] = (here == near[6 : 6 + T, :]).astype(f32)
    ending[...] = (here == near[7 + T : 8 + T, :]).astype(f32)
    before = near[pl.ds(7, PARTS, stride=run), :]
    for i in range(run):
        visible_out[i * 8 : (i + 1) * 8, :] = (near[pl.ds(8 + i, PARTS, stride=run), :] == before).astype(f32)
    for i in range(2):
        proj[i, 0:8, :] = jnp.zeros((8, cb_size), f32)
    raw_out[0:8, :] = jnp.zeros((8, channels), f32)
    head[...] = jnp.zeros(head.shape, f32)
    small[1].wait()

    def norm_rows(g, _):
        part = pl.ds(pl.multiple_of(g * 16, 16), 16)
        x = tok[part, :].astype(f32)
        scale = lax.rsqrt(jnp.sum(x * x, axis=-1, keepdims=True) * (1.0 / depth) + epsilon)
        normed[part, :] = (x * scale * gain[...]).astype(bf16)
        return 0

    for c, copy in enumerate(tok_copies):
        copy.wait()
        lax.fori_loop(c * chunk // 16, (c + 1) * chunk // 16, norm_rows, 0)
    for copy in small[2:]:
        copy.wait()

    def epilogue(cb):
        cols = pl.ds(pl.multiple_of(cb * cb_size, cb_size), cb_size)
        feats = []
        m1 = jnp.concatenate([keep_out[...]] * (cb_size // 128), axis=1)
        m2 = jnp.concatenate([twice[...]] * (cb_size // 128), axis=1)
        query = total[0].astype(bf16).astype(f32)
        raw_out[8 : 8 + T, cols] = query
        head[4:6, :] = query[T - 2 : T]
        for i in range(2):
            p = total[i + 1].astype(bf16).astype(f32)
            proj[i, 8 : 8 + T, :] = p
            tap = [taps[j, i + 1 : i + 2, cols] for j in range(3)]
            feats.append(
                tap[0] * p + m1 * (tap[1] * proj[i, 7 : 7 + T, :]) + m2 * (tap[2] * proj[i, 6 : 6 + T, :]))
            head[2 * i : 2 * i + 2, :] = proj[i, 8:10, :]
            head[6 + 2 * i : 8 + 2 * i, :] = proj[i, 6 + T : 8 + T, :]
        block_out[poles : poles + HEAD, cols] = head[...].astype(bf16)
        product = feats[0] * feats[1]
        back = 7.0 - lax.broadcasted_iota(jnp.int32, (8, 128), 0).astype(f32)
        for lane in range(cb_size // 128):
            tile = cb * (cb_size // 128) + lane
            lanes = pl.ds(pl.multiple_of(tile * 128, 128), 128)
            prod_out[tile] = product[:, lane * 128 : lane * 128 + 128]
            r16 = rates[:, lanes]
            jump = jnp.exp(-8.0 * r16)
            leap = [jnp.broadcast_to(jump[n : n + 1], (8, 128)) for n in range(poles)]

            def eight(g, sums):
                part = pl.ds(pl.multiple_of(g * 8, 8), 8)
                p = prod_out[tile, part, :] * ending[part, :]
                return tuple(sums[n] * leap[n] + p for n in range(poles))

            sums = lax.fori_loop(
                0, T // 8, eight, tuple(jnp.zeros((8, 128), f32) for _ in range(poles)), unroll=4)
            ends = [
                jnp.sum(sums[n] * jnp.exp(-back * r16[n : n + 1]), axis=0, keepdims=True) for n in range(poles)
            ]
            block_out[0:poles, lanes] = jnp.concatenate(ends, axis=0).astype(bf16)

    def step_body(step, _):
        cb, kc, slot = step // kcs, step % kcs, step % slots
        fetch(step).wait()
        lhs = normed[:, pl.ds(pl.multiple_of(kc * kc_size, kc_size), kc_size)]
        for i in range(3):
            part = jnp.dot(lhs, ring[slot, i], preferred_element_type=f32)
            total[i] = jnp.where(kc == 0, part, total[i] + part)

        @pl.when(step + slots < steps)
        def _():
            fetch(step + slots).start()

        @pl.when(kc == kcs - 1)
        def _():
            epilogue(cb)

        return 0

    total[...] = jnp.zeros(total.shape, f32)
    lax.fori_loop(0, steps, step_body, 0)


def front(position, ids2, tokens, gain, weight3, taps, rates, residues, skip):
    T, depth = tokens.shape
    channels, poles = weight3.shape[2], rates.shape[0]
    cb_size, kc_size, slots = 256, 2048, 5
    geometry = (T, depth, channels, cb_size, kc_size, slots, poles)
    kept = [pltpu.VMEM(a.shape, a.dtype) for a in (taps, rates, residues, skip)]
    ids2, tokens, gain, weight3, taps, rates, residues, skip = [
        pltpu.with_memory_space_constraint(a, pltpu.HBM)
        for a in (ids2, tokens, gain, weight3, taps, rates, residues, skip)
    ]
    return pl.pallas_call(
        functools.partial(front_kernel, geometry),
        out_shape=[
            jax.ShapeDtypeStruct((T + 8, channels), f32),
            jax.ShapeDtypeStruct((channels // 128, T, 128), f32),
            jax.ShapeDtypeStruct((poles + HEAD, channels), bf16),
            jax.ShapeDtypeStruct((T, 128), f32),
            jax.ShapeDtypeStruct((T, 128), f32),
            jax.ShapeDtypeStruct((T, 128), f32),
        ] + kept,
        in_specs=[smem()] + [hbm()] * 8,
        out_specs=[vmem()] * 10,
        scratch_shapes=[
            pltpu.VMEM(ids2.shape, ids2.dtype),
            pltpu.VMEM(gain.shape, f32),
            pltpu.VMEM((T, depth), bf16),
            pltpu.VMEM((T, depth), bf16),
            pltpu.VMEM((slots, 3, kc_size, cb_size), bf16),
            pltpu.VMEM((3, T, cb_size), f32),
            pltpu.VMEM((2, T + 8, cb_size), f32),
            pltpu.VMEM((HEAD, cb_size), f32),
            pltpu.VMEM((ids2.shape[0] * 128 + 8, 128), f32),
            pltpu.VMEM((T + 8, 128), f32),
            pltpu.VMEM((T, 128), f32),
            pltpu.SemaphoreType.DMA((6,)),
            pltpu.SemaphoreType.DMA((4,)),
            pltpu.SemaphoreType.DMA((slots,)),
        ],
        compiler_params=pltpu.CompilerParams(vmem_limit_bytes=28 * MIB),
        name="front",
    )(position, ids2, tokens, gain, weight3, taps, rates, residues, skip)


def expm1(x):
    series = jnp.ones_like(x)
    for k in range(9, 1, -1):
        series = 1.0 + series * x * (1.0 / k)
    return jnp.where(jnp.abs(x) < 0.5, x * series, jnp.exp(x) - 1.0)


def local_kernel(
    poles, first, slot, lane_position, prod_ref, keep_ref, twice_ref, raw_ref, taps_ref, rates_ref, residues_ref, skip_ref,
    out_ref, _, local_out, state_out, pole_out, query_out, window_out, sem,
):
    copy = columns(lane_position[0], slot, out_ref, window_out, sem)
    copy.start()
    tiles, T, _ = local_out.shape
    run = T // PARTS
    mine = slice(first * 128, (first + tiles) * 128)
    pole_out[...] = residues_ref[:, mine] * jnp.sqrt(-expm1(-2.0 * rates_ref[:, mine]))

    def tile_body(tile, _):
        lanes = pl.ds(pl.multiple_of((first + tile) * 128, 128), 128)
        d16 = jnp.exp(-rates_ref[:, lanes])
        w16 = pole_out[:, pl.ds(pl.multiple_of(tile * 128, 128), 128)]
        decay = [jnp.broadcast_to(d16[n : n + 1], (8, 128)) for n in range(poles)]
        weight = [jnp.broadcast_to(w16[n : n + 1], (8, 128)) for n in range(poles)]
        skip = skip_ref[0:1, lanes]

        def token(i, states):
            at = pl.ds(i, PARTS, stride=run)
            p, keep = prod_ref[first + tile, at, :], keep_ref[at, :]
            after = [states[n] * decay[n] * keep + p for n in range(poles)]
            local_out[tile, at, :] = tree([skip * p] + [weight[n] * after[n] for n in range(poles)])
            return tuple(after)

        states = lax.fori_loop(0, run, token, tuple(jnp.zeros((8, 128), f32) for _ in range(poles)), unroll=2)
        for n in range(poles):
            state_out[tile, pl.ds(n, PARTS, stride=poles), :] = states[n]
        tap = [taps_ref[j, 0:1, lanes] for j in range(3)]
        query_out[tile] = (
            tap[0] * raw_ref[8 : 8 + T, lanes]
            + keep_ref[...] * (tap[1] * raw_ref[7 : 7 + T, lanes])
            + twice_ref[...] * (tap[2] * raw_ref[6 : 6 + T, lanes]))
        return 0

    lax.fori_loop(0, tiles, tile_body, 0)
    copy.wait()


def tree(terms):
    while len(terms) > 1:
        terms = [a + b for a, b in zip(terms[0::2], terms[1::2])] + terms[len(terms) // 2 * 2 :]
    return terms[0]


def local_pass(
    first, tiles, slot, lane_position, product, keep, twice, raw, taps, rates, residues, skip, out_weight, width, after,
):
    T, poles = product.shape[1], rates.shape[0]
    return pl.pallas_call(
        functools.partial(local_kernel, poles, first, slot),
        out_shape=(
            jax.ShapeDtypeStruct((tiles, T, 128), f32),
            jax.ShapeDtypeStruct((tiles, PARTS * poles, 128), f32),
            jax.ShapeDtypeStruct((poles, tiles * 128), f32),
            jax.ShapeDtypeStruct((tiles, T, 128), f32),
            jax.ShapeDtypeStruct((out_weight.shape[0], 2 * width), bf16),
        ),
        in_specs=[smem()] + [vmem()] * 8 + [hbm(), pl.BlockSpec(memory_space=pl.ANY)],
        out_specs=[vmem()] * 5,
        scratch_shapes=[pltpu.SemaphoreType.DMA((STREAMS,))],
        compiler_params=pltpu.CompilerParams(vmem_limit_bytes=8 * MIB),
        cost_estimate=pl.CostEstimate(flops=6 * T * poles * tiles * 128, bytes_accessed=8 * MIB, transcendentals=0),
        name="local_pass",
    )(lane_position, product, keep, twice, raw, taps, rates, residues, skip, out_weight, after)


def first_products(first, last, taps, ids_ref, base):
    s01, s0m1 = same_id(ids_ref, base + 1, base), same_id(ids_ref, base, base - 1)
    s0m2, s1m1 = same_id(ids_ref, base, base - 2), same_id(ids_ref, base + 1, base - 1)

    def shift(i):
        near, far = last[i][1:2], last[i][0:1]
        t1, t2 = taps[1][i : i + 1], taps[2][i : i + 1]
        return s0m1 * (t1 * near) + s0m2 * (t2 * far), s1m1 * (t2 * near)

    def plain(i):
        t0, t1 = taps[0][i : i + 1], taps[1][i : i + 1]
        return t0 * first[i][0:1], t0 * first[i][1:2] + s01 * (t1 * first[i][0:1])

    k, v, dk, dv = plain(1), plain(2), shift(1), shift(2)
    delta = [(k[j] + dk[j]) * (v[j] + dv[j]) - k[j] * v[j] for j in range(2)]
    return shift(0), delta


def unpack(block, poles):
    first = [None, block[poles : poles + 2], block[poles + 2 : poles + 4]]
    last = [block[poles + 4 + 2 * i : poles + 6 + 2 * i] for i in range(3)]
    return block[0:poles], first, last


def joined_state(low_state, low_last, up_state, up_first, taps, rates, ids_ref, base, length):
    _, delta = first_products(up_first, low_last, taps, ids_ref, base)
    grown = low_state + delta[0] * jnp.exp(rates) + delta[1] * jnp.exp(2.0 * rates)
    open_ = same_id(ids_ref, base + length - 1, base - 1)
    return up_state + grown * (jnp.exp(-rates * jnp.float32(length)) * open_)


def join_kernel(T, poles, span, position, ids_ref, mine_ref, other_ref, taps_ref, rates_ref, _, out):
    me = position[0]
    is_upper = (me // span) % 2 == 1
    base = (me // (2 * span)) * (2 * span * T) + span * T
    mine, other = mine_ref[...].astype(f32), other_ref[...].astype(f32)
    lower, upper = jnp.where(is_upper, other, mine), jnp.where(is_upper, mine, other)
    taps = [taps_ref[j] for j in range(3)]
    low_state, _, low_last = unpack(lower, poles)
    up_state, up_first, _ = unpack(upper, poles)
    state = joined_state(low_state, low_last, up_state, up_first, taps, rates_ref[...], ids_ref, base, span * T)
    out[0:poles, :] = state.astype(bf16)
    row = lax.broadcasted_iota(jnp.int32, (HEAD, lower.shape[1]), 0)
    out[poles : poles + HEAD, :] = jnp.where(row < 4, lower[poles:], upper[poles:]).astype(bf16)


def join(span, T, position, ids, mine, other, taps, rates, after):
    poles = rates.shape[0]
    return pl.pallas_call(
        functools.partial(join_kernel, T, poles, span),
        out_shape=jax.ShapeDtypeStruct(mine.shape, bf16),
        in_specs=[smem(), smem()] + [vmem()] * 4 + [pl.BlockSpec(memory_space=pl.ANY)],
        out_specs=vmem(),
        compiler_params=pltpu.CompilerParams(vmem_limit_bytes=4 * MIB),
        name="join",
    )(position, ids, mine, other, taps, rates, after)


def gate_kernel(
    T, poles, spans, cuts, position, lane_position, ids_ref, block_ref, visible_ref, taps_ref, rates_ref, skip_ref,
    window_ref, out_ref, *rest,
):
    arrived, rest = rest[: len(spans)], rest[len(spans) :]
    parts, rest = [rest[4 * c : 4 * c + 4] for c in range(cuts)], rest[4 * cuts :]
    gated_out, send_out, mine_out, third_out, carry, full, sem = rest
    run = T // PARTS
    tiles = block_ref.shape[1] // 128
    copy = columns(lane_position[0], 2, out_ref, third_out, sem)
    copy.start()
    me = position[0]
    base = me * T
    taps = [taps_ref[j] for j in range(3)]
    rates, skip = rates_ref[...], skip_ref[...]
    weight = jnp.concatenate([pole_ref[...] for _, _, pole_ref, _ in parts], axis=1)
    each = tiles // cuts
    prior = jnp.zeros(block_ref.shape, f32)
    prior_state, prior_first, prior_last = unpack(prior, poles)
    for span, ref in zip(spans, arrived):
        state, first, last = unpack(ref[...].astype(f32), poles)
        upper, held = (me // span) % 2 == 1, me % span
        if span == 1:
            both = state
        else:
            both = joined_state(
                state, last, prior_state, prior_first, taps, rates, ids_ref, (me - held) * T, held * T)
        fresh = upper & (held == 0)
        prior_state = jnp.where(fresh, state, jnp.where(upper, both, prior_state))
        prior_first = [None] + [jnp.where(upper, first[i], prior_first[i]) for i in (1, 2)]
        prior_last = [jnp.where(fresh, last[i], prior_last[i]) for i in range(3)]
    _, first, _ = unpack(block_ref[...].astype(f32), poles)
    q_shift, delta = first_products(first, prior_last, taps, ids_ref, base)
    second = delta[1] * jnp.exp(rates)
    now = prior_state + (delta[0] + second) * jnp.exp(rates)
    fix0 = skip * delta[0] - jnp.sum(weight * second, axis=0, keepdims=True)
    fix1 = skip * delta[1]
    jump = jnp.exp(-rates * float(run))
    for s in range(PARTS):
        part = slice(s * poles, (s + 1) * poles)
        began = weight * now
        for tile in range(tiles):
            carry[tile, part, :] = began[:, tile * 128 : tile * 128 + 128]
        if s < PARTS - 1:
            whole = same_id(ids_ref, base + s * run + run - 1, base + s * run - 1)
            ends = jnp.concatenate([parts[tile // each][1][tile % each, part, :] for tile in range(tiles)], axis=1)
            now = now * (jump * whole) + ends

    def lane_body(cut, inner, _):
        tile = cut * each + inner
        lanes = pl.ds(pl.multiple_of(tile * 128, 128), 128)
        d16 = jnp.exp(-rates_ref[:, lanes])
        decay = [jnp.broadcast_to(d16[n : n + 1], (8, 128)) for n in range(poles)]
        start = tuple(carry[tile, pl.ds(n, PARTS, stride=poles), :] for n in range(poles))

        def token(i, states):
            after = [states[n] * decay[n] for n in range(poles)]
            see = visible_ref[pl.ds(pl.multiple_of(i * 8, 8), 8), :]
            at = pl.ds(i, PARTS, stride=run)
            full[tile, at, :] = parts[cut][0][inner, at, :] + see * tree(list(after))
            return tuple(after)

        lax.fori_loop(0, run, token, start, unroll=4)
        return 0

    for cut in range(cuts):
        lax.fori_loop(0, each, functools.partial(lane_body, cut), 0)
    row = lax.broadcasted_iota(jnp.int32, (16, 128), 0)
    for tile in range(tiles):
        lanes = slice(tile * 128, tile * 128 + 128)
        query_ref = parts[tile // each][3].at[tile % each]
        gated_out[:, lanes] = (query_ref[...] * full[tile]).astype(bf16)
        top_q, top = query_ref[0:16, :], full[tile, 0:16, :]
        top_q = top_q + jnp.where(row == 0, q_shift[0][:, lanes], 0.0) + jnp.where(row == 1, q_shift[1][:, lanes], 0.0)
        top = top + jnp.where(row == 0, fix0[:, lanes], 0.0) + jnp.where(row == 1, fix1[:, lanes], 0.0)
        gated_out[0:16, lanes] = (top_q * top).astype(bf16)
    share(lane_position[0], gated_out, window_ref, send_out, mine_out)
    copy.wait()


def target(index, slot):
    chip = index // 2
    if slot == 0:
        return 3 - 3 * (chip % 2)
    if slot == 1:
        return jnp.where(chip < 2, 2, 1)
    if slot == 2:
        return jnp.where(chip < 2, 1 + 2 * chip, 2 * (chip - 2))
    return chip


class Copies:
    def __init__(self, copies):
        self.copies = copies

    def start(self):
        for copy in self.copies:
            copy.start()

    def wait(self):
        for copy in self.copies:
            copy.wait()


STREAMS = 4


def columns(index, slot, out_ref, window, sem):
    channels, both = window.shape
    start = pl.multiple_of(target(index, slot) * both, both)
    each = channels // STREAMS
    return Copies([
        pltpu.make_async_copy(
            out_ref.at[pl.ds(k * each, each), pl.ds(start, both)], window.at[pl.ds(k * each, each)], sem.at[k])
        for k in range(STREAMS)
    ])


def share(index, gated_ref, window, send_out, mine_out):
    width = send_out.shape[1]
    tile = 256
    core = index % 2

    for j in range(width // tile):
        at = slice(j * tile, j * tile + tile)
        for out, half in ((send_out, 1 - core), (mine_out, core)):
            cols = pl.ds(pl.multiple_of(half * width + j * tile, tile), tile)
            out[:, at] = jnp.dot(gated_ref[...], window[:, cols], preferred_element_type=f32).astype(out.dtype)


def share_kernel(count, lane_position, gated_ref, *rest):
    windows, outs = rest[:count], rest[count:]
    for k, window in enumerate(windows):
        share(lane_position[0], gated_ref, window, outs[2 * k], outs[2 * k + 1])


def shares(lane_position, gated, windows, width):
    T, channels = gated.shape
    count = len(windows)
    return pl.pallas_call(
        functools.partial(share_kernel, count),
        out_shape=[jax.ShapeDtypeStruct((T, width), d) for _ in windows for d in (bf16, f32)],
        in_specs=[smem(), vmem()] + [vmem()] * count,
        out_specs=[vmem()] * (2 * count),
        compiler_params=pltpu.CompilerParams(vmem_limit_bytes=4 * MIB),
        cost_estimate=pl.CostEstimate(
            flops=4 * T * channels * width * count, bytes_accessed=4 * channels * width * count, transcendentals=0),
        name="shares",
    )(lane_position, gated, *windows)


def late_share_kernel(slot, lane_position, gated_ref, out_ref, send_out, mine_out, window, sem):
    copy = columns(lane_position[0], slot, out_ref, window, sem)
    copy.start()
    copy.wait()
    share(lane_position[0], gated_ref, window, send_out, mine_out)


def late_share(slot, lane_position, gated, out_weight, width):
    T, channels = gated.shape
    return pl.pallas_call(
        functools.partial(late_share_kernel, slot),
        out_shape=[jax.ShapeDtypeStruct((T, width), d) for d in (bf16, f32)],
        in_specs=[smem(), vmem(), hbm()],
        out_specs=[vmem()] * 2,
        scratch_shapes=[pltpu.VMEM((channels, 2 * width), bf16), pltpu.SemaphoreType.DMA((STREAMS,))],
        compiler_params=pltpu.CompilerParams(vmem_limit_bytes=6 * MIB),
        cost_estimate=pl.CostEstimate(
            flops=4 * T * channels * width, bytes_accessed=4 * channels * width, transcendentals=0),
        name="late_share",
    )(lane_position, gated, out_weight)


def gate(T, spans, arrived, position, lane_position, ids, parts, block, visible, taps, rates, skip, window, out_weight, width):
    poles, channels = rates.shape
    return pl.pallas_call(
        functools.partial(gate_kernel, T, poles, tuple(spans), len(parts)),
        out_shape=[
            jax.ShapeDtypeStruct((T, channels), bf16),
            jax.ShapeDtypeStruct((T, width), bf16),
            jax.ShapeDtypeStruct((T, width), f32),
            pltpu.VMEM(window.shape, bf16),
        ],
        in_specs=[smem()] * 3 + [vmem()] * 6 + [hbm()] + [vmem()] * (len(spans) + 4 * len(parts)),
        out_specs=[vmem()] * 4,
        scratch_shapes=[
            pltpu.VMEM((channels // 128, PARTS * poles, 128), f32),
            pltpu.VMEM((channels // 128, T, 128), f32),
            pltpu.SemaphoreType.DMA((STREAMS,)),
        ],
        compiler_params=pltpu.CompilerParams(vmem_limit_bytes=8 * MIB),
        name="gate",
    )(position, lane_position, ids, block, visible, taps, rates, skip, window, out_weight, *arrived,
      *[a for part in parts for a in part])


def total(*terms):
    return functools.reduce(lambda a, b: a + b, [t.astype(f32) for t in terms]).astype(bf16)


def merge_kernel(count, has_inner, lane_position, *rest):
    terms, picks, out = rest[:count], rest[count:-1], rest[-1]
    value = terms[0][...].astype(f32)
    for term in terms[1:]:
        value = value + term[...].astype(f32)
    chip = lane_position[0] // 2
    inner = (chip == 1) | (chip == 2)
    for pick, wanted in zip(picks, (inner, jnp.logical_not(inner)) if has_inner else (jnp.logical_not(inner),)):
        value = value + jnp.where(wanted, pick[...].astype(f32), 0.0)
    out[...] = value.astype(out.dtype)


def merge(lane_position, dtype, terms, inner=None, outer=None):
    picks = [a for a in (inner, outer) if a is not None]
    terms = [pltpu.with_memory_space_constraint(a, pltpu.VMEM) for a in (*terms, *picks)]
    return pl.pallas_call(
        functools.partial(merge_kernel, len(terms) - len(picks), inner is not None),
        out_shape=jax.ShapeDtypeStruct(terms[0].shape, dtype),
        in_specs=[smem()] + [vmem()] * len(terms),
        out_specs=vmem(),
        compiler_params=pltpu.CompilerParams(vmem_limit_bytes=3 * MIB),
        name="merge",
    )(lane_position, *terms)


def halves_kernel(_, mine_ref, other_ref, top_out, bottom_out):
    rows = top_out.shape[0]
    value = (mine_ref[...] + other_ref[...].astype(f32)).astype(bf16)
    top_out[...] = value[:rows]
    bottom_out[...] = value[rows:]


def halves(lane_position, mine, other):
    terms = [pltpu.with_memory_space_constraint(a, pltpu.VMEM) for a in (mine, other)]
    return pl.pallas_call(
        halves_kernel,
        out_shape=(jax.ShapeDtypeStruct((mine.shape[0] // 2, mine.shape[1]), bf16),) * 2,
        in_specs=[smem()] + [vmem()] * 2,
        out_specs=[vmem()] * 2,
        compiler_params=pltpu.CompilerParams(vmem_limit_bytes=3 * MIB),
        name="halves",
    )(lane_position, *terms)


def own_kernel(lane_position, mine_ref, other_ref, near_ref, middle_ref, end_ref, again_ref, out):
    rows = middle_ref.shape[0]
    chip = lane_position[0] // 2
    outer = (chip == 0) | (chip == 3)
    value = mine_ref[...] + other_ref[...].astype(f32) + jnp.where(outer, near_ref[...].astype(f32), 0.0)
    out[0:rows, :] = value[:rows] + (middle_ref[...].astype(f32) + end_ref[...].astype(f32))
    out[rows:, :] = value[rows:] + again_ref[...].astype(f32)


def gather_own(lane_position, mine, *others):
    terms = [pltpu.with_memory_space_constraint(a, pltpu.VMEM) for a in (mine, *others)]
    return pl.pallas_call(
        own_kernel,
        out_shape=jax.ShapeDtypeStruct(mine.shape, f32),
        in_specs=[smem()] + [vmem()] * len(terms),
        out_specs=vmem(),
        compiler_params=pltpu.CompilerParams(vmem_limit_bytes=3 * MIB),
        name="gather_own",
    )(lane_position, *terms)


def scatter_line(lane_position, gated, send, mine, window, third, out_weight, width):
    pair = [(m, m ^ 1) for m in range(8)]

    def along(hops):
        return [(a * 2 + c, b * 2 + c) for a, b in hops for c in range(2)]

    near = along([(0, 1), (1, 0), (2, 3), (3, 2)])
    traded = lax.ppermute(send, "mp", pair)
    far = merge(lane_position, bf16, (mine, traded))
    from_near = lax.ppermute(far, "mp", near)
    send, mine = shares(lane_position, gated, [window], width)
    top, bottom = halves(lane_position, mine, lax.ppermute(send, "mp", pair))
    beside = lax.ppermute(bottom, "mp", near)
    from_middle = lax.ppermute(top, "mp", along([(1, 2), (2, 1)]))
    from_end = lax.ppermute(top, "mp", along([(0, 2), (3, 1)]))
    send2, mine2 = shares(lane_position, gated, [third], width)
    mine2 = merge(lane_position, f32, (mine2, lax.ppermute(send2, "mp", pair)))
    onward = merge(lane_position, bf16, (mine2,), inner=from_near)
    from_round = lax.ppermute(onward, "mp", along([(0, 1), (1, 3), (3, 2), (2, 0)]))
    send3, mine3 = late_share(3, lane_position, gated, out_weight, width)
    both = merge(lane_position, bf16, (bottom, beside))
    again = lax.ppermute(both, "mp", along([(1, 2), (2, 1)]))
    own = gather_own(lane_position, mine3, lax.ppermute(send3, "mp", pair), from_near, from_middle, from_end, again)
    return total(own, from_round)


def shifted(value, axis, steps):
    count = lax.axis_size(axis)
    leading, last = (max(0, -steps), min(count, count - steps))
    return lax.ppermute(value, axis, [(source, source + steps) for source in range(leading, last)])


def project(block, norm_gain, weights):
    floats = block.astype(jnp.float32)
    mean_square = jnp.mean(floats * floats, axis=-1, keepdims=True)
    normed = (floats * lax.rsqrt(mean_square + epsilon) * norm_gain[None, :]).astype(jnp.bfloat16)
    return jnp.dot(normed, weights, preferred_element_type=jnp.float32).astype(jnp.bfloat16)


def general(
    tokens, norm_gain, in_weight, short_filter, rates, residues, skip, out_weight, segment_ids
):
    tok_rows = tokens.shape[0]
    model_width = tokens.shape[1]
    channels = in_weight.shape[2]
    filter_taps = short_filter.shape[0]
    pole_count = rates.shape[0]
    device_index = lax.axis_index("ctx")
    row_offset = device_index * tok_rows
    weights = in_weight.reshape(model_width, 3 * channels)
    projected = project(tokens, norm_gain, weights)
    previous = shifted(projected[tok_rows - (filter_taps - 1) :], "ctx", 1)
    extended = jnp.concatenate([previous, projected], axis=0)
    padded_ids = jnp.concatenate([jnp.full((filter_taps,), -1, jnp.int32), segment_ids], axis=0)
    window = lax.dynamic_slice_in_dim(padded_ids, row_offset, tok_rows + filter_taps, 0)
    local_ids = window[filter_taps:]
    taps_table = short_filter.reshape(filter_taps, 3 * channels)
    featured = jnp.zeros((tok_rows, 3 * channels), jnp.float32)
    for lag_index in range(filter_taps):
        begin = filter_taps - 1 - lag_index
        lagged = extended[begin : begin + tok_rows].astype(jnp.float32)
        matches = window[filter_taps - lag_index : filter_taps - lag_index + tok_rows] == local_ids
        term = taps_table[lag_index][None, :] * lagged
        featured = featured + jnp.where(matches[:, None], term, jnp.zeros_like(term))
    query_part = featured[:, :channels]
    key_part = featured[:, channels : 2 * channels]
    value_part = featured[:, 2 * channels :]
    product = key_part * value_part
    offsets = jnp.arange(tok_rows, dtype=jnp.float32)
    center = float(tok_rows // 2)
    growth = jnp.exp(-(offsets - center)[:, None, None] * rates[None])
    shrinkage = jnp.exp((offsets - center)[:, None, None] * rates[None])
    weighted = (shrinkage * product[:, None, :]).reshape(tok_rows, pole_count * channels)
    visible = (offsets[:, None] >= offsets[None, :]) & (local_ids[:, None] == local_ids[None, :])
    in_block = jnp.dot(visible.astype(jnp.float32), weighted, precision=lax.Precision.HIGHEST)
    in_block = in_block.reshape(tok_rows, pole_count, channels) * growth
    survives = local_ids == window[filter_taps - 1]
    block_factor = jnp.exp(-rates * tok_rows)
    block_end = in_block[tok_rows - 1]
    block_ends = lax.all_gather(block_end[None], "ctx", axis=0, tiled=True)
    shard_count = segment_ids.shape[0] // tok_rows
    last_ids = segment_ids.reshape(shard_count, tok_rows)[:, tok_rows - 1]
    prior_ids = jnp.concatenate([jnp.full((1,), -1, jnp.int32), last_ids[:-1]], axis=0)
    shard_decays = block_factor[None] * (last_ids == prior_ids).astype(jnp.float32)[:, None, None]

    def absorb(running, inputs):
        shard, factor, shard_end = inputs
        advanced = running * factor + shard_end
        return (jnp.where(shard < device_index, advanced, running), None)

    incoming, _ = lax.scan(
        absorb,
        jnp.zeros_like(block_end),
        (jnp.arange(shard_count, dtype=jnp.int32), shard_decays, block_ends),
    )
    carried = incoming[None] * jnp.exp(-(offsets + 1.0)[:, None, None] * rates[None])
    carried = carried * survives.astype(jnp.float32)[:, None, None]
    states = in_block + carried
    pole_weight = residues * jnp.sqrt(-jnp.expm1(-2.0 * rates))
    longconv = jnp.sum(pole_weight[None] * states, axis=1)
    gated = (query_part * (longconv + skip[None, :] * product)).astype(jnp.bfloat16)
    partial_terms = jnp.dot(gated, out_weight, preferred_element_type=jnp.float32)
    return lax.psum_scatter(partial_terms, "mp", scatter_dimension=1, tiled=True).astype(
        jnp.bfloat16
    )


def local(tokens, norm_gain, in_weight, short_filter, rates, residues, skip, out_weight, segment_ids):
    T = tokens.shape[0]
    shards = lax.axis_size("ctx")
    me = lax.axis_index("ctx")
    position = me.astype(jnp.int32)[None]
    lane_position = lax.axis_index("mp").astype(jnp.int32)[None]
    width = out_weight.shape[1] // lax.axis_size("mp")
    weight3 = jnp.transpose(in_weight, (1, 0, 2))
    out_weight = pltpu.with_memory_space_constraint(out_weight, pltpu.HBM)
    raw, product, block, keep, twice, visible, taps, rates, residues, skip = front(
        position, segment_ids.reshape(-1, 128), tokens, norm_gain[None], weight3, short_filter, rates, residues, skip[None])
    cuts = shards.bit_length() - 1
    each = product.shape[0] // cuts
    group, spans, arrived, parts, windows = block, [], [], [], []
    for k in range(cuts):
        span = 1 << k
        other = lax.ppermute(group, "ctx", [(a, a ^ span) for a in range(shards)])
        spans.append(span)
        arrived.append(other)
        *part, window = local_pass(
            k * each, each, min(k, 1), lane_position, product, keep, twice, raw, taps, rates, residues, skip,
            out_weight, width, group)
        parts.append(part)
        windows.append(window)
        if k < cuts - 1:
            group = join(span, T, position, segment_ids, group, other, taps, rates, part[0])
    gated, send, mine, third = gate(T, spans, arrived, position, lane_position, segment_ids, parts, block, visible, taps, rates,
                             skip, windows[0], out_weight, width)
    return scatter_line(lane_position, gated, send, mine, windows[1], third, out_weight, width)


def solution(mesh):
    placed = (
        P("ctx", None),
        P(),
        P(None, None, "mp"),
        P(None, None, "mp"),
        P(None, "mp"),
        P(None, "mp"),
        P("mp"),
        P("mp", None),
        P(),
    )
    shards, groups = mesh.shape["ctx"], mesh.shape["mp"]

    def body(tokens, norm_gain, in_weight, *rest):
        suits = groups == 8 and shards & (shards - 1) == 0 and shards > 2
        suits = suits and in_weight.shape[2] % 512 == 0 and in_weight.shape[0] % 2048 == 0
        suits = suits and tokens.shape[0] % 64 == 0 and rest[-1].shape[0] % 128 == 0 and rest[1].shape[0] % 8 == 0
        return (local if suits else general)(tokens, norm_gain, in_weight, *rest)

    return jax.shard_map(
        body, mesh=mesh, in_specs=placed, out_specs=P("ctx", "mp"), check_vma=False
    )
```

```python
import functools
import jax
import jax.numpy as jnp
from jax import lax
from jax.experimental import pallas as pl
from jax.experimental.pallas import tpu as pltpu
from jax.sharding import PartitionSpec as P

epsilon = 1e-06
f32 = jnp.float32
bf16 = jnp.bfloat16

PARTS = 8
HEAD = 16
MIB = 1 << 20


def vmem():
    return pl.BlockSpec(memory_space=pltpu.VMEM)


def smem():
    return pl.BlockSpec(memory_space=pltpu.SMEM)


def same_id(ids_ref, a, b):
    def get(t):
        return jnp.where(t < 0, -1, ids_ref[jnp.maximum(t, 0)])

    return (get(a) == get(b)).astype(f32)


def hbm():
    return pl.BlockSpec(memory_space=pltpu.HBM)


def front_kernel(
    geometry, position, ids_ref, tokens_ref, gain_ref, weight_ref, taps_ref, rates_ref, residues_ref, skip_ref,
    raw_out, prod_out, block_out, keep_out, twice, visible_out, taps, rates, residues, skip,
    ids, gain, tok, normed, ring, total, proj, head, idcol, near, ending, sem, tok_sem, ring_sem,
):
    T, depth, channels, cb_size, kc_size, slots, poles = geometry
    run = T // PARTS
    kcs, cbs = depth // kc_size, channels // cb_size
    steps = kcs * cbs
    base = pl.multiple_of(position[0] * T, 8)

    def fetch(step):
        cb, kc, slot = step // kcs, step % kcs, step % slots
        return pltpu.make_async_copy(
            weight_ref.at[:, pl.ds(pl.multiple_of(kc * kc_size, kc_size), kc_size),
                          pl.ds(pl.multiple_of(cb * cb_size, cb_size), cb_size)],
            ring.at[slot], ring_sem.at[slot])

    small = [
        pltpu.make_async_copy(a, b, sem.at[i])
        for i, (a, b) in enumerate(
            ((ids_ref, ids), (gain_ref, gain), (taps_ref, taps), (rates_ref, rates), (residues_ref, residues),
             (skip_ref, skip)))
    ]
    small[0].start()
    small[1].start()
    chunk = T // 4
    tok_copies = [
        pltpu.make_async_copy(tokens_ref.at[pl.ds(c * chunk, chunk)], tok.at[pl.ds(c * chunk, chunk)], tok_sem.at[c])
        for c in range(4)
    ]
    for copy in tok_copies:
        copy.start()
    for copy in small[2:]:
        copy.start()
    for s in range(min(slots, steps)):
        fetch(s).start()

    small[0].wait()
    idcol[0:8, :] = jnp.full((8, 128), -1.0, f32)
    for b in range(ids.shape[0]):
        row = ids[b : b + 1, :].astype(f32)
        idcol[8 + b * 128 : 8 + (b + 1) * 128, :] = jnp.broadcast_to(row, (128, 128)).T
    near[...] = idcol[pl.ds(base, T + 8), :]
    here = near[8 : 8 + T, :]
    keep_out[...] = (here == near[7 : 7 + T, :]).astype(f32)
    twice[...] = (here == near[6 : 6 + T, :]).astype(f32)
    ending[...] = (here == near[7 + T : 8 + T, :]).astype(f32)
    before = near[pl.ds(7, PARTS, stride=run), :]
    for i in range(run):
        visible_out[i * 8 : (i + 1) * 8, :] = (near[pl.ds(8 + i, PARTS, stride=run), :] == before).astype(f32)
    for i in range(2):
        proj[i, 0:8, :] = jnp.zeros((8, cb_size), f32)
    raw_out[0:8, :] = jnp.zeros((8, channels), f32)
    head[...] = jnp.zeros(head.shape, f32)
    small[1].wait()

    def norm_rows(g, _):
        part = pl.ds(pl.multiple_of(g * 16, 16), 16)
        x = tok[part, :].astype(f32)
        scale = lax.rsqrt(jnp.sum(x * x, axis=-1, keepdims=True) * (1.0 / depth) + epsilon)
        normed[part, :] = (x * scale * gain[...]).astype(bf16)
        return 0

    for c, copy in enumerate(tok_copies):
        copy.wait()
        lax.fori_loop(c * chunk // 16, (c + 1) * chunk // 16, norm_rows, 0)
    for copy in small[2:]:
        copy.wait()

    def epilogue(cb):
        cols = pl.ds(pl.multiple_of(cb * cb_size, cb_size), cb_size)
        feats = []
        m1 = jnp.concatenate([keep_out[...]] * (cb_size // 128), axis=1)
        m2 = jnp.concatenate([twice[...]] * (cb_size // 128), axis=1)
        query = total[0].astype(bf16).astype(f32)
        raw_out[8 : 8 + T, cols] = query
        head[4:6, :] = query[T - 2 : T]
        for i in range(2):
            p = total[i + 1].astype(bf16).astype(f32)
            proj[i, 8 : 8 + T, :] = p
            tap = [taps[j, i + 1 : i + 2, cols] for j in range(3)]
            feats.append(
                tap[0] * p + m1 * (tap[1] * proj[i, 7 : 7 + T, :]) + m2 * (tap[2] * proj[i, 6 : 6 + T, :]))
            head[2 * i : 2 * i + 2, :] = proj[i, 8:10, :]
            head[6 + 2 * i : 8 + 2 * i, :] = proj[i, 6 + T : 8 + T, :]
        block_out[poles : poles + HEAD, cols] = head[...].astype(bf16)
        product = feats[0] * feats[1]
        back = 7.0 - lax.broadcasted_iota(jnp.int32, (8, 128), 0).astype(f32)
        for lane in range(cb_size // 128):
            tile = cb * (cb_size // 128) + lane
            lanes = pl.ds(pl.multiple_of(tile * 128, 128), 128)
            prod_out[tile] = product[:, lane * 128 : lane * 128 + 128]
            r16 = rates[:, lanes]
            jump = jnp.exp(-8.0 * r16)
            leap = [jnp.broadcast_to(jump[n : n + 1], (8, 128)) for n in range(poles)]

            def eight(g, sums):
                part = pl.ds(pl.multiple_of(g * 8, 8), 8)
                p = prod_out[tile, part, :] * ending[part, :]
                return tuple(sums[n] * leap[n] + p for n in range(poles))

            sums = lax.fori_loop(
                0, T // 8, eight, tuple(jnp.zeros((8, 128), f32) for _ in range(poles)), unroll=4)
            ends = [
                jnp.sum(sums[n] * jnp.exp(-back * r16[n : n + 1]), axis=0, keepdims=True) for n in range(poles)
            ]
            block_out[0:poles, lanes] = jnp.concatenate(ends, axis=0).astype(bf16)

    def step_body(step, _):
        cb, kc, slot = step // kcs, step % kcs, step % slots
        fetch(step).wait()
        lhs = normed[:, pl.ds(pl.multiple_of(kc * kc_size, kc_size), kc_size)]
        for i in range(3):
            part = jnp.dot(lhs, ring[slot, i], preferred_element_type=f32)
            total[i] = jnp.where(kc == 0, part, total[i] + part)

        @pl.when(step + slots < steps)
        def _():
            fetch(step + slots).start()

        @pl.when(kc == kcs - 1)
        def _():
            epilogue(cb)

        return 0

    total[...] = jnp.zeros(total.shape, f32)
    lax.fori_loop(0, steps, step_body, 0)


def front(position, ids2, tokens, gain, weight3, taps, rates, residues, skip):
    T, depth = tokens.shape
    channels, poles = weight3.shape[2], rates.shape[0]
    cb_size, kc_size, slots = 256, 2048, 5
    geometry = (T, depth, channels, cb_size, kc_size, slots, poles)
    kept = [pltpu.VMEM(a.shape, a.dtype) for a in (taps, rates, residues, skip)]
    ids2, tokens, gain, weight3, taps, rates, residues, skip = [
        pltpu.with_memory_space_constraint(a, pltpu.HBM)
        for a in (ids2, tokens, gain, weight3, taps, rates, residues, skip)
    ]
    return pl.pallas_call(
        functools.partial(front_kernel, geometry),
        out_shape=[
            jax.ShapeDtypeStruct((T + 8, channels), f32),
            jax.ShapeDtypeStruct((channels // 128, T, 128), f32),
            jax.ShapeDtypeStruct((poles + HEAD, channels), bf16),
            jax.ShapeDtypeStruct((T, 128), f32),
            jax.ShapeDtypeStruct((T, 128), f32),
            jax.ShapeDtypeStruct((T, 128), f32),
        ] + kept,
        in_specs=[smem()] + [hbm()] * 8,
        out_specs=[vmem()] * 10,
        scratch_shapes=[
            pltpu.VMEM(ids2.shape, ids2.dtype),
            pltpu.VMEM(gain.shape, f32),
            pltpu.VMEM((T, depth), bf16),
            pltpu.VMEM((T, depth), bf16),
            pltpu.VMEM((slots, 3, kc_size, cb_size), bf16),
            pltpu.VMEM((3, T, cb_size), f32),
            pltpu.VMEM((2, T + 8, cb_size), f32),
            pltpu.VMEM((HEAD, cb_size), f32),
            pltpu.VMEM((ids2.shape[0] * 128 + 8, 128), f32),
            pltpu.VMEM((T + 8, 128), f32),
            pltpu.VMEM((T, 128), f32),
            pltpu.SemaphoreType.DMA((6,)),
            pltpu.SemaphoreType.DMA((4,)),
            pltpu.SemaphoreType.DMA((slots,)),
        ],
        compiler_params=pltpu.CompilerParams(vmem_limit_bytes=28 * MIB),
        name="front",
    )(position, ids2, tokens, gain, weight3, taps, rates, residues, skip)


def expm1(x):
    series = jnp.ones_like(x)
    for k in range(9, 1, -1):
        series = 1.0 + series * x * (1.0 / k)
    return jnp.where(jnp.abs(x) < 0.5, x * series, jnp.exp(x) - 1.0)


def local_kernel(
    poles, first, slot, lane_position, prod_ref, keep_ref, twice_ref, raw_ref, taps_ref, rates_ref, residues_ref, skip_ref,
    out_ref, _, local_out, state_out, pole_out, query_out, window_out, sem,
):
    copy = columns(lane_position[0], slot, out_ref, window_out, sem)
    copy.start()
    tiles, T, _ = local_out.shape
    run = T // PARTS
    mine = slice(first * 128, (first + tiles) * 128)
    pole_out[...] = residues_ref[:, mine] * jnp.sqrt(-expm1(-2.0 * rates_ref[:, mine]))

    def tile_body(tile, _):
        lanes = pl.ds(pl.multiple_of((first + tile) * 128, 128), 128)
        d16 = jnp.exp(-rates_ref[:, lanes])
        w16 = pole_out[:, pl.ds(pl.multiple_of(tile * 128, 128), 128)]
        decay = [jnp.broadcast_to(d16[n : n + 1], (8, 128)) for n in range(poles)]
        weight = [jnp.broadcast_to(w16[n : n + 1], (8, 128)) for n in range(poles)]
        skip = skip_ref[0:1, lanes]

        def token(i, states):
            at = pl.ds(i, PARTS, stride=run)
            p, keep = prod_ref[first + tile, at, :], keep_ref[at, :]
            after = [states[n] * decay[n] * keep + p for n in range(poles)]
            local_out[tile, at, :] = tree([skip * p] + [weight[n] * after[n] for n in range(poles)])
            return tuple(after)

        states = lax.fori_loop(0, run, token, tuple(jnp.zeros((8, 128), f32) for _ in range(poles)), unroll=2)
        for n in range(poles):
            state_out[tile, pl.ds(n, PARTS, stride=poles), :] = states[n]
        tap = [taps_ref[j, 0:1, lanes] for j in range(3)]
        query_out[tile] = (
            tap[0] * raw_ref[8 : 8 + T, lanes]
            + keep_ref[...] * (tap[1] * raw_ref[7 : 7 + T, lanes])
            + twice_ref[...] * (tap[2] * raw_ref[6 : 6 + T, lanes]))
        return 0

    lax.fori_loop(0, tiles, tile_body, 0)
    copy.wait()


def tree(terms):
    while len(terms) > 1:
        terms = [a + b for a, b in zip(terms[0::2], terms[1::2])] + terms[len(terms) // 2 * 2 :]
    return terms[0]


def local_pass(
    first, tiles, slot, lane_position, product, keep, twice, raw, taps, rates, residues, skip, out_weight, width, after,
):
    T, poles = product.shape[1], rates.shape[0]
    return pl.pallas_call(
        functools.partial(local_kernel, poles, first, slot),
        out_shape=(
            jax.ShapeDtypeStruct((tiles, T, 128), f32),
            jax.ShapeDtypeStruct((tiles, PARTS * poles, 128), f32),
            jax.ShapeDtypeStruct((poles, tiles * 128), f32),
            jax.ShapeDtypeStruct((tiles, T, 128), f32),
            jax.ShapeDtypeStruct((out_weight.shape[0], 2 * width), bf16),
        ),
        in_specs=[smem()] + [vmem()] * 8 + [hbm(), pl.BlockSpec(memory_space=pl.ANY)],
        out_specs=[vmem()] * 5,
        scratch_shapes=[pltpu.SemaphoreType.DMA((STREAMS,))],
        compiler_params=pltpu.CompilerParams(vmem_limit_bytes=8 * MIB),
        cost_estimate=pl.CostEstimate(flops=6 * T * poles * tiles * 128, bytes_accessed=8 * MIB, transcendentals=0),
        name="local_pass",
    )(lane_position, product, keep, twice, raw, taps, rates, residues, skip, out_weight, after)


def first_products(first, last, taps, ids_ref, base):
    s01, s0m1 = same_id(ids_ref, base + 1, base), same_id(ids_ref, base, base - 1)
    s0m2, s1m1 = same_id(ids_ref, base, base - 2), same_id(ids_ref, base + 1, base - 1)

    def shift(i):
        near, far = last[i][1:2], last[i][0:1]
        t1, t2 = taps[1][i : i + 1], taps[2][i : i + 1]
        return s0m1 * (t1 * near) + s0m2 * (t2 * far), s1m1 * (t2 * near)

    def plain(i):
        t0, t1 = taps[0][i : i + 1], taps[1][i : i + 1]
        return t0 * first[i][0:1], t0 * first[i][1:2] + s01 * (t1 * first[i][0:1])

    k, v, dk, dv = plain(1), plain(2), shift(1), shift(2)
    delta = [(k[j] + dk[j]) * (v[j] + dv[j]) - k[j] * v[j] for j in range(2)]
    return shift(0), delta


def unpack(block, poles):
    first = [None, block[poles : poles + 2], block[poles + 2 : poles + 4]]
    last = [block[poles + 4 + 2 * i : poles + 6 + 2 * i] for i in range(3)]
    return block[0:poles], first, last


def joined_state(low_state, low_last, up_state, up_first, taps, rates, ids_ref, base, length):
    _, delta = first_products(up_first, low_last, taps, ids_ref, base)
    grown = low_state + delta[0] * jnp.exp(rates) + delta[1] * jnp.exp(2.0 * rates)
    open_ = same_id(ids_ref, base + length - 1, base - 1)
    return up_state + grown * (jnp.exp(-rates * jnp.float32(length)) * open_)


def join_kernel(T, poles, span, position, ids_ref, mine_ref, other_ref, taps_ref, rates_ref, _, out):
    me = position[0]
    is_upper = (me // span) % 2 == 1
    base = (me // (2 * span)) * (2 * span * T) + span * T
    mine, other = mine_ref[...].astype(f32), other_ref[...].astype(f32)
    lower, upper = jnp.where(is_upper, other, mine), jnp.where(is_upper, mine, other)
    taps = [taps_ref[j] for j in range(3)]
    low_state, _, low_last = unpack(lower, poles)
    up_state, up_first, _ = unpack(upper, poles)
    state = joined_state(low_state, low_last, up_state, up_first, taps, rates_ref[...], ids_ref, base, span * T)
    out[0:poles, :] = state.astype(bf16)
    row = lax.broadcasted_iota(jnp.int32, (HEAD, lower.shape[1]), 0)
    out[poles : poles + HEAD, :] = jnp.where(row < 4, lower[poles:], upper[poles:]).astype(bf16)


def join(span, T, position, ids, mine, other, taps, rates, after):
    poles = rates.shape[0]
    return pl.pallas_call(
        functools.partial(join_kernel, T, poles, span),
        out_shape=jax.ShapeDtypeStruct(mine.shape, bf16),
        in_specs=[smem(), smem()] + [vmem()] * 4 + [pl.BlockSpec(memory_space=pl.ANY)],
        out_specs=vmem(),
        compiler_params=pltpu.CompilerParams(vmem_limit_bytes=4 * MIB),
        name="join",
    )(position, ids, mine, other, taps, rates, after)


def gate_kernel(
    T, poles, spans, cuts, position, lane_position, ids_ref, block_ref, visible_ref, taps_ref, rates_ref, skip_ref,
    window_ref, out_ref, *rest,
):
    arrived, rest = rest[: len(spans)], rest[len(spans) :]
    parts, rest = [rest[4 * c : 4 * c + 4] for c in range(cuts)], rest[4 * cuts :]
    gated_out, send_out, third_out, carry, full, sem = rest
    run = T // PARTS
    tiles = block_ref.shape[1] // 128
    copy = columns(lane_position[0], 2, out_ref, third_out, sem)
    copy.start()
    me = position[0]
    base = me * T
    taps = [taps_ref[j] for j in range(3)]
    rates, skip = rates_ref[...], skip_ref[...]
    weight = jnp.concatenate([pole_ref[...] for _, _, pole_ref, _ in parts], axis=1)
    each = tiles // cuts
    prior = jnp.zeros(block_ref.shape, f32)
    prior_state, prior_first, prior_last = unpack(prior, poles)
    for span, ref in zip(spans, arrived):
        state, first, last = unpack(ref[...].astype(f32), poles)
        upper, held = (me // span) % 2 == 1, me % span
        if span == 1:
            both = state
        else:
            both = joined_state(
                state, last, prior_state, prior_first, taps, rates, ids_ref, (me - held) * T, held * T)
        fresh = upper & (held == 0)
        prior_state = jnp.where(fresh, state, jnp.where(upper, both, prior_state))
        prior_first = [None] + [jnp.where(upper, first[i], prior_first[i]) for i in (1, 2)]
        prior_last = [jnp.where(fresh, last[i], prior_last[i]) for i in range(3)]
    _, first, _ = unpack(block_ref[...].astype(f32), poles)
    q_shift, delta = first_products(first, prior_last, taps, ids_ref, base)
    second = delta[1] * jnp.exp(rates)
    now = prior_state + (delta[0] + second) * jnp.exp(rates)
    fix0 = skip * delta[0] - jnp.sum(weight * second, axis=0, keepdims=True)
    fix1 = skip * delta[1]
    jump = jnp.exp(-rates * float(run))
    for s in range(PARTS):
        part = slice(s * poles, (s + 1) * poles)
        began = weight * now
        for tile in range(tiles):
            carry[tile, part, :] = began[:, tile * 128 : tile * 128 + 128]
        if s < PARTS - 1:
            whole = same_id(ids_ref, base + s * run + run - 1, base + s * run - 1)
            ends = jnp.concatenate([parts[tile // each][1][tile % each, part, :] for tile in range(tiles)], axis=1)
            now = now * (jump * whole) + ends

    def lane_body(cut, inner, _):
        tile = cut * each + inner
        lanes = pl.ds(pl.multiple_of(tile * 128, 128), 128)
        d16 = jnp.exp(-rates_ref[:, lanes])
        decay = [jnp.broadcast_to(d16[n : n + 1], (8, 128)) for n in range(poles)]
        start = tuple(carry[tile, pl.ds(n, PARTS, stride=poles), :] for n in range(poles))

        def token(i, states):
            after = [states[n] * decay[n] for n in range(poles)]
            see = visible_ref[pl.ds(pl.multiple_of(i * 8, 8), 8), :]
            at = pl.ds(i, PARTS, stride=run)
            full[tile, at, :] = parts[cut][0][inner, at, :] + see * tree(list(after))
            return tuple(after)

        lax.fori_loop(0, run, token, start, unroll=4)
        return 0

    for cut in range(cuts):
        lax.fori_loop(0, each, functools.partial(lane_body, cut), 0)
    row = lax.broadcasted_iota(jnp.int32, (16, 128), 0)
    for tile in range(tiles):
        lanes = slice(tile * 128, tile * 128 + 128)
        query_ref = parts[tile // each][3].at[tile % each]
        gated_out[:, lanes] = (query_ref[...] * full[tile]).astype(bf16)
        top_q, top = query_ref[0:16, :], full[tile, 0:16, :]
        top_q = top_q + jnp.where(row == 0, q_shift[0][:, lanes], 0.0) + jnp.where(row == 1, q_shift[1][:, lanes], 0.0)
        top = top + jnp.where(row == 0, fix0[:, lanes], 0.0) + jnp.where(row == 1, fix1[:, lanes], 0.0)
        gated_out[0:16, lanes] = (top_q * top).astype(bf16)
    share(lane_position[0], gated_out, window_ref, send_out, None)
    copy.wait()


def target(index, slot):
    chip = index // 2
    if slot == 0:
        return 3 - 3 * (chip % 2)
    if slot == 1:
        return jnp.where(chip < 2, 2, 1)
    if slot == 2:
        return jnp.where(chip < 2, 1 + 2 * chip, 2 * (chip - 2))
    return chip


class Copies:
    def __init__(self, copies):
        self.copies = copies

    def start(self):
        for copy in self.copies:
            copy.start()

    def wait(self):
        for copy in self.copies:
            copy.wait()


STREAMS = 4


def columns(index, slot, out_ref, window, sem):
    channels, both = window.shape
    start = pl.multiple_of(target(index, slot) * both, both)
    each = channels // STREAMS
    return Copies([
        pltpu.make_async_copy(
            out_ref.at[pl.ds(k * each, each), pl.ds(start, both)], window.at[pl.ds(k * each, each)], sem.at[k])
        for k in range(STREAMS)
    ])


def share(index, gated_ref, window, send_out, mine_out):
    width = window.shape[1] // 2
    tile = 256
    core = index % 2

    for out, half in ((send_out, 1 - core), (mine_out, core)):
        for j in range(width // tile if out is not None else 0):
            at = slice(j * tile, j * tile + tile)
            cols = pl.ds(pl.multiple_of(half * width + j * tile, tile), tile)
            out[:, at] = jnp.dot(gated_ref[...], window[:, cols], preferred_element_type=f32).astype(out.dtype)


def share_kernel(count, lane_position, gated_ref, *rest):
    windows, outs = rest[:count], rest[count:]
    for k, window in enumerate(windows):
        share(lane_position[0], gated_ref, window, outs[2 * k], outs[2 * k + 1])


def shares(lane_position, gated, windows, width):
    T, channels = gated.shape
    count = len(windows)
    return pl.pallas_call(
        functools.partial(share_kernel, count),
        out_shape=[jax.ShapeDtypeStruct((T, width), d) for _ in windows for d in (bf16, f32)],
        in_specs=[smem(), vmem()] + [vmem()] * count,
        out_specs=[vmem()] * (2 * count),
        compiler_params=pltpu.CompilerParams(vmem_limit_bytes=4 * MIB),
        cost_estimate=pl.CostEstimate(
            flops=4 * T * channels * width * count, bytes_accessed=4 * channels * width * count, transcendentals=0),
        name="shares",
    )(lane_position, gated, *windows)


def second_kernel(lane_position, gated_ref, first_ref, second_ref, first_mine, send_out, mine_out):
    share(lane_position[0], gated_ref, second_ref, send_out, mine_out)
    share(lane_position[0], gated_ref, first_ref, None, first_mine)


def second_shares(lane_position, gated, first, second, width):
    T, channels = gated.shape
    return pl.pallas_call(
        second_kernel,
        out_shape=[jax.ShapeDtypeStruct((T, width), d) for d in (f32, bf16, f32)],
        in_specs=[smem()] + [vmem()] * 3,
        out_specs=[vmem()] * 3,
        compiler_params=pltpu.CompilerParams(vmem_limit_bytes=4 * MIB),
        cost_estimate=pl.CostEstimate(
            flops=6 * T * channels * width, bytes_accessed=6 * channels * width, transcendentals=0),
        name="second_shares",
    )(lane_position, gated, first, second)


def late_share_kernel(slot, lane_position, gated_ref, out_ref, send_out, mine_out, window, sem):
    copy = columns(lane_position[0], slot, out_ref, window, sem)
    copy.start()
    copy.wait()
    share(lane_position[0], gated_ref, window, send_out, mine_out)


def late_share(slot, lane_position, gated, out_weight, width):
    T, channels = gated.shape
    return pl.pallas_call(
        functools.partial(late_share_kernel, slot),
        out_shape=[jax.ShapeDtypeStruct((T, width), d) for d in (bf16, f32)],
        in_specs=[smem(), vmem(), hbm()],
        out_specs=[vmem()] * 2,
        scratch_shapes=[pltpu.VMEM((channels, 2 * width), bf16), pltpu.SemaphoreType.DMA((STREAMS,))],
        compiler_params=pltpu.CompilerParams(vmem_limit_bytes=6 * MIB),
        cost_estimate=pl.CostEstimate(
            flops=4 * T * channels * width, bytes_accessed=4 * channels * width, transcendentals=0),
        name="late_share",
    )(lane_position, gated, out_weight)


def gate(T, spans, arrived, position, lane_position, ids, parts, block, visible, taps, rates, skip, window, out_weight, width):
    poles, channels = rates.shape
    return pl.pallas_call(
        functools.partial(gate_kernel, T, poles, tuple(spans), len(parts)),
        out_shape=[
            jax.ShapeDtypeStruct((T, channels), bf16),
            jax.ShapeDtypeStruct((T, width), bf16),
            pltpu.VMEM(window.shape, bf16),
        ],
        in_specs=[smem()] * 3 + [vmem()] * 6 + [hbm()] + [vmem()] * (len(spans) + 4 * len(parts)),
        out_specs=[vmem()] * 3,
        scratch_shapes=[
            pltpu.VMEM((channels // 128, PARTS * poles, 128), f32),
            pltpu.VMEM((channels // 128, T, 128), f32),
            pltpu.SemaphoreType.DMA((STREAMS,)),
        ],
        compiler_params=pltpu.CompilerParams(vmem_limit_bytes=8 * MIB),
        name="gate",
    )(position, lane_position, ids, block, visible, taps, rates, skip, window, out_weight, *arrived,
      *[a for part in parts for a in part])


def total(*terms):
    return functools.reduce(lambda a, b: a + b, [t.astype(f32) for t in terms]).astype(bf16)


def merge_kernel(count, has_inner, lane_position, *rest):
    terms, picks, out = rest[:count], rest[count:-1], rest[-1]
    value = terms[0][...].astype(f32)
    for term in terms[1:]:
        value = value + term[...].astype(f32)
    chip = lane_position[0] // 2
    inner = (chip == 1) | (chip == 2)
    for pick, wanted in zip(picks, (inner, jnp.logical_not(inner)) if has_inner else (jnp.logical_not(inner),)):
        value = value + jnp.where(wanted, pick[...].astype(f32), 0.0)
    out[...] = value.astype(out.dtype)


def merge(lane_position, dtype, terms, inner=None, outer=None):
    picks = [a for a in (inner, outer) if a is not None]
    terms = [pltpu.with_memory_space_constraint(a, pltpu.VMEM) for a in (*terms, *picks)]
    return pl.pallas_call(
        functools.partial(merge_kernel, len(terms) - len(picks), inner is not None),
        out_shape=jax.ShapeDtypeStruct(terms[0].shape, dtype),
        in_specs=[smem()] + [vmem()] * len(terms),
        out_specs=vmem(),
        compiler_params=pltpu.CompilerParams(vmem_limit_bytes=3 * MIB),
        name="merge",
    )(lane_position, *terms)


def halves_kernel(_, mine_ref, other_ref, top_out, bottom_out):
    rows = top_out.shape[0]
    value = (mine_ref[...] + other_ref[...].astype(f32)).astype(bf16)
    top_out[...] = value[:rows]
    bottom_out[...] = value[rows:]


def halves(lane_position, mine, other):
    terms = [pltpu.with_memory_space_constraint(a, pltpu.VMEM) for a in (mine, other)]
    return pl.pallas_call(
        halves_kernel,
        out_shape=(jax.ShapeDtypeStruct((mine.shape[0] // 2, mine.shape[1]), bf16),) * 2,
        in_specs=[smem()] + [vmem()] * 2,
        out_specs=[vmem()] * 2,
        compiler_params=pltpu.CompilerParams(vmem_limit_bytes=3 * MIB),
        name="halves",
    )(lane_position, *terms)


def own_kernel(lane_position, mine_ref, other_ref, near_ref, middle_ref, end_ref, again_ref, out):
    rows = middle_ref.shape[0]
    chip = lane_position[0] // 2
    outer = (chip == 0) | (chip == 3)
    value = mine_ref[...] + other_ref[...].astype(f32) + jnp.where(outer, near_ref[...].astype(f32), 0.0)
    out[0:rows, :] = value[:rows] + (middle_ref[...].astype(f32) + end_ref[...].astype(f32))
    out[rows:, :] = value[rows:] + again_ref[...].astype(f32)


def gather_own(lane_position, mine, *others):
    terms = [pltpu.with_memory_space_constraint(a, pltpu.VMEM) for a in (mine, *others)]
    return pl.pallas_call(
        own_kernel,
        out_shape=jax.ShapeDtypeStruct(mine.shape, f32),
        in_specs=[smem()] + [vmem()] * len(terms),
        out_specs=vmem(),
        compiler_params=pltpu.CompilerParams(vmem_limit_bytes=3 * MIB),
        name="gather_own",
    )(lane_position, *terms)


def scatter_line(lane_position, gated, send, windows, third, out_weight, width):
    pair = [(m, m ^ 1) for m in range(8)]

    def along(hops):
        return [(a * 2 + c, b * 2 + c) for a, b in hops for c in range(2)]

    near = along([(0, 1), (1, 0), (2, 3), (3, 2)])
    traded = lax.ppermute(send, "mp", pair)
    first_mine, send, mine = second_shares(lane_position, gated, *windows, width)
    far = merge(lane_position, bf16, (first_mine, traded))
    from_near = lax.ppermute(far, "mp", near)
    top, bottom = halves(lane_position, mine, lax.ppermute(send, "mp", pair))
    beside = lax.ppermute(bottom, "mp", near)
    from_middle = lax.ppermute(top, "mp", along([(1, 2), (2, 1)]))
    from_end = lax.ppermute(top, "mp", along([(0, 2), (3, 1)]))
    send2, mine2 = shares(lane_position, gated, [third], width)
    mine2 = merge(lane_position, f32, (mine2, lax.ppermute(send2, "mp", pair)))
    onward = merge(lane_position, bf16, (mine2,), inner=from_near)
    from_round = lax.ppermute(onward, "mp", along([(0, 1), (1, 3), (3, 2), (2, 0)]))
    send3, mine3 = late_share(3, lane_position, gated, out_weight, width)
    both = merge(lane_position, bf16, (bottom, beside))
    again = lax.ppermute(both, "mp", along([(1, 2), (2, 1)]))
    own = gather_own(lane_position, mine3, lax.ppermute(send3, "mp", pair), from_near, from_middle, from_end, again)
    return total(own, from_round)


def shifted(value, axis, steps):
    count = lax.axis_size(axis)
    leading, last = (max(0, -steps), min(count, count - steps))
    return lax.ppermute(value, axis, [(source, source + steps) for source in range(leading, last)])


def project(block, norm_gain, weights):
    floats = block.astype(jnp.float32)
    mean_square = jnp.mean(floats * floats, axis=-1, keepdims=True)
    normed = (floats * lax.rsqrt(mean_square + epsilon) * norm_gain[None, :]).astype(jnp.bfloat16)
    return jnp.dot(normed, weights, preferred_element_type=jnp.float32).astype(jnp.bfloat16)


def general(
    tokens, norm_gain, in_weight, short_filter, rates, residues, skip, out_weight, segment_ids
):
    tok_rows = tokens.shape[0]
    model_width = tokens.shape[1]
    channels = in_weight.shape[2]
    filter_taps = short_filter.shape[0]
    pole_count = rates.shape[0]
    device_index = lax.axis_index("ctx")
    row_offset = device_index * tok_rows
    weights = in_weight.reshape(model_width, 3 * channels)
    projected = project(tokens, norm_gain, weights)
    previous = shifted(projected[tok_rows - (filter_taps - 1) :], "ctx", 1)
    extended = jnp.concatenate([previous, projected], axis=0)
    padded_ids = jnp.concatenate([jnp.full((filter_taps,), -1, jnp.int32), segment_ids], axis=0)
    window = lax.dynamic_slice_in_dim(padded_ids, row_offset, tok_rows + filter_taps, 0)
    local_ids = window[filter_taps:]
    taps_table = short_filter.reshape(filter_taps, 3 * channels)
    featured = jnp.zeros((tok_rows, 3 * channels), jnp.float32)
    for lag_index in range(filter_taps):
        begin = filter_taps - 1 - lag_index
        lagged = extended[begin : begin + tok_rows].astype(jnp.float32)
        matches = window[filter_taps - lag_index : filter_taps - lag_index + tok_rows] == local_ids
        term = taps_table[lag_index][None, :] * lagged
        featured = featured + jnp.where(matches[:, None], term, jnp.zeros_like(term))
    query_part = featured[:, :channels]
    key_part = featured[:, channels : 2 * channels]
    value_part = featured[:, 2 * channels :]
    product = key_part * value_part
    offsets = jnp.arange(tok_rows, dtype=jnp.float32)
    center = float(tok_rows // 2)
    growth = jnp.exp(-(offsets - center)[:, None, None] * rates[None])
    shrinkage = jnp.exp((offsets - center)[:, None, None] * rates[None])
    weighted = (shrinkage * product[:, None, :]).reshape(tok_rows, pole_count * channels)
    visible = (offsets[:, None] >= offsets[None, :]) & (local_ids[:, None] == local_ids[None, :])
    in_block = jnp.dot(visible.astype(jnp.float32), weighted, precision=lax.Precision.HIGHEST)
    in_block = in_block.reshape(tok_rows, pole_count, channels) * growth
    survives = local_ids == window[filter_taps - 1]
    block_factor = jnp.exp(-rates * tok_rows)
    block_end = in_block[tok_rows - 1]
    block_ends = lax.all_gather(block_end[None], "ctx", axis=0, tiled=True)
    shard_count = segment_ids.shape[0] // tok_rows
    last_ids = segment_ids.reshape(shard_count, tok_rows)[:, tok_rows - 1]
    prior_ids = jnp.concatenate([jnp.full((1,), -1, jnp.int32), last_ids[:-1]], axis=0)
    shard_decays = block_factor[None] * (last_ids == prior_ids).astype(jnp.float32)[:, None, None]

    def absorb(running, inputs):
        shard, factor, shard_end = inputs
        advanced = running * factor + shard_end
        return (jnp.where(shard < device_index, advanced, running), None)

    incoming, _ = lax.scan(
        absorb,
        jnp.zeros_like(block_end),
        (jnp.arange(shard_count, dtype=jnp.int32), shard_decays, block_ends),
    )
    carried = incoming[None] * jnp.exp(-(offsets + 1.0)[:, None, None] * rates[None])
    carried = carried * survives.astype(jnp.float32)[:, None, None]
    states = in_block + carried
    pole_weight = residues * jnp.sqrt(-jnp.expm1(-2.0 * rates))
    longconv = jnp.sum(pole_weight[None] * states, axis=1)
    gated = (query_part * (longconv + skip[None, :] * product)).astype(jnp.bfloat16)
    partial_terms = jnp.dot(gated, out_weight, preferred_element_type=jnp.float32)
    return lax.psum_scatter(partial_terms, "mp", scatter_dimension=1, tiled=True).astype(
        jnp.bfloat16
    )


def local(tokens, norm_gain, in_weight, short_filter, rates, residues, skip, out_weight, segment_ids):
    T = tokens.shape[0]
    shards = lax.axis_size("ctx")
    me = lax.axis_index("ctx")
    position = me.astype(jnp.int32)[None]
    lane_position = lax.axis_index("mp").astype(jnp.int32)[None]
    width = out_weight.shape[1] // lax.axis_size("mp")
    weight3 = jnp.transpose(in_weight, (1, 0, 2))
    out_weight = pltpu.with_memory_space_constraint(out_weight, pltpu.HBM)
    raw, product, block, keep, twice, visible, taps, rates, residues, skip = front(
        position, segment_ids.reshape(-1, 128), tokens, norm_gain[None], weight3, short_filter, rates, residues, skip[None])
    cuts = shards.bit_length() - 1
    each = product.shape[0] // cuts
    group, spans, arrived, parts, windows = block, [], [], [], []
    for k in range(cuts):
        span = 1 << k
        other = lax.ppermute(group, "ctx", [(a, a ^ span) for a in range(shards)])
        spans.append(span)
        arrived.append(other)
        *part, window = local_pass(
            k * each, each, min(k, 1), lane_position, product, keep, twice, raw, taps, rates, residues, skip,
            out_weight, width, group)
        parts.append(part)
        windows.append(window)
        if k < cuts - 1:
            group = join(span, T, position, segment_ids, group, other, taps, rates, part[0])
    gated, send, third = gate(T, spans, arrived, position, lane_position, segment_ids, parts, block, visible, taps, rates,
                             skip, windows[0], out_weight, width)
    return scatter_line(lane_position, gated, send, windows[:2], third, out_weight, width)


def solution(mesh):
    placed = (
        P("ctx", None),
        P(),
        P(None, None, "mp"),
        P(None, None, "mp"),
        P(None, "mp"),
        P(None, "mp"),
        P("mp"),
        P("mp", None),
        P(),
    )
    shards, groups = mesh.shape["ctx"], mesh.shape["mp"]

    def body(tokens, norm_gain, in_weight, *rest):
        suits = groups == 8 and shards & (shards - 1) == 0 and shards > 2
        suits = suits and in_weight.shape[2] % 512 == 0 and in_weight.shape[0] % 2048 == 0
        suits = suits and tokens.shape[0] % 64 == 0 and rest[-1].shape[0] % 128 == 0 and rest[1].shape[0] % 8 == 0
        return (local if suits else general)(tokens, norm_gain, in_weight, *rest)

    return jax.shard_map(
        body, mesh=mesh, in_specs=placed, out_specs=P("ctx", "mp"), check_vma=False
    )
```

```python
import functools
import jax
import jax.numpy as jnp
from jax import lax
from jax.experimental import pallas as pl
from jax.experimental.pallas import tpu as pltpu
from jax.sharding import PartitionSpec as P

epsilon = 1e-06
f32 = jnp.float32
bf16 = jnp.bfloat16

PARTS = 8
HEAD = 16
MIB = 1 << 20


def vmem():
    return pl.BlockSpec(memory_space=pltpu.VMEM)


def smem():
    return pl.BlockSpec(memory_space=pltpu.SMEM)


def same_id(ids_ref, a, b):
    def get(t):
        return jnp.where(t < 0, -1, ids_ref[jnp.maximum(t, 0)])

    return (get(a) == get(b)).astype(f32)


def hbm():
    return pl.BlockSpec(memory_space=pltpu.HBM)


def front_kernel(
    geometry, position, ids_ref, tokens_ref, gain_ref, weight_ref, taps_ref, rates_ref, residues_ref, skip_ref,
    raw_out, prod_out, block_out, keep_out, twice, visible_out, taps, rates, residues, skip,
    ids, gain, tok, normed, ring, total, proj, head, idcol, near, ending, sem, tok_sem, ring_sem,
):
    T, depth, channels, cb_size, kc_size, slots, poles = geometry
    run = T // PARTS
    kcs, cbs = depth // kc_size, channels // cb_size
    steps = kcs * cbs
    base = pl.multiple_of(position[0] * T, 8)

    def fetch(step):
        cb, kc, slot = step // kcs, step % kcs, step % slots
        return pltpu.make_async_copy(
            weight_ref.at[:, pl.ds(pl.multiple_of(kc * kc_size, kc_size), kc_size),
                          pl.ds(pl.multiple_of(cb * cb_size, cb_size), cb_size)],
            ring.at[slot], ring_sem.at[slot])

    small = [
        pltpu.make_async_copy(a, b, sem.at[i])
        for i, (a, b) in enumerate(
            ((ids_ref, ids), (gain_ref, gain), (taps_ref, taps), (rates_ref, rates), (residues_ref, residues),
             (skip_ref, skip)))
    ]
    small[0].start()
    small[1].start()
    chunk = T // 4
    tok_copies = [
        pltpu.make_async_copy(tokens_ref.at[pl.ds(c * chunk, chunk)], tok.at[pl.ds(c * chunk, chunk)], tok_sem.at[c])
        for c in range(4)
    ]
    for copy in tok_copies:
        copy.start()
    for copy in small[2:]:
        copy.start()
    for s in range(min(slots, steps)):
        fetch(s).start()

    small[0].wait()
    idcol[0:8, :] = jnp.full((8, 128), -1.0, f32)
    for b in range(ids.shape[0]):
        row = ids[b : b + 1, :].astype(f32)
        idcol[8 + b * 128 : 8 + (b + 1) * 128, :] = jnp.broadcast_to(row, (128, 128)).T
    near[...] = idcol[pl.ds(base, T + 8), :]
    here = near[8 : 8 + T, :]
    keep_out[...] = (here == near[7 : 7 + T, :]).astype(f32)
    twice[...] = (here == near[6 : 6 + T, :]).astype(f32)
    ending[...] = (here == near[7 + T : 8 + T, :]).astype(f32)
    before = near[pl.ds(7, PARTS, stride=run), :]
    for i in range(run):
        visible_out[i * 8 : (i + 1) * 8, :] = (near[pl.ds(8 + i, PARTS, stride=run), :] == before).astype(f32)
    for i in range(2):
        proj[i, 0:8, :] = jnp.zeros((8, cb_size), f32)
    raw_out[0:8, :] = jnp.zeros((8, channels), f32)
    head[...] = jnp.zeros(head.shape, f32)
    small[1].wait()

    def norm_rows(g, _):
        part = pl.ds(pl.multiple_of(g * 16, 16), 16)
        x = tok[part, :].astype(f32)
        scale = lax.rsqrt(jnp.sum(x * x, axis=-1, keepdims=True) * (1.0 / depth) + epsilon)
        normed[part, :] = (x * scale * gain[...]).astype(bf16)
        return 0

    for c, copy in enumerate(tok_copies):
        copy.wait()
        lax.fori_loop(c * chunk // 16, (c + 1) * chunk // 16, norm_rows, 0)
    for copy in small[2:]:
        copy.wait()

    def epilogue(cb):
        cols = pl.ds(pl.multiple_of(cb * cb_size, cb_size), cb_size)
        feats = []
        m1 = jnp.concatenate([keep_out[...]] * (cb_size // 128), axis=1)
        m2 = jnp.concatenate([twice[...]] * (cb_size // 128), axis=1)
        query = total[0].astype(bf16).astype(f32)
        raw_out[8 : 8 + T, cols] = query
        head[4:6, :] = query[T - 2 : T]
        for i in range(2):
            p = total[i + 1].astype(bf16).astype(f32)
            proj[i, 8 : 8 + T, :] = p
            tap = [taps[j, i + 1 : i + 2, cols] for j in range(3)]
            feats.append(
                tap[0] * p + m1 * (tap[1] * proj[i, 7 : 7 + T, :]) + m2 * (tap[2] * proj[i, 6 : 6 + T, :]))
            head[2 * i : 2 * i + 2, :] = proj[i, 8:10, :]
            head[6 + 2 * i : 8 + 2 * i, :] = proj[i, 6 + T : 8 + T, :]
        block_out[poles : poles + HEAD, cols] = head[...].astype(bf16)
        product = feats[0] * feats[1]
        back = 7.0 - lax.broadcasted_iota(jnp.int32, (8, 128), 0).astype(f32)
        for lane in range(cb_size // 128):
            tile = cb * (cb_size // 128) + lane
            lanes = pl.ds(pl.multiple_of(tile * 128, 128), 128)
            prod_out[tile] = product[:, lane * 128 : lane * 128 + 128]
            r16 = rates[:, lanes]
            jump = jnp.exp(-8.0 * r16)
            leap = [jnp.broadcast_to(jump[n : n + 1], (8, 128)) for n in range(poles)]

            def eight(g, sums):
                part = pl.ds(pl.multiple_of(g * 8, 8), 8)
                p = prod_out[tile, part, :] * ending[part, :]
                return tuple(sums[n] * leap[n] + p for n in range(poles))

            sums = lax.fori_loop(
                0, T // 8, eight, tuple(jnp.zeros((8, 128), f32) for _ in range(poles)), unroll=T // 8)
            ends = [
                jnp.sum(sums[n] * jnp.exp(-back * r16[n : n + 1]), axis=0, keepdims=True) for n in range(poles)
            ]
            block_out[0:poles, lanes] = jnp.concatenate(ends, axis=0).astype(bf16)

    def step_body(step, _):
        cb, kc, slot = step // kcs, step % kcs, step % slots
        fetch(step).wait()
        lhs = normed[:, pl.ds(pl.multiple_of(kc * kc_size, kc_size), kc_size)]
        for i in range(3):
            part = jnp.dot(lhs, ring[slot, i], preferred_element_type=f32)
            total[i] = jnp.where(kc == 0, part, total[i] + part)

        @pl.when(step + slots < steps)
        def _():
            fetch(step + slots).start()

        @pl.when(kc == kcs - 1)
        def _():
            epilogue(cb)

        return 0

    total[...] = jnp.zeros(total.shape, f32)
    lax.fori_loop(0, steps, step_body, 0)


def front(position, ids2, tokens, gain, weight3, taps, rates, residues, skip):
    T, depth = tokens.shape
    channels, poles = weight3.shape[2], rates.shape[0]
    cb_size, kc_size, slots = 256, 2048, 5
    geometry = (T, depth, channels, cb_size, kc_size, slots, poles)
    kept = [pltpu.VMEM(a.shape, a.dtype) for a in (taps, rates, residues, skip)]
    ids2, tokens, gain, weight3, taps, rates, residues, skip = [
        pltpu.with_memory_space_constraint(a, pltpu.HBM)
        for a in (ids2, tokens, gain, weight3, taps, rates, residues, skip)
    ]
    return pl.pallas_call(
        functools.partial(front_kernel, geometry),
        out_shape=[
            jax.ShapeDtypeStruct((T + 8, channels), f32),
            jax.ShapeDtypeStruct((channels // 128, T, 128), f32),
            jax.ShapeDtypeStruct((poles + HEAD, channels), bf16),
            jax.ShapeDtypeStruct((T, 128), f32),
            jax.ShapeDtypeStruct((T, 128), f32),
            jax.ShapeDtypeStruct((T, 128), f32),
        ] + kept,
        in_specs=[smem()] + [hbm()] * 8,
        out_specs=[vmem()] * 10,
        scratch_shapes=[
            pltpu.VMEM(ids2.shape, ids2.dtype),
            pltpu.VMEM(gain.shape, f32),
            pltpu.VMEM((T, depth), bf16),
            pltpu.VMEM((T, depth), bf16),
            pltpu.VMEM((slots, 3, kc_size, cb_size), bf16),
            pltpu.VMEM((3, T, cb_size), f32),
            pltpu.VMEM((2, T + 8, cb_size), f32),
            pltpu.VMEM((HEAD, cb_size), f32),
            pltpu.VMEM((ids2.shape[0] * 128 + 8, 128), f32),
            pltpu.VMEM((T + 8, 128), f32),
            pltpu.VMEM((T, 128), f32),
            pltpu.SemaphoreType.DMA((6,)),
            pltpu.SemaphoreType.DMA((4,)),
            pltpu.SemaphoreType.DMA((slots,)),
        ],
        compiler_params=pltpu.CompilerParams(vmem_limit_bytes=28 * MIB),
        name="front",
    )(position, ids2, tokens, gain, weight3, taps, rates, residues, skip)


def expm1(x):
    series = jnp.ones_like(x)
    for k in range(9, 1, -1):
        series = 1.0 + series * x * (1.0 / k)
    return jnp.where(jnp.abs(x) < 0.5, x * series, jnp.exp(x) - 1.0)


def local_kernel(
    poles, first, slot, lane_position, prod_ref, keep_ref, twice_ref, raw_ref, taps_ref, rates_ref, residues_ref, skip_ref,
    out_ref, _, local_out, state_out, pole_out, query_out, window_out, sem,
):
    copy = columns(lane_position[0], slot, out_ref, window_out, sem)
    copy.start()
    tiles, T, _ = local_out.shape
    run = T // PARTS
    mine = slice(first * 128, (first + tiles) * 128)
    pole_out[...] = residues_ref[:, mine] * jnp.sqrt(-expm1(-2.0 * rates_ref[:, mine]))

    def tile_body(tile, _):
        lanes = pl.ds(pl.multiple_of((first + tile) * 128, 128), 128)
        d16 = jnp.exp(-rates_ref[:, lanes])
        w16 = pole_out[:, pl.ds(pl.multiple_of(tile * 128, 128), 128)]
        decay = [jnp.broadcast_to(d16[n : n + 1], (8, 128)) for n in range(poles)]
        weight = [jnp.broadcast_to(w16[n : n + 1], (8, 128)) for n in range(poles)]
        skip = skip_ref[0:1, lanes]

        def token(i, states):
            at = pl.ds(i, PARTS, stride=run)
            p, keep = prod_ref[first + tile, at, :], keep_ref[at, :]
            after = [states[n] * decay[n] * keep + p for n in range(poles)]
            local_out[tile, at, :] = tree([skip * p] + [weight[n] * after[n] for n in range(poles)])
            return tuple(after)

        states = lax.fori_loop(0, run, token, tuple(jnp.zeros((8, 128), f32) for _ in range(poles)), unroll=2)
        for n in range(poles):
            state_out[tile, pl.ds(n, PARTS, stride=poles), :] = states[n]
        tap = [taps_ref[j, 0:1, lanes] for j in range(3)]
        query_out[tile] = (
            tap[0] * raw_ref[8 : 8 + T, lanes]
            + keep_ref[...] * (tap[1] * raw_ref[7 : 7 + T, lanes])
            + twice_ref[...] * (tap[2] * raw_ref[6 : 6 + T, lanes]))
        return 0

    lax.fori_loop(0, tiles, tile_body, 0)
    copy.wait()


def tree(terms):
    while len(terms) > 1:
        terms = [a + b for a, b in zip(terms[0::2], terms[1::2])] + terms[len(terms) // 2 * 2 :]
    return terms[0]


def local_pass(
    first, tiles, slot, lane_position, product, keep, twice, raw, taps, rates, residues, skip, out_weight, width, after,
):
    T, poles = product.shape[1], rates.shape[0]
    return pl.pallas_call(
        functools.partial(local_kernel, poles, first, slot),
        out_shape=(
            jax.ShapeDtypeStruct((tiles, T, 128), f32),
            jax.ShapeDtypeStruct((tiles, PARTS * poles, 128), f32),
            jax.ShapeDtypeStruct((poles, tiles * 128), f32),
            jax.ShapeDtypeStruct((tiles, T, 128), f32),
            jax.ShapeDtypeStruct((out_weight.shape[0], 2 * width), bf16),
        ),
        in_specs=[smem()] + [vmem()] * 8 + [hbm(), pl.BlockSpec(memory_space=pl.ANY)],
        out_specs=[vmem()] * 5,
        scratch_shapes=[pltpu.SemaphoreType.DMA((STREAMS,))],
        compiler_params=pltpu.CompilerParams(vmem_limit_bytes=8 * MIB),
        cost_estimate=pl.CostEstimate(flops=6 * T * poles * tiles * 128, bytes_accessed=8 * MIB, transcendentals=0),
        name="local_pass",
    )(lane_position, product, keep, twice, raw, taps, rates, residues, skip, out_weight, after)


def first_products(first, last, taps, ids_ref, base):
    s01, s0m1 = same_id(ids_ref, base + 1, base), same_id(ids_ref, base, base - 1)
    s0m2, s1m1 = same_id(ids_ref, base, base - 2), same_id(ids_ref, base + 1, base - 1)

    def shift(i):
        near, far = last[i][1:2], last[i][0:1]
        t1, t2 = taps[1][i : i + 1], taps[2][i : i + 1]
        return s0m1 * (t1 * near) + s0m2 * (t2 * far), s1m1 * (t2 * near)

    def plain(i):
        t0, t1 = taps[0][i : i + 1], taps[1][i : i + 1]
        return t0 * first[i][0:1], t0 * first[i][1:2] + s01 * (t1 * first[i][0:1])

    k, v, dk, dv = plain(1), plain(2), shift(1), shift(2)
    delta = [(k[j] + dk[j]) * (v[j] + dv[j]) - k[j] * v[j] for j in range(2)]
    return shift(0), delta


def unpack(block, poles):
    first = [None, block[poles : poles + 2], block[poles + 2 : poles + 4]]
    last = [block[poles + 4 + 2 * i : poles + 6 + 2 * i] for i in range(3)]
    return block[0:poles], first, last


def joined_state(low_state, low_last, up_state, up_first, taps, rates, ids_ref, base, length):
    _, delta = first_products(up_first, low_last, taps, ids_ref, base)
    grown = low_state + delta[0] * jnp.exp(rates) + delta[1] * jnp.exp(2.0 * rates)
    open_ = same_id(ids_ref, base + length - 1, base - 1)
    return up_state + grown * (jnp.exp(-rates * jnp.float32(length)) * open_)


def join_kernel(T, poles, span, position, ids_ref, mine_ref, other_ref, taps_ref, rates_ref, _, out):
    me = position[0]
    is_upper = (me // span) % 2 == 1
    base = (me // (2 * span)) * (2 * span * T) + span * T
    mine, other = mine_ref[...].astype(f32), other_ref[...].astype(f32)
    lower, upper = jnp.where(is_upper, other, mine), jnp.where(is_upper, mine, other)
    taps = [taps_ref[j] for j in range(3)]
    low_state, _, low_last = unpack(lower, poles)
    up_state, up_first, _ = unpack(upper, poles)
    state = joined_state(low_state, low_last, up_state, up_first, taps, rates_ref[...], ids_ref, base, span * T)
    out[0:poles, :] = state.astype(bf16)
    row = lax.broadcasted_iota(jnp.int32, (HEAD, lower.shape[1]), 0)
    out[poles : poles + HEAD, :] = jnp.where(row < 4, lower[poles:], upper[poles:]).astype(bf16)


def join(span, T, position, ids, mine, other, taps, rates, after):
    poles = rates.shape[0]
    return pl.pallas_call(
        functools.partial(join_kernel, T, poles, span),
        out_shape=jax.ShapeDtypeStruct(mine.shape, bf16),
        in_specs=[smem(), smem()] + [vmem()] * 4 + [pl.BlockSpec(memory_space=pl.ANY)],
        out_specs=vmem(),
        compiler_params=pltpu.CompilerParams(vmem_limit_bytes=4 * MIB),
        name="join",
    )(position, ids, mine, other, taps, rates, after)


def gate_kernel(
    T, poles, spans, cuts, position, lane_position, ids_ref, block_ref, visible_ref, taps_ref, rates_ref, skip_ref,
    window_ref, out_ref, *rest,
):
    arrived, rest = rest[: len(spans)], rest[len(spans) :]
    parts, rest = [rest[4 * c : 4 * c + 4] for c in range(cuts)], rest[4 * cuts :]
    gated_out, send_out, third_out, carry, full, sem = rest
    run = T // PARTS
    tiles = block_ref.shape[1] // 128
    copy = columns(lane_position[0], 2, out_ref, third_out, sem)
    copy.start()
    me = position[0]
    base = me * T
    taps = [taps_ref[j] for j in range(3)]
    rates, skip = rates_ref[...], skip_ref[...]
    weight = jnp.concatenate([pole_ref[...] for _, _, pole_ref, _ in parts], axis=1)
    each = tiles // cuts
    prior = jnp.zeros(block_ref.shape, f32)
    prior_state, prior_first, prior_last = unpack(prior, poles)
    for span, ref in zip(spans, arrived):
        state, first, last = unpack(ref[...].astype(f32), poles)
        upper, held = (me // span) % 2 == 1, me % span
        if span == 1:
            both = state
        else:
            both = joined_state(
                state, last, prior_state, prior_first, taps, rates, ids_ref, (me - held) * T, held * T)
        fresh = upper & (held == 0)
        prior_state = jnp.where(fresh, state, jnp.where(upper, both, prior_state))
        prior_first = [None] + [jnp.where(upper, first[i], prior_first[i]) for i in (1, 2)]
        prior_last = [jnp.where(fresh, last[i], prior_last[i]) for i in range(3)]
    _, first, _ = unpack(block_ref[...].astype(f32), poles)
    q_shift, delta = first_products(first, prior_last, taps, ids_ref, base)
    second = delta[1] * jnp.exp(rates)
    now = prior_state + (delta[0] + second) * jnp.exp(rates)
    fix0 = skip * delta[0] - jnp.sum(weight * second, axis=0, keepdims=True)
    fix1 = skip * delta[1]
    jump = jnp.exp(-rates * float(run))
    for s in range(PARTS):
        part = slice(s * poles, (s + 1) * poles)
        began = weight * now
        for tile in range(tiles):
            carry[tile, part, :] = began[:, tile * 128 : tile * 128 + 128]
        if s < PARTS - 1:
            whole = same_id(ids_ref, base + s * run + run - 1, base + s * run - 1)
            ends = jnp.concatenate([parts[tile // each][1][tile % each, part, :] for tile in range(tiles)], axis=1)
            now = now * (jump * whole) + ends

    def lane_body(cut, inner, _):
        tile = cut * each + inner
        lanes = pl.ds(pl.multiple_of(tile * 128, 128), 128)
        d16 = jnp.exp(-rates_ref[:, lanes])
        decay = [jnp.broadcast_to(d16[n : n + 1], (8, 128)) for n in range(poles)]
        start = tuple(carry[tile, pl.ds(n, PARTS, stride=poles), :] for n in range(poles))

        def token(i, states):
            after = [states[n] * decay[n] for n in range(poles)]
            see = visible_ref[pl.ds(pl.multiple_of(i * 8, 8), 8), :]
            at = pl.ds(i, PARTS, stride=run)
            full[tile, at, :] = parts[cut][0][inner, at, :] + see * tree(list(after))
            return tuple(after)

        lax.fori_loop(0, run, token, start, unroll=4)
        return 0

    for cut in range(cuts):
        lax.fori_loop(0, each, functools.partial(lane_body, cut), 0)
    row = lax.broadcasted_iota(jnp.int32, (16, 128), 0)
    for tile in range(tiles):
        lanes = slice(tile * 128, tile * 128 + 128)
        query_ref = parts[tile // each][3].at[tile % each]
        gated_out[:, lanes] = (query_ref[...] * full[tile]).astype(bf16)
        top_q, top = query_ref[0:16, :], full[tile, 0:16, :]
        top_q = top_q + jnp.where(row == 0, q_shift[0][:, lanes], 0.0) + jnp.where(row == 1, q_shift[1][:, lanes], 0.0)
        top = top + jnp.where(row == 0, fix0[:, lanes], 0.0) + jnp.where(row == 1, fix1[:, lanes], 0.0)
        gated_out[0:16, lanes] = (top_q * top).astype(bf16)
    share(lane_position[0], gated_out, window_ref, send_out, None)
    copy.wait()


def target(index, slot):
    chip = index // 2
    if slot == 0:
        return 3 - 3 * (chip % 2)
    if slot == 1:
        return jnp.where(chip < 2, 2, 1)
    if slot == 2:
        return jnp.where(chip < 2, 1 + 2 * chip, 2 * (chip - 2))
    return chip


class Copies:
    def __init__(self, copies):
        self.copies = copies

    def start(self):
        for copy in self.copies:
            copy.start()

    def wait(self):
        for copy in self.copies:
            copy.wait()


STREAMS = 4


def columns(index, slot, out_ref, window, sem):
    channels, both = window.shape
    start = pl.multiple_of(target(index, slot) * both, both)
    each = channels // STREAMS
    return Copies([
        pltpu.make_async_copy(
            out_ref.at[pl.ds(k * each, each), pl.ds(start, both)], window.at[pl.ds(k * each, each)], sem.at[k])
        for k in range(STREAMS)
    ])


def share(index, gated_ref, window, send_out, mine_out):
    width = window.shape[1] // 2
    tile = 256
    core = index % 2

    for out, half in ((send_out, 1 - core), (mine_out, core)):
        for j in range(width // tile if out is not None else 0):
            at = slice(j * tile, j * tile + tile)
            cols = pl.ds(pl.multiple_of(half * width + j * tile, tile), tile)
            out[:, at] = jnp.dot(gated_ref[...], window[:, cols], preferred_element_type=f32).astype(out.dtype)


def share_kernel(count, lane_position, gated_ref, *rest):
    windows, outs = rest[:count], rest[count:]
    for k, window in enumerate(windows):
        share(lane_position[0], gated_ref, window, outs[2 * k], outs[2 * k + 1])


def shares(lane_position, gated, windows, width):
    T, channels = gated.shape
    count = len(windows)
    return pl.pallas_call(
        functools.partial(share_kernel, count),
        out_shape=[jax.ShapeDtypeStruct((T, width), d) for _ in windows for d in (bf16, f32)],
        in_specs=[smem(), vmem()] + [vmem()] * count,
        out_specs=[vmem()] * (2 * count),
        compiler_params=pltpu.CompilerParams(vmem_limit_bytes=4 * MIB),
        cost_estimate=pl.CostEstimate(
            flops=4 * T * channels * width * count, bytes_accessed=4 * channels * width * count, transcendentals=0),
        name="shares",
    )(lane_position, gated, *windows)


def second_kernel(lane_position, gated_ref, first_ref, second_ref, first_mine, send_out, mine_out):
    share(lane_position[0], gated_ref, second_ref, send_out, mine_out)
    share(lane_position[0], gated_ref, first_ref, None, first_mine)


def second_shares(lane_position, gated, first, second, width):
    T, channels = gated.shape
    return pl.pallas_call(
        second_kernel,
        out_shape=[jax.ShapeDtypeStruct((T, width), d) for d in (f32, bf16, f32)],
        in_specs=[smem()] + [vmem()] * 3,
        out_specs=[vmem()] * 3,
        compiler_params=pltpu.CompilerParams(vmem_limit_bytes=4 * MIB),
        cost_estimate=pl.CostEstimate(
            flops=6 * T * channels * width, bytes_accessed=6 * channels * width, transcendentals=0),
        name="second_shares",
    )(lane_position, gated, first, second)


def late_share_kernel(slot, lane_position, gated_ref, out_ref, send_out, mine_out, window, sem):
    copy = columns(lane_position[0], slot, out_ref, window, sem)
    copy.start()
    copy.wait()
    share(lane_position[0], gated_ref, window, send_out, mine_out)


def late_share(slot, lane_position, gated, out_weight, width):
    T, channels = gated.shape
    return pl.pallas_call(
        functools.partial(late_share_kernel, slot),
        out_shape=[jax.ShapeDtypeStruct((T, width), d) for d in (bf16, f32)],
        in_specs=[smem(), vmem(), hbm()],
        out_specs=[vmem()] * 2,
        scratch_shapes=[pltpu.VMEM((channels, 2 * width), bf16), pltpu.SemaphoreType.DMA((STREAMS,))],
        compiler_params=pltpu.CompilerParams(vmem_limit_bytes=6 * MIB),
        cost_estimate=pl.CostEstimate(
            flops=4 * T * channels * width, bytes_accessed=4 * channels * width, transcendentals=0),
        name="late_share",
    )(lane_position, gated, out_weight)


def gate(T, spans, arrived, position, lane_position, ids, parts, block, visible, taps, rates, skip, window, out_weight, width):
    poles, channels = rates.shape
    return pl.pallas_call(
        functools.partial(gate_kernel, T, poles, tuple(spans), len(parts)),
        out_shape=[
            jax.ShapeDtypeStruct((T, channels), bf16),
            jax.ShapeDtypeStruct((T, width), bf16),
            pltpu.VMEM(window.shape, bf16),
        ],
        in_specs=[smem()] * 3 + [vmem()] * 6 + [hbm()] + [vmem()] * (len(spans) + 4 * len(parts)),
        out_specs=[vmem()] * 3,
        scratch_shapes=[
            pltpu.VMEM((channels // 128, PARTS * poles, 128), f32),
            pltpu.VMEM((channels // 128, T, 128), f32),
            pltpu.SemaphoreType.DMA((STREAMS,)),
        ],
        compiler_params=pltpu.CompilerParams(vmem_limit_bytes=8 * MIB),
        name="gate",
    )(position, lane_position, ids, block, visible, taps, rates, skip, window, out_weight, *arrived,
      *[a for part in parts for a in part])


def total(*terms):
    return functools.reduce(lambda a, b: a + b, [t.astype(f32) for t in terms]).astype(bf16)


def merge_kernel(count, has_inner, lane_position, *rest):
    terms, picks, out = rest[:count], rest[count:-1], rest[-1]
    value = terms[0][...].astype(f32)
    for term in terms[1:]:
        value = value + term[...].astype(f32)
    chip = lane_position[0] // 2
    inner = (chip == 1) | (chip == 2)
    for pick, wanted in zip(picks, (inner, jnp.logical_not(inner)) if has_inner else (jnp.logical_not(inner),)):
        value = value + jnp.where(wanted, pick[...].astype(f32), 0.0)
    out[...] = value.astype(out.dtype)


def merge(lane_position, dtype, terms, inner=None, outer=None):
    picks = [a for a in (inner, outer) if a is not None]
    terms = [pltpu.with_memory_space_constraint(a, pltpu.VMEM) for a in (*terms, *picks)]
    return pl.pallas_call(
        functools.partial(merge_kernel, len(terms) - len(picks), inner is not None),
        out_shape=jax.ShapeDtypeStruct(terms[0].shape, dtype),
        in_specs=[smem()] + [vmem()] * len(terms),
        out_specs=vmem(),
        compiler_params=pltpu.CompilerParams(vmem_limit_bytes=3 * MIB),
        name="merge",
    )(lane_position, *terms)


def halves_kernel(_, mine_ref, other_ref, top_out, bottom_out):
    rows = top_out.shape[0]
    value = (mine_ref[...] + other_ref[...].astype(f32)).astype(bf16)
    top_out[...] = value[:rows]
    bottom_out[...] = value[rows:]


def halves(lane_position, mine, other):
    terms = [pltpu.with_memory_space_constraint(a, pltpu.VMEM) for a in (mine, other)]
    return pl.pallas_call(
        halves_kernel,
        out_shape=(jax.ShapeDtypeStruct((mine.shape[0] // 2, mine.shape[1]), bf16),) * 2,
        in_specs=[smem()] + [vmem()] * 2,
        out_specs=[vmem()] * 2,
        compiler_params=pltpu.CompilerParams(vmem_limit_bytes=3 * MIB),
        name="halves",
    )(lane_position, *terms)


def own_kernel(lane_position, mine_ref, other_ref, near_ref, middle_ref, end_ref, again_ref, out):
    rows = middle_ref.shape[0]
    chip = lane_position[0] // 2
    outer = (chip == 0) | (chip == 3)
    value = mine_ref[...] + other_ref[...].astype(f32) + jnp.where(outer, near_ref[...].astype(f32), 0.0)
    out[0:rows, :] = value[:rows] + (middle_ref[...].astype(f32) + end_ref[...].astype(f32))
    out[rows:, :] = value[rows:] + again_ref[...].astype(f32)


def gather_own(lane_position, mine, *others):
    terms = [pltpu.with_memory_space_constraint(a, pltpu.VMEM) for a in (mine, *others)]
    return pl.pallas_call(
        own_kernel,
        out_shape=jax.ShapeDtypeStruct(mine.shape, f32),
        in_specs=[smem()] + [vmem()] * len(terms),
        out_specs=vmem(),
        compiler_params=pltpu.CompilerParams(vmem_limit_bytes=3 * MIB),
        name="gather_own",
    )(lane_position, *terms)


def scatter_line(lane_position, gated, send, windows, third, out_weight, width):
    pair = [(m, m ^ 1) for m in range(8)]

    def along(hops):
        return [(a * 2 + c, b * 2 + c) for a, b in hops for c in range(2)]

    near = along([(0, 1), (1, 0), (2, 3), (3, 2)])
    traded = lax.ppermute(send, "mp", pair)
    first_mine, send, mine = second_shares(lane_position, gated, *windows, width)
    far = merge(lane_position, bf16, (first_mine, traded))
    from_near = lax.ppermute(far, "mp", near)
    traded = lax.ppermute(send, "mp", pair)
    top, bottom = halves(lane_position, mine, traded)
    beside = lax.ppermute(bottom, "mp", near)
    from_middle = lax.ppermute(top, "mp", along([(1, 2), (2, 1)]))
    from_end = lax.ppermute(top, "mp", along([(0, 2), (3, 1)]))
    send2, mine2 = shares(lane_position, gated, [third], width)
    mine2 = merge(lane_position, f32, (mine2, lax.ppermute(send2, "mp", pair)))
    onward = merge(lane_position, bf16, (mine2,), inner=from_near)
    from_round = lax.ppermute(onward, "mp", along([(0, 1), (1, 3), (3, 2), (2, 0)]))
    send3, mine3 = late_share(3, lane_position, gated, out_weight, width)
    both = merge(lane_position, bf16, (bottom, beside))
    again = lax.ppermute(both, "mp", along([(1, 2), (2, 1)]))
    own = gather_own(lane_position, mine3, lax.ppermute(send3, "mp", pair), from_near, from_middle, from_end, again)
    return total(own, from_round)


def shifted(value, axis, steps):
    count = lax.axis_size(axis)
    leading, last = (max(0, -steps), min(count, count - steps))
    return lax.ppermute(value, axis, [(source, source + steps) for source in range(leading, last)])


def project(block, norm_gain, weights):
    floats = block.astype(jnp.float32)
    mean_square = jnp.mean(floats * floats, axis=-1, keepdims=True)
    normed = (floats * lax.rsqrt(mean_square + epsilon) * norm_gain[None, :]).astype(jnp.bfloat16)
    return jnp.dot(normed, weights, preferred_element_type=jnp.float32).astype(jnp.bfloat16)


def general(
    tokens, norm_gain, in_weight, short_filter, rates, residues, skip, out_weight, segment_ids
):
    tok_rows = tokens.shape[0]
    model_width = tokens.shape[1]
    channels = in_weight.shape[2]
    filter_taps = short_filter.shape[0]
    pole_count = rates.shape[0]
    device_index = lax.axis_index("ctx")
    row_offset = device_index * tok_rows
    weights = in_weight.reshape(model_width, 3 * channels)
    projected = project(tokens, norm_gain, weights)
    previous = shifted(projected[tok_rows - (filter_taps - 1) :], "ctx", 1)
    extended = jnp.concatenate([previous, projected], axis=0)
    padded_ids = jnp.concatenate([jnp.full((filter_taps,), -1, jnp.int32), segment_ids], axis=0)
    window = lax.dynamic_slice_in_dim(padded_ids, row_offset, tok_rows + filter_taps, 0)
    local_ids = window[filter_taps:]
    taps_table = short_filter.reshape(filter_taps, 3 * channels)
    featured = jnp.zeros((tok_rows, 3 * channels), jnp.float32)
    for lag_index in range(filter_taps):
        begin = filter_taps - 1 - lag_index
        lagged = extended[begin : begin + tok_rows].astype(jnp.float32)
        matches = window[filter_taps - lag_index : filter_taps - lag_index + tok_rows] == local_ids
        term = taps_table[lag_index][None, :] * lagged
        featured = featured + jnp.where(matches[:, None], term, jnp.zeros_like(term))
    query_part = featured[:, :channels]
    key_part = featured[:, channels : 2 * channels]
    value_part = featured[:, 2 * channels :]
    product = key_part * value_part
    offsets = jnp.arange(tok_rows, dtype=jnp.float32)
    center = float(tok_rows // 2)
    growth = jnp.exp(-(offsets - center)[:, None, None] * rates[None])
    shrinkage = jnp.exp((offsets - center)[:, None, None] * rates[None])
    weighted = (shrinkage * product[:, None, :]).reshape(tok_rows, pole_count * channels)
    visible = (offsets[:, None] >= offsets[None, :]) & (local_ids[:, None] == local_ids[None, :])
    in_block = jnp.dot(visible.astype(jnp.float32), weighted, precision=lax.Precision.HIGHEST)
    in_block = in_block.reshape(tok_rows, pole_count, channels) * growth
    survives = local_ids == window[filter_taps - 1]
    block_factor = jnp.exp(-rates * tok_rows)
    block_end = in_block[tok_rows - 1]
    block_ends = lax.all_gather(block_end[None], "ctx", axis=0, tiled=True)
    shard_count = segment_ids.shape[0] // tok_rows
    last_ids = segment_ids.reshape(shard_count, tok_rows)[:, tok_rows - 1]
    prior_ids = jnp.concatenate([jnp.full((1,), -1, jnp.int32), last_ids[:-1]], axis=0)
    shard_decays = block_factor[None] * (last_ids == prior_ids).astype(jnp.float32)[:, None, None]

    def absorb(running, inputs):
        shard, factor, shard_end = inputs
        advanced = running * factor + shard_end
        return (jnp.where(shard < device_index, advanced, running), None)

    incoming, _ = lax.scan(
        absorb,
        jnp.zeros_like(block_end),
        (jnp.arange(shard_count, dtype=jnp.int32), shard_decays, block_ends),
    )
    carried = incoming[None] * jnp.exp(-(offsets + 1.0)[:, None, None] * rates[None])
    carried = carried * survives.astype(jnp.float32)[:, None, None]
    states = in_block + carried
    pole_weight = residues * jnp.sqrt(-jnp.expm1(-2.0 * rates))
    longconv = jnp.sum(pole_weight[None] * states, axis=1)
    gated = (query_part * (longconv + skip[None, :] * product)).astype(jnp.bfloat16)
    partial_terms = jnp.dot(gated, out_weight, preferred_element_type=jnp.float32)
    return lax.psum_scatter(partial_terms, "mp", scatter_dimension=1, tiled=True).astype(
        jnp.bfloat16
    )


def local(tokens, norm_gain, in_weight, short_filter, rates, residues, skip, out_weight, segment_ids):
    T = tokens.shape[0]
    shards = lax.axis_size("ctx")
    me = lax.axis_index("ctx")
    position = me.astype(jnp.int32)[None]
    lane_position = lax.axis_index("mp").astype(jnp.int32)[None]
    width = out_weight.shape[1] // lax.axis_size("mp")
    weight3 = jnp.transpose(in_weight, (1, 0, 2))
    out_weight = pltpu.with_memory_space_constraint(out_weight, pltpu.HBM)
    raw, product, block, keep, twice, visible, taps, rates, residues, skip = front(
        position, segment_ids.reshape(-1, 128), tokens, norm_gain[None], weight3, short_filter, rates, residues, skip[None])
    cuts = shards.bit_length() - 1
    each = product.shape[0] // cuts
    group, spans, arrived, parts, windows = block, [], [], [], []
    for k in range(cuts):
        span = 1 << k
        other = lax.ppermute(group, "ctx", [(a, a ^ span) for a in range(shards)])
        spans.append(span)
        arrived.append(other)
        *part, window = local_pass(
            k * each, each, min(k, 1), lane_position, product, keep, twice, raw, taps, rates, residues, skip,
            out_weight, width, group)
        parts.append(part)
        windows.append(window)
        if k < cuts - 1:
            group = join(span, T, position, segment_ids, group, other, taps, rates, part[0])
    gated, send, third = gate(T, spans, arrived, position, lane_position, segment_ids, parts, block, visible, taps, rates,
                             skip, windows[0], out_weight, width)
    return scatter_line(lane_position, gated, send, windows[:2], third, out_weight, width)


def solution(mesh):
    placed = (
        P("ctx", None),
        P(),
        P(None, None, "mp"),
        P(None, None, "mp"),
        P(None, "mp"),
        P(None, "mp"),
        P("mp"),
        P("mp", None),
        P(),
    )
    shards, groups = mesh.shape["ctx"], mesh.shape["mp"]

    def body(tokens, norm_gain, in_weight, *rest):
        suits = groups == 8 and shards & (shards - 1) == 0 and shards > 2
        suits = suits and in_weight.shape[2] % 512 == 0 and in_weight.shape[0] % 2048 == 0
        suits = suits and tokens.shape[0] % 64 == 0 and rest[-1].shape[0] % 128 == 0 and rest[1].shape[0] % 8 == 0
        return (local if suits else general)(tokens, norm_gain, in_weight, *rest)

    return jax.shard_map(
        body, mesh=mesh, in_specs=placed, out_specs=P("ctx", "mp"), check_vma=False
    )
```
